32 devices in a mesh: dp: 8 (over z, x), mp: 4 (over y, core).
Axes of the slice: x: 2, y: 2, z: 4, core: 2. Of those that a mesh axis runs over, the one named last changes fastest.
Arguments:
- x_src: bfloat16 [4096, 1152], P('dp', 'mp')
- cotangent: bfloat16 [4096, 1152], P('dp', 'mp'), may hold values from -6 to 6
- route_dest: int32 [4096], P('dp'), may hold values from 0 to 2047, as said below
- route_count: int32 [8], P('dp'), may hold values from 8 to 512, as said below
- item_grid: int32 [8, 2], P('dp'), may hold values from 6 to 32, as said below
- noise_bin: int32 [8], P('dp'), may hold values from 0 to 15
- cond: bfloat16 [8, 1152], P('dp')
- w_ada: bfloat16 [1152, 6, 1152], P('dp', None, 'mp'), may hold values from -0.1875 to 0.1875
- b_ada: bfloat16 [6, 1152], P(None, 'mp'), may hold values from -3 to 3
- w_qkv: bfloat16 [1152, 3, 1152], P('dp', None, 'mp'), may hold values from -0.1875 to 0.1875
- q_gain: float32 [72], replicated, may hold values from 0.25 to 1.75
- k_gain: float32 [72], replicated, may hold values from 0.25 to 1.75
- w_out: bfloat16 [1152, 1152], P('mp', 'dp'), may hold values from -1.5 to 1.5
- w_gu: bfloat16 [1152, 2, 3072], P('dp', None, 'mp'), may hold values from -0.1875 to 0.1875
- w_down: bfloat16 [3072, 1152], P('mp', 'dp'), may hold values from -0.109375 to 0.109375
Outputs:
- out: bfloat16 [4096, 1152], P('dp', 'mp')
- grad_in: bfloat16 [4096, 1152], P('dp', 'mp')
- grad_cond: float32 [8, 1152], P('dp')
- grad_ada: float32 [1152, 6, 1152], P('dp', None, 'mp')
- grad_bada: float32 [6, 1152], P(None, 'mp')
- grad_qkv: float32 [1152, 3, 1152], P('dp', None, 'mp')
- grad_qgain: float32 [72], replicated
- grad_kgain: float32 [72], replicated
- grad_out: float32 [1152, 1152], P('mp', 'dp')
- grad_gu: float32 [1152, 2, 3072], P('dp', None, 'mp')
- grad_down: float32 [3072, 1152], P('mp', 'dp')
- stats: float32 [3], replicated
The draws below stay inside these ranges and needn't reach their ends.
Inputs may be any that keep to these rules, and one draw needn't show every extreme that they name: `route_dest`: slots 0 to route_count[s] - 1 of device s name distinct working rows (device r // 256, row r mod 256); every working row is named exactly once over all devices; device s names route_count[s] // 8, one more or one fewer rows of each device; no device names more than 64 rows of one device, and some pair of devices reaches 64 in every draw; slots from route_count[s] on hold 0. `route_count`: every count is a multiple of 8; some device holds 512 rows in every draw. `item_grid`: height times width is at most 256; the item's valid rows are the first height times width rows of its block; in every draw one item is 16 by 16.
All inputs are finite; a program needn't handle non-finite values.
Results may differ from the reference program's by a relative error of at most 0.012.
The reference program's roundings to bfloat16 on the way count: a program that leaves them out, or rounds other values in their place, can miss the bound.
Values may be sent and summed in bfloat16 or wider, within the bound.
A program may use at most 192 MiB of HBM per device.

```python
import math
import jax
import jax.numpy as jnp
from jax import lax

D = 1152
H = 16
DH = 72
FF = 3072
DC = 1152
GRID = 16
NBINS = 16
BLK_DEV = 1
BLOCK = 256
ROWS_DEV = 256
SRC_CAP = 512
ITEMS = 8
N_DP = 8


def route_plan(key):
    base = jax.random.fold_in(key, 7)
    k_share, k_rank, k_sign, k_rows, k_slots = jax.random.split(base, 5)
    peers = N_DP
    mean_rows = ROWS_DEV // N_DP
    groups = peers // 4
    offset = jax.random.randint(k_share, (groups,), -(mean_rows // 2), mean_rows // 2)
    shares = jnp.stack([jnp.full((groups,), 2 * mean_rows, jnp.int32), jnp.full((groups,), mean_rows // 2, jnp.int32), mean_rows + offset, mean_rows // 2 - offset], axis=1).reshape(peers)
    tilt = jnp.tile(jnp.array([0, 1, -1, 0], jnp.int32), groups)
    order = jax.random.permutation(k_rank, peers)
    shares = shares[order]
    tilt = tilt[order]
    signs = jax.random.permutation(k_sign, jnp.concatenate([jnp.ones((peers // 2,), jnp.int32), -jnp.ones((peers // 2,), jnp.int32)]))
    sends = shares[:, None] + tilt[:, None] * signs[None, :]
    col_start = jnp.cumsum(sends, axis=0) - sends
    col_end = col_start + sends
    position = jnp.arange(ROWS_DEV, dtype=jnp.int32)
    label = jnp.sum((position[None, :, None] >= col_end.T[:, None, :]).astype(jnp.int32), axis=2)
    dest_rows = jax.vmap(lambda sub_key: jax.random.permutation(sub_key, ROWS_DEV))(jax.random.split(k_rows, peers))
    row_start = jnp.cumsum(sends, axis=1) - sends
    dst_index = jnp.broadcast_to(jnp.arange(peers, dtype=jnp.int32)[:, None], (peers, ROWS_DEV))
    src_slot = row_start[label, dst_index] + position[None, :] - col_start[label, dst_index]
    counts = jnp.sum(sends, axis=1)
    slot_ids = jnp.arange(SRC_CAP, dtype=jnp.int32)[None, :]
    scores = jax.random.randint(k_slots, (peers, SRC_CAP), 0, 1 << 15) * SRC_CAP + slot_ids
    scores = jnp.where(slot_ids < counts[:, None], scores, (1 << 28) + slot_ids)
    ranked = jnp.argsort(scores, axis=1)
    new_pos = jnp.zeros((peers, SRC_CAP), jnp.int32).at[jnp.arange(peers)[:, None], ranked].set(jnp.broadcast_to(slot_ids, (peers, SRC_CAP)))
    dest = jnp.zeros((peers, SRC_CAP), jnp.int32).at[label, new_pos[label, src_slot]].set(dst_index * ROWS_DEV + dest_rows)
    return (dest, counts.astype(jnp.int32))


def draw_route_dest(key, part):
    return route_plan(key)[0].reshape(-1)


def draw_route_count(key, part):
    return route_plan(key)[1]


def draw_x_src(key, part):
    dest = route_plan(key)[0].reshape(-1)
    rise = (dest // ROWS_DEV).astype(jnp.float32) / (N_DP - 1)
    sub_key = jax.random.fold_in(key, 21)
    values = jax.random.normal(sub_key, (N_DP * SRC_CAP, D), jnp.float32)
    scale = jnp.sqrt(1.0 + 2.0 * rise)
    return (values * scale[:, None]).astype(jnp.bfloat16)


def draw_cond(key, part):
    rise = (jnp.arange(ITEMS) // BLK_DEV).astype(jnp.float32) / (N_DP - 1)
    sub_key = jax.random.fold_in(key, 41)
    values = jax.random.normal(sub_key, (ITEMS, DC), jnp.float32)
    scale = jnp.sqrt(1.0 + 2.0 * rise)
    return (values * scale[:, None]).astype(jnp.bfloat16)


def draw_item_grid(key, part):
    base = jax.random.fold_in(key, 31)
    k_width, k_cut, k_pick = jax.random.split(base, 3)
    width = jax.random.randint(k_width, (ITEMS,), GRID // 2, 2 * GRID + 1)
    tallest = BLOCK // width
    height = tallest - jax.random.randint(k_cut, (ITEMS,), 0, tallest // 4 + 1)
    chosen = jax.random.randint(k_pick, (), 0, ITEMS)
    marker = jnp.arange(ITEMS) == chosen
    width = jnp.where(marker, GRID, width)
    height = jnp.where(marker, GRID, height)
    return jnp.stack([height, width], axis=1).astype(jnp.int32)


def touch_ends(entries, own_key, low, high):
    longest = entries.shape.index(max(entries.shape))
    spots = []
    for shift in (0, 1):
        where = [jax.random.randint(jax.random.fold_in(own_key, axis), (), 0, length) for axis, length in enumerate(entries.shape)]
        where[longest] = (where[longest] + shift) % entries.shape[longest]
        spots.append(tuple(where))
    return entries.at[spots[0]].set(low).at[spots[1]].set(high)


def steps_of(rng, extent, cuts, smallest, largest):
    factor_of = 1.0
    for dim, blocks in cuts:
        steps = jax.random.uniform(jax.random.fold_in(jax.random.fold_in(rng, 6), dim), (blocks,), jnp.float32, smallest / len(cuts), largest / len(cuts))
        factor_of = factor_of * jnp.repeat(jnp.exp(steps), extent[dim] // blocks).reshape((-1,) + (1,) * (len(extent) - 1 - dim))
    return factor_of


def centred(key, extent, deviation, most, shards=(), held_as=jnp.bfloat16):
    entries = deviation * jax.random.normal(key, extent, jnp.float32)
    if shards:
        entries = entries * steps_of(key, extent, shards, -0.22, 0.18)
    return jnp.clip(entries, -most, most).astype(held_as)


def setup_inputs(seed: int = 0) -> dict:
    seeds = jax.random.split(jax.random.key(seed), 16)
    return {
        "x_src": draw_x_src(jax.random.fold_in(seeds[15], 71), 0),
        "cotangent": centred(seeds[1], (N_DP * SRC_CAP, D), 1.0, 6.0, ((0, 8), (1, 4))),
        "route_dest": draw_route_dest(jax.random.fold_in(seeds[15], 71), 0),
        "route_count": draw_route_count(jax.random.fold_in(seeds[15], 71), 0),
        "item_grid": draw_item_grid(jax.random.fold_in(seeds[15], 71), 0),
        "noise_bin": touch_ends(jax.random.randint(seeds[5], (ITEMS,), 0, NBINS), jax.random.fold_in(seeds[5], 1), 0, NBINS - 1).astype(jnp.int32),
        "cond": draw_cond(jax.random.fold_in(seeds[15], 71), 0),
        "w_ada": centred(seeds[7], (DC, 6, D), DC ** -0.5, 0.1875, ((0, 8), (2, 4))),
        "b_ada": centred(seeds[8], (6, D), 0.5, 3.0, ((1, 4),)),
        "w_qkv": centred(seeds[9], (D, 3, D), D ** -0.5, 0.1875, ((0, 8), (2, 4))),
        "q_gain": jnp.clip(1.0 + 0.15 * jax.random.normal(seeds[10], (DH,), jnp.float32), 0.25, 1.75),
        "k_gain": jnp.clip(1.0 + 0.15 * jax.random.normal(seeds[11], (DH,), jnp.float32), 0.25, 1.75),
        "w_out": centred(seeds[12], (D, D), (D // 64) ** -0.5, 1.5, ((0, 4), (1, 8))),
        "w_gu": centred(seeds[13], (D, 2, FF), D ** -0.5, 0.1875, ((0, 8), (2, 4))),
        "w_down": centred(seeds[14], (FF, D), FF ** -0.5, 0.109375, ((0, 4), (1, 8))),
    }


epsilon = 1e-06

@jax.custom_vjp
def low(v):
    return lax.optimization_barrier(v.astype(jnp.bfloat16)).astype(jnp.float32)

@jax.custom_vjp
def low_back(v):
    return v

def low_keep(v):
    return (low(v), None)

def low_pass(kept, grad):
    return (grad,)

def back_keep(v):
    return (v, None)

def back_low(kept, grad):
    return (low(grad),)
low.defvjp(low_keep, low_pass)
low_back.defvjp(back_keep, back_low)

def product(form, left, right):
    return jnp.einsum(form, left, right, precision=lax.Precision.HIGHEST)

def norm_rows(values):
    return values * lax.rsqrt(lax.optimization_barrier(jnp.mean(values * values, axis=-1, keepdims=True)) + epsilon)

def rotate(values, cos_h, sin_h, cos_w, sin_w, sign):
    quarter = values.shape[-1] // 4
    first = values[..., :quarter]
    second = values[..., quarter:2 * quarter]
    third = values[..., 2 * quarter:3 * quarter]
    fourth = values[..., 3 * quarter:]
    return jnp.concatenate([first * cos_h - sign * second * sin_h, sign * first * sin_h + second * cos_h, third * cos_w - sign * fourth * sin_w, sign * third * sin_w + fourth * cos_w], axis=-1)

def angle_tables(grid, block, head_dim):
    quarter = head_dim // 4
    place = lax.broadcasted_iota(jnp.int32, (grid.shape[0], block), 1)
    width = grid[:, 1:2]
    height_pos = (place // width).astype(jnp.float32)
    width_pos = (place % width).astype(jnp.float32)
    freqs = jnp.exp(-math.log(10000.0) * jnp.arange(quarter).astype(jnp.float32) / quarter)
    angle_h = (height_pos[:, :, None] * freqs)[:, :, None, :]
    angle_w = (width_pos[:, :, None] * freqs)[:, :, None, :]
    return (jnp.cos(angle_h), jnp.sin(angle_h), jnp.cos(angle_w), jnp.sin(angle_w))

def make_layer(item_grid):
    items = N_DP * BLK_DEV
    per_group = math.gcd(items, max(1, 4096 // BLOCK))
    groups = items // per_group

    def layer(rows_in, cond, w_ada, b_ada, w_qkv, q_gain, k_gain, w_out, w_gu, w_down):
        silu_cond = low(jax.nn.silu(cond))
        modulation = low(low_back(product('id,dkc->ikc', silu_cond, w_ada) + b_ada))

        def run_group(pieces):
            rows_grp, mod_grp, grid_grp = pieces
            count = rows_grp.shape[0]
            cos_h, sin_h, cos_w, sin_w = angle_tables(grid_grp, BLOCK, DH)
            place = lax.broadcasted_iota(jnp.int32, (count, BLOCK), 1)
            valid = place < (grid_grp[:, 0] * grid_grp[:, 1])[:, None]
            valid_wide = valid.astype(jnp.float32)[:, :, None]
            parts = [mod_grp[:, index][:, None, :] for index in range(6)]
            shift_one, scale_one, gate_one, shift_two, scale_two, gate_two = parts
            hidden_one = low(norm_rows(rows_grp) * (1.0 + scale_one) + shift_one)
            qkv = low_back(product('gbd,dkc->gbkc', hidden_one, w_qkv))
            query = qkv[:, :, 0].reshape(count, BLOCK, H, DH)
            keys = qkv[:, :, 1].reshape(count, BLOCK, H, DH)
            value = qkv[:, :, 2].reshape(count, BLOCK, H, DH)
            query_low = low(rotate(norm_rows(query) * q_gain, cos_h, sin_h, cos_w, sin_w, 1.0) * DH ** (-0.5))
            key_low = low(rotate(norm_rows(keys) * k_gain, cos_h, sin_h, cos_w, sin_w, 1.0))
            value_low = low(value)
            scores = low_back(product('gqhc,gkhc->ghqk', query_low, key_low))
            scores = jnp.where(valid[:, None, None, :], scores, -1e+30)
            prob_low = low(jax.nn.softmax(scores, axis=-1))
            attn_low = low(low_back(product('ghqk,gkhc->gqhc', prob_low, value_low)))
            attention = low_back(product('gqhc,hcd->gqd', attn_low, w_out.reshape(H, DH, D)))
            middle = rows_grp + gate_one * attention
            hidden_two = low(norm_rows(middle) * (1.0 + scale_two) + shift_two)
            gate_up = low_back(product('gbd,dkf->gbkf', hidden_two, w_gu))
            inner = low(jax.nn.silu(gate_up[:, :, 0]) * gate_up[:, :, 1])
            feed = low_back(product('gbf,fd->gbd', inner, w_down))
            result = middle + gate_two * feed
            squares = jnp.stack([jnp.sum(valid_wide * (gate_one * attention) ** 2), jnp.sum(valid_wide * (gate_two * feed) ** 2)])
            return (result, squares)
        outputs, squares = lax.map(jax.checkpoint(run_group), (rows_in.reshape(groups, per_group, BLOCK, D), modulation.reshape(groups, per_group, 6, D), item_grid.reshape(groups, per_group, 2)))
        return (outputs.reshape(items, BLOCK, D), lax.optimization_barrier(jnp.sum(squares, axis=0)))
    return layer

def reference(x_src, cotangent, route_dest, route_count, item_grid, noise_bin, cond, w_ada, b_ada, w_qkv, q_gain, k_gain, w_out, w_gu, w_down):
    items = N_DP * BLK_DEV
    total_rows = N_DP * ROWS_DEV
    slot_all = jnp.arange(N_DP * SRC_CAP).astype(jnp.int32)
    live = slot_all % SRC_CAP < route_count[slot_all // SRC_CAP]
    target = jnp.where(live, route_dest, total_rows).astype(jnp.int32)
    source_of = jnp.zeros((total_rows,), jnp.int32).at[target].set(slot_all, mode='drop')
    rows_in = x_src[source_of].astype(jnp.float32).reshape(items, BLOCK, D)
    grads_in = cotangent[source_of].astype(jnp.float32).reshape(items, BLOCK, D)
    place = lax.broadcasted_iota(jnp.int32, (items, BLOCK), 1)
    valid_wide = (place < (item_grid[:, 0] * item_grid[:, 1])[:, None]).astype(jnp.float32)
    tallies = lax.optimization_barrier(jnp.sum((noise_bin[:, None] == jnp.arange(NBINS)[None, :]).astype(jnp.float32), axis=0))
    weight = items / (NBINS * tallies[noise_bin])
    top_grad = grads_in * (weight[:, None, None] * valid_wide[:, :, None])
    layer = make_layer(item_grid)
    primal = (rows_in, cond.astype(jnp.float32), w_ada.astype(jnp.float32), b_ada.astype(jnp.float32), w_qkv.astype(jnp.float32), q_gain.astype(jnp.float32), k_gain.astype(jnp.float32), w_out.astype(jnp.float32), w_gu.astype(jnp.float32), w_down.astype(jnp.float32))
    (outputs, branch_sq), pullback = jax.vjp(layer, *primal)
    grads = pullback((top_grad, jnp.zeros_like(branch_sq)))
    res_sq = jnp.sum(valid_wide[:, :, None] * outputs * outputs)
    valid_total = jnp.sum(valid_wide)
    stats = jnp.sqrt(jnp.stack([res_sq, branch_sq[0], branch_sq[1]]) / (valid_total * D))
    safe = jnp.minimum(target, total_rows - 1)
    out_src = jnp.where(live[:, None], outputs.reshape(total_rows, D)[safe], 0.0).astype(jnp.bfloat16)
    grad_src = jnp.where(live[:, None], grads[0].reshape(total_rows, D)[safe], 0.0).astype(jnp.bfloat16)
    return (out_src, grad_src, grads[1], grads[2], grads[3], grads[4], grads[5], grads[6], grads[7], grads[8], grads[9], stats)
```

```python
import math

import jax
import jax.numpy as jnp
from jax import lax
from jax.sharding import PartitionSpec as P

D = 1152
DH = 72
NBINS = 16
BLOCK = 256
ROWS_DEV = 256
SRC_CAP = 512


epsilon = 1e-06


def grad_share(part, dim):
    sent = part.astype(jnp.bfloat16)
    total = lax.psum_scatter(sent, "dp", scatter_dimension=dim, tiled=True)
    return total.astype(jnp.float32)


def norm_rows(values):
    scale = lax.rsqrt(jnp.mean(values * values, axis=-1, keepdims=True) + epsilon)
    return (values * scale, scale)


def norm_back(grad_normed, normed, scale):
    return scale * (grad_normed - normed * jnp.mean(grad_normed * normed, axis=-1, keepdims=True))


def rotate(values, cos_h, sin_h, cos_w, sin_w, sign):
    quarter = values.shape[-1] // 4
    first = values[..., :quarter]
    second = values[..., quarter : 2 * quarter]
    third = values[..., 2 * quarter : 3 * quarter]
    fourth = values[..., 3 * quarter :]
    return jnp.concatenate(
        [
            first * cos_h - sign * second * sin_h,
            sign * first * sin_h + second * cos_h,
            third * cos_w - sign * fourth * sin_w,
            sign * third * sin_w + fourth * cos_w,
        ],
        axis=-1,
    )


def angle_tables(grid, block, head_dim):
    quarter = head_dim // 4
    place = lax.broadcasted_iota(jnp.int32, (grid.shape[0], block), 1)
    width = grid[:, 1:2]
    height_pos = (place // width).astype(jnp.float32)
    width_pos = (place % width).astype(jnp.float32)
    freqs = jnp.exp(-math.log(10000.0) * jnp.arange(quarter).astype(jnp.float32) / quarter)
    angle_h = (height_pos[:, :, None] * freqs)[:, :, None, :]
    angle_w = (width_pos[:, :, None] * freqs)[:, :, None, :]
    return (jnp.cos(angle_h), jnp.sin(angle_h), jnp.cos(angle_w), jnp.sin(angle_w))


def row_share(values):
    return lax.psum_scatter(values, "mp", scatter_dimension=0, tiled=True)


def row_whole(values):
    return lax.all_gather(values, "mp", axis=0, tiled=True)


def body(
    x_src,
    cotangent,
    route_dest,
    route_count,
    item_grid,
    noise_bin,
    cond,
    w_ada,
    b_ada,
    w_qkv,
    q_gain,
    k_gain,
    w_out,
    w_gu,
    w_down,
):
    peers = lax.axis_size("dp")
    model_rank = lax.axis_index("mp")
    blocks_here = item_grid.shape[0]
    local_width = x_src.shape[1]
    heads_here = local_width // DH
    slot_rows = 2 * ROWS_DEV // peers
    share = ROWS_DEV // lax.axis_size("mp")
    row_first = model_rank * share
    live = jnp.arange(SRC_CAP) < route_count[0]
    target = route_dest // ROWS_DEV
    member = (target[:, None] == jnp.arange(peers)[None, :]) & live[:, None]
    running = jnp.cumsum(member.astype(jnp.int32), axis=0)
    rank_in = jnp.sum(running * member, axis=1) - 1
    place = jnp.where(live, target * slot_rows + rank_in, peers * slot_rows)
    send_rows = (
        jnp.zeros((peers * slot_rows, local_width), jnp.bfloat16).at[place].set(x_src, mode="drop")
    )
    send_grads = (
        jnp.zeros((peers * slot_rows, local_width), jnp.bfloat16)
        .at[place]
        .set(cotangent, mode="drop")
    )
    send_index = (
        jnp.full((peers * slot_rows,), ROWS_DEV, jnp.int32)
        .at[place]
        .set(route_dest % ROWS_DEV, mode="drop")
    )
    recv_rows, recv_grads, recv_index = (
        lax.all_to_all(
            send_rows.reshape(peers, slot_rows, local_width),
            "dp",
            split_axis=0,
            concat_axis=0,
            tiled=True,
        ),
        lax.all_to_all(
            send_grads.reshape(peers, slot_rows, local_width),
            "dp",
            split_axis=0,
            concat_axis=0,
            tiled=True,
        ),
        lax.all_to_all(
            send_index.reshape(peers, slot_rows), "dp", split_axis=0, concat_axis=0, tiled=True
        ),
    )
    flat_index = recv_index.reshape(-1)
    rows_cols = (
        jnp.zeros((ROWS_DEV, local_width), jnp.bfloat16)
        .at[flat_index]
        .set(recv_rows.reshape(-1, local_width), mode="drop")
    )
    grads_cols = (
        jnp.zeros((ROWS_DEV, local_width), jnp.bfloat16)
        .at[flat_index]
        .set(recv_grads.reshape(-1, local_width), mode="drop")
    )
    qkv_full, out_full, gu_full, down_full = (
        lax.all_gather(w_qkv, "dp", axis=0, tiled=True),
        lax.all_gather(w_out, "dp", axis=1, tiled=True),
        lax.all_gather(w_gu, "dp", axis=0, tiled=True),
        lax.all_gather(w_down, "dp", axis=1, tiled=True),
    )
    cond_wide = cond.astype(jnp.float32)
    cond_sig = jax.nn.sigmoid(cond_wide)
    silu_cond = (cond_wide * cond_sig).astype(jnp.bfloat16)
    ada_rows = w_ada.shape[0]
    silu_all = lax.all_gather(silu_cond, "dp", axis=0, tiled=True)
    silu_own = lax.dynamic_slice_in_dim(silu_all, lax.axis_index("dp") * ada_rows, ada_rows, 1)
    mod_sums = jnp.einsum("id,dkc->ikc", silu_own, w_ada, preferred_element_type=jnp.float32)
    mod_part = (
        lax.psum_scatter(mod_sums, "dp", scatter_dimension=0, tiled=True)
        + b_ada.astype(jnp.float32)
    ).astype(jnp.bfloat16)
    rows_full, grads_full, mod_full = (
        lax.all_gather(rows_cols, "mp", axis=1, tiled=True),
        lax.all_gather(grads_cols, "mp", axis=1, tiled=True),
        lax.all_gather(mod_part, "mp", axis=2, tiled=True),
    )
    modulation = mod_full.astype(jnp.float32)
    shift_one = modulation[:, 0][:, None, :]
    scale_one = modulation[:, 1][:, None, :]
    gate_two = modulation[:, 5][:, None, :]
    resid = rows_full.astype(jnp.float32).reshape(blocks_here, BLOCK, D)
    normed_one, inv_one = norm_rows(resid)
    hidden_one = (normed_one * (1.0 + scale_one) + shift_one).astype(jnp.bfloat16)
    qkv = jnp.einsum("ibd,dkc->ibkc", hidden_one, qkv_full, preferred_element_type=jnp.float32)
    query = qkv[:, :, 0].reshape(blocks_here, BLOCK, heads_here, DH)
    keys = qkv[:, :, 1].reshape(blocks_here, BLOCK, heads_here, DH)
    value = qkv[:, :, 2].reshape(blocks_here, BLOCK, heads_here, DH)
    query_normed, query_inv = norm_rows(query)
    key_normed, key_inv = norm_rows(keys)
    cos_h, sin_h, cos_w, sin_w = angle_tables(item_grid, BLOCK, DH)
    query_low = (
        rotate(query_normed * q_gain, cos_h, sin_h, cos_w, sin_w, 1.0) * DH ** (-0.5)
    ).astype(jnp.bfloat16)
    key_low = rotate(key_normed * k_gain, cos_h, sin_h, cos_w, sin_w, 1.0).astype(jnp.bfloat16)
    value_low = value.astype(jnp.bfloat16)
    positions = lax.broadcasted_iota(jnp.int32, (blocks_here, BLOCK), 1)
    valid = positions < (item_grid[:, 0] * item_grid[:, 1])[:, None]
    key_ok = valid[:, None, None, :]
    valid_wide = valid.astype(jnp.float32)[:, :, None]
    valid_share = lax.dynamic_slice_in_dim(
        valid.astype(jnp.float32).reshape(ROWS_DEV), row_first, share, 0
    )[:, None]
    bin_onehot = (noise_bin[:, None] == jnp.arange(NBINS)[None, :]).astype(jnp.float32)
    bin_local = jnp.sum(bin_onehot, axis=0) * (model_rank == 0).astype(jnp.float32)

    def masked_scores():
        raw = jnp.einsum("iqhc,ikhc->ihqk", query_low, key_low, preferred_element_type=jnp.float32)
        return jnp.where(key_ok, raw, -1e30)

    scores = masked_scores()
    top = jnp.max(scores, axis=-1, keepdims=True)
    log_total = top + jnp.log(jnp.sum(jnp.exp(scores - top), axis=-1, keepdims=True))
    prob_low = jnp.exp(scores - log_total).astype(jnp.bfloat16)
    attn_low = jnp.einsum(
        "ihqk,ikhc->iqhc", prob_low, value_low, preferred_element_type=jnp.float32
    ).astype(jnp.bfloat16)
    out_heads = out_full.reshape(heads_here, DH, D)
    attn_part = jnp.einsum("iqhc,hcd->iqd", attn_low, out_heads, preferred_element_type=jnp.float32)

    def own_rows_of(values):
        return lax.dynamic_slice_in_dim(values.reshape(ROWS_DEV, D), row_first, share, 0)

    row_item = (row_first + jnp.arange(share)) // BLOCK
    item_onehot = (row_item[:, None] == jnp.arange(blocks_here)[None, :]).astype(jnp.float32)

    def per_item(values):
        return jnp.einsum("si,sd->id", item_onehot, values, precision=lax.Precision.HIGHEST)

    mod_rows = jnp.einsum("si,ikd->skd", item_onehot, modulation, precision=lax.Precision.HIGHEST)
    scale_one_r = mod_rows[:, 1]
    gate_one_r = mod_rows[:, 2]
    shift_two_r = mod_rows[:, 3]
    scale_two_r = mod_rows[:, 4]
    gate_two_r = mod_rows[:, 5]
    resid_share = own_rows_of(resid)
    normed_one_share = own_rows_of(normed_one)
    inv_one_share = lax.dynamic_slice_in_dim(inv_one.reshape(ROWS_DEV, 1), row_first, share, 0)
    attention_share = row_share(attn_part.reshape(ROWS_DEV, D))
    mid_share = resid_share + gate_one_r * attention_share
    normed_two_share, inv_two_share = norm_rows(mid_share)
    hidden_two_share = (normed_two_share * (1.0 + scale_two_r) + shift_two_r).astype(jnp.bfloat16)
    hidden_two = row_whole(hidden_two_share).reshape(blocks_here, BLOCK, D)
    gate_up = jnp.einsum("ibd,dkf->ibkf", hidden_two, gu_full, preferred_element_type=jnp.float32)
    gate_raw = gate_up[:, :, 0]
    up_raw = gate_up[:, :, 1]
    gate_sig = jax.nn.sigmoid(gate_raw)
    gate_act = gate_raw * gate_sig
    inner = (gate_act * up_raw).astype(jnp.bfloat16)
    feed_part = jnp.einsum("ibf,fd->ibd", inner, down_full, preferred_element_type=jnp.float32)
    feed_part, kept = (feed_part, (inner, up_raw, gate_raw, gate_sig, gate_act))
    feed_share = row_share(feed_part.reshape(ROWS_DEV, D))
    result_share = mid_share + gate_two_r * feed_share
    result_whole = row_whole(result_share.astype(jnp.bfloat16))
    squares = jnp.stack(
        [
            jnp.sum(valid_share * result_share * result_share),
            jnp.sum(valid_share * (gate_one_r * attention_share) ** 2),
            jnp.sum(valid_share * (gate_two_r * feed_share) ** 2),
        ]
    )
    square_total, valid_total, bin_total = lax.psum(
        (squares, jnp.sum(valid_share), bin_local), ("dp", "mp")
    )
    stats_value = jnp.sqrt(square_total / (valid_total * D))
    item_count = jnp.sum(bin_onehot * bin_total[None, :], axis=1)
    weight_value = blocks_here * peers / (NBINS * item_count)
    top_grad = grads_full.astype(jnp.float32).reshape(blocks_here, BLOCK, D) * (
        weight_value[:, None, None] * valid_wide
    )
    top_share = own_rows_of(top_grad)
    feed_grad = (gate_two * top_grad).astype(jnp.bfloat16)
    grad_gate_two = per_item(top_share * feed_share)
    inner, up_raw, gate_raw, gate_sig, gate_act = kept
    inner_grad = jnp.einsum("ibd,fd->ibf", feed_grad, down_full, preferred_element_type=jnp.float32)
    grad_down_part = jnp.einsum("ibf,ibd->fd", inner, feed_grad, preferred_element_type=jnp.float32)
    gate_grad = (inner_grad * up_raw * gate_sig * (1.0 + gate_raw * (1.0 - gate_sig))).astype(
        jnp.bfloat16
    )
    up_grad = (inner_grad * gate_act).astype(jnp.bfloat16)
    gate_up_grad = jnp.stack([gate_grad, up_grad], axis=2)
    grad_gu_part = jnp.einsum(
        "ibd,ibkf->dkf", hidden_two, gate_up_grad, preferred_element_type=jnp.float32
    )
    hidden_two_part = jnp.einsum(
        "ibkf,dkf->ibd", gate_up_grad, gu_full, preferred_element_type=jnp.float32
    )
    grad_down, grad_gu, hidden_two_part = (grad_down_part, grad_gu_part, hidden_two_part)
    h2_grad_share = row_share(hidden_two_part.reshape(ROWS_DEV, D))
    grad_shift_two = per_item(h2_grad_share)
    grad_scale_two = per_item(h2_grad_share * normed_two_share)
    mid_grad_share = top_share + norm_back(
        h2_grad_share * (1.0 + scale_two_r), normed_two_share, inv_two_share
    )
    attention_grad_share = (gate_one_r * mid_grad_share).astype(jnp.bfloat16)
    grad_gate_one = per_item(mid_grad_share * attention_share)
    attention_grad = row_whole(attention_grad_share).reshape(blocks_here, BLOCK, D)
    attn_low_grad = jnp.einsum(
        "iqd,hcd->iqhc", attention_grad, out_heads, preferred_element_type=jnp.float32
    ).astype(jnp.bfloat16)
    grad_out_part = jnp.einsum(
        "iqhc,iqd->hcd", attn_low, attention_grad, preferred_element_type=jnp.float32
    ).reshape(local_width, D)
    prob_full = jnp.exp(masked_scores() - log_total)
    prob_grad = jnp.einsum(
        "iqhc,ikhc->ihqk", attn_low_grad, value_low, preferred_element_type=jnp.float32
    )
    value_grad = jnp.einsum(
        "ihqk,iqhc->ikhc", prob_low, attn_low_grad, preferred_element_type=jnp.float32
    )
    score_grad = (
        prob_full * (prob_grad - jnp.sum(prob_full * prob_grad, axis=-1, keepdims=True))
    ).astype(jnp.bfloat16)
    query_rot_grad = jnp.einsum(
        "ihqk,ikhc->iqhc", score_grad, key_low, preferred_element_type=jnp.float32
    ) * DH ** (-0.5)
    key_rot_grad = jnp.einsum(
        "ihqk,iqhc->ikhc", score_grad, query_low, preferred_element_type=jnp.float32
    )
    query_scaled_grad = rotate(query_rot_grad, cos_h, sin_h, cos_w, sin_w, -1.0)
    key_scaled_grad = rotate(key_rot_grad, cos_h, sin_h, cos_w, sin_w, -1.0)
    qgain_local = jnp.sum(query_scaled_grad * query_normed, axis=(0, 1, 2))
    kgain_local = jnp.sum(key_scaled_grad * key_normed, axis=(0, 1, 2))
    query_grad = norm_back(query_scaled_grad * q_gain, query_normed, query_inv)
    key_grad = norm_back(key_scaled_grad * k_gain, key_normed, key_inv)
    qkv_grad = jnp.stack(
        [
            query_grad.reshape(blocks_here, BLOCK, local_width),
            key_grad.reshape(blocks_here, BLOCK, local_width),
            value_grad.reshape(blocks_here, BLOCK, local_width),
        ],
        axis=2,
    ).astype(jnp.bfloat16)
    grad_qkv_part = jnp.einsum(
        "ibd,ibkc->dkc", hidden_one, qkv_grad, preferred_element_type=jnp.float32
    )
    hidden_one_part = jnp.einsum(
        "ibkc,dkc->ibd", qkv_grad, qkv_full, preferred_element_type=jnp.float32
    )
    grad_out, grad_qkv, qgain_part, kgain_part, hidden_one_part = (
        grad_out_part,
        grad_qkv_part,
        qgain_local,
        kgain_local,
        hidden_one_part,
    )
    h1_grad_share = row_share(hidden_one_part.reshape(ROWS_DEV, D))
    grad_shift_one = per_item(h1_grad_share)
    grad_scale_one = per_item(h1_grad_share * normed_one_share)
    input_share = mid_grad_share + norm_back(
        h1_grad_share * (1.0 + scale_one_r), normed_one_share, inv_one_share
    )
    input_whole = row_whole(input_share.astype(jnp.bfloat16))
    mod_partial = jnp.stack(
        [
            grad_shift_one,
            grad_scale_one,
            grad_gate_one,
            grad_shift_two,
            grad_scale_two,
            grad_gate_two,
        ],
        axis=1,
    )
    mod_grad = lax.psum(mod_partial, "mp").astype(jnp.bfloat16)
    mod_grad_own = lax.dynamic_slice_in_dim(mod_grad, model_rank * local_width, local_width, 2)
    mod_all = lax.all_gather(mod_grad_own, "dp", axis=0, tiled=True)
    cond_part = jnp.einsum("ikc,dkc->id", mod_all, w_ada, preferred_element_type=jnp.float32)
    cond_sum = lax.psum(cond_part, "mp")
    cond_total = lax.all_to_all(
        cond_sum.reshape(peers, blocks_here, ada_rows), "dp", split_axis=0, concat_axis=0, tiled=True
    )
    cond_total = jnp.moveaxis(cond_total, 0, 1).reshape(blocks_here, peers * ada_rows)
    grad_cond = cond_total * cond_sig * (1.0 + cond_wide * (1.0 - cond_sig))
    grad_ada = jnp.einsum("ir,ikc->rkc", silu_own, mod_all, preferred_element_type=jnp.float32)
    grad_bada = jnp.sum(mod_all.astype(jnp.float32), axis=0)
    qgain_total, kgain_total = lax.psum((qgain_part, kgain_part), ("dp", "mp"))
    qkv_own, out_own, gu_own, down_own = (
        grad_share(grad_qkv, 0),
        grad_share(grad_out, 1),
        grad_share(grad_gu, 0),
        grad_share(grad_down, 1),
    )
    result_cols = lax.dynamic_slice_in_dim(result_whole, model_rank * local_width, local_width, 1)
    input_cols = lax.dynamic_slice_in_dim(input_whole, model_rank * local_width, local_width, 1)
    back_index = jnp.minimum(flat_index, ROWS_DEV - 1)
    back_rows = result_cols[back_index].reshape(peers, slot_rows, local_width)
    back_grads = input_cols[back_index].reshape(peers, slot_rows, local_width)
    returned_rows, returned_grads = (
        lax.all_to_all(back_rows, "dp", split_axis=0, concat_axis=0, tiled=True),
        lax.all_to_all(back_grads, "dp", split_axis=0, concat_axis=0, tiled=True),
    )
    pick = jnp.minimum(place, peers * slot_rows - 1)
    empty = jnp.zeros((), jnp.bfloat16)
    out_rows = jnp.where(live[:, None], returned_rows.reshape(-1, local_width)[pick], empty)
    out_grads = jnp.where(live[:, None], returned_grads.reshape(-1, local_width)[pick], empty)
    return (
        out_rows,
        out_grads,
        grad_cond,
        grad_ada,
        grad_bada,
        qkv_own,
        qgain_total,
        kgain_total,
        out_own,
        gu_own,
        down_own,
        stats_value,
    )


def solution(mesh):
    return jax.shard_map(
        body,
        mesh=mesh,
        in_specs=(
            P("dp", "mp"),
            P("dp", "mp"),
            P("dp"),
            P("dp"),
            P("dp", None),
            P("dp"),
            P("dp", None),
            P("dp", None, "mp"),
            P(None, "mp"),
            P("dp", None, "mp"),
            P(),
            P(),
            P("mp", "dp"),
            P("dp", None, "mp"),
            P("mp", "dp"),
        ),
        out_specs=(
            P("dp", "mp"),
            P("dp", "mp"),
            P("dp", None),
            P("dp", None, "mp"),
            P(None, "mp"),
            P("dp", None, "mp"),
            P(),
            P(),
            P("mp", "dp"),
            P("dp", None, "mp"),
            P("mp", "dp"),
            P(),
        ),
        check_vma=False,
    )
```

```python
import functools
import math

import jax
import jax.numpy as jnp
from jax import lax
from jax.experimental import pallas as pl
from jax.experimental.pallas import tpu as pltpu
from jax.sharding import PartitionSpec as P

D = 1152
DH = 72
NBINS = 16
BLOCK = 256
ROWS_DEV = 256
SRC_CAP = 512


epsilon = 1e-06


def grad_share(part, dim):
    sent = part.astype(jnp.bfloat16)
    total = lax.psum_scatter(sent, "dp", scatter_dimension=dim, tiled=True)
    return total.astype(jnp.float32)


def norm_rows(values):
    scale = lax.rsqrt(jnp.mean(values * values, axis=-1, keepdims=True) + epsilon)
    return (values * scale, scale)


def norm_back(grad_normed, normed, scale):
    return scale * (grad_normed - normed * jnp.mean(grad_normed * normed, axis=-1, keepdims=True))


def rotate(values, cos_h, sin_h, cos_w, sin_w, sign):
    quarter = values.shape[-1] // 4
    first = values[..., :quarter]
    second = values[..., quarter : 2 * quarter]
    third = values[..., 2 * quarter : 3 * quarter]
    fourth = values[..., 3 * quarter :]
    return jnp.concatenate(
        [
            first * cos_h - sign * second * sin_h,
            sign * first * sin_h + second * cos_h,
            third * cos_w - sign * fourth * sin_w,
            sign * third * sin_w + fourth * cos_w,
        ],
        axis=-1,
    )


def angle_tables(grid, block, head_dim):
    quarter = head_dim // 4
    place = lax.broadcasted_iota(jnp.int32, (grid.shape[0], block), 1)
    width = grid[:, 1:2]
    height_pos = (place // width).astype(jnp.float32)
    width_pos = (place % width).astype(jnp.float32)
    freqs = jnp.exp(-math.log(10000.0) * jnp.arange(quarter).astype(jnp.float32) / quarter)
    angle_h = (height_pos[:, :, None] * freqs)[:, :, None, :]
    angle_w = (width_pos[:, :, None] * freqs)[:, :, None, :]
    return (jnp.cos(angle_h), jnp.sin(angle_h), jnp.cos(angle_w), jnp.sin(angle_w))


def row_share(values):
    return lax.psum_scatter(values, "mp", scatter_dimension=0, tiled=True)


def row_whole(values):
    return lax.all_gather(values, "mp", axis=0, tiled=True)


def body(
    x_src,
    cotangent,
    route_dest,
    route_count,
    item_grid,
    noise_bin,
    cond,
    w_ada,
    b_ada,
    w_qkv,
    q_gain,
    k_gain,
    w_out,
    w_gu,
    w_down,
):
    peers = lax.axis_size("dp")
    model_rank = lax.axis_index("mp")
    blocks_here = item_grid.shape[0]
    local_width = x_src.shape[1]
    heads_here = local_width // DH
    slot_rows = 2 * ROWS_DEV // peers
    share = ROWS_DEV // lax.axis_size("mp")
    row_first = model_rank * share
    live = jnp.arange(SRC_CAP) < route_count[0]
    target = route_dest // ROWS_DEV
    member = (target[:, None] == jnp.arange(peers)[None, :]) & live[:, None]
    running = jnp.cumsum(member.astype(jnp.int32), axis=0)
    rank_in = jnp.sum(running * member, axis=1) - 1
    place = jnp.where(live, target * slot_rows + rank_in, peers * slot_rows)
    send_rows = (
        jnp.zeros((peers * slot_rows, local_width), jnp.bfloat16).at[place].set(x_src, mode="drop")
    )
    send_grads = (
        jnp.zeros((peers * slot_rows, local_width), jnp.bfloat16)
        .at[place]
        .set(cotangent, mode="drop")
    )
    send_index = (
        jnp.full((peers * slot_rows,), ROWS_DEV, jnp.int32)
        .at[place]
        .set(route_dest % ROWS_DEV, mode="drop")
    )
    recv_rows, recv_grads, recv_index = (
        lax.all_to_all(
            send_rows.reshape(peers, slot_rows, local_width),
            "dp",
            split_axis=0,
            concat_axis=0,
            tiled=True,
        ),
        lax.all_to_all(
            send_grads.reshape(peers, slot_rows, local_width),
            "dp",
            split_axis=0,
            concat_axis=0,
            tiled=True,
        ),
        lax.all_to_all(
            send_index.reshape(peers, slot_rows), "dp", split_axis=0, concat_axis=0, tiled=True
        ),
    )
    flat_index = recv_index.reshape(-1)
    rows_cols = (
        jnp.zeros((ROWS_DEV, local_width), jnp.bfloat16)
        .at[flat_index]
        .set(recv_rows.reshape(-1, local_width), mode="drop")
    )
    grads_cols = (
        jnp.zeros((ROWS_DEV, local_width), jnp.bfloat16)
        .at[flat_index]
        .set(recv_grads.reshape(-1, local_width), mode="drop")
    )
    qkv_full, out_full, gu_full, down_full = (
        lax.all_gather(w_qkv, "dp", axis=0, tiled=True),
        lax.all_gather(w_out, "dp", axis=1, tiled=True),
        lax.all_gather(w_gu, "dp", axis=0, tiled=True),
        lax.all_gather(w_down, "dp", axis=1, tiled=True),
    )
    cond_wide = cond.astype(jnp.float32)
    cond_sig = jax.nn.sigmoid(cond_wide)
    silu_cond = (cond_wide * cond_sig).astype(jnp.bfloat16)
    ada_rows = w_ada.shape[0]
    silu_all = lax.all_gather(silu_cond, "dp", axis=0, tiled=True)
    silu_own = lax.dynamic_slice_in_dim(silu_all, lax.axis_index("dp") * ada_rows, ada_rows, 1)
    mod_sums = jnp.einsum("id,dkc->ikc", silu_own, w_ada, preferred_element_type=jnp.float32)
    mod_part = (
        lax.psum_scatter(mod_sums, "dp", scatter_dimension=0, tiled=True)
        + b_ada.astype(jnp.float32)
    ).astype(jnp.bfloat16)
    rows_full, grads_full, mod_full = (
        lax.all_gather(rows_cols, "mp", axis=1, tiled=True),
        lax.all_gather(grads_cols, "mp", axis=1, tiled=True),
        lax.all_gather(mod_part, "mp", axis=2, tiled=True),
    )
    modulation = mod_full.astype(jnp.float32)
    shift_one = modulation[:, 0][:, None, :]
    scale_one = modulation[:, 1][:, None, :]
    gate_two = modulation[:, 5][:, None, :]
    resid = rows_full.astype(jnp.float32).reshape(blocks_here, BLOCK, D)
    normed_one, inv_one = norm_rows(resid)
    hidden_one = (normed_one * (1.0 + scale_one) + shift_one).astype(jnp.bfloat16)
    qkv = jnp.einsum("ibd,dkc->ibkc", hidden_one, qkv_full, preferred_element_type=jnp.float32)
    query = qkv[:, :, 0].reshape(blocks_here, BLOCK, heads_here, DH)
    keys = qkv[:, :, 1].reshape(blocks_here, BLOCK, heads_here, DH)
    value = qkv[:, :, 2].reshape(blocks_here, BLOCK, heads_here, DH)
    query_normed, query_inv = norm_rows(query)
    key_normed, key_inv = norm_rows(keys)
    cos_h, sin_h, cos_w, sin_w = angle_tables(item_grid, BLOCK, DH)
    query_low = (
        rotate(query_normed * q_gain, cos_h, sin_h, cos_w, sin_w, 1.0) * DH ** (-0.5)
    ).astype(jnp.bfloat16)
    key_low = rotate(key_normed * k_gain, cos_h, sin_h, cos_w, sin_w, 1.0).astype(jnp.bfloat16)
    value_low = value.astype(jnp.bfloat16)
    positions = lax.broadcasted_iota(jnp.int32, (blocks_here, BLOCK), 1)
    valid = positions < (item_grid[:, 0] * item_grid[:, 1])[:, None]
    key_ok = valid[:, None, None, :]
    valid_wide = valid.astype(jnp.float32)[:, :, None]
    valid_share = lax.dynamic_slice_in_dim(
        valid.astype(jnp.float32).reshape(ROWS_DEV), row_first, share, 0
    )[:, None]
    bin_onehot = (noise_bin[:, None] == jnp.arange(NBINS)[None, :]).astype(jnp.float32)
    bin_local = jnp.sum(bin_onehot, axis=0) * (model_rank == 0).astype(jnp.float32)

    def masked_scores():
        raw = jnp.einsum("iqhc,ikhc->ihqk", query_low, key_low, preferred_element_type=jnp.float32)
        return jnp.where(key_ok, raw, -1e30)

    scores = masked_scores()
    top = jnp.max(scores, axis=-1, keepdims=True)
    log_total = top + jnp.log(jnp.sum(jnp.exp(scores - top), axis=-1, keepdims=True))
    prob_low = jnp.exp(scores - log_total).astype(jnp.bfloat16)
    attn_low = jnp.einsum(
        "ihqk,ikhc->iqhc", prob_low, value_low, preferred_element_type=jnp.float32
    ).astype(jnp.bfloat16)
    out_heads = out_full.reshape(heads_here, DH, D)
    attn_part = jnp.einsum("iqhc,hcd->iqd", attn_low, out_heads, preferred_element_type=jnp.float32)

    def own_rows_of(values):
        return lax.dynamic_slice_in_dim(values.reshape(ROWS_DEV, D), row_first, share, 0)

    row_item = (row_first + jnp.arange(share)) // BLOCK
    item_onehot = (row_item[:, None] == jnp.arange(blocks_here)[None, :]).astype(jnp.float32)

    def per_item(values):
        return jnp.einsum("si,sd->id", item_onehot, values, precision=lax.Precision.HIGHEST)

    mod_rows = jnp.einsum("si,ikd->skd", item_onehot, modulation, precision=lax.Precision.HIGHEST)
    scale_one_r = mod_rows[:, 1]
    gate_one_r = mod_rows[:, 2]
    shift_two_r = mod_rows[:, 3]
    scale_two_r = mod_rows[:, 4]
    gate_two_r = mod_rows[:, 5]
    resid_share = own_rows_of(resid)
    normed_one_share = own_rows_of(normed_one)
    inv_one_share = lax.dynamic_slice_in_dim(inv_one.reshape(ROWS_DEV, 1), row_first, share, 0)
    attention_share = row_share(attn_part.reshape(ROWS_DEV, D))
    mid_share = resid_share + gate_one_r * attention_share
    normed_two_share, inv_two_share = norm_rows(mid_share)
    hidden_two_share = (normed_two_share * (1.0 + scale_two_r) + shift_two_r).astype(jnp.bfloat16)
    hidden_two = row_whole(hidden_two_share).reshape(blocks_here, BLOCK, D)
    gate_up = jnp.einsum("ibd,dkf->ibkf", hidden_two, gu_full, preferred_element_type=jnp.float32)
    gate_raw = gate_up[:, :, 0]
    up_raw = gate_up[:, :, 1]
    gate_sig = jax.nn.sigmoid(gate_raw)
    gate_act = gate_raw * gate_sig
    inner = (gate_act * up_raw).astype(jnp.bfloat16)
    feed_part = jnp.einsum("ibf,fd->ibd", inner, down_full, preferred_element_type=jnp.float32)
    feed_part, kept = (feed_part, (inner, up_raw, gate_raw, gate_sig, gate_act))
    feed_share = row_share(feed_part.reshape(ROWS_DEV, D))
    result_share = mid_share + gate_two_r * feed_share
    result_whole = row_whole(result_share.astype(jnp.bfloat16))
    squares = jnp.stack(
        [
            jnp.sum(valid_share * result_share * result_share),
            jnp.sum(valid_share * (gate_one_r * attention_share) ** 2),
            jnp.sum(valid_share * (gate_two_r * feed_share) ** 2),
        ]
    )
    square_total, valid_total, bin_total = lax.psum(
        (squares, jnp.sum(valid_share), bin_local), ("dp", "mp")
    )
    stats_value = jnp.sqrt(square_total / (valid_total * D))
    item_count = jnp.sum(bin_onehot * bin_total[None, :], axis=1)
    weight_value = blocks_here * peers / (NBINS * item_count)
    top_grad = grads_full.astype(jnp.float32).reshape(blocks_here, BLOCK, D) * (
        weight_value[:, None, None] * valid_wide
    )
    top_share = own_rows_of(top_grad)
    feed_grad = (gate_two * top_grad).astype(jnp.bfloat16)
    grad_gate_two = per_item(top_share * feed_share)
    inner, up_raw, gate_raw, gate_sig, gate_act = kept
    inner_grad = jnp.einsum("ibd,fd->ibf", feed_grad, down_full, preferred_element_type=jnp.float32)
    grad_down_part = jnp.einsum("ibf,ibd->fd", inner, feed_grad, preferred_element_type=jnp.float32)
    gate_grad = (inner_grad * up_raw * gate_sig * (1.0 + gate_raw * (1.0 - gate_sig))).astype(
        jnp.bfloat16
    )
    up_grad = (inner_grad * gate_act).astype(jnp.bfloat16)
    gate_up_grad = jnp.stack([gate_grad, up_grad], axis=2)
    grad_gu_part = jnp.einsum(
        "ibd,ibkf->dkf", hidden_two, gate_up_grad, preferred_element_type=jnp.float32
    )
    hidden_two_part = jnp.einsum(
        "ibkf,dkf->ibd", gate_up_grad, gu_full, preferred_element_type=jnp.float32
    )
    grad_down, grad_gu, hidden_two_part = (grad_down_part, grad_gu_part, hidden_two_part)
    h2_grad_share = row_share(hidden_two_part.reshape(ROWS_DEV, D))
    grad_shift_two = per_item(h2_grad_share)
    grad_scale_two = per_item(h2_grad_share * normed_two_share)
    mid_grad_share = top_share + norm_back(
        h2_grad_share * (1.0 + scale_two_r), normed_two_share, inv_two_share
    )
    attention_grad_share = (gate_one_r * mid_grad_share).astype(jnp.bfloat16)
    grad_gate_one = per_item(mid_grad_share * attention_share)
    attention_grad = row_whole(attention_grad_share).reshape(blocks_here, BLOCK, D)
    attn_low_grad = jnp.einsum(
        "iqd,hcd->iqhc", attention_grad, out_heads, preferred_element_type=jnp.float32
    ).astype(jnp.bfloat16)
    grad_out_part = jnp.einsum(
        "iqhc,iqd->hcd", attn_low, attention_grad, preferred_element_type=jnp.float32
    ).reshape(local_width, D)
    prob_full = jnp.exp(masked_scores() - log_total)
    prob_grad = jnp.einsum(
        "iqhc,ikhc->ihqk", attn_low_grad, value_low, preferred_element_type=jnp.float32
    )
    value_grad = jnp.einsum(
        "ihqk,iqhc->ikhc", prob_low, attn_low_grad, preferred_element_type=jnp.float32
    )
    score_grad = (
        prob_full * (prob_grad - jnp.sum(prob_full * prob_grad, axis=-1, keepdims=True))
    ).astype(jnp.bfloat16)
    query_rot_grad = jnp.einsum(
        "ihqk,ikhc->iqhc", score_grad, key_low, preferred_element_type=jnp.float32
    ) * DH ** (-0.5)
    key_rot_grad = jnp.einsum(
        "ihqk,iqhc->ikhc", score_grad, query_low, preferred_element_type=jnp.float32
    )
    query_scaled_grad = rotate(query_rot_grad, cos_h, sin_h, cos_w, sin_w, -1.0)
    key_scaled_grad = rotate(key_rot_grad, cos_h, sin_h, cos_w, sin_w, -1.0)
    qgain_local = jnp.sum(query_scaled_grad * query_normed, axis=(0, 1, 2))
    kgain_local = jnp.sum(key_scaled_grad * key_normed, axis=(0, 1, 2))
    query_grad = norm_back(query_scaled_grad * q_gain, query_normed, query_inv)
    key_grad = norm_back(key_scaled_grad * k_gain, key_normed, key_inv)
    qkv_grad = jnp.stack(
        [
            query_grad.reshape(blocks_here, BLOCK, local_width),
            key_grad.reshape(blocks_here, BLOCK, local_width),
            value_grad.reshape(blocks_here, BLOCK, local_width),
        ],
        axis=2,
    ).astype(jnp.bfloat16)
    grad_qkv_part = jnp.einsum(
        "ibd,ibkc->dkc", hidden_one, qkv_grad, preferred_element_type=jnp.float32
    )
    hidden_one_part = jnp.einsum(
        "ibkc,dkc->ibd", qkv_grad, qkv_full, preferred_element_type=jnp.float32
    )
    grad_out, grad_qkv, qgain_part, kgain_part, hidden_one_part = (
        grad_out_part,
        grad_qkv_part,
        qgain_local,
        kgain_local,
        hidden_one_part,
    )
    h1_grad_share = row_share(hidden_one_part.reshape(ROWS_DEV, D))
    grad_shift_one = per_item(h1_grad_share)
    grad_scale_one = per_item(h1_grad_share * normed_one_share)
    input_share = mid_grad_share + norm_back(
        h1_grad_share * (1.0 + scale_one_r), normed_one_share, inv_one_share
    )
    input_whole = row_whole(input_share.astype(jnp.bfloat16))
    mod_partial = jnp.stack(
        [
            grad_shift_one,
            grad_scale_one,
            grad_gate_one,
            grad_shift_two,
            grad_scale_two,
            grad_gate_two,
        ],
        axis=1,
    )
    mod_grad = lax.psum(mod_partial, "mp").astype(jnp.bfloat16)
    mod_grad_own = lax.dynamic_slice_in_dim(mod_grad, model_rank * local_width, local_width, 2)
    mod_all = lax.all_gather(mod_grad_own, "dp", axis=0, tiled=True)
    cond_part = jnp.einsum("ikc,dkc->id", mod_all, w_ada, preferred_element_type=jnp.float32)
    cond_sum = lax.psum(cond_part, "mp")
    cond_total = lax.all_to_all(
        cond_sum.reshape(peers, blocks_here, ada_rows), "dp", split_axis=0, concat_axis=0, tiled=True
    )
    cond_total = jnp.moveaxis(cond_total, 0, 1).reshape(blocks_here, peers * ada_rows)
    grad_cond = cond_total * cond_sig * (1.0 + cond_wide * (1.0 - cond_sig))
    grad_ada = jnp.einsum("ir,ikc->rkc", silu_own, mod_all, preferred_element_type=jnp.float32)
    grad_bada = jnp.sum(mod_all.astype(jnp.float32), axis=0)
    qgain_total, kgain_total = lax.psum((qgain_part, kgain_part), ("dp", "mp"))
    qkv_own, out_own, gu_own, down_own = (
        grad_share(grad_qkv, 0),
        grad_share(grad_out, 1),
        grad_share(grad_gu, 0),
        grad_share(grad_down, 1),
    )
    result_cols = lax.dynamic_slice_in_dim(result_whole, model_rank * local_width, local_width, 1)
    input_cols = lax.dynamic_slice_in_dim(input_whole, model_rank * local_width, local_width, 1)
    back_index = jnp.minimum(flat_index, ROWS_DEV - 1)
    back_rows = result_cols[back_index].reshape(peers, slot_rows, local_width)
    back_grads = input_cols[back_index].reshape(peers, slot_rows, local_width)
    returned_rows, returned_grads = (
        lax.all_to_all(back_rows, "dp", split_axis=0, concat_axis=0, tiled=True),
        lax.all_to_all(back_grads, "dp", split_axis=0, concat_axis=0, tiled=True),
    )
    pick = jnp.minimum(place, peers * slot_rows - 1)
    empty = jnp.zeros((), jnp.bfloat16)
    out_rows = jnp.where(live[:, None], returned_rows.reshape(-1, local_width)[pick], empty)
    out_grads = jnp.where(live[:, None], returned_grads.reshape(-1, local_width)[pick], empty)
    return (
        out_rows,
        out_grads,
        grad_cond,
        grad_ada,
        grad_bada,
        qkv_own,
        qgain_total,
        kgain_total,
        out_own,
        gu_own,
        down_own,
        stats_value,
    )


MESH = pl.DeviceIdType.MESH
f32 = jnp.float32
bf16 = jnp.bfloat16
LANE_INDEX = 288
META = 1152
PAD = 128


def nn(left, right):
    return jnp.dot(left, right, preferred_element_type=f32)


def nt(left, right):
    return lax.dot_general(left, right, (((1,), (1,)), ((), ())), preferred_element_type=f32)


def tn(left, right):
    return lax.dot_general(left, right, (((0,), (0,)), ((), ())), preferred_element_type=f32)


def loop(count, step):
    def run(index, carry):
        step(index)
        return carry

    lax.fori_loop(0, count, run, 0)


def at128(index, size):
    return pl.ds(pl.multiple_of(index, 128), size)


def at16(index, size):
    return pl.ds(pl.multiple_of(index, 16), size)


GROUPS = (("down", 768), ("gu", 1536), ("out", 288), ("qkv", 864))


def scratch_list():
    vm = pltpu.VMEM
    items = {
        "sem": pltpu.SemaphoreType.DMA((400,)),
        "arow": vm((1, 1280), f32),
        "arec": vm((8, 1, 1280), f32),
        "amat": vm((8, 1280), f32),
        "xe": vm((384, 512), bf16),
        "ce": vm((384, 512), bf16),
        "place": vm((512, 512), bf16),
        "sx": vm((512, 384), bf16),
        "rx": vm((512, 384), bf16),
        "sg": vm((512, 384), bf16),
        "rg": vm((512, 384), bf16),
        "spread": vm((512, 256), bf16),
        "rb": vm((4, 256, 384), bf16),
        "gb": vm((4, 256, 384), bf16),
        "pms": vm((8, 6, 1, 288), f32),
        "pmr": vm((8, 6, 1, 288), f32),
        "mdb": vm((4, 6, 1, 288), f32),
        "modf": vm((8, 1152), f32),
        "h1": vm((256, 1152), bf16),
        "h1t": vm((1152, 256), bf16),
        "w1": vm((1152, 1152), bf16),
        "w2": vm((1152, 1536), bf16),
        "w3": vm((1152, 768), bf16),
        "wp1": vm((144, 1152), bf16),
        "wp2": vm((144, 1536), bf16),
        "wo": vm((1152, 288), bf16),
        "qkv": vm((256, 1024), f32),
        "qn": vm((4, 256, 128), f32),
        "kn": vm((4, 256, 128), f32),
        "qi": vm((4, 256, 1), f32),
        "ki": vm((4, 256, 1), f32),
        "ql": vm((4, 256, 128), bf16),
        "kl": vm((4, 256, 128), bf16),
        "vl": vm((4, 256, 128), bf16),
        "pf": vm((4, 256, 256), f32),
        "cosv": vm((256, 128), f32),
        "sinv": vm((256, 128), f32),
        "al": vm((256, 288), bf16),
        "rsa": vm((256, 1152), bf16),
        "rra": vm((4, 64, 1152), bf16),
        "rsf": vm((256, 1152), bf16),
        "rrf": vm((4, 64, 1152), bf16),
        "rsh2": vm((256, 1152), bf16),
        "rrh2": vm((4, 64, 1152), bf16),
        "rsh1": vm((256, 1152), bf16),
        "rrh1": vm((4, 64, 1152), bf16),
        "h2": vm((256, 1152), bf16),
        "h2t": vm((1152, 256), bf16),
        "ag": vm((256, 1152), bf16),
        "agt": vm((1152, 256), bf16),
        "gr": vm((256, 768), f32),
        "ur": vm((256, 768), f32),
        "inner": vm((256, 768), bf16),
        "gug": vm((256, 1536), bf16),
        "fg": vm((256, 1152), bf16),
        "fgt": vm((1152, 256), bf16),
        "da": vm((256, 384), f32),
        "dqkv": vm((256, 864), bf16),
        "share": vm((8, 64, 1152), f32),
        "invs": vm((2, 64, 1), f32),
        "gpart": vm((8, 1152), f32),
        "ras": vm((4, 64, 384), bf16),
        "rar": vm((4, 64, 384), bf16),
        "ias": vm((4, 64, 384), bf16),
        "iar": vm((4, 64, 384), bf16),
        "bs": vm((512, 384), bf16),
        "br": vm((512, 384), bf16),
        "bgs": vm((512, 384), bf16),
        "bgr": vm((512, 384), bf16),
        "hs": vm((4, 7, 1, 288), f32),
        "hr": vm((4, 7, 1, 288), f32),
        "gs": vm((7, 1, 288), f32),
        "grec": vm((8, 7, 1, 288), f32),
        "ms": vm((8, 6, 288), f32),
        "cps": vm((8, 144), f32),
        "cpr": vm((4, 8, 144), f32),
        "cts": vm((8, 1, 144), f32),
        "ctr": vm((8, 1, 144), f32),
    }
    for name, width in GROUPS:
        items["cs_" + name] = vm((4, 144, width), bf16)
        items["cr_" + name] = vm((4, 144, width), bf16)
        items["xs_" + name] = vm((2, 144, width), bf16)
        items["xr_" + name] = vm((2, 144, width), bf16)
        items["zs_" + name] = vm((2, 144, width), bf16)
        items["zr_" + name] = vm((2, 144, width), bf16)
    return items


class Refs:
    pass


ARGS = [
    "xt",
    "ct",
    "dest",
    "count",
    "grid",
    "bin",
    "cond",
    "wada",
    "bada",
    "wqkv",
    "qg",
    "kg",
    "woin",
    "wgu",
    "wdn",
    "outt",
    "gint",
    "gcond",
    "gada",
    "gbada",
    "gqkv",
    "gqg",
    "gkg",
    "gout",
    "ggu",
    "gdn",
    "stats",
]


def block_kernel(names, *refs):
    r = Refs()
    for name, ref in zip(ARGS + names, refs):
        setattr(r, name, ref)
    dp = lax.axis_index("dp")
    mp = lax.axis_index("mp")
    z, x, y, c = dp // 2, dp % 2, mp // 2, mp % 2
    zh, zl = z // 2, z % 2
    item = (2 * zh + c) * 2 + x
    tp = y * 2 + zl
    home = zl == c
    away = zl != c
    sem = r.sem
    taken = [0]

    def sems(count):
        first = taken[0]
        taken[0] += count
        return first

    def device(zz, xx, yy, cc):
        return (zz * 2 + xx, yy * 2 + cc)

    def worker(index, part):
        zi, xi = index // 2, index % 2
        return device(2 * (zi // 2) + part % 2, xi, part // 2, zi % 2)

    def mate(step):
        return device(2 * zh + (zl ^ (step & 1)), x, y ^ (step >> 1), c)

    def remote(src, dst, ss, rs, dev):
        return pltpu.make_async_remote_copy(
            src_ref=src,
            dst_ref=dst,
            send_sem=sem.at[ss],
            recv_sem=sem.at[rs],
            device_id=dev,
            device_id_type=MESH,
        )

    pending = []

    def send(src, dst, ss, rs, dev):
        copy = remote(src, dst, ss, rs, dev)
        copy.start()
        pending.append(copy.wait_send)

    def send_unless(same, src, dst, ss, rs, dev):
        other = jnp.logical_not(same)

        @pl.when(same)
        def _():
            pltpu.make_async_copy(src, dst, sem.at[rs]).start()

        @pl.when(other)
        def _():
            remote(src, dst, ss, rs, dev).start()

        def finish():
            @pl.when(other)
            def _():
                remote(src, dst, ss, rs, dev).wait_send()

        pending.append(finish)

    def arrived(dst, rs):
        pltpu.make_async_copy(dst, dst, sem.at[rs]).wait()

    def to_workers(source, target, base, slot_of):
        for step in range(8):
            index = (dp + step) % 8
            args = (source(index), target(dp), base + step, base + 8 + slot_of(dp), worker(index, mp))
            if step == 0:
                send_unless(home, *args)
            else:
                send(*args)

    def to_homes(source, target, base):
        for step in range(8):
            index = (dp + step) % 8
            args = (source(index), target(item), base + step, base + 8 + item, (index, tp))
            if step == 0:
                send_unless(home, *args)
            else:
                send(*args)

    groups = ((r.wp1, r.w1), (r.wp2, r.w2), (r.wdn, r.w3))
    w_base = [sems(2 + 2 + 4 + 8) for _ in groups]

    def slot(ref, index):
        return ref.at[at16(index * 144, 144)]

    def gather_z(g):
        src, full = groups[g]
        base = w_base[g]
        for rel in range(2):
            zt = c + 2 * (zh ^ rel)
            args = (src, slot(full, dp), base + rel, base + 8 + dp, device(zt, x, y, zl))
            if rel == 0:
                send_unless(home, *args)
            else:
                send(*args)

    def gather_forward(g):
        full = groups[g][1]
        base = w_base[g]
        for rel in range(2):
            s = (c + 2 * (zh ^ rel)) * 2 + x
            arrived(slot(full, s), base + 8 + s)
            send(slot(full, s), slot(full, s), base + 2 + rel, base + 8 + s, device(z, 1 - x, y, c))
            send(slot(full, s), slot(full, s), base + 4 + rel, base + 8 + s, device(z, x, y, 1 - c))

    def gather_cross(g):
        full = groups[g][1]
        base = w_base[g]
        for rel in range(2):
            s = (c + 2 * (zh ^ rel)) * 2 + 1 - x
            arrived(slot(full, s), base + 8 + s)
            send(slot(full, s), slot(full, s), base + 6 + rel, base + 8 + s, device(z, x, y, 1 - c))

    def gather_done(g):
        full = groups[g][1]
        base = w_base[g]
        for rel in range(2):
            for xx in range(2):
                s = (1 - c + 2 * rel) * 2 + xx
                arrived(slot(full, s), base + 8 + s)

    def mates_send(source, target, base):
        for step in range(1, 4):
            send(source(tp ^ step), target(step), base + step, base + 4 + step, mate(step))

    def scatter_send(name, base):
        buf, rec = getattr(r, "rs" + name), getattr(r, "rr" + name)
        mates_send(lambda t: buf.at[at16(t * 64, 64)], lambda step: rec.at[step], base)

    def scatter_sum(name, base):
        buf, rec = getattr(r, "rs" + name), getattr(r, "rr" + name)
        total = buf[at16(tp * 64, 64), :].astype(f32)
        for step in range(1, 4):
            arrived(rec.at[step], base + 4 + step)
            total = total + rec[step].astype(f32)
        return total

    def rows_send(buf, base):
        mine = buf.at[at16(tp * 64, 64)]
        mates_send(lambda t: mine, lambda step: mine, base)

    def rows_wait(buf, base):
        for step in range(1, 4):
            arrived(buf.at[at16((tp ^ step) * 64, 64)], base + 4 + step)

    def slots_send(buf, base):
        mine = buf.at[tp]
        mates_send(lambda t: mine, lambda step: mine, base)

    def slots_wait(buf, base):
        for step in range(1, 4):
            arrived(buf.at[tp ^ step], base + 4 + step)

    g_base = {name: sems(4 + 4 + 2 + 2 + 2 + 2) for name, _ in GROUPS}

    def block(left, right, s):
        return nn(left[at16(s * 144, 144), :], right[...])

    def reduce_core(name, left, right):
        base = g_base[name]
        cs, cr = getattr(r, "cs_" + name), getattr(r, "cr_" + name)

        def step(q):
            s = (1 - c + 2 * (q // 2)) * 2 + q % 2
            cs[q] = block(left, right, s).astype(bf16)

        for q in range(4):
            step(q)
            send(cs.at[q], cr.at[q], base + q, base + 4 + q, device(z, x, y, 1 - c))

    def reduce_x(name, left, right):
        base = g_base[name]
        cr, xs, xr = (getattr(r, k + name) for k in ("cr_", "xs_", "xr_"))
        for rel in range(2):
            q = 2 * rel + 1 - x
            part = block(left, right, (c + 2 * rel) * 2 + 1 - x)
            arrived(cr.at[q], base + 4 + q)
            xs[rel] = (part + cr[q].astype(f32)).astype(bf16)
            send(xs.at[rel], xr.at[rel], base + 8 + rel, base + 10 + rel, device(z, 1 - x, y, c))

    def reduce_z(name, left, right):
        base = g_base[name]
        cr, xr, zs, zr = (getattr(r, k + name) for k in ("cr_", "xr_", "zs_", "zr_"))
        for near in range(2):
            rel = zh ^ near
            q = 2 * rel + x
            part = block(left, right, (c + 2 * rel) * 2 + x)
            arrived(cr.at[q], base + 4 + q)
            part = part + cr[q].astype(f32)
            arrived(xr.at[rel], base + 10 + rel)
            zs[near] = (part + xr[rel].astype(f32)).astype(bf16)
            args = (
                zs.at[near], zr.at[zh], base + 12 + near, base + 14 + zh,
                device(c + 2 * rel, x, y, zl),
            )
            if near == 0:
                send_unless(home, *args)
            else:
                send(*args)

    def reduce_end(name):
        base = g_base[name]
        zr = getattr(r, "zr_" + name)
        for half in range(2):
            arrived(zr.at[half], base + 14 + half)
        return zr[0].astype(f32) + zr[1].astype(f32)

    def transpose(src, dst):
        def step(j):
            dst[at128(j * 128, 128), :] = src[:, at128(j * 128, 128)].T

        loop(9, step)

    lane128 = lax.broadcasted_iota(jnp.int32, (1, PAD), 1)
    head_lane = lane128 < 72
    quarter = lane128 // 18
    even = quarter % 2 == 0

    def swap(v):
        return jnp.where(even, pltpu.roll(v, PAD - 18, 1), pltpu.roll(v, 18, 1))

    def norm_of(v):
        inv = lax.rsqrt(jnp.mean(v * v, axis=-1, keepdims=True) + epsilon)
        return v * inv, inv

    def back(g, normed, inv):
        return inv * (g - normed * jnp.mean(g * normed, axis=-1, keepdims=True))

    cond = r.cond[...].astype(f32)
    sig_c = jax.nn.sigmoid(cond)
    r.arow[0:1, 0:META] = (cond * sig_c).astype(bf16).astype(f32)
    meta = jnp.where(lane128 == 0, r.bin[0].astype(f32), 0.0)
    meta = jnp.where(lane128 == 1, r.grid[0, 0].astype(f32), meta)
    meta = jnp.where(lane128 == 2, r.grid[0, 1].astype(f32), meta)
    r.arow[0:1, META : META + 128] = meta
    a_base = sems(16)
    r.arec[dp] = r.arow[...]
    for step in range(1, 8):
        index = (dp + step) % 8
        send(r.arow, r.arec.at[dp], a_base + step, a_base + 8 + dp, (index, mp))

    for p in range(3):
        r.wp1[:, 288 * p : 288 * p + 288] = r.wqkv[p]
    r.wp1[:, 864:1152] = r.woin[...]
    gather_z(0)

    dest = r.dest[...]
    lane512 = lax.broadcasted_iota(jnp.int32, (1, 512), 1)
    live = lane512 < r.count[0]
    target = dest >> 8
    within = dest & 255
    owner = lax.broadcasted_iota(jnp.int32, (8, 512), 0)
    member = jnp.where((owner == target) & live, 1.0, 0.0)
    upper = lax.broadcasted_iota(jnp.int32, (512, 512), 0) <= lax.broadcasted_iota(
        jnp.int32, (512, 512), 1
    )
    running = nn(member.astype(bf16), jnp.where(upper, 1.0, 0.0).astype(bf16))
    rank = jnp.sum(running * member, axis=0, keepdims=True).astype(jnp.int32) - 1
    spot = jnp.where(live, target * 64 + rank, -1)
    slots = lax.broadcasted_iota(jnp.int32, (512, 512), 0)
    r.place[...] = jnp.where(slots == spot, 1.0, 0.0).astype(bf16)
    r.xe[0:288, :] = r.xt[...]
    top_row = lax.broadcasted_iota(jnp.int32, (96, 512), 0) == 0
    r.xe[288:384, :] = jnp.where(top_row, within + 1, 0).astype(f32).astype(bf16)
    r.sx[...] = nt(r.place[...], r.xe[...]).astype(bf16)
    x_base = sems(16)
    to_workers(
        lambda i: r.sx.at[at16(i * 64, 64)], lambda i: r.rx.at[at16(i * 64, 64)], x_base, lambda i: i
    )
    r.ce[0:288, :] = r.ct[...]
    r.ce[288:384, :] = jnp.zeros((96, 512), bf16)
    r.sg[...] = nt(r.place[...], r.ce[...]).astype(bf16)
    r.wp2[:, 0:768] = r.wgu[:, 0, :]
    r.wp2[:, 768:1536] = r.wgu[:, 1, :]

    for step in range(1, 8):
        index = (dp + step) % 8
        arrived(r.arec.at[index], a_base + 8 + index)
    for i in range(8):
        r.amat[i : i + 1, :] = r.arec[i]
    pick = lax.broadcasted_iota(jnp.int32, (1152, 144), 0) == (
        lax.broadcasted_iota(jnp.int32, (1152, 144), 1) + 144 * dp
    )
    silu_own = nn(r.amat[:, 0:META].astype(bf16), jnp.where(pick, 1.0, 0.0).astype(bf16)).astype(bf16)
    first = (dp == 0).astype(f32)
    for k in range(6):
        part = nn(silu_own, r.wada[k]) + first * r.bada[k : k + 1, :].astype(f32)
        for i in range(8):
            r.pms[i, k] = part[i : i + 1, :]
    m_base = sems(16)
    to_workers(lambda i: r.pms.at[i], lambda i: r.pmr.at[i], m_base, lambda i: i)
    ada_gather = sems(8)

    gather_forward(0)

    for s in range(8):
        arrived(r.rx.at[pl.ds(s * 64, 64)], x_base + 8 + s)
    number = r.rx[:, 288:289].astype(jnp.int32)
    r.spread[...] = jnp.where(
        number == lax.broadcasted_iota(jnp.int32, (512, 256), 1) + 1, 1.0, 0.0
    ).astype(bf16)
    r.rb[tp] = tn(r.spread[...], r.rx[...]).astype(bf16)
    rb_base = sems(8)
    slots_send(r.rb, rb_base)

    for s in range(8):
        arrived(r.pmr.at[s], m_base + 8 + s)
    total = r.pmr[0]
    for s in range(1, 8):
        total = total + r.pmr[s]
    r.mdb[tp] = total.astype(bf16).astype(f32)
    slots_send(r.mdb, ada_gather)

    gather_z(1)
    t_base = sems(16)
    to_workers(
        lambda i: r.sg.at[at16(i * 64, 64)], lambda i: r.rg.at[at16(i * 64, 64)], t_base, lambda i: i
    )
    gather_z(2)
    gather_cross(0)

    about = r.arec[item]
    height = about[:, META + 1 : META + 2]
    width = about[:, META + 2 : META + 3]
    bins = r.amat[:, META : META + 1]
    alike = jnp.sum(
        jnp.where(bins == about[:, META : META + 1], 1.0, 0.0), axis=0, keepdims=True
    )
    weight = 8.0 / (NBINS * alike)
    spots = lax.broadcasted_iota(jnp.int32, (256, 1), 0).astype(f32)
    high = jnp.floor((spots + 0.5) / width)
    wide = spots - high * width
    freq = jnp.exp(-math.log(10000.0) * (lane128 - 18 * quarter).astype(f32) / 18.0)
    angle = jnp.where(quarter < 2, high, wide) * freq
    r.cosv[...] = jnp.where(head_lane, jnp.cos(angle), 0.0)
    r.sinv[...] = jnp.where(head_lane, jnp.where(even, -jnp.sin(angle), jnp.sin(angle)), 0.0)
    used = height * width
    key_ok = lax.broadcasted_iota(jnp.int32, (1, 256), 1).astype(f32) < used
    row_first = (tp * 64).astype(f32)
    share_spots = lax.broadcasted_iota(jnp.int32, (64, 1), 0).astype(f32) + row_first
    valid_share = jnp.where(share_spots < used, 1.0, 0.0)

    slots_wait(r.mdb, ada_gather)
    for k in range(6):
        for t in range(4):
            r.modf[k : k + 1, 288 * t : 288 * t + 288] = r.mdb[t, k]
    slots_wait(r.rb, rb_base)

    def joined(buf, start):
        return jnp.concatenate(
            [buf[t, at16(start, 64), 0:288].astype(f32) for t in range(4)], axis=-1
        )

    def first_hidden(i):
        normed, _ = norm_of(joined(r.rb, i * 64))
        shift, scale = r.modf[0:1, :], r.modf[1:2, :]
        r.h1[at16(i * 64, 64), :] = (normed * (1.0 + scale) + shift).astype(bf16)

    loop(4, first_hidden)
    RESID, NORM1, ATT, MID, NORM2, TOP, MIDG = range(7)
    mine = joined(r.rb, tp * 64)
    normed, inv = norm_of(mine)
    r.share[RESID] = mine
    r.share[NORM1] = normed
    r.invs[0] = inv
    gather_done(0)

    def project(j):
        r.qkv[:, at128(j * 256, 256)] = nn(r.h1[...], r.w1[:, at128(j * 256, 256)])

    loop(4, project)
    gather_forward(1)

    scale_q = 72 ** (-0.5)
    gains = {"q": r.qg[...], "k": r.kg[...]}
    for h in range(4):
        for kind, offset, normed_ref, inv_ref, low_ref in (
            ("q", 0, r.qn, r.qi, r.ql),
            ("k", 288, r.kn, r.ki, r.kl),
        ):
            lane = offset + 72 * h
            v = jnp.where(head_lane, r.qkv[:, lane : lane + 128], 0.0)
            inv = lax.rsqrt(jnp.sum(v * v, axis=-1, keepdims=True) * (1.0 / 72) + epsilon)
            v = v * inv
            normed_ref[h] = v
            inv_ref[h] = inv
            v = v * gains[kind]
            v = v * r.cosv[...] + swap(v) * r.sinv[...]
            if kind == "q":
                v = v * scale_q
            low_ref[h] = v.astype(bf16)
        lane = 576 + 72 * h
        r.vl[h] = jnp.where(head_lane, r.qkv[:, lane : lane + 128], 0.0).astype(bf16)
    for h in range(4):
        scores = jnp.where(key_ok, nt(r.ql[h], r.kl[h]), -1e30)
        scores = jnp.exp(scores - jnp.max(scores, axis=-1, keepdims=True))
        prob = scores / jnp.sum(scores, axis=-1, keepdims=True)
        r.pf[h] = prob
        r.al[:, 72 * h : 72 * h + 72] = nn(prob.astype(bf16), r.vl[h])[:, 0:72].astype(bf16)

    r.wo[...] = r.w1[:, 864:1152]

    def project_out(j):
        r.rsa[:, at128(j * 384, 384)] = nt(r.al[...], r.wo[at128(j * 384, 384), :]).astype(bf16)

    loop(3, project_out)
    a_rs = sems(8)
    scatter_send("a", a_rs)
    gather_cross(1)
    gather_forward(2)
    attention = scatter_sum("a", a_rs)
    r.share[ATT] = attention
    middle = r.share[RESID] + r.modf[2:3, :] * attention
    r.share[MID] = middle
    normed, inv = norm_of(middle)
    r.share[NORM2] = normed
    r.invs[1] = inv
    r.h2[at16(tp * 64, 64), :] = (normed * (1.0 + r.modf[4:5, :]) + r.modf[3:4, :]).astype(bf16)
    h2_ag = sems(8)
    rows_send(r.h2, h2_ag)

    for s in range(8):
        arrived(r.rg.at[pl.ds(s * 64, 64)], t_base + 8 + s)
    r.gb[tp] = tn(r.spread[...], r.rg[...]).astype(bf16)
    gb_base = sems(8)
    slots_send(r.gb, gb_base)
    transpose(r.h1, r.h1t)
    slots_wait(r.gb, gb_base)

    def feed_rows(i):
        rows = lax.broadcasted_iota(jnp.int32, (64, 1), 0).astype(f32) + (i * 64).astype(f32)
        factor = jnp.where(rows < used, weight, 0.0)
        r.fg[at16(i * 64, 64), :] = (joined(r.gb, i * 64) * factor * r.modf[5:6, :]).astype(bf16)

    loop(4, feed_rows)
    r.share[TOP] = joined(r.gb, tp * 64) * (weight * valid_share)
    transpose(r.fg, r.fgt)

    rows_wait(r.h2, h2_ag)
    gather_done(1)

    def swiglu(j):
        gate = nn(r.h2[...], r.w2[:, at128(j * 256, 256)])
        up = nn(r.h2[...], r.w2[:, at128(768 + j * 256, 256)])
        r.gr[:, at128(j * 256, 256)] = gate
        r.ur[:, at128(j * 256, 256)] = up
        r.inner[:, at128(j * 256, 256)] = (gate * jax.nn.sigmoid(gate) * up).astype(bf16)

    loop(3, swiglu)
    gather_cross(2)
    reduce_core("down", r.fgt, r.inner)
    gather_done(2)

    def swiglu_back(j):
        grad = nn(r.fg[...], r.w3[:, at128(j * 256, 256)])
        gate = r.gr[:, at128(j * 256, 256)]
        up = r.ur[:, at128(j * 256, 256)]
        sig = jax.nn.sigmoid(gate)
        r.gug[:, at128(j * 256, 256)] = (grad * up * sig * (1.0 + gate * (1.0 - sig))).astype(bf16)
        r.gug[:, at128(768 + j * 256, 256)] = (grad * (gate * sig)).astype(bf16)

    loop(3, swiglu_back)

    def hidden_back(j):
        r.rsh2[:, at128(j * 384, 384)] = nt(r.gug[...], r.w2[at128(j * 384, 384), :]).astype(bf16)

    loop(3, hidden_back)
    h2_rs = sems(8)
    scatter_send("h2", h2_rs)
    reduce_x("down", r.fgt, r.inner)

    def feed_out(j):
        r.rsf[:, at128(j * 384, 384)] = nt(r.inner[...], r.w3[at128(j * 384, 384), :]).astype(bf16)

    loop(3, feed_out)
    f_rs = sems(8)
    scatter_send("f", f_rs)
    grad_h2 = scatter_sum("h2", h2_rs)
    normed = r.share[NORM2]
    r.gpart[3:4, :] = jnp.sum(grad_h2, axis=0, keepdims=True)
    r.gpart[4:5, :] = jnp.sum(grad_h2 * normed, axis=0, keepdims=True)
    mid_grad = r.share[TOP] + back(grad_h2 * (1.0 + r.modf[4:5, :]), normed, r.invs[1])
    r.share[MIDG] = mid_grad
    r.gpart[2:3, :] = jnp.sum(mid_grad * r.share[ATT], axis=0, keepdims=True)
    r.ag[at16(tp * 64, 64), :] = (r.modf[2:3, :] * mid_grad).astype(bf16)
    ag_ag = sems(8)
    rows_send(r.ag, ag_ag)

    transpose(r.h2, r.h2t)
    reduce_core("gu", r.h2t, r.gug)
    reduce_z("down", r.fgt, r.inner)

    feed = scatter_sum("f", f_rs)
    fed = r.modf[5:6, :] * feed
    result = r.share[MID] + fed
    r.gpart[5:6, :] = jnp.sum(r.share[TOP] * feed, axis=0, keepdims=True)
    att = r.modf[2:3, :] * r.share[ATT]

    def total_of(v):
        return jnp.sum(jnp.sum(v, axis=0, keepdims=True), axis=1, keepdims=True)

    squares = [total_of(valid_share * v * v) for v in (result, att, fed)]
    low_result = result.astype(bf16)
    for t in range(4):
        r.ras[t, :, 0:288] = low_result[:, 288 * t : 288 * t + 288]
    ra_base = sems(8)
    r.rar[tp] = r.ras[tp]
    mates_send(lambda t: r.ras.at[t], lambda step: r.rar.at[tp], ra_base)

    rows_wait(r.ag, ag_ag)
    r.da[:, 0:288] = nn(r.ag[...], r.wo[...])
    reduce_x("gu", r.h2t, r.gug)
    qsum = jnp.zeros((1, PAD), f32)
    ksum = jnp.zeros((1, PAD), f32)
    for h in range(4):
        grad = jnp.where(head_lane, r.da[:, 72 * h : 72 * h + 128], 0.0).astype(bf16)
        prob = r.pf[h]
        prob_grad = nt(grad, r.vl[h])
        mixed = jnp.sum(prob * prob_grad, axis=-1, keepdims=True)
        score = (prob * (prob_grad - mixed)).astype(bf16)
        value_grad = tn(prob.astype(bf16), grad)
        r.dqkv[:, 576 + 72 * h : 648 + 72 * h] = value_grad[:, 0:72].astype(bf16)
        for kind, offset, normed_ref, inv_ref in (
            ("q", 0, r.qn, r.qi),
            ("k", 288, r.kn, r.ki),
        ):
            if kind == "q":
                turned = nn(score, r.kl[h]) * scale_q
            else:
                turned = tn(score, r.ql[h])
            turned = turned * r.cosv[...] - swap(turned) * r.sinv[...]
            normed = normed_ref[h]
            along = jnp.sum(turned * normed, axis=0, keepdims=True)
            if kind == "q":
                qsum = qsum + along
            else:
                ksum = ksum + along
            g = turned * gains[kind]
            mean = jnp.sum(g * normed, axis=-1, keepdims=True) * (1.0 / 72)
            g = inv_ref[h] * (g - normed * mean)
            r.dqkv[:, offset + 72 * h : offset + 72 * h + 72] = g[:, 0:72].astype(bf16)

    def first_back(j):
        r.rsh1[:, at128(j * 384, 384)] = nt(r.dqkv[...], r.w1[at128(j * 384, 384), 0:864]).astype(bf16)

    loop(3, first_back)
    h1_rs = sems(8)
    scatter_send("h1", h1_rs)
    reduce_core("qkv", r.h1t, r.dqkv)
    reduce_x("qkv", r.h1t, r.dqkv)
    transpose(r.ag, r.agt)
    reduce_core("out", r.agt, r.al)
    reduce_z("gu", r.h2t, r.gug)
    reduce_x("out", r.agt, r.al)

    for step in range(1, 4):
        arrived(r.rar.at[tp ^ step], ra_base + 4 + step)
    rar = jnp.concatenate([r.rar[t] for t in range(4)], axis=0)
    r.bs[...] = nn(r.spread[...], rar).astype(bf16)
    b_base = sems(16)
    to_homes(lambda i: r.bs.at[at16(i * 64, 64)], lambda i: r.br.at[at16(i * 64, 64)], b_base)

    grad_h1 = scatter_sum("h1", h1_rs)
    normed = r.share[NORM1]
    r.gpart[0:1, :] = jnp.sum(grad_h1, axis=0, keepdims=True)
    r.gpart[1:2, :] = jnp.sum(grad_h1 * normed, axis=0, keepdims=True)
    in_grad = r.share[MIDG] + back(grad_h1 * (1.0 + r.modf[1:2, :]), normed, r.invs[0])
    low_grad = in_grad.astype(bf16)
    for t in range(4):
        r.ias[t, :, 0:288] = low_grad[:, 288 * t : 288 * t + 288]
    ia_base = sems(8)
    r.iar[tp] = r.ias[tp]
    mates_send(lambda t: r.ias.at[t], lambda step: r.iar.at[tp], ia_base)

    numbers = jnp.concatenate(
        [qsum[:, 0:72], ksum[:, 0:72], squares[0], squares[1], squares[2],
         total_of(valid_share), jnp.zeros((1, 288 - 148), f32)],
        axis=-1,
    )
    for t in range(4):
        for k in range(6):
            r.hs[t, k] = r.gpart[k : k + 1, 288 * t : 288 * t + 288]
        r.hs[t, 6] = numbers
    h_base = sems(8)
    r.hr[tp] = r.hs[tp]
    mates_send(lambda t: r.hs.at[t], lambda step: r.hr.at[tp], h_base)
    reduce_z("qkv", r.h1t, r.dqkv)
    reduce_z("out", r.agt, r.al)
    for step in range(1, 4):
        arrived(r.iar.at[tp ^ step], ia_base + 4 + step)
    iar = jnp.concatenate([r.iar[t] for t in range(4)], axis=0)
    r.bgs[...] = nn(r.spread[...], iar).astype(bf16)
    bg_base = sems(16)
    to_homes(lambda i: r.bgs.at[at16(i * 64, 64)], lambda i: r.bgr.at[at16(i * 64, 64)], bg_base)
    for step in range(1, 4):
        arrived(r.hr.at[tp ^ step], h_base + 4 + step)
    total = r.hr[0] + r.hr[1] + r.hr[2] + r.hr[3]
    for k in range(6):
        r.gs[k] = total[k].astype(bf16).astype(f32)
    r.gs[6] = total[6]
    g2_base = sems(16)
    to_homes(lambda i: r.gs, lambda i: r.grec.at[i], g2_base)
    for i in range(8):
        arrived(r.grec.at[i], g2_base + 8 + i)
    for i in range(8):
        for k in range(6):
            r.ms[i, k : k + 1, :] = r.grec[i, k]
    cond_part = jnp.zeros((8, 144), f32)
    for k in range(6):
        grads = jnp.concatenate([r.grec[i, k] for i in range(8)], axis=0)
        low = grads.astype(bf16)
        r.gada[k] = tn(silu_own, low)
        r.gbada[k : k + 1, :] = jnp.sum(grads, axis=0, keepdims=True)
        cond_part = cond_part + nt(low, r.wada[k])
    totals = r.grec[0, 6]
    for i in range(1, 8):
        totals = totals + r.grec[i, 6]
    r.gqg[...] = totals[:, 0:72]
    r.gkg[...] = totals[:, 72:144]
    ratio = totals[:, 144:147] / (totals[:, 147:148] * 1152.0)
    r.stats[...] = jnp.sqrt(ratio)
    r.cps[...] = cond_part
    c_base = sems(8)
    r.cpr[mp] = cond_part
    for step in range(1, 4):
        send(r.cps, r.cpr.at[mp], c_base + step, c_base + 4 + step, (dp, mp ^ step))
    for step in range(1, 4):
        arrived(r.cpr.at[mp ^ step], c_base + 4 + step)
    cond_sum = r.cpr[0] + r.cpr[1] + r.cpr[2] + r.cpr[3]
    for i in range(8):
        r.cts[i] = cond_sum[i : i + 1, :]
    ct_base = sems(16)
    r.ctr[dp] = r.cts[dp]
    for step in range(1, 8):
        index = (dp + step) % 8
        send(r.cts.at[index], r.ctr.at[dp], ct_base + step, ct_base + 8 + dp, (index, mp))

    r.gdn[...] = reduce_end("down")
    grad = reduce_end("gu")
    r.ggu[:, 0, :] = grad[:, 0:768]
    r.ggu[:, 1, :] = grad[:, 768:1536]
    for i in range(8):
        arrived(r.br.at[pl.ds(i * 64, 64)], b_base + 8 + i)
    r.outt[...] = tn(r.br[:, 0:288], r.place[...]).astype(bf16)
    grad = reduce_end("qkv")
    for p in range(3):
        r.gqkv[p] = grad[:, 288 * p : 288 * p + 288]
    r.gout[...] = reduce_end("out")
    for i in range(8):
        arrived(r.bgr.at[pl.ds(i * 64, 64)], bg_base + 8 + i)
    r.gint[...] = tn(r.bgr[:, 0:288], r.place[...]).astype(bf16)
    for step in range(1, 8):
        index = (dp + step) % 8
        arrived(r.ctr.at[index], ct_base + 8 + index)
    for s in range(8):
        r.gcond[0:1, 144 * s : 144 * s + 144] = r.ctr[s]
    cond = r.cond[...].astype(f32)
    sig_c = jax.nn.sigmoid(cond)
    r.gcond[...] = r.gcond[...] * sig_c * (1.0 + cond * (1.0 - sig_c))
    for finish in pending:
        finish()
    assert taken[0] <= 400


def body_kernel(
    x_src, cotangent, route_dest, route_count, item_grid, noise_bin, cond, w_ada, b_ada,
    w_qkv, q_gain, k_gain, w_out, w_gu, w_down,
):
    scratch = scratch_list()
    vmem = pl.BlockSpec(memory_space=pltpu.VMEM)
    smem = pl.BlockSpec(memory_space=pltpu.SMEM)
    shapes = [
        ((288, 512), bf16), ((288, 512), bf16), ((1, 1152), f32), ((6, 144, 288), f32),
        ((6, 288), f32), ((3, 144, 288), f32), ((1, 72), f32), ((1, 72), f32),
        ((144, 288), f32), ((144, 2, 768), f32), ((144, 768), f32), ((1, 3), f32),
    ]
    gain = lambda v: jnp.pad(v.reshape(1, DH), ((0, 0), (0, PAD - DH)))
    outs = pl.pallas_call(
        functools.partial(block_kernel, list(scratch)),
        out_shape=[jax.ShapeDtypeStruct(s, d) for s, d in shapes],
        in_specs=[vmem, vmem, vmem, smem, smem, smem] + [vmem] * 9,
        out_specs=[vmem] * len(shapes),
        scratch_shapes=list(scratch.values()),
        compiler_params=pltpu.CompilerParams(
            has_side_effects=True, vmem_limit_bytes=67000000
        ),
        name="block",
    )(
        x_src.T, cotangent.T, route_dest.reshape(1, SRC_CAP), route_count, item_grid, noise_bin,
        cond, jnp.transpose(w_ada, (1, 0, 2)), b_ada, jnp.transpose(w_qkv, (1, 0, 2)),
        gain(q_gain), gain(k_gain), w_out.T, w_gu, w_down.T,
    )
    (outt, gint, gcond, gada, gbada, gqkv, gqg, gkg, gout, ggu, gdn, stats) = outs
    return (
        outt.T, gint.T, gcond, jnp.transpose(gada, (1, 0, 2)), gbada,
        jnp.transpose(gqkv, (1, 0, 2)), gqg.reshape(DH), gkg.reshape(DH), gout.T, ggu, gdn.T,
        stats.reshape(3),
    )


def solution(mesh):
    one_kernel = mesh.shape["dp"] == 8 and mesh.shape["mp"] == 4
    return jax.shard_map(
        body_kernel if one_kernel else body,
        mesh=mesh,
        in_specs=(
            P("dp", "mp"),
            P("dp", "mp"),
            P("dp"),
            P("dp"),
            P("dp", None),
            P("dp"),
            P("dp", None),
            P("dp", None, "mp"),
            P(None, "mp"),
            P("dp", None, "mp"),
            P(),
            P(),
            P("mp", "dp"),
            P("dp", None, "mp"),
            P("mp", "dp"),
        ),
        out_specs=(
            P("dp", "mp"),
            P("dp", "mp"),
            P("dp", None),
            P("dp", None, "mp"),
            P(None, "mp"),
            P("dp", None, "mp"),
            P(),
            P(),
            P("mp", "dp"),
            P("dp", None, "mp"),
            P("mp", "dp"),
            P(),
        ),
        check_vma=False,
    )
```

```python
import functools
import math

import jax
import jax.numpy as jnp
from jax import lax
from jax.experimental import pallas as pl
from jax.experimental.pallas import tpu as pltpu
from jax.sharding import PartitionSpec as P

D = 1152
DH = 72
NBINS = 16
BLOCK = 256
ROWS_DEV = 256
SRC_CAP = 512


epsilon = 1e-06


def grad_share(part, dim):
    sent = part.astype(jnp.bfloat16)
    total = lax.psum_scatter(sent, "dp", scatter_dimension=dim, tiled=True)
    return total.astype(jnp.float32)


def norm_rows(values):
    scale = lax.rsqrt(jnp.mean(values * values, axis=-1, keepdims=True) + epsilon)
    return (values * scale, scale)


def norm_back(grad_normed, normed, scale):
    return scale * (grad_normed - normed * jnp.mean(grad_normed * normed, axis=-1, keepdims=True))


def rotate(values, cos_h, sin_h, cos_w, sin_w, sign):
    quarter = values.shape[-1] // 4
    first = values[..., :quarter]
    second = values[..., quarter : 2 * quarter]
    third = values[..., 2 * quarter : 3 * quarter]
    fourth = values[..., 3 * quarter :]
    return jnp.concatenate(
        [
            first * cos_h - sign * second * sin_h,
            sign * first * sin_h + second * cos_h,
            third * cos_w - sign * fourth * sin_w,
            sign * third * sin_w + fourth * cos_w,
        ],
        axis=-1,
    )


def angle_tables(grid, block, head_dim):
    quarter = head_dim // 4
    place = lax.broadcasted_iota(jnp.int32, (grid.shape[0], block), 1)
    width = grid[:, 1:2]
    height_pos = (place // width).astype(jnp.float32)
    width_pos = (place % width).astype(jnp.float32)
    freqs = jnp.exp(-math.log(10000.0) * jnp.arange(quarter).astype(jnp.float32) / quarter)
    angle_h = (height_pos[:, :, None] * freqs)[:, :, None, :]
    angle_w = (width_pos[:, :, None] * freqs)[:, :, None, :]
    return (jnp.cos(angle_h), jnp.sin(angle_h), jnp.cos(angle_w), jnp.sin(angle_w))


def row_share(values):
    return lax.psum_scatter(values, "mp", scatter_dimension=0, tiled=True)


def row_whole(values):
    return lax.all_gather(values, "mp", axis=0, tiled=True)


def body(
    x_src,
    cotangent,
    route_dest,
    route_count,
    item_grid,
    noise_bin,
    cond,
    w_ada,
    b_ada,
    w_qkv,
    q_gain,
    k_gain,
    w_out,
    w_gu,
    w_down,
):
    peers = lax.axis_size("dp")
    model_rank = lax.axis_index("mp")
    blocks_here = item_grid.shape[0]
    local_width = x_src.shape[1]
    heads_here = local_width // DH
    slot_rows = 2 * ROWS_DEV // peers
    share = ROWS_DEV // lax.axis_size("mp")
    row_first = model_rank * share
    live = jnp.arange(SRC_CAP) < route_count[0]
    target = route_dest // ROWS_DEV
    member = (target[:, None] == jnp.arange(peers)[None, :]) & live[:, None]
    running = jnp.cumsum(member.astype(jnp.int32), axis=0)
    rank_in = jnp.sum(running * member, axis=1) - 1
    place = jnp.where(live, target * slot_rows + rank_in, peers * slot_rows)
    send_rows = (
        jnp.zeros((peers * slot_rows, local_width), jnp.bfloat16).at[place].set(x_src, mode="drop")
    )
    send_grads = (
        jnp.zeros((peers * slot_rows, local_width), jnp.bfloat16)
        .at[place]
        .set(cotangent, mode="drop")
    )
    send_index = (
        jnp.full((peers * slot_rows,), ROWS_DEV, jnp.int32)
        .at[place]
        .set(route_dest % ROWS_DEV, mode="drop")
    )
    recv_rows, recv_grads, recv_index = (
        lax.all_to_all(
            send_rows.reshape(peers, slot_rows, local_width),
            "dp",
            split_axis=0,
            concat_axis=0,
            tiled=True,
        ),
        lax.all_to_all(
            send_grads.reshape(peers, slot_rows, local_width),
            "dp",
            split_axis=0,
            concat_axis=0,
            tiled=True,
        ),
        lax.all_to_all(
            send_index.reshape(peers, slot_rows), "dp", split_axis=0, concat_axis=0, tiled=True
        ),
    )
    flat_index = recv_index.reshape(-1)
    rows_cols = (
        jnp.zeros((ROWS_DEV, local_width), jnp.bfloat16)
        .at[flat_index]
        .set(recv_rows.reshape(-1, local_width), mode="drop")
    )
    grads_cols = (
        jnp.zeros((ROWS_DEV, local_width), jnp.bfloat16)
        .at[flat_index]
        .set(recv_grads.reshape(-1, local_width), mode="drop")
    )
    qkv_full, out_full, gu_full, down_full = (
        lax.all_gather(w_qkv, "dp", axis=0, tiled=True),
        lax.all_gather(w_out, "dp", axis=1, tiled=True),
        lax.all_gather(w_gu, "dp", axis=0, tiled=True),
        lax.all_gather(w_down, "dp", axis=1, tiled=True),
    )
    cond_wide = cond.astype(jnp.float32)
    cond_sig = jax.nn.sigmoid(cond_wide)
    silu_cond = (cond_wide * cond_sig).astype(jnp.bfloat16)
    ada_rows = w_ada.shape[0]
    silu_all = lax.all_gather(silu_cond, "dp", axis=0, tiled=True)
    silu_own = lax.dynamic_slice_in_dim(silu_all, lax.axis_index("dp") * ada_rows, ada_rows, 1)
    mod_sums = jnp.einsum("id,dkc->ikc", silu_own, w_ada, preferred_element_type=jnp.float32)
    mod_part = (
        lax.psum_scatter(mod_sums, "dp", scatter_dimension=0, tiled=True)
        + b_ada.astype(jnp.float32)
    ).astype(jnp.bfloat16)
    rows_full, grads_full, mod_full = (
        lax.all_gather(rows_cols, "mp", axis=1, tiled=True),
        lax.all_gather(grads_cols, "mp", axis=1, tiled=True),
        lax.all_gather(mod_part, "mp", axis=2, tiled=True),
    )
    modulation = mod_full.astype(jnp.float32)
    shift_one = modulation[:, 0][:, None, :]
    scale_one = modulation[:, 1][:, None, :]
    gate_two = modulation[:, 5][:, None, :]
    resid = rows_full.astype(jnp.float32).reshape(blocks_here, BLOCK, D)
    normed_one, inv_one = norm_rows(resid)
    hidden_one = (normed_one * (1.0 + scale_one) + shift_one).astype(jnp.bfloat16)
    qkv = jnp.einsum("ibd,dkc->ibkc", hidden_one, qkv_full, preferred_element_type=jnp.float32)
    query = qkv[:, :, 0].reshape(blocks_here, BLOCK, heads_here, DH)
    keys = qkv[:, :, 1].reshape(blocks_here, BLOCK, heads_here, DH)
    value = qkv[:, :, 2].reshape(blocks_here, BLOCK, heads_here, DH)
    query_normed, query_inv = norm_rows(query)
    key_normed, key_inv = norm_rows(keys)
    cos_h, sin_h, cos_w, sin_w = angle_tables(item_grid, BLOCK, DH)
    query_low = (
        rotate(query_normed * q_gain, cos_h, sin_h, cos_w, sin_w, 1.0) * DH ** (-0.5)
    ).astype(jnp.bfloat16)
    key_low = rotate(key_normed * k_gain, cos_h, sin_h, cos_w, sin_w, 1.0).astype(jnp.bfloat16)
    value_low = value.astype(jnp.bfloat16)
    positions = lax.broadcasted_iota(jnp.int32, (blocks_here, BLOCK), 1)
    valid = positions < (item_grid[:, 0] * item_grid[:, 1])[:, None]
    key_ok = valid[:, None, None, :]
    valid_wide = valid.astype(jnp.float32)[:, :, None]
    valid_share = lax.dynamic_slice_in_dim(
        valid.astype(jnp.float32).reshape(ROWS_DEV), row_first, share, 0
    )[:, None]
    bin_onehot = (noise_bin[:, None] == jnp.arange(NBINS)[None, :]).astype(jnp.float32)
    bin_local = jnp.sum(bin_onehot, axis=0) * (model_rank == 0).astype(jnp.float32)

    def masked_scores():
        raw = jnp.einsum("iqhc,ikhc->ihqk", query_low, key_low, preferred_element_type=jnp.float32)
        return jnp.where(key_ok, raw, -1e30)

    scores = masked_scores()
    top = jnp.max(scores, axis=-1, keepdims=True)
    log_total = top + jnp.log(jnp.sum(jnp.exp(scores - top), axis=-1, keepdims=True))
    prob_low = jnp.exp(scores - log_total).astype(jnp.bfloat16)
    attn_low = jnp.einsum(
        "ihqk,ikhc->iqhc", prob_low, value_low, preferred_element_type=jnp.float32
    ).astype(jnp.bfloat16)
    out_heads = out_full.reshape(heads_here, DH, D)
    attn_part = jnp.einsum("iqhc,hcd->iqd", attn_low, out_heads, preferred_element_type=jnp.float32)

    def own_rows_of(values):
        return lax.dynamic_slice_in_dim(values.reshape(ROWS_DEV, D), row_first, share, 0)

    row_item = (row_first + jnp.arange(share)) // BLOCK
    item_onehot = (row_item[:, None] == jnp.arange(blocks_here)[None, :]).astype(jnp.float32)

    def per_item(values):
        return jnp.einsum("si,sd->id", item_onehot, values, precision=lax.Precision.HIGHEST)

    mod_rows = jnp.einsum("si,ikd->skd", item_onehot, modulation, precision=lax.Precision.HIGHEST)
    scale_one_r = mod_rows[:, 1]
    gate_one_r = mod_rows[:, 2]
    shift_two_r = mod_rows[:, 3]
    scale_two_r = mod_rows[:, 4]
    gate_two_r = mod_rows[:, 5]
    resid_share = own_rows_of(resid)
    normed_one_share = own_rows_of(normed_one)
    inv_one_share = lax.dynamic_slice_in_dim(inv_one.reshape(ROWS_DEV, 1), row_first, share, 0)
    attention_share = row_share(attn_part.reshape(ROWS_DEV, D))
    mid_share = resid_share + gate_one_r * attention_share
    normed_two_share, inv_two_share = norm_rows(mid_share)
    hidden_two_share = (normed_two_share * (1.0 + scale_two_r) + shift_two_r).astype(jnp.bfloat16)
    hidden_two = row_whole(hidden_two_share).reshape(blocks_here, BLOCK, D)
    gate_up = jnp.einsum("ibd,dkf->ibkf", hidden_two, gu_full, preferred_element_type=jnp.float32)
    gate_raw = gate_up[:, :, 0]
    up_raw = gate_up[:, :, 1]
    gate_sig = jax.nn.sigmoid(gate_raw)
    gate_act = gate_raw * gate_sig
    inner = (gate_act * up_raw).astype(jnp.bfloat16)
    feed_part = jnp.einsum("ibf,fd->ibd", inner, down_full, preferred_element_type=jnp.float32)
    feed_part, kept = (feed_part, (inner, up_raw, gate_raw, gate_sig, gate_act))
    feed_share = row_share(feed_part.reshape(ROWS_DEV, D))
    result_share = mid_share + gate_two_r * feed_share
    result_whole = row_whole(result_share.astype(jnp.bfloat16))
    squares = jnp.stack(
        [
            jnp.sum(valid_share * result_share * result_share),
            jnp.sum(valid_share * (gate_one_r * attention_share) ** 2),
            jnp.sum(valid_share * (gate_two_r * feed_share) ** 2),
        ]
    )
    square_total, valid_total, bin_total = lax.psum(
        (squares, jnp.sum(valid_share), bin_local), ("dp", "mp")
    )
    stats_value = jnp.sqrt(square_total / (valid_total * D))
    item_count = jnp.sum(bin_onehot * bin_total[None, :], axis=1)
    weight_value = blocks_here * peers / (NBINS * item_count)
    top_grad = grads_full.astype(jnp.float32).reshape(blocks_here, BLOCK, D) * (
        weight_value[:, None, None] * valid_wide
    )
    top_share = own_rows_of(top_grad)
    feed_grad = (gate_two * top_grad).astype(jnp.bfloat16)
    grad_gate_two = per_item(top_share * feed_share)
    inner, up_raw, gate_raw, gate_sig, gate_act = kept
    inner_grad = jnp.einsum("ibd,fd->ibf", feed_grad, down_full, preferred_element_type=jnp.float32)
    grad_down_part = jnp.einsum("ibf,ibd->fd", inner, feed_grad, preferred_element_type=jnp.float32)
    gate_grad = (inner_grad * up_raw * gate_sig * (1.0 + gate_raw * (1.0 - gate_sig))).astype(
        jnp.bfloat16
    )
    up_grad = (inner_grad * gate_act).astype(jnp.bfloat16)
    gate_up_grad = jnp.stack([gate_grad, up_grad], axis=2)
    grad_gu_part = jnp.einsum(
        "ibd,ibkf->dkf", hidden_two, gate_up_grad, preferred_element_type=jnp.float32
    )
    hidden_two_part = jnp.einsum(
        "ibkf,dkf->ibd", gate_up_grad, gu_full, preferred_element_type=jnp.float32
    )
    grad_down, grad_gu, hidden_two_part = (grad_down_part, grad_gu_part, hidden_two_part)
    h2_grad_share = row_share(hidden_two_part.reshape(ROWS_DEV, D))
    grad_shift_two = per_item(h2_grad_share)
    grad_scale_two = per_item(h2_grad_share * normed_two_share)
    mid_grad_share = top_share + norm_back(
        h2_grad_share * (1.0 + scale_two_r), normed_two_share, inv_two_share
    )
    attention_grad_share = (gate_one_r * mid_grad_share).astype(jnp.bfloat16)
    grad_gate_one = per_item(mid_grad_share * attention_share)
    attention_grad = row_whole(attention_grad_share).reshape(blocks_here, BLOCK, D)
    attn_low_grad = jnp.einsum(
        "iqd,hcd->iqhc", attention_grad, out_heads, preferred_element_type=jnp.float32
    ).astype(jnp.bfloat16)
    grad_out_part = jnp.einsum(
        "iqhc,iqd->hcd", attn_low, attention_grad, preferred_element_type=jnp.float32
    ).reshape(local_width, D)
    prob_full = jnp.exp(masked_scores() - log_total)
    prob_grad = jnp.einsum(
        "iqhc,ikhc->ihqk", attn_low_grad, value_low, preferred_element_type=jnp.float32
    )
    value_grad = jnp.einsum(
        "ihqk,iqhc->ikhc", prob_low, attn_low_grad, preferred_element_type=jnp.float32
    )
    score_grad = (
        prob_full * (prob_grad - jnp.sum(prob_full * prob_grad, axis=-1, keepdims=True))
    ).astype(jnp.bfloat16)
    query_rot_grad = jnp.einsum(
        "ihqk,ikhc->iqhc", score_grad, key_low, preferred_element_type=jnp.float32
    ) * DH ** (-0.5)
    key_rot_grad = jnp.einsum(
        "ihqk,iqhc->ikhc", score_grad, query_low, preferred_element_type=jnp.float32
    )
    query_scaled_grad = rotate(query_rot_grad, cos_h, sin_h, cos_w, sin_w, -1.0)
    key_scaled_grad = rotate(key_rot_grad, cos_h, sin_h, cos_w, sin_w, -1.0)
    qgain_local = jnp.sum(query_scaled_grad * query_normed, axis=(0, 1, 2))
    kgain_local = jnp.sum(key_scaled_grad * key_normed, axis=(0, 1, 2))
    query_grad = norm_back(query_scaled_grad * q_gain, query_normed, query_inv)
    key_grad = norm_back(key_scaled_grad * k_gain, key_normed, key_inv)
    qkv_grad = jnp.stack(
        [
            query_grad.reshape(blocks_here, BLOCK, local_width),
            key_grad.reshape(blocks_here, BLOCK, local_width),
            value_grad.reshape(blocks_here, BLOCK, local_width),
        ],
        axis=2,
    ).astype(jnp.bfloat16)
    grad_qkv_part = jnp.einsum(
        "ibd,ibkc->dkc", hidden_one, qkv_grad, preferred_element_type=jnp.float32
    )
    hidden_one_part = jnp.einsum(
        "ibkc,dkc->ibd", qkv_grad, qkv_full, preferred_element_type=jnp.float32
    )
    grad_out, grad_qkv, qgain_part, kgain_part, hidden_one_part = (
        grad_out_part,
        grad_qkv_part,
        qgain_local,
        kgain_local,
        hidden_one_part,
    )
    h1_grad_share = row_share(hidden_one_part.reshape(ROWS_DEV, D))
    grad_shift_one = per_item(h1_grad_share)
    grad_scale_one = per_item(h1_grad_share * normed_one_share)
    input_share = mid_grad_share + norm_back(
        h1_grad_share * (1.0 + scale_one_r), normed_one_share, inv_one_share
    )
    input_whole = row_whole(input_share.astype(jnp.bfloat16))
    mod_partial = jnp.stack(
        [
            grad_shift_one,
            grad_scale_one,
            grad_gate_one,
            grad_shift_two,
            grad_scale_two,
            grad_gate_two,
        ],
        axis=1,
    )
    mod_grad = lax.psum(mod_partial, "mp").astype(jnp.bfloat16)
    mod_grad_own = lax.dynamic_slice_in_dim(mod_grad, model_rank * local_width, local_width, 2)
    mod_all = lax.all_gather(mod_grad_own, "dp", axis=0, tiled=True)
    cond_part = jnp.einsum("ikc,dkc->id", mod_all, w_ada, preferred_element_type=jnp.float32)
    cond_sum = lax.psum(cond_part, "mp")
    cond_total = lax.all_to_all(
        cond_sum.reshape(peers, blocks_here, ada_rows), "dp", split_axis=0, concat_axis=0, tiled=True
    )
    cond_total = jnp.moveaxis(cond_total, 0, 1).reshape(blocks_here, peers * ada_rows)
    grad_cond = cond_total * cond_sig * (1.0 + cond_wide * (1.0 - cond_sig))
    grad_ada = jnp.einsum("ir,ikc->rkc", silu_own, mod_all, preferred_element_type=jnp.float32)
    grad_bada = jnp.sum(mod_all.astype(jnp.float32), axis=0)
    qgain_total, kgain_total = lax.psum((qgain_part, kgain_part), ("dp", "mp"))
    qkv_own, out_own, gu_own, down_own = (
        grad_share(grad_qkv, 0),
        grad_share(grad_out, 1),
        grad_share(grad_gu, 0),
        grad_share(grad_down, 1),
    )
    result_cols = lax.dynamic_slice_in_dim(result_whole, model_rank * local_width, local_width, 1)
    input_cols = lax.dynamic_slice_in_dim(input_whole, model_rank * local_width, local_width, 1)
    back_index = jnp.minimum(flat_index, ROWS_DEV - 1)
    back_rows = result_cols[back_index].reshape(peers, slot_rows, local_width)
    back_grads = input_cols[back_index].reshape(peers, slot_rows, local_width)
    returned_rows, returned_grads = (
        lax.all_to_all(back_rows, "dp", split_axis=0, concat_axis=0, tiled=True),
        lax.all_to_all(back_grads, "dp", split_axis=0, concat_axis=0, tiled=True),
    )
    pick = jnp.minimum(place, peers * slot_rows - 1)
    empty = jnp.zeros((), jnp.bfloat16)
    out_rows = jnp.where(live[:, None], returned_rows.reshape(-1, local_width)[pick], empty)
    out_grads = jnp.where(live[:, None], returned_grads.reshape(-1, local_width)[pick], empty)
    return (
        out_rows,
        out_grads,
        grad_cond,
        grad_ada,
        grad_bada,
        qkv_own,
        qgain_total,
        kgain_total,
        out_own,
        gu_own,
        down_own,
        stats_value,
    )


MESH = pl.DeviceIdType.MESH
f32 = jnp.float32
bf16 = jnp.bfloat16
LANE_INDEX = 288
META = 1152
PAD = 128


def nn(left, right):
    return jnp.dot(left, right, preferred_element_type=f32)


def nt(left, right):
    return lax.dot_general(left, right, (((1,), (1,)), ((), ())), preferred_element_type=f32)


def tn(left, right):
    return lax.dot_general(left, right, (((0,), (0,)), ((), ())), preferred_element_type=f32)


def loop(count, step):
    def run(index, carry):
        step(index)
        return carry

    lax.fori_loop(0, count, run, 0)


def at128(index, size):
    return pl.ds(pl.multiple_of(index, 128), size)


def at16(index, size):
    return pl.ds(pl.multiple_of(index, 16), size)


GROUPS = (("c0", 768), ("c1", 768), ("c2", 768), ("out", 288), ("qkv", 864))


def scratch_list():
    vm = pltpu.VMEM
    items = {
        "sem": pltpu.SemaphoreType.DMA((400,)),
        "arow": vm((1, 1280), f32),
        "arec": vm((8, 1, 1280), f32),
        "amat": vm((8, 1280), f32),
        "xe": vm((384, 512), bf16),
        "place": vm((512, 512), bf16),
        "sx": vm((512, 384), bf16),
        "rx": vm((512, 384), bf16),
        "sg": vm((512, 256), bf16),
        "rg": vm((512, 256), bf16),
        "spread": vm((512, 256), bf16),
        "rb": vm((4, 256, 384), bf16),
        "gb": vm((4, 256, 256), bf16),
        "pms": vm((8, 6, 1, 288), f32),
        "pmr": vm((8, 6, 1, 288), f32),
        "mdb": vm((4, 6, 1, 288), f32),
        "modf": vm((8, 1152), f32),
        "h1": vm((256, 1152), bf16),
        "h1t": vm((1152, 256), bf16),
        "w1": vm((1152, 896), bf16),
        "wc0": vm((1152, 768), bf16),
        "wc1": vm((1152, 768), bf16),
        "wc2": vm((1152, 768), bf16),
        "wp1": vm((144, 896), bf16),
        "wp": vm((3, 144, 768), bf16),
        "wo": vm((1152, 288), bf16),
        "qkv": vm((256, 1024), f32),
        "qn": vm((4, 256, 128), f32),
        "kn": vm((4, 256, 128), f32),
        "qi": vm((4, 256, 1), f32),
        "ki": vm((4, 256, 1), f32),
        "ql": vm((4, 256, 128), bf16),
        "kl": vm((4, 256, 128), bf16),
        "vl": vm((4, 256, 128), bf16),
        "pf": vm((4, 256, 256), f32),
        "cosv": vm((256, 128), f32),
        "sinv": vm((256, 128), f32),
        "al": vm((256, 288), bf16),
        "rsa": vm((256, 1152), bf16),
        "rra": vm((3, 64, 1152), bf16),
        "rta": vm((64, 1152), bf16),
        "rsf": vm((256, 1152), bf16),
        "rrf": vm((3, 64, 1152), bf16),
        "rtf": vm((64, 1152), bf16),
        "rsh2": vm((256, 1152), bf16),
        "rrh2": vm((3, 64, 1152), bf16),
        "rth2": vm((64, 1152), bf16),
        "rsh1": vm((256, 1152), bf16),
        "rrh1": vm((3, 64, 1152), bf16),
        "rth1": vm((64, 1152), bf16),
        "h2": vm((256, 1152), bf16),
        "h2t": vm((1152, 256), bf16),
        "ag": vm((256, 1152), bf16),
        "agt": vm((1152, 256), bf16),
        "h2sum": vm((256, 1152), f32),
        "inner": vm((3, 256, 256), bf16),
        "gug": vm((3, 256, 512), bf16),
        "fg": vm((256, 1152), bf16),
        "fgt": vm((1152, 256), bf16),
        "da": vm((256, 384), f32),
        "dqkv": vm((256, 864), bf16),
        "share": vm((8, 64, 1152), f32),
        "invs": vm((2, 64, 1), f32),
        "gpart": vm((8, 1152), f32),
        "ras": vm((4, 64, 256), bf16),
        "rar": vm((4, 64, 256), bf16),
        "ias": vm((4, 64, 384), bf16),
        "iar": vm((4, 64, 384), bf16),
        "bs": vm((512, 256), bf16),
        "br": vm((512, 256), bf16),
        "bgs": vm((512, 384), bf16),
        "bgr": vm((512, 384), bf16),
        "hs": vm((4, 7, 1, 288), f32),
        "hr": vm((4, 7, 1, 288), f32),
        "gs": vm((7, 1, 288), f32),
        "grec": vm((8, 7, 1, 288), f32),
        "ms": vm((8, 6, 288), f32),
        "cps": vm((8, 144), f32),
        "cpr": vm((4, 8, 144), f32),
        "cts": vm((8, 1, 144), f32),
        "ctr": vm((8, 1, 144), f32),
    }
    for name, width in GROUPS:
        items["cs_" + name] = vm((4, 144, width), bf16)
        items["cr_" + name] = vm((4, 144, width), bf16)
        items["xs_" + name] = vm((2, 144, width), bf16)
        items["xr_" + name] = vm((2, 144, width), bf16)
        items["zs_" + name] = vm((2, 144, width), bf16)
        items["zr_" + name] = vm((2, 144, width), bf16)
    return items


class Refs:
    pass


ARGS = [
    "xt",
    "ct",
    "dest",
    "count",
    "grid",
    "bin",
    "cond",
    "wada",
    "bada",
    "wqkv",
    "qg",
    "kg",
    "woin",
    "wgu",
    "wdn",
    "outt",
    "gint",
    "gcond",
    "gada",
    "gbada",
    "gqkv",
    "gqg",
    "gkg",
    "gout",
    "ggu",
    "gdn",
    "stats",
]


def block_kernel(names, *refs):
    r = Refs()
    for name, ref in zip(ARGS + names, refs):
        setattr(r, name, ref)
    dp = lax.axis_index("dp")
    mp = lax.axis_index("mp")
    z, x, y, c = dp // 2, dp % 2, mp // 2, mp % 2
    zh, zl = z // 2, z % 2
    item = (2 * zh + c) * 2 + x
    tp = y * 2 + zl
    home = zl == c
    away = zl != c
    sem = r.sem
    taken = [0]

    def sems(count):
        first = taken[0]
        taken[0] += count
        return first

    def device(zz, xx, yy, cc):
        return (zz * 2 + xx, yy * 2 + cc)

    def worker(index, part):
        zi, xi = index // 2, index % 2
        return device(2 * (zi // 2) + part % 2, xi, part // 2, zi % 2)

    def mate(step):
        return device(2 * zh + (zl ^ (step & 1)), x, y ^ (step >> 1), c)

    def remote(src, dst, ss, rs, dev):
        return pltpu.make_async_remote_copy(
            src_ref=src,
            dst_ref=dst,
            send_sem=sem.at[ss],
            recv_sem=sem.at[rs],
            device_id=dev,
            device_id_type=MESH,
        )

    pending = []

    def send(src, dst, ss, rs, dev):
        copy = remote(src, dst, ss, rs, dev)
        copy.start()
        pending.append(copy.wait_send)

    def send_unless(same, src, dst, ss, rs, dev):
        other = jnp.logical_not(same)

        @pl.when(same)
        def _():
            pltpu.make_async_copy(src, dst, sem.at[rs]).start()

        @pl.when(other)
        def _():
            remote(src, dst, ss, rs, dev).start()

        def finish():
            @pl.when(other)
            def _():
                remote(src, dst, ss, rs, dev).wait_send()

        pending.append(finish)

    def arrived(dst, rs):
        pltpu.make_async_copy(dst, dst, sem.at[rs]).wait()

    def to_workers(source, target, base, slot_of):
        for step in range(8):
            index = (dp + step) % 8
            args = (source(index), target(dp), base + step, base + 8 + slot_of(dp), worker(index, mp))
            if step == 0:
                send_unless(home, *args)
            else:
                send(*args)

    def to_homes(source, target, base):
        for step in range(8):
            index = (dp + step) % 8
            args = (source(index), target(item), base + step, base + 8 + item, (index, tp))
            if step == 0:
                send_unless(home, *args)
            else:
                send(*args)

    groups = {
        "attn": (r.wp1, r.w1),
        "wo": (r.woin, r.wo),
        "c0": (r.wp.at[0], r.wc0),
        "c1": (r.wp.at[1], r.wc1),
        "c2": (r.wp.at[2], r.wc2),
    }
    w_base = {g: sems(2 + 2 + 4 + 8) for g in groups}

    def slot(ref, index):
        return ref.at[at16(index * 144, 144)]

    def gather_z(g, rels=(1, 0)):
        src, full = groups[g]
        base = w_base[g]
        for rel in rels:
            zt = c + 2 * (zh ^ rel)
            args = (src, slot(full, dp), base + rel, base + 8 + dp, device(zt, x, y, zl))
            if rel == 0:
                send_unless(home, *args)
            else:
                send(*args)

    def gather_x(g, rel):
        full, base = groups[g][1], w_base[g]
        s = (c + 2 * (zh ^ rel)) * 2 + x
        mine = slot(full, s)
        arrived(mine, base + 8 + s)
        send(mine, mine, base + 2 + rel, base + 8 + s, device(z, 1 - x, y, c))
        send(mine, mine, base + 4 + rel, base + 8 + s, device(z, x, y, 1 - c))

    def gather_core(g, rel):
        full, base = groups[g][1], w_base[g]
        s = (c + 2 * (zh ^ rel)) * 2 + 1 - x
        mine = slot(full, s)
        arrived(mine, base + 8 + s)
        send(mine, mine, base + 6 + rel, base + 8 + s, device(z, x, y, 1 - c))

    def gather_done(g):
        full, base = groups[g][1], w_base[g]
        for rel in range(2):
            for xx in range(2):
                s = (1 - c + 2 * rel) * 2 + xx
                arrived(slot(full, s), base + 8 + s)

    z_mate = device(2 * zh + 1 - zl, x, y, c)
    y_mate = device(z, x, 1 - y, c)

    class Gather:
        def __init__(self, view):
            self.view, self.base = view, sems(6)
            mine = view(tp)
            send(mine, mine, self.base, self.base + 3, z_mate)
            send(mine, mine, self.base + 1, self.base + 4, y_mate)

        def relay(self):
            other = self.view(tp ^ 1)
            arrived(other, self.base + 3)
            send(other, other, self.base + 2, self.base + 5, y_mate)

        def done(self):
            arrived(self.view(tp ^ 2), self.base + 4)
            arrived(self.view(tp ^ 3), self.base + 5)

    class Scatter:
        def __init__(self, name):
            self.base = sems(6)
            self.sent, self.rec, self.sum = (getattr(r, k + name) for k in ("rs", "rr", "rt"))
            for step, t in enumerate((tp ^ 3, tp ^ 2)):
                send(self.view(t), self.rec.at[step], self.base + step, self.base + 3 + step, y_mate)

        def view(self, t):
            return self.sent.at[at16(t * 64, 64)]

        def relay(self):
            arrived(self.rec.at[0], self.base + 3)
            both = self.view(tp ^ 1)[...].astype(f32) + self.rec[0].astype(f32)
            self.sum[...] = both.astype(bf16)
            send(self.sum, self.rec.at[2], self.base + 2, self.base + 5, z_mate)

        def total(self):
            arrived(self.rec.at[1], self.base + 4)
            total = self.view(tp)[...].astype(f32) + self.rec[1].astype(f32)
            arrived(self.rec.at[2], self.base + 5)
            return total + self.rec[2].astype(f32)

    def rows_view(buf):
        return lambda t: buf.at[at16(t * 64, 64)]

    def mates_send(source, target, base):
        for step in range(1, 4):
            send(source(tp ^ step), target(step), base + step, base + 4 + step, mate(step))

    g_base = {name: sems(4 + 4 + 2 + 2 + 2 + 2) for name, _ in GROUPS}

    def block(name, s):
        rows = at16(s * 144, 144)
        if name == "out":
            return nn(r.agt[rows, :], r.al[...])
        if name == "qkv":
            return nn(r.h1t[rows, :], r.dqkv[...])
        k = int(name[1:])
        return jnp.concatenate(
            [nn(r.h2t[rows, :], r.gug[k]), nn(r.fgt[rows, :], r.inner[k])], axis=-1
        )

    def reduce_core(name):
        base = g_base[name]
        cs, cr = getattr(r, "cs_" + name), getattr(r, "cr_" + name)

        for xx in (1 - x, x):
            for rel in (1 - zh, zh):
                q = 2 * rel + xx
                cs[q] = block(name, (1 - c + 2 * rel) * 2 + xx).astype(bf16)
                send(cs.at[q], cr.at[q], base + q, base + 4 + q, device(z, x, y, 1 - c))

    def reduce_x(name, far):
        base = g_base[name]
        cr, xs, xr = (getattr(r, k + name) for k in ("cr_", "xs_", "xr_"))
        rel = zh ^ far
        q = 2 * rel + 1 - x
        part = block(name, (c + 2 * rel) * 2 + 1 - x)
        arrived(cr.at[q], base + 4 + q)
        xs[rel] = (part + cr[q].astype(f32)).astype(bf16)
        send(xs.at[rel], xr.at[rel], base + 8 + rel, base + 10 + rel, device(z, 1 - x, y, c))

    def reduce_z(name, far):
        base = g_base[name]
        cr, xr, zs, zr = (getattr(r, k + name) for k in ("cr_", "xr_", "zs_", "zr_"))
        rel = zh ^ far
        q = 2 * rel + x
        part = block(name, (c + 2 * rel) * 2 + x)
        arrived(cr.at[q], base + 4 + q)
        part = part + cr[q].astype(f32)
        arrived(xr.at[rel], base + 10 + rel)
        zs[far] = (part + xr[rel].astype(f32)).astype(bf16)
        args = (
            zs.at[far], zr.at[zh], base + 12 + far, base + 14 + zh,
            device(c + 2 * rel, x, y, zl),
        )
        if far == 0:
            send_unless(home, *args)
        else:
            send(*args)

    def reduce_end(name):
        base = g_base[name]
        zr = getattr(r, "zr_" + name)
        for half in range(2):
            arrived(zr.at[half], base + 14 + half)
        return zr[0].astype(f32) + zr[1].astype(f32)

    def transpose(src, dst):
        def step(j):
            dst[at128(j * 128, 128), :] = src[:, at128(j * 128, 128)].T

        loop(9, step)

    lane128 = lax.broadcasted_iota(jnp.int32, (1, PAD), 1)
    head_lane = lane128 < 72
    quarter = lane128 // 18
    even = quarter % 2 == 0

    def swap(v):
        return jnp.where(even, pltpu.roll(v, PAD - 18, 1), pltpu.roll(v, 18, 1))

    def norm_of(v):
        inv = lax.rsqrt(jnp.mean(v * v, axis=-1, keepdims=True) + epsilon)
        return v * inv, inv

    def back(g, normed, inv):
        return inv * (g - normed * jnp.mean(g * normed, axis=-1, keepdims=True))

    barrier = pltpu.get_barrier_semaphore()
    for i in range(8):
        for j in range(4):
            if i or j:
                pl.semaphore_signal(
                    barrier, inc=1, device_id=((dp + i) % 8, mp ^ j), device_id_type=MESH
                )

    cond = r.cond[...].astype(f32)
    sig_c = jax.nn.sigmoid(cond)
    r.arow[0:1, 0:META] = (cond * sig_c).astype(bf16).astype(f32)
    meta = jnp.where(lane128 == 0, r.bin[0].astype(f32), 0.0)
    meta = jnp.where(lane128 == 1, r.grid[0, 0].astype(f32), meta)
    meta = jnp.where(lane128 == 2, r.grid[0, 1].astype(f32), meta)
    r.arow[0:1, META : META + 128] = meta
    r.arec[dp] = r.arow[...]

    dest = r.dest[...]
    lane512 = lax.broadcasted_iota(jnp.int32, (1, 512), 1)
    live = lane512 < r.count[0]
    target = dest >> 8
    within = dest & 255
    owner = lax.broadcasted_iota(jnp.int32, (8, 512), 0)
    member = jnp.where((owner == target) & live, 1.0, 0.0)
    upper = lax.broadcasted_iota(jnp.int32, (512, 512), 0) <= lax.broadcasted_iota(
        jnp.int32, (512, 512), 1
    )
    running = nn(member.astype(bf16), jnp.where(upper, 1.0, 0.0).astype(bf16))
    rank = jnp.sum(running * member, axis=0, keepdims=True).astype(jnp.int32) - 1
    spot = jnp.where(live, target * 64 + rank, -1)
    slots = lax.broadcasted_iota(jnp.int32, (512, 512), 0)
    r.place[...] = jnp.where(slots == spot, 1.0, 0.0).astype(bf16)
    r.xe[0:288, :] = r.xt[...]
    top_row = lax.broadcasted_iota(jnp.int32, (32, 512), 0) == 0
    r.xe[288:320, :] = jnp.where(top_row, within + 1, 0).astype(f32).astype(bf16)
    r.xe[320:352, :] = r.ct[256:288, :]
    r.xe[352:384, :] = jnp.zeros((32, 512), bf16)
    r.sx[...] = nt(r.place[...], r.xe[...]).astype(bf16)
    for p in range(3):
        r.wp1[:, 288 * p : 288 * p + 288] = r.wqkv[p]
    r.wp1[:, 864:896] = jnp.zeros((144, 32), bf16)

    pl.semaphore_wait(barrier, 31)
    a_base = sems(16)
    for step in range(1, 8):
        index = (dp + step) % 8
        send(r.arow, r.arec.at[dp], a_base + step, a_base + 8 + dp, (index, mp))
    x_base = sems(16)
    to_workers(
        lambda i: r.sx.at[at16(i * 64, 64)], lambda i: r.rx.at[at16(i * 64, 64)], x_base, lambda i: i
    )
    for k in range(3):
        r.wp[k, :, 0:256] = r.wgu[:, 0, 256 * k : 256 * k + 256]
        r.wp[k, :, 256:512] = r.wgu[:, 1, 256 * k : 256 * k + 256]
        r.wp[k, :, 512:768] = r.wdn[:, 256 * k : 256 * k + 256]
    r.sg[...] = nt(r.place[...], r.ct[0:256, :]).astype(bf16)

    for step in range(1, 8):
        index = (dp + step) % 8
        arrived(r.arec.at[index], a_base + 8 + index)
    for i in range(8):
        r.amat[i : i + 1, :] = r.arec[i]
    pick = lax.broadcasted_iota(jnp.int32, (1152, 144), 0) == (
        lax.broadcasted_iota(jnp.int32, (1152, 144), 1) + 144 * dp
    )
    silu_own = nn(r.amat[:, 0:META].astype(bf16), jnp.where(pick, 1.0, 0.0).astype(bf16)).astype(bf16)
    first = (dp == 0).astype(f32)
    for k in range(6):
        part = nn(silu_own, r.wada[k]) + first * r.bada[k : k + 1, :].astype(f32)
        for i in range(8):
            r.pms[i, k] = part[i : i + 1, :]
    m_base = sems(16)
    to_workers(lambda i: r.pms.at[i], lambda i: r.pmr.at[i], m_base, lambda i: i)
    gather_z("attn")
    gather_z("wo")

    about = r.arec[item]
    height = about[:, META + 1 : META + 2]
    width = about[:, META + 2 : META + 3]
    bins = r.amat[:, META : META + 1]
    alike = jnp.sum(
        jnp.where(bins == about[:, META : META + 1], 1.0, 0.0), axis=0, keepdims=True
    )
    weight = 8.0 / (NBINS * alike)
    spots = lax.broadcasted_iota(jnp.int32, (256, 1), 0).astype(f32)
    high = jnp.floor((spots + 0.5) / width)
    wide = spots - high * width
    freq = jnp.exp(-math.log(10000.0) * (lane128 - 18 * quarter).astype(f32) / 18.0)
    angle = jnp.where(quarter < 2, high, wide) * freq
    r.cosv[...] = jnp.where(head_lane, jnp.cos(angle), 0.0)
    r.sinv[...] = jnp.where(head_lane, jnp.where(even, -jnp.sin(angle), jnp.sin(angle)), 0.0)
    used = height * width
    key_ok = lax.broadcasted_iota(jnp.int32, (1, 256), 1).astype(f32) < used
    row_first = (tp * 64).astype(f32)
    share_spots = lax.broadcasted_iota(jnp.int32, (64, 1), 0).astype(f32) + row_first
    valid_share = jnp.where(share_spots < used, 1.0, 0.0)

    for s in range(8):
        arrived(r.rx.at[pl.ds(s * 64, 64)], x_base + 8 + s)
    number = r.rx[:, 288:289].astype(jnp.int32)
    r.spread[...] = jnp.where(
        number == lax.broadcasted_iota(jnp.int32, (512, 256), 1) + 1, 1.0, 0.0
    ).astype(bf16)
    r.rb[tp] = tn(r.spread[...], r.rx[...]).astype(bf16)
    rb_all = Gather(lambda t: r.rb.at[t])

    gather_x("attn", 0)
    gather_x("attn", 1)
    for s in range(8):
        arrived(r.pmr.at[s], m_base + 8 + s)
    total = r.pmr[0]
    for s in range(1, 8):
        total = total + r.pmr[s]
    r.mdb[tp] = total.astype(bf16).astype(f32)
    mdb_all = Gather(lambda t: r.mdb.at[t])
    rb_all.relay()
    mdb_all.relay()
    t_base = sems(16)
    to_workers(
        lambda i: r.sg.at[at16(i * 64, 64)], lambda i: r.rg.at[at16(i * 64, 64)], t_base, lambda i: i
    )
    gather_z("c0")
    gather_z("c1")
    gather_core("attn", 0)
    gather_core("attn", 1)

    gather_x("wo", 0)
    gather_x("wo", 1)
    rb_all.done()
    mdb_all.done()
    for k in range(6):
        for t in range(4):
            r.modf[k : k + 1, 288 * t : 288 * t + 288] = r.mdb[t, k]

    def joined(start):
        return jnp.concatenate(
            [r.rb[t, at16(start, 64), 0:288].astype(f32) for t in range(4)], axis=-1
        )

    def joined_grad(start):
        parts = []
        for t in range(4):
            parts.append(r.gb[t, at16(start, 64), :].astype(f32))
            parts.append(r.rb[t, at16(start, 64), 320:352].astype(f32))
        return jnp.concatenate(parts, axis=-1)

    def first_hidden(i):
        normed, _ = norm_of(joined(i * 64))
        shift, scale = r.modf[0:1, :], r.modf[1:2, :]
        r.h1[at16(i * 64, 64), :] = (normed * (1.0 + scale) + shift).astype(bf16)

    loop(4, first_hidden)
    RESID, NORM1, ATT, MID, NORM2, TOP, MIDG = range(7)
    mine = joined(tp * 64)
    normed, inv = norm_of(mine)
    r.share[RESID] = mine
    r.share[NORM1] = normed
    r.invs[0] = inv
    gather_done("attn")

    def project(j):
        r.qkv[:, at128(j * 256, 256)] = nn(r.h1[...], r.w1[:, at128(j * 256, 256)])

    loop(3, project)
    r.qkv[:, 768:896] = nn(r.h1[...], r.w1[:, 768:896])

    gather_x("c0", 0)
    gather_core("wo", 0)
    gather_core("wo", 1)
    scale_q = 72 ** (-0.5)
    pad = jnp.zeros((1, PAD - 72), f32)
    gains = {k: jnp.concatenate([g[...], pad], axis=-1) for k, g in (("q", r.qg), ("k", r.kg))}
    for h in range(4):
        for kind, offset, normed_ref, inv_ref, low_ref in (
            ("q", 0, r.qn, r.qi, r.ql),
            ("k", 288, r.kn, r.ki, r.kl),
        ):
            lane = offset + 72 * h
            v = jnp.where(head_lane, r.qkv[:, lane : lane + 128], 0.0)
            inv = lax.rsqrt(jnp.sum(v * v, axis=-1, keepdims=True) * (1.0 / 72) + epsilon)
            v = v * inv
            normed_ref[h] = v
            inv_ref[h] = inv
            v = v * gains[kind]
            v = v * r.cosv[...] + swap(v) * r.sinv[...]
            if kind == "q":
                v = v * scale_q
            low_ref[h] = v.astype(bf16)
        lane = 576 + 72 * h
        r.vl[h] = jnp.where(head_lane, r.qkv[:, lane : lane + 128], 0.0).astype(bf16)
    for h in range(4):
        scores = jnp.where(key_ok, nt(r.ql[h], r.kl[h]), -1e30)
        scores = jnp.exp(scores - jnp.max(scores, axis=-1, keepdims=True))
        prob = scores / jnp.sum(scores, axis=-1, keepdims=True)
        r.pf[h] = prob
        r.al[:, 72 * h : 72 * h + 72] = nn(prob.astype(bf16), r.vl[h])[:, 0:72].astype(bf16)

    gather_done("wo")

    def project_out(j):
        r.rsa[:, at128(j * 384, 384)] = nt(r.al[...], r.wo[at128(j * 384, 384), :]).astype(bf16)

    loop(3, project_out)
    sum_a = Scatter("a")
    sum_a.relay()

    gather_z("c2", (1,))
    gather_x("c0", 1)
    gather_core("c0", 0)
    gather_x("c1", 0)
    gather_x("c1", 1)
    for s in range(8):
        arrived(r.rg.at[pl.ds(s * 64, 64)], t_base + 8 + s)
    r.gb[tp] = tn(r.spread[...], r.rg[...]).astype(bf16)
    gb_all = Gather(lambda t: r.gb.at[t])
    attention = sum_a.total()
    r.share[ATT] = attention
    middle = r.share[RESID] + r.modf[2:3, :] * attention
    r.share[MID] = middle
    normed, inv = norm_of(middle)
    r.share[NORM2] = normed
    r.invs[1] = inv
    r.h2[at16(tp * 64, 64), :] = (normed * (1.0 + r.modf[4:5, :]) + r.modf[3:4, :]).astype(bf16)
    h2_all = Gather(rows_view(r.h2))
    gather_z("c2", (0,))
    gather_core("c0", 1)
    gather_x("c2", 0)
    gb_all.relay()
    h2_all.relay()
    gather_x("c2", 1)
    gather_core("c1", 0)
    gather_core("c1", 1)
    transpose(r.h1, r.h1t)
    chunks = (r.wc0, r.wc1, r.wc2)

    def swiglu(k):
        full = chunks[k]
        gate = nn(r.h2[...], full[:, 0:256])
        up = nn(r.h2[...], full[:, 256:512])
        grad = nn(r.fg[...], full[:, 512:768])
        sig = jax.nn.sigmoid(gate)
        act = gate * sig
        r.inner[k] = (act * up).astype(bf16)
        r.gug[k, :, 0:256] = (grad * up * sig * (1.0 + gate * (1.0 - sig))).astype(bf16)
        r.gug[k, :, 256:512] = (grad * act).astype(bf16)

    def hidden_back(k):
        full = chunks[k]

        def step(j):
            rows = at128(j * 384, 384)
            part = nt(r.gug[k], full[rows, 0:512])
            if k > 0:
                part = part + r.h2sum[:, rows]
            if k < 2:
                r.h2sum[:, rows] = part
            else:
                r.rsh2[:, rows] = part.astype(bf16)

        loop(3, step)

    gb_all.done()
    def feed_rows(i):
        rows = lax.broadcasted_iota(jnp.int32, (64, 1), 0).astype(f32) + (i * 64).astype(f32)
        factor = jnp.where(rows < used, weight, 0.0)
        r.fg[at16(i * 64, 64), :] = (joined_grad(i * 64) * factor * r.modf[5:6, :]).astype(bf16)

    loop(4, feed_rows)
    r.share[TOP] = joined_grad(tp * 64) * (weight * valid_share)
    transpose(r.fg, r.fgt)

    h2_all.done()
    gather_done("c0")
    swiglu(0)
    transpose(r.h2, r.h2t)
    reduce_core("c0")
    gather_core("c2", 0)
    gather_done("c1")
    swiglu(1)
    reduce_x("c0", 1)
    reduce_x("c0", 0)
    reduce_core("c1")
    gather_core("c2", 1)
    hidden_back(0)
    hidden_back(1)
    gather_done("c2")
    swiglu(2)
    hidden_back(2)
    sum_h2 = Scatter("h2")
    reduce_x("c1", 1)
    reduce_z("c0", 1)
    reduce_x("c1", 0)
    reduce_core("c2")
    reduce_x("c2", 1)
    reduce_x("c2", 0)
    sum_h2.relay()
    reduce_z("c0", 0)

    def feed_out(j):
        rows = at128(j * 384, 384)
        part = nt(r.inner[0], r.wc0[rows, 512:768])
        part = part + nt(r.inner[1], r.wc1[rows, 512:768])
        part = part + nt(r.inner[2], r.wc2[rows, 512:768])
        r.rsf[:, rows] = part.astype(bf16)

    loop(3, feed_out)
    sum_f = Scatter("f")
    reduce_z("c1", 1)
    grad_h2 = sum_h2.total()
    normed = r.share[NORM2]
    r.gpart[3:4, :] = jnp.sum(grad_h2, axis=0, keepdims=True)
    r.gpart[4:5, :] = jnp.sum(grad_h2 * normed, axis=0, keepdims=True)
    mid_grad = r.share[TOP] + back(grad_h2 * (1.0 + r.modf[4:5, :]), normed, r.invs[1])
    r.share[MIDG] = mid_grad
    r.gpart[2:3, :] = jnp.sum(mid_grad * r.share[ATT], axis=0, keepdims=True)
    r.ag[at16(tp * 64, 64), :] = (r.modf[2:3, :] * mid_grad).astype(bf16)
    ag_all = Gather(rows_view(r.ag))
    reduce_z("c1", 0)
    sum_f.relay()

    ag_all.relay()
    reduce_z("c2", 1)
    ag_all.done()
    r.da[:, 0:288] = nn(r.ag[...], r.wo[...])
    transpose(r.ag, r.agt)

    reduce_core("out")
    def total_of(v):
        return jnp.sum(jnp.sum(v, axis=0, keepdims=True), axis=1, keepdims=True)

    squares = []
    kept = []

    def result_part():
        feed = sum_f.total()
        fed = r.modf[5:6, :] * feed
        result = r.share[MID] + fed
        r.gpart[5:6, :] = jnp.sum(r.share[TOP] * feed, axis=0, keepdims=True)
        att = r.modf[2:3, :] * r.share[ATT]

        squares[:] = [total_of(valid_share * v * v) for v in (result, att, fed)]
        low_result = result.astype(bf16)
        for t in range(4):
            r.ras[t] = low_result[:, 288 * t : 288 * t + 256]
            r.ias[t, :, 320:352] = low_result[:, 288 * t + 256 : 288 * t + 288]
        ra_base = sems(8)
        kept.append(ra_base)
        r.rar[tp] = r.ras[tp]
        mates_send(lambda t: r.ras.at[t], lambda step: r.rar.at[tp], ra_base)

    def rows_part():
        ra_base = kept[0]
        for step in range(1, 4):
            arrived(r.rar.at[tp ^ step], ra_base + 4 + step)
        rar = jnp.concatenate([r.rar[t] for t in range(4)], axis=0)
        r.bs[...] = nn(r.spread[...], rar).astype(bf16)
        b_base = sems(16)
        to_homes(lambda i: r.bs.at[at16(i * 64, 64)], lambda i: r.br.at[at16(i * 64, 64)], b_base)

        kept.append(b_base)

    def first_pump():
        result_part()
        reduce_x("out", 1)
        reduce_x("out", 0)

    def second_pump():
        reduce_z("c2", 0)

    def third_pump():
        rows_part()
        reduce_z("out", 1)

    pumps = [None, first_pump, second_pump, third_pump]

    qsum = jnp.zeros((1, PAD), f32)
    ksum = jnp.zeros((1, PAD), f32)
    for h in range(4):
        if h > 0:
            pumps[h]()
        grad = jnp.where(head_lane, r.da[:, 72 * h : 72 * h + 128], 0.0).astype(bf16)
        prob = r.pf[h]
        prob_grad = nt(grad, r.vl[h])
        mixed = jnp.sum(prob * prob_grad, axis=-1, keepdims=True)
        score = (prob * (prob_grad - mixed)).astype(bf16)
        value_grad = tn(prob.astype(bf16), grad)
        r.dqkv[:, 576 + 72 * h : 648 + 72 * h] = value_grad[:, 0:72].astype(bf16)
        for kind, offset, normed_ref, inv_ref in (
            ("q", 0, r.qn, r.qi),
            ("k", 288, r.kn, r.ki),
        ):
            if kind == "q":
                turned = nn(score, r.kl[h]) * scale_q
            else:
                turned = tn(score, r.ql[h])
            turned = turned * r.cosv[...] - swap(turned) * r.sinv[...]
            normed = normed_ref[h]
            along = jnp.sum(turned * normed, axis=0, keepdims=True)
            if kind == "q":
                qsum = qsum + along
            else:
                ksum = ksum + along
            g = turned * gains[kind]
            mean = jnp.sum(g * normed, axis=-1, keepdims=True) * (1.0 / 72)
            g = inv_ref[h] * (g - normed * mean)
            r.dqkv[:, offset + 72 * h : offset + 72 * h + 72] = g[:, 0:72].astype(bf16)

    def first_back(j):
        r.rsh1[:, at128(j * 384, 384)] = nt(r.dqkv[...], r.w1[at128(j * 384, 384), 0:864]).astype(bf16)

    loop(3, first_back)
    sum_h1 = Scatter("h1")
    reduce_z("out", 0)
    reduce_core("qkv")
    reduce_x("qkv", 1)
    reduce_x("qkv", 0)
    sum_h1.relay()
    grad_h1 = sum_h1.total()
    normed = r.share[NORM1]
    r.gpart[0:1, :] = jnp.sum(grad_h1, axis=0, keepdims=True)
    r.gpart[1:2, :] = jnp.sum(grad_h1 * normed, axis=0, keepdims=True)
    in_grad = r.share[MIDG] + back(grad_h1 * (1.0 + r.modf[1:2, :]), normed, r.invs[0])
    low_grad = in_grad.astype(bf16)
    for t in range(4):
        r.ias[t, :, 0:288] = low_grad[:, 288 * t : 288 * t + 288]
    numbers = jnp.concatenate(
        [qsum[:, 0:72], ksum[:, 0:72], squares[0], squares[1], squares[2],
         total_of(valid_share), jnp.zeros((1, 288 - 148), f32)],
        axis=-1,
    )
    for t in range(4):
        for k in range(6):
            r.hs[t, k] = r.gpart[k : k + 1, 288 * t : 288 * t + 288]
        r.hs[t, 6] = numbers
    h_base = sems(8)
    r.hr[tp] = r.hs[tp]
    mates_send(lambda t: r.hs.at[t], lambda step: r.hr.at[tp], h_base)
    ia_base = sems(8)
    r.iar[tp] = r.ias[tp]
    mates_send(lambda t: r.ias.at[t], lambda step: r.iar.at[tp], ia_base)

    for step in range(1, 4):
        arrived(r.hr.at[tp ^ step], h_base + 4 + step)
    total = r.hr[0] + r.hr[1] + r.hr[2] + r.hr[3]
    for k in range(6):
        r.gs[k] = total[k].astype(bf16).astype(f32)
    r.gs[6] = total[6]
    g2_base = sems(16)
    to_homes(lambda i: r.gs, lambda i: r.grec.at[i], g2_base)
    reduce_z("qkv", 1)
    for step in range(1, 4):
        arrived(r.iar.at[tp ^ step], ia_base + 4 + step)
    iar = jnp.concatenate([r.iar[t] for t in range(4)], axis=0)
    r.bgs[...] = nn(r.spread[...], iar).astype(bf16)
    bg_base = sems(16)
    to_homes(lambda i: r.bgs.at[at16(i * 64, 64)], lambda i: r.bgr.at[at16(i * 64, 64)], bg_base)
    reduce_z("qkv", 0)
    for i in range(8):
        arrived(r.grec.at[i], g2_base + 8 + i)
    cond_part = jnp.zeros((8, 144), f32)
    for k in range(6):
        grads = jnp.concatenate([r.grec[i, k] for i in range(8)], axis=0)
        low = grads.astype(bf16)
        r.gada[k] = tn(silu_own, low)
        r.gbada[k : k + 1, :] = jnp.sum(grads, axis=0, keepdims=True)
        cond_part = cond_part + nt(low, r.wada[k])
    totals = r.grec[0, 6]
    for i in range(1, 8):
        totals = totals + r.grec[i, 6]
    r.gqg[...] = totals[:, 0:72]
    r.gkg[...] = totals[:, 72:144]
    ratio = totals[:, 144:147] / (totals[:, 147:148] * 1152.0)
    r.stats[...] = jnp.sqrt(ratio)
    r.cps[...] = cond_part
    c_base = sems(8)
    r.cpr[mp] = cond_part
    for step in range(1, 4):
        send(r.cps, r.cpr.at[mp], c_base + step, c_base + 4 + step, (dp, mp ^ step))
    for step in range(1, 4):
        arrived(r.cpr.at[mp ^ step], c_base + 4 + step)
    cond_sum = r.cpr[0] + r.cpr[1] + r.cpr[2] + r.cpr[3]
    for i in range(8):
        r.cts[i] = cond_sum[i : i + 1, :]
    ct_base = sems(16)
    r.ctr[dp] = r.cts[dp]
    for step in range(1, 8):
        index = (dp + step) % 8
        send(r.cts.at[index], r.ctr.at[dp], ct_base + step, ct_base + 8 + dp, (index, mp))

    for k in range(3):
        grad = reduce_end(f"c{k}")
        lanes = slice(256 * k, 256 * k + 256)
        r.ggu[:, 0, lanes] = grad[:, 0:256]
        r.ggu[:, 1, lanes] = grad[:, 256:512]
        r.gdn[:, lanes] = grad[:, 512:768]
    for i in range(8):
        arrived(r.br.at[pl.ds(i * 64, 64)], kept[1] + 8 + i)
    r.outt[0:256, :] = tn(r.br[...], r.place[...]).astype(bf16)
    grad = reduce_end("qkv")
    for p in range(3):
        r.gqkv[p] = grad[:, 288 * p : 288 * p + 288]
    r.gout[...] = reduce_end("out")
    for i in range(8):
        arrived(r.bgr.at[pl.ds(i * 64, 64)], bg_base + 8 + i)
    both = tn(r.bgr[...], r.place[...]).astype(bf16)
    r.gint[...] = both[0:288, :]
    r.outt[256:288, :] = both[320:352, :]
    for step in range(1, 8):
        index = (dp + step) % 8
        arrived(r.ctr.at[index], ct_base + 8 + index)
    for s in range(8):
        r.gcond[0:1, 144 * s : 144 * s + 144] = r.ctr[s]
    cond = r.cond[...].astype(f32)
    sig_c = jax.nn.sigmoid(cond)
    r.gcond[...] = r.gcond[...] * sig_c * (1.0 + cond * (1.0 - sig_c))
    for finish in pending:
        finish()
    assert taken[0] <= 400


def copy_out(*refs):
    count = len(refs) // 2
    sem = refs[-1]
    copies = [pltpu.make_async_copy(refs[i], refs[count + i], sem.at[i]) for i in range(count)]
    for copy in copies:
        copy.start()
    for copy in copies:
        copy.wait()


def body_kernel(
    x_src, cotangent, route_dest, route_count, item_grid, noise_bin, cond, w_ada, b_ada,
    w_qkv, q_gain, k_gain, w_out, w_gu, w_down,
):
    scratch = scratch_list()
    vmem = pl.BlockSpec(memory_space=pltpu.VMEM)
    smem = pl.BlockSpec(memory_space=pltpu.SMEM)
    shapes = [
        ((288, 512), bf16), ((288, 512), bf16), ((1, 1152), f32), ((6, 144, 288), f32),
        ((6, 288), f32), ((3, 144, 288), f32), ((1, 72), f32), ((1, 72), f32),
        ((144, 288), f32), ((144, 2, 768), f32), ((144, 768), f32), ((1, 3), f32),
    ]
    outs = pl.pallas_call(
        functools.partial(block_kernel, list(scratch)),
        out_shape=[jax.ShapeDtypeStruct(s, d) for s, d in shapes],
        in_specs=[vmem, vmem, vmem, smem, smem, smem] + [vmem] * 9,
        out_specs=[vmem] * len(shapes),
        scratch_shapes=list(scratch.values()),
        compiler_params=pltpu.CompilerParams(
            has_side_effects=True, vmem_limit_bytes=67000000, collective_id=0
        ),
        name="block",
    )(
        x_src.T, cotangent.T, route_dest.reshape(1, SRC_CAP), route_count, item_grid, noise_bin,
        cond, jnp.transpose(w_ada, (1, 0, 2)), b_ada, jnp.transpose(w_qkv, (1, 0, 2)),
        q_gain.reshape(1, DH), k_gain.reshape(1, DH), w_out.T, w_gu, w_down.T,
    )
    outs = pl.pallas_call(
        copy_out,
        out_shape=[jax.ShapeDtypeStruct(s, d) for s, d in shapes],
        in_specs=[vmem] * len(shapes),
        out_specs=[pl.BlockSpec(memory_space=pl.ANY)] * len(shapes),
        scratch_shapes=[pltpu.SemaphoreType.DMA((len(shapes),))],
        name="store",
    )(*outs)
    (outt, gint, gcond, gada, gbada, gqkv, gqg, gkg, gout, ggu, gdn, stats) = outs
    return (
        outt.T, gint.T, gcond, jnp.transpose(gada, (1, 0, 2)), gbada,
        jnp.transpose(gqkv, (1, 0, 2)), gqg.reshape(DH), gkg.reshape(DH), gout.T, ggu, gdn.T,
        stats.reshape(3),
    )


def solution(mesh):
    one_kernel = mesh.shape["dp"] == 8 and mesh.shape["mp"] == 4
    return jax.shard_map(
        body_kernel if one_kernel else body,
        mesh=mesh,
        in_specs=(
            P("dp", "mp"),
            P("dp", "mp"),
            P("dp"),
            P("dp"),
            P("dp", None),
            P("dp"),
            P("dp", None),
            P("dp", None, "mp"),
            P(None, "mp"),
            P("dp", None, "mp"),
            P(),
            P(),
            P("mp", "dp"),
            P("dp", None, "mp"),
            P("mp", "dp"),
        ),
        out_specs=(
            P("dp", "mp"),
            P("dp", "mp"),
            P("dp", None),
            P("dp", None, "mp"),
            P(None, "mp"),
            P("dp", None, "mp"),
            P(),
            P(),
            P("mp", "dp"),
            P("dp", None, "mp"),
            P("mp", "dp"),
            P(),
        ),
        check_vma=False,
    )
```

```python
import functools
import math

import jax
import jax.numpy as jnp
from jax import lax
from jax.experimental import pallas as pl
from jax.experimental.pallas import tpu as pltpu
from jax.sharding import PartitionSpec as P

D = 1152
DH = 72
NBINS = 16
BLOCK = 256
ROWS_DEV = 256
SRC_CAP = 512


epsilon = 1e-06


def grad_share(part, dim):
    sent = part.astype(jnp.bfloat16)
    total = lax.psum_scatter(sent, "dp", scatter_dimension=dim, tiled=True)
    return total.astype(jnp.float32)


def norm_rows(values):
    scale = lax.rsqrt(jnp.mean(values * values, axis=-1, keepdims=True) + epsilon)
    return (values * scale, scale)


def norm_back(grad_normed, normed, scale):
    return scale * (grad_normed - normed * jnp.mean(grad_normed * normed, axis=-1, keepdims=True))


def rotate(values, cos_h, sin_h, cos_w, sin_w, sign):
    quarter = values.shape[-1] // 4
    first = values[..., :quarter]
    second = values[..., quarter : 2 * quarter]
    third = values[..., 2 * quarter : 3 * quarter]
    fourth = values[..., 3 * quarter :]
    return jnp.concatenate(
        [
            first * cos_h - sign * second * sin_h,
            sign * first * sin_h + second * cos_h,
            third * cos_w - sign * fourth * sin_w,
            sign * third * sin_w + fourth * cos_w,
        ],
        axis=-1,
    )


def angle_tables(grid, block, head_dim):
    quarter = head_dim // 4
    place = lax.broadcasted_iota(jnp.int32, (grid.shape[0], block), 1)
    width = grid[:, 1:2]
    height_pos = (place // width).astype(jnp.float32)
    width_pos = (place % width).astype(jnp.float32)
    freqs = jnp.exp(-math.log(10000.0) * jnp.arange(quarter).astype(jnp.float32) / quarter)
    angle_h = (height_pos[:, :, None] * freqs)[:, :, None, :]
    angle_w = (width_pos[:, :, None] * freqs)[:, :, None, :]
    return (jnp.cos(angle_h), jnp.sin(angle_h), jnp.cos(angle_w), jnp.sin(angle_w))


def row_share(values):
    return lax.psum_scatter(values, "mp", scatter_dimension=0, tiled=True)


def row_whole(values):
    return lax.all_gather(values, "mp", axis=0, tiled=True)


def body(
    x_src,
    cotangent,
    route_dest,
    route_count,
    item_grid,
    noise_bin,
    cond,
    w_ada,
    b_ada,
    w_qkv,
    q_gain,
    k_gain,
    w_out,
    w_gu,
    w_down,
):
    peers = lax.axis_size("dp")
    model_rank = lax.axis_index("mp")
    blocks_here = item_grid.shape[0]
    local_width = x_src.shape[1]
    heads_here = local_width // DH
    slot_rows = 2 * ROWS_DEV // peers
    share = ROWS_DEV // lax.axis_size("mp")
    row_first = model_rank * share
    live = jnp.arange(SRC_CAP) < route_count[0]
    target = route_dest // ROWS_DEV
    member = (target[:, None] == jnp.arange(peers)[None, :]) & live[:, None]
    running = jnp.cumsum(member.astype(jnp.int32), axis=0)
    rank_in = jnp.sum(running * member, axis=1) - 1
    place = jnp.where(live, target * slot_rows + rank_in, peers * slot_rows)
    send_rows = (
        jnp.zeros((peers * slot_rows, local_width), jnp.bfloat16).at[place].set(x_src, mode="drop")
    )
    send_grads = (
        jnp.zeros((peers * slot_rows, local_width), jnp.bfloat16)
        .at[place]
        .set(cotangent, mode="drop")
    )
    send_index = (
        jnp.full((peers * slot_rows,), ROWS_DEV, jnp.int32)
        .at[place]
        .set(route_dest % ROWS_DEV, mode="drop")
    )
    recv_rows, recv_grads, recv_index = (
        lax.all_to_all(
            send_rows.reshape(peers, slot_rows, local_width),
            "dp",
            split_axis=0,
            concat_axis=0,
            tiled=True,
        ),
        lax.all_to_all(
            send_grads.reshape(peers, slot_rows, local_width),
            "dp",
            split_axis=0,
            concat_axis=0,
            tiled=True,
        ),
        lax.all_to_all(
            send_index.reshape(peers, slot_rows), "dp", split_axis=0, concat_axis=0, tiled=True
        ),
    )
    flat_index = recv_index.reshape(-1)
    rows_cols = (
        jnp.zeros((ROWS_DEV, local_width), jnp.bfloat16)
        .at[flat_index]
        .set(recv_rows.reshape(-1, local_width), mode="drop")
    )
    grads_cols = (
        jnp.zeros((ROWS_DEV, local_width), jnp.bfloat16)
        .at[flat_index]
        .set(recv_grads.reshape(-1, local_width), mode="drop")
    )
    qkv_full, out_full, gu_full, down_full = (
        lax.all_gather(w_qkv, "dp", axis=0, tiled=True),
        lax.all_gather(w_out, "dp", axis=1, tiled=True),
        lax.all_gather(w_gu, "dp", axis=0, tiled=True),
        lax.all_gather(w_down, "dp", axis=1, tiled=True),
    )
    cond_wide = cond.astype(jnp.float32)
    cond_sig = jax.nn.sigmoid(cond_wide)
    silu_cond = (cond_wide * cond_sig).astype(jnp.bfloat16)
    ada_rows = w_ada.shape[0]
    silu_all = lax.all_gather(silu_cond, "dp", axis=0, tiled=True)
    silu_own = lax.dynamic_slice_in_dim(silu_all, lax.axis_index("dp") * ada_rows, ada_rows, 1)
    mod_sums = jnp.einsum("id,dkc->ikc", silu_own, w_ada, preferred_element_type=jnp.float32)
    mod_part = (
        lax.psum_scatter(mod_sums, "dp", scatter_dimension=0, tiled=True)
        + b_ada.astype(jnp.float32)
    ).astype(jnp.bfloat16)
    rows_full, grads_full, mod_full = (
        lax.all_gather(rows_cols, "mp", axis=1, tiled=True),
        lax.all_gather(grads_cols, "mp", axis=1, tiled=True),
        lax.all_gather(mod_part, "mp", axis=2, tiled=True),
    )
    modulation = mod_full.astype(jnp.float32)
    shift_one = modulation[:, 0][:, None, :]
    scale_one = modulation[:, 1][:, None, :]
    gate_two = modulation[:, 5][:, None, :]
    resid = rows_full.astype(jnp.float32).reshape(blocks_here, BLOCK, D)
    normed_one, inv_one = norm_rows(resid)
    hidden_one = (normed_one * (1.0 + scale_one) + shift_one).astype(jnp.bfloat16)
    qkv = jnp.einsum("ibd,dkc->ibkc", hidden_one, qkv_full, preferred_element_type=jnp.float32)
    query = qkv[:, :, 0].reshape(blocks_here, BLOCK, heads_here, DH)
    keys = qkv[:, :, 1].reshape(blocks_here, BLOCK, heads_here, DH)
    value = qkv[:, :, 2].reshape(blocks_here, BLOCK, heads_here, DH)
    query_normed, query_inv = norm_rows(query)
    key_normed, key_inv = norm_rows(keys)
    cos_h, sin_h, cos_w, sin_w = angle_tables(item_grid, BLOCK, DH)
    query_low = (
        rotate(query_normed * q_gain, cos_h, sin_h, cos_w, sin_w, 1.0) * DH ** (-0.5)
    ).astype(jnp.bfloat16)
    key_low = rotate(key_normed * k_gain, cos_h, sin_h, cos_w, sin_w, 1.0).astype(jnp.bfloat16)
    value_low = value.astype(jnp.bfloat16)
    positions = lax.broadcasted_iota(jnp.int32, (blocks_here, BLOCK), 1)
    valid = positions < (item_grid[:, 0] * item_grid[:, 1])[:, None]
    key_ok = valid[:, None, None, :]
    valid_wide = valid.astype(jnp.float32)[:, :, None]
    valid_share = lax.dynamic_slice_in_dim(
        valid.astype(jnp.float32).reshape(ROWS_DEV), row_first, share, 0
    )[:, None]
    bin_onehot = (noise_bin[:, None] == jnp.arange(NBINS)[None, :]).astype(jnp.float32)
    bin_local = jnp.sum(bin_onehot, axis=0) * (model_rank == 0).astype(jnp.float32)

    def masked_scores():
        raw = jnp.einsum("iqhc,ikhc->ihqk", query_low, key_low, preferred_element_type=jnp.float32)
        return jnp.where(key_ok, raw, -1e30)

    scores = masked_scores()
    top = jnp.max(scores, axis=-1, keepdims=True)
    log_total = top + jnp.log(jnp.sum(jnp.exp(scores - top), axis=-1, keepdims=True))
    prob_low = jnp.exp(scores - log_total).astype(jnp.bfloat16)
    attn_low = jnp.einsum(
        "ihqk,ikhc->iqhc", prob_low, value_low, preferred_element_type=jnp.float32
    ).astype(jnp.bfloat16)
    out_heads = out_full.reshape(heads_here, DH, D)
    attn_part = jnp.einsum("iqhc,hcd->iqd", attn_low, out_heads, preferred_element_type=jnp.float32)

    def own_rows_of(values):
        return lax.dynamic_slice_in_dim(values.reshape(ROWS_DEV, D), row_first, share, 0)

    row_item = (row_first + jnp.arange(share)) // BLOCK
    item_onehot = (row_item[:, None] == jnp.arange(blocks_here)[None, :]).astype(jnp.float32)

    def per_item(values):
        return jnp.einsum("si,sd->id", item_onehot, values, precision=lax.Precision.HIGHEST)

    mod_rows = jnp.einsum("si,ikd->skd", item_onehot, modulation, precision=lax.Precision.HIGHEST)
    scale_one_r = mod_rows[:, 1]
    gate_one_r = mod_rows[:, 2]
    shift_two_r = mod_rows[:, 3]
    scale_two_r = mod_rows[:, 4]
    gate_two_r = mod_rows[:, 5]
    resid_share = own_rows_of(resid)
    normed_one_share = own_rows_of(normed_one)
    inv_one_share = lax.dynamic_slice_in_dim(inv_one.reshape(ROWS_DEV, 1), row_first, share, 0)
    attention_share = row_share(attn_part.reshape(ROWS_DEV, D))
    mid_share = resid_share + gate_one_r * attention_share
    normed_two_share, inv_two_share = norm_rows(mid_share)
    hidden_two_share = (normed_two_share * (1.0 + scale_two_r) + shift_two_r).astype(jnp.bfloat16)
    hidden_two = row_whole(hidden_two_share).reshape(blocks_here, BLOCK, D)
    gate_up = jnp.einsum("ibd,dkf->ibkf", hidden_two, gu_full, preferred_element_type=jnp.float32)
    gate_raw = gate_up[:, :, 0]
    up_raw = gate_up[:, :, 1]
    gate_sig = jax.nn.sigmoid(gate_raw)
    gate_act = gate_raw * gate_sig
    inner = (gate_act * up_raw).astype(jnp.bfloat16)
    feed_part = jnp.einsum("ibf,fd->ibd", inner, down_full, preferred_element_type=jnp.float32)
    feed_part, kept = (feed_part, (inner, up_raw, gate_raw, gate_sig, gate_act))
    feed_share = row_share(feed_part.reshape(ROWS_DEV, D))
    result_share = mid_share + gate_two_r * feed_share
    result_whole = row_whole(result_share.astype(jnp.bfloat16))
    squares = jnp.stack(
        [
            jnp.sum(valid_share * result_share * result_share),
            jnp.sum(valid_share * (gate_one_r * attention_share) ** 2),
            jnp.sum(valid_share * (gate_two_r * feed_share) ** 2),
        ]
    )
    square_total, valid_total, bin_total = lax.psum(
        (squares, jnp.sum(valid_share), bin_local), ("dp", "mp")
    )
    stats_value = jnp.sqrt(square_total / (valid_total * D))
    item_count = jnp.sum(bin_onehot * bin_total[None, :], axis=1)
    weight_value = blocks_here * peers / (NBINS * item_count)
    top_grad = grads_full.astype(jnp.float32).reshape(blocks_here, BLOCK, D) * (
        weight_value[:, None, None] * valid_wide
    )
    top_share = own_rows_of(top_grad)
    feed_grad = (gate_two * top_grad).astype(jnp.bfloat16)
    grad_gate_two = per_item(top_share * feed_share)
    inner, up_raw, gate_raw, gate_sig, gate_act = kept
    inner_grad = jnp.einsum("ibd,fd->ibf", feed_grad, down_full, preferred_element_type=jnp.float32)
    grad_down_part = jnp.einsum("ibf,ibd->fd", inner, feed_grad, preferred_element_type=jnp.float32)
    gate_grad = (inner_grad * up_raw * gate_sig * (1.0 + gate_raw * (1.0 - gate_sig))).astype(
        jnp.bfloat16
    )
    up_grad = (inner_grad * gate_act).astype(jnp.bfloat16)
    gate_up_grad = jnp.stack([gate_grad, up_grad], axis=2)
    grad_gu_part = jnp.einsum(
        "ibd,ibkf->dkf", hidden_two, gate_up_grad, preferred_element_type=jnp.float32
    )
    hidden_two_part = jnp.einsum(
        "ibkf,dkf->ibd", gate_up_grad, gu_full, preferred_element_type=jnp.float32
    )
    grad_down, grad_gu, hidden_two_part = (grad_down_part, grad_gu_part, hidden_two_part)
    h2_grad_share = row_share(hidden_two_part.reshape(ROWS_DEV, D))
    grad_shift_two = per_item(h2_grad_share)
    grad_scale_two = per_item(h2_grad_share * normed_two_share)
    mid_grad_share = top_share + norm_back(
        h2_grad_share * (1.0 + scale_two_r), normed_two_share, inv_two_share
    )
    attention_grad_share = (gate_one_r * mid_grad_share).astype(jnp.bfloat16)
    grad_gate_one = per_item(mid_grad_share * attention_share)
    attention_grad = row_whole(attention_grad_share).reshape(blocks_here, BLOCK, D)
    attn_low_grad = jnp.einsum(
        "iqd,hcd->iqhc", attention_grad, out_heads, preferred_element_type=jnp.float32
    ).astype(jnp.bfloat16)
    grad_out_part = jnp.einsum(
        "iqhc,iqd->hcd", attn_low, attention_grad, preferred_element_type=jnp.float32
    ).reshape(local_width, D)
    prob_full = jnp.exp(masked_scores() - log_total)
    prob_grad = jnp.einsum(
        "iqhc,ikhc->ihqk", attn_low_grad, value_low, preferred_element_type=jnp.float32
    )
    value_grad = jnp.einsum(
        "ihqk,iqhc->ikhc", prob_low, attn_low_grad, preferred_element_type=jnp.float32
    )
    score_grad = (
        prob_full * (prob_grad - jnp.sum(prob_full * prob_grad, axis=-1, keepdims=True))
    ).astype(jnp.bfloat16)
    query_rot_grad = jnp.einsum(
        "ihqk,ikhc->iqhc", score_grad, key_low, preferred_element_type=jnp.float32
    ) * DH ** (-0.5)
    key_rot_grad = jnp.einsum(
        "ihqk,iqhc->ikhc", score_grad, query_low, preferred_element_type=jnp.float32
    )
    query_scaled_grad = rotate(query_rot_grad, cos_h, sin_h, cos_w, sin_w, -1.0)
    key_scaled_grad = rotate(key_rot_grad, cos_h, sin_h, cos_w, sin_w, -1.0)
    qgain_local = jnp.sum(query_scaled_grad * query_normed, axis=(0, 1, 2))
    kgain_local = jnp.sum(key_scaled_grad * key_normed, axis=(0, 1, 2))
    query_grad = norm_back(query_scaled_grad * q_gain, query_normed, query_inv)
    key_grad = norm_back(key_scaled_grad * k_gain, key_normed, key_inv)
    qkv_grad = jnp.stack(
        [
            query_grad.reshape(blocks_here, BLOCK, local_width),
            key_grad.reshape(blocks_here, BLOCK, local_width),
            value_grad.reshape(blocks_here, BLOCK, local_width),
        ],
        axis=2,
    ).astype(jnp.bfloat16)
    grad_qkv_part = jnp.einsum(
        "ibd,ibkc->dkc", hidden_one, qkv_grad, preferred_element_type=jnp.float32
    )
    hidden_one_part = jnp.einsum(
        "ibkc,dkc->ibd", qkv_grad, qkv_full, preferred_element_type=jnp.float32
    )
    grad_out, grad_qkv, qgain_part, kgain_part, hidden_one_part = (
        grad_out_part,
        grad_qkv_part,
        qgain_local,
        kgain_local,
        hidden_one_part,
    )
    h1_grad_share = row_share(hidden_one_part.reshape(ROWS_DEV, D))
    grad_shift_one = per_item(h1_grad_share)
    grad_scale_one = per_item(h1_grad_share * normed_one_share)
    input_share = mid_grad_share + norm_back(
        h1_grad_share * (1.0 + scale_one_r), normed_one_share, inv_one_share
    )
    input_whole = row_whole(input_share.astype(jnp.bfloat16))
    mod_partial = jnp.stack(
        [
            grad_shift_one,
            grad_scale_one,
            grad_gate_one,
            grad_shift_two,
            grad_scale_two,
            grad_gate_two,
        ],
        axis=1,
    )
    mod_grad = lax.psum(mod_partial, "mp").astype(jnp.bfloat16)
    mod_grad_own = lax.dynamic_slice_in_dim(mod_grad, model_rank * local_width, local_width, 2)
    mod_all = lax.all_gather(mod_grad_own, "dp", axis=0, tiled=True)
    cond_part = jnp.einsum("ikc,dkc->id", mod_all, w_ada, preferred_element_type=jnp.float32)
    cond_sum = lax.psum(cond_part, "mp")
    cond_total = lax.all_to_all(
        cond_sum.reshape(peers, blocks_here, ada_rows), "dp", split_axis=0, concat_axis=0, tiled=True
    )
    cond_total = jnp.moveaxis(cond_total, 0, 1).reshape(blocks_here, peers * ada_rows)
    grad_cond = cond_total * cond_sig * (1.0 + cond_wide * (1.0 - cond_sig))
    grad_ada = jnp.einsum("ir,ikc->rkc", silu_own, mod_all, preferred_element_type=jnp.float32)
    grad_bada = jnp.sum(mod_all.astype(jnp.float32), axis=0)
    qgain_total, kgain_total = lax.psum((qgain_part, kgain_part), ("dp", "mp"))
    qkv_own, out_own, gu_own, down_own = (
        grad_share(grad_qkv, 0),
        grad_share(grad_out, 1),
        grad_share(grad_gu, 0),
        grad_share(grad_down, 1),
    )
    result_cols = lax.dynamic_slice_in_dim(result_whole, model_rank * local_width, local_width, 1)
    input_cols = lax.dynamic_slice_in_dim(input_whole, model_rank * local_width, local_width, 1)
    back_index = jnp.minimum(flat_index, ROWS_DEV - 1)
    back_rows = result_cols[back_index].reshape(peers, slot_rows, local_width)
    back_grads = input_cols[back_index].reshape(peers, slot_rows, local_width)
    returned_rows, returned_grads = (
        lax.all_to_all(back_rows, "dp", split_axis=0, concat_axis=0, tiled=True),
        lax.all_to_all(back_grads, "dp", split_axis=0, concat_axis=0, tiled=True),
    )
    pick = jnp.minimum(place, peers * slot_rows - 1)
    empty = jnp.zeros((), jnp.bfloat16)
    out_rows = jnp.where(live[:, None], returned_rows.reshape(-1, local_width)[pick], empty)
    out_grads = jnp.where(live[:, None], returned_grads.reshape(-1, local_width)[pick], empty)
    return (
        out_rows,
        out_grads,
        grad_cond,
        grad_ada,
        grad_bada,
        qkv_own,
        qgain_total,
        kgain_total,
        out_own,
        gu_own,
        down_own,
        stats_value,
    )


MESH = pl.DeviceIdType.MESH
f32 = jnp.float32
bf16 = jnp.bfloat16
LANE_INDEX = 288
META = 1152
PAD = 128


def nn(left, right):
    return jnp.dot(left, right, preferred_element_type=f32)


def nt(left, right):
    return lax.dot_general(left, right, (((1,), (1,)), ((), ())), preferred_element_type=f32)


def tn(left, right):
    return lax.dot_general(left, right, (((0,), (0,)), ((), ())), preferred_element_type=f32)


def loop(count, step):
    def run(index, carry):
        step(index)
        return carry

    lax.fori_loop(0, count, run, 0)


def at128(index, size):
    return pl.ds(pl.multiple_of(index, 128), size)


def at16(index, size):
    return pl.ds(pl.multiple_of(index, 16), size)


GROUPS = (("c0", 768), ("c1", 768), ("c2", 768), ("out", 288), ("qkv", 864))


def scratch_list():
    vm = pltpu.VMEM
    items = dict(
        sem=pltpu.SemaphoreType.DMA((126,)),
        arow=vm((1, 1280), f32),
        arec=vm((8, 1, 1280), f32),
        amat=vm((8, 1280), f32),
        xe=vm((384, 512), bf16),
        place=vm((512, 512), bf16),
        sx=vm((512, 384), bf16),
        rx=vm((512, 384), bf16),
        sg=vm((512, 256), bf16),
        rg=vm((512, 256), bf16),
        spread=vm((512, 256), bf16),
        rb=vm((4, 256, 384), bf16),
        gb=vm((4, 256, 256), bf16),
        pms=vm((8, 6, 1, 288), f32),
        pmr=vm((8, 6, 1, 288), f32),
        mdb=vm((4, 6, 1, 288), f32),
        modf=vm((8, 1152), f32),
        h1=vm((256, 1152), bf16),
        h1t=vm((1152, 256), bf16),
        w1=vm((1152, 896), bf16),
        wc0=vm((1152, 768), bf16),
        wc1=vm((1152, 768), bf16),
        wc2=vm((1152, 768), bf16),
        wp1=vm((144, 896), bf16),
        wp=vm((3, 144, 768), bf16),
        wo=vm((1152, 288), bf16),
        qkv=vm((256, 1024), f32),
        qn=vm((4, 256, 128), f32),
        kn=vm((4, 256, 128), f32),
        qi=vm((4, 256, 1), f32),
        ki=vm((4, 256, 1), f32),
        ql=vm((4, 256, 128), bf16),
        kl=vm((4, 256, 128), bf16),
        vl=vm((4, 256, 128), bf16),
        pf=vm((4, 256, 256), f32),
        cosv=vm((256, 128), f32),
        sinv=vm((256, 128), f32),
        al=vm((256, 288), bf16),
        rsa=vm((256, 1152), bf16),
        rra=vm((3, 64, 1152), bf16),
        rta=vm((64, 1152), bf16),
        rsf=vm((256, 1152), bf16),
        rrf=vm((3, 64, 1152), bf16),
        rtf=vm((64, 1152), bf16),
        rsh2=vm((256, 1152), bf16),
        rrh2=vm((3, 64, 1152), bf16),
        rth2=vm((64, 1152), bf16),
        rsh1=vm((256, 1152), bf16),
        rrh1=vm((3, 64, 1152), bf16),
        rth1=vm((64, 1152), bf16),
        h2=vm((256, 1152), bf16),
        h2t=vm((1152, 256), bf16),
        ag=vm((256, 1152), bf16),
        agt=vm((1152, 256), bf16),
        h2sum=vm((256, 1152), f32),
        inner=vm((3, 256, 256), bf16),
        gug=vm((3, 256, 512), bf16),
        fg=vm((256, 1152), bf16),
        fgt=vm((1152, 256), bf16),
        da=vm((256, 384), f32),
        dqkv=vm((256, 864), bf16),
        share=vm((8, 64, 1152), f32),
        invs=vm((2, 64, 1), f32),
        gpart=vm((8, 1152), f32),
        ras=vm((4, 64, 256), bf16),
        rar=vm((4, 64, 256), bf16),
        ias=vm((4, 64, 384), bf16),
        iar=vm((4, 64, 384), bf16),
        bs=vm((512, 256), bf16),
        br=vm((512, 256), bf16),
        bgs=vm((512, 384), bf16),
        bgr=vm((512, 384), bf16),
        hs=vm((4, 7, 1, 288), f32),
        hr=vm((4, 7, 1, 288), f32),
        gs=vm((7, 1, 288), f32),
        grec=vm((8, 7, 1, 288), f32),
        ms=vm((8, 6, 288), f32),
        cps=vm((8, 144), f32),
        cpr=vm((4, 8, 144), f32),
        cts=vm((8, 1, 144), f32),
        ctr=vm((8, 1, 144), f32),
    )
    for name, width in GROUPS:
        items["cs_" + name] = vm((4, 144, width), bf16)
        items["cr_" + name] = vm((4, 144, width), bf16)
        items["xs_" + name] = vm((2, 144, width), bf16)
        items["xr_" + name] = vm((2, 144, width), bf16)
        items["zs_" + name] = vm((2, 144, width), bf16)
        items["zr_" + name] = vm((2, 144, width), bf16)
    return items


class Refs:
    pass


def block_kernel(
    names, xt, ct, dest, count, grid, bin, cond, wada, bada, wqkv, qg, kg, woin, wgu, wdn, outt, gint, gcond, gada, gbada, gqkv, gqg, gkg, gout, ggu, gdn, stats, *scratch
):
    r = Refs()
    r.__dict__.update(locals())
    for name, ref in zip(names, scratch):
        setattr(r, name, ref)
    dp = lax.axis_index("dp")
    mp = lax.axis_index("mp")
    z, x, y, c = dp // 2, dp % 2, mp // 2, mp % 2
    zh, zl = z // 2, z % 2
    item = (2 * zh + c) * 2 + x
    tp = y * 2 + zl
    home = zl == c
    away = zl != c
    sem = r.sem
    taken = [0]

    def sems(count):
        first = taken[0]
        taken[0] += count
        return first

    def device(zz, xx, yy, cc):
        return (zz * 2 + xx, yy * 2 + cc)

    def worker(index, part):
        zi, xi = index // 2, index % 2
        return device(2 * (zi // 2) + part % 2, xi, part // 2, zi % 2)

    def mate(step):
        return device(2 * zh + (zl ^ (step & 1)), x, y ^ (step >> 1), c)

    def remote(src, dst, ss, rs, dev):
        return pltpu.make_async_remote_copy(
            src_ref=src,
            dst_ref=dst,
            send_sem=sem.at[ss],
            recv_sem=sem.at[rs],
            device_id=dev,
            device_id_type=MESH,
        )

    pending = []

    def start(src, dst, ss, rs, dev):
        remote(src, dst, ss, rs, dev).start()

    def start_unless(same, src, dst, ss, rs, dev):
        @pl.when(same)
        def _():
            pltpu.make_async_copy(src, dst, sem.at[rs]).start()

        @pl.when(jnp.logical_not(same))
        def _():
            remote(src, dst, ss, rs, dev).start()

    def arrived(dst, rs):
        pltpu.make_async_copy(dst, dst, sem.at[rs]).wait()

    def sent(ref, ss):
        pending.append(lambda: arrived(ref, ss))

    def sent_or_kept(size, count, ss):
        def finish():
            @pl.when(home)
            def _():
                arrived(size(count - 1), ss)

            @pl.when(away)
            def _():
                arrived(size(count), ss)

        pending.append(finish)

    def to_workers(source, target, size):
        base = sems(2)
        for step in range(8):
            index = (dp + step) % 8
            args = (source(index), target(dp), base, base + 1, worker(index, mp))
            if step == 0:
                start_unless(home, *args)
            else:
                start(*args)
        sent_or_kept(size, 8, base)
        return base + 1

    def to_homes(source, target, size):
        base = sems(2)
        for step in range(8):
            index = (dp + step) % 8
            args = (source(index), target(item), base, base + 1, (index, tp))
            if step == 0:
                start_unless(home, *args)
            else:
                start(*args)
        sent_or_kept(size, 8, base)
        return base + 1

    def to_others(source, target, size):
        base = sems(2)
        for step in range(1, 8):
            index = (dp + step) % 8
            start(source(index), target, base, base + 1, (index, mp))
        sent(size, base)
        return base + 1

    def slots64(ref):
        return lambda i: ref.at[at16(i * 64, 64)]

    def first64(ref):
        return lambda n: ref.at[pl.ds(0, 64 * n)]

    def head_of(ref):
        return lambda n: ref.at[pl.ds(0, n)]

    groups = {
        "attn": (r.wp1, r.w1),
        "wo": (r.woin, r.wo),
        "c0": (r.wp.at[0], r.wc0),
        "c1": (r.wp.at[1], r.wc1),
        "c2": (r.wp.at[2], r.wc2),
    }
    w_base = {g: sems(6) for g in groups}

    def slot(ref, index):
        return ref.at[at16(index * 144, 144)]

    for g in groups:
        whole = groups[g][1]
        sent_or_kept(lambda n, whole=whole: whole.at[pl.ds(0, 144 * n)], 8, w_base[g] + 5)

    def gather_z(g, rels=(1, 0)):
        src, full = groups[g]
        base = w_base[g]
        for rel in rels:
            zt = c + 2 * (zh ^ rel)
            args = (src, slot(full, dp), base + 5, base + rel, device(zt, x, y, zl))
            if rel == 0:
                start_unless(home, *args)
            else:
                start(*args)

    def gather_x(g, rel):
        full, base = groups[g][1], w_base[g]
        mine = slot(full, (c + 2 * (zh ^ rel)) * 2 + x)
        arrived(mine, base + rel)
        start(mine, mine, base + 5, base + 2 + rel, device(z, 1 - x, y, c))
        start(mine, mine, base + 5, base + 4, device(z, x, y, 1 - c))

    def gather_core(g, rel):
        full, base = groups[g][1], w_base[g]
        mine = slot(full, (c + 2 * (zh ^ rel)) * 2 + 1 - x)
        arrived(mine, base + 2 + rel)
        start(mine, mine, base + 5, base + 4, device(z, x, y, 1 - c))

    def gather_done(g):
        arrived(groups[g][1].at[pl.ds(0, 144 * 4)], w_base[g] + 4)

    z_mate = device(2 * zh + 1 - zl, x, y, c)
    y_mate = device(z, x, 1 - y, c)

    class Gather:
        def __init__(self, view, size):
            self.view, self.size, self.base = view, size, sems(3)
            mine = view(tp)
            start(mine, mine, self.base, self.base + 1, z_mate)
            start(mine, mine, self.base, self.base + 2, y_mate)
            sent(size(3), self.base)

        def relay(self):
            other = self.view(tp ^ 1)
            arrived(other, self.base + 1)
            start(other, other, self.base, self.base + 2, y_mate)

        def done(self):
            arrived(self.size(2), self.base + 2)

    class Scatter:
        def __init__(self, name):
            self.base = sems(3)
            self.sent, self.rec, self.sum = (getattr(r, k + name) for k in ("rs", "rr", "rt"))
            start(self.view(tp ^ 3), self.rec.at[0], self.base, self.base + 1, y_mate)
            start(self.view(tp ^ 2), self.rec.at[1], self.base, self.base + 2, y_mate)
            sent(self.rec, self.base)

        def view(self, t):
            return self.sent.at[at16(t * 64, 64)]

        def relay(self):
            arrived(self.rec.at[0], self.base + 1)
            both = self.view(tp ^ 1)[...].astype(f32) + self.rec[0].astype(f32)
            self.sum[...] = both.astype(bf16)
            start(self.sum, self.rec.at[2], self.base, self.base + 2, z_mate)

        def total(self):
            arrived(self.rec.at[pl.ds(1, 2)], self.base + 2)
            total = self.view(tp)[...].astype(f32) + self.rec[1].astype(f32)
            return total + self.rec[2].astype(f32)

    def rows_view(buf):
        return lambda t: buf.at[at16(t * 64, 64)]

    def mates_send(source, target, size):
        base = sems(2)
        for step in range(1, 4):
            start(source(tp ^ step), target, base, base + 1, mate(step))
        sent(size, base)
        return base + 1

    g_base = {name: sems(9) for name, _ in GROUPS}

    def block(name, s):
        rows = at16(s * 144, 144)
        if name == "out":
            return nn(r.agt[rows, :], r.al[...])
        if name == "qkv":
            return nn(r.h1t[rows, :], r.dqkv[...])
        k = int(name[1:])
        return jnp.concatenate(
            [nn(r.h2t[rows, :], r.gug[k]), nn(r.fgt[rows, :], r.inner[k])], axis=-1
        )

    for name, _ in GROUPS:
        buf = getattr(r, "cs_" + name)
        sent(buf, g_base[name] + 7)
        sent_or_kept(head_of(buf), 4, g_base[name] + 8)

    def reduce_core(name):
        base = g_base[name]
        cs, cr = getattr(r, "cs_" + name), getattr(r, "cr_" + name)
        for xx in (1 - x, x):
            for rel in (1 - zh, zh):
                q = 2 * rel + xx
                cs[q] = block(name, (1 - c + 2 * rel) * 2 + xx).astype(bf16)
                start(cs.at[q], cr.at[q], base + 7, base + q, device(z, x, y, 1 - c))

    def reduce_x(name, far):
        base = g_base[name]
        cr, xs, xr = (getattr(r, k + name) for k in ("cr_", "xs_", "xr_"))
        rel = zh ^ far
        q = 2 * rel + 1 - x
        part = block(name, (c + 2 * rel) * 2 + 1 - x)
        arrived(cr.at[q], base + q)
        xs[rel] = (part + cr[q].astype(f32)).astype(bf16)
        start(xs.at[rel], xr.at[rel], base + 8, base + 4 + rel, device(z, 1 - x, y, c))

    def reduce_z(name, far):
        base = g_base[name]
        cr, xr, zs, zr = (getattr(r, k + name) for k in ("cr_", "xr_", "zs_", "zr_"))
        rel = zh ^ far
        q = 2 * rel + x
        part = block(name, (c + 2 * rel) * 2 + x)
        arrived(cr.at[q], base + q)
        part = part + cr[q].astype(f32)
        arrived(xr.at[rel], base + 4 + rel)
        zs[far] = (part + xr[rel].astype(f32)).astype(bf16)
        args = (zs.at[far], zr.at[zh], base + 8, base + 6, device(c + 2 * rel, x, y, zl))
        if far == 0:
            start_unless(home, *args)
        else:
            start(*args)

    def reduce_end(name):
        zr = getattr(r, "zr_" + name)
        arrived(zr, g_base[name] + 6)
        return zr[0].astype(f32) + zr[1].astype(f32)

    def transpose(src, dst):
        def step(j):
            dst[at128(j * 128, 128), :] = src[:, at128(j * 128, 128)].T

        loop(9, step)

    lane128 = lax.broadcasted_iota(jnp.int32, (1, PAD), 1)
    head_lane = lane128 < 72
    quarter = lane128 // 18
    even = quarter % 2 == 0

    def swap(v):
        return jnp.where(even, pltpu.roll(v, PAD - 18, 1), pltpu.roll(v, 18, 1))

    def norm_of(v):
        inv = lax.rsqrt(jnp.mean(v * v, axis=-1, keepdims=True) + epsilon)
        return v * inv, inv

    def back(g, normed, inv):
        return inv * (g - normed * jnp.mean(g * normed, axis=-1, keepdims=True))

    barrier = pltpu.get_barrier_semaphore()
    for i in range(8):
        for j in range(4):
            if i or j:
                pl.semaphore_signal(
                    barrier, inc=1, device_id=((dp + i) % 8, mp ^ j), device_id_type=MESH
                )

    cond = r.cond[...].astype(f32)
    sig_c = jax.nn.sigmoid(cond)
    r.arow[0:1, 0:META] = (cond * sig_c).astype(bf16).astype(f32)
    meta = jnp.where(lane128 == 0, r.bin[0].astype(f32), 0.0)
    meta = jnp.where(lane128 == 1, r.grid[0, 0].astype(f32), meta)
    meta = jnp.where(lane128 == 2, r.grid[0, 1].astype(f32), meta)
    r.arow[0:1, META : META + 128] = meta
    r.arec[dp] = r.arow[...]

    dest = r.dest[...]
    lane512 = lax.broadcasted_iota(jnp.int32, (1, 512), 1)
    live = lane512 < r.count[0]
    target = dest >> 8
    within = dest & 255
    owner = lax.broadcasted_iota(jnp.int32, (8, 512), 0)
    member = jnp.where((owner == target) & live, 1.0, 0.0)
    upper = lax.broadcasted_iota(jnp.int32, (512, 512), 0) <= lax.broadcasted_iota(
        jnp.int32, (512, 512), 1
    )
    running = nn(member.astype(bf16), jnp.where(upper, 1.0, 0.0).astype(bf16))
    rank = jnp.sum(running * member, axis=0, keepdims=True).astype(jnp.int32) - 1
    spot = jnp.where(live, target * 64 + rank, -1)
    slots = lax.broadcasted_iota(jnp.int32, (512, 512), 0)
    r.place[...] = jnp.where(slots == spot, 1.0, 0.0).astype(bf16)
    r.xe[0:288, :] = r.xt[...]
    top_row = lax.broadcasted_iota(jnp.int32, (32, 512), 0) == 0
    r.xe[288:320, :] = jnp.where(top_row, within + 1, 0).astype(f32).astype(bf16)
    r.xe[320:352, :] = r.ct[256:288, :]
    r.xe[352:384, :] = jnp.zeros((32, 512), bf16)
    r.sx[...] = nt(r.place[...], r.xe[...]).astype(bf16)
    for p in range(3):
        r.wp1[:, 288 * p : 288 * p + 288] = r.wqkv[p]
    r.wp1[:, 864:896] = jnp.zeros((144, 32), bf16)

    pl.semaphore_wait(barrier, 31)
    a_in = to_others(lambda i: r.arow, r.arec.at[dp], r.arec.at[pl.ds(0, 7)])
    x_in = to_workers(slots64(r.sx), slots64(r.rx), first64(r.rx))
    for k in range(3):
        r.wp[k, :, 0:256] = r.wgu[:, 0, 256 * k : 256 * k + 256]
        r.wp[k, :, 256:512] = r.wgu[:, 1, 256 * k : 256 * k + 256]
        r.wp[k, :, 512:768] = r.wdn[:, 256 * k : 256 * k + 256]
    r.sg[...] = nt(r.place[...], r.ct[0:256, :]).astype(bf16)

    arrived(r.arec.at[pl.ds(0, 7)], a_in)
    for i in range(8):
        r.amat[i : i + 1, :] = r.arec[i]
    pick = lax.broadcasted_iota(jnp.int32, (1152, 144), 0) == (
        lax.broadcasted_iota(jnp.int32, (1152, 144), 1) + 144 * dp
    )
    silu_own = nn(r.amat[:, 0:META].astype(bf16), jnp.where(pick, 1.0, 0.0).astype(bf16)).astype(bf16)
    first = (dp == 0).astype(f32)
    for k in range(6):
        part = nn(silu_own, r.wada[k]) + first * r.bada[k : k + 1, :].astype(f32)
        for i in range(8):
            r.pms[i, k] = part[i : i + 1, :]
    m_in = to_workers(lambda i: r.pms.at[i], lambda i: r.pmr.at[i], head_of(r.pmr))
    gather_z("attn")
    gather_z("wo")

    about = r.arec[item]
    height = about[:, META + 1 : META + 2]
    width = about[:, META + 2 : META + 3]
    bins = r.amat[:, META : META + 1]
    alike = jnp.sum(
        jnp.where(bins == about[:, META : META + 1], 1.0, 0.0), axis=0, keepdims=True
    )
    weight = 8.0 / (NBINS * alike)
    spots = lax.broadcasted_iota(jnp.int32, (256, 1), 0).astype(f32)
    high = jnp.floor((spots + 0.5) / width)
    wide = spots - high * width
    freq = jnp.exp(-math.log(10000.0) * (lane128 - 18 * quarter).astype(f32) / 18.0)
    angle = jnp.where(quarter < 2, high, wide) * freq
    r.cosv[...] = jnp.where(head_lane, jnp.cos(angle), 0.0)
    r.sinv[...] = jnp.where(head_lane, jnp.where(even, -jnp.sin(angle), jnp.sin(angle)), 0.0)
    used = height * width
    key_ok = lax.broadcasted_iota(jnp.int32, (1, 256), 1).astype(f32) < used
    row_first = (tp * 64).astype(f32)
    share_spots = lax.broadcasted_iota(jnp.int32, (64, 1), 0).astype(f32) + row_first
    valid_share = jnp.where(share_spots < used, 1.0, 0.0)

    arrived(r.rx, x_in)
    number = r.rx[:, 288:289].astype(jnp.int32)
    r.spread[...] = jnp.where(
        number == lax.broadcasted_iota(jnp.int32, (512, 256), 1) + 1, 1.0, 0.0
    ).astype(bf16)
    r.rb[tp] = tn(r.spread[...], r.rx[...]).astype(bf16)
    rb_all = Gather(lambda t: r.rb.at[t], head_of(r.rb))

    gather_x("attn", 0)
    gather_x("attn", 1)
    arrived(r.pmr, m_in)
    total = r.pmr[0]
    for s in range(1, 8):
        total = total + r.pmr[s]
    r.mdb[tp] = total.astype(bf16).astype(f32)
    mdb_all = Gather(lambda t: r.mdb.at[t], head_of(r.mdb))
    rb_all.relay()
    mdb_all.relay()
    t_in = to_workers(slots64(r.sg), slots64(r.rg), first64(r.rg))
    gather_z("c0")
    gather_z("c1")
    gather_core("attn", 0)
    gather_core("attn", 1)

    gather_x("wo", 0)
    gather_x("wo", 1)
    rb_all.done()
    mdb_all.done()
    for k in range(6):
        for t in range(4):
            r.modf[k : k + 1, 288 * t : 288 * t + 288] = r.mdb[t, k]

    def joined(start):
        return jnp.concatenate(
            [r.rb[t, at16(start, 64), 0:288].astype(f32) for t in range(4)], axis=-1
        )

    def joined_grad(start):
        parts = []
        for t in range(4):
            parts.append(r.gb[t, at16(start, 64), :].astype(f32))
            parts.append(r.rb[t, at16(start, 64), 320:352].astype(f32))
        return jnp.concatenate(parts, axis=-1)

    def first_hidden(i):
        normed, _ = norm_of(joined(i * 64))
        shift, scale = r.modf[0:1, :], r.modf[1:2, :]
        r.h1[at16(i * 64, 64), :] = (normed * (1.0 + scale) + shift).astype(bf16)

    loop(4, first_hidden)
    RESID, NORM1, ATT, MID, NORM2, TOP, MIDG = range(7)
    mine = joined(tp * 64)
    normed, inv = norm_of(mine)
    r.share[RESID] = mine
    r.share[NORM1] = normed
    r.invs[0] = inv
    gather_done("attn")

    def project(j):
        r.qkv[:, at128(j * 256, 256)] = nn(r.h1[...], r.w1[:, at128(j * 256, 256)])

    loop(3, project)
    r.qkv[:, 768:896] = nn(r.h1[...], r.w1[:, 768:896])

    gather_x("c0", 0)
    gather_core("wo", 0)
    gather_core("wo", 1)
    scale_q = 72 ** (-0.5)
    pad = jnp.zeros((1, PAD - 72), f32)
    gains = {k: jnp.concatenate([g[...], pad], axis=-1) for k, g in (("q", r.qg), ("k", r.kg))}
    def turn_heads(h):
        for kind, offset, normed_ref, inv_ref, low_ref in (
            ("q", 0, r.qn, r.qi, r.ql),
            ("k", 288, r.kn, r.ki, r.kl),
        ):
            lane = offset + 72 * h
            v = jnp.where(head_lane, r.qkv[:, lane : lane + 128], 0.0)
            inv = lax.rsqrt(jnp.sum(v * v, axis=-1, keepdims=True) * (1.0 / 72) + epsilon)
            v = v * inv
            normed_ref[h] = v
            inv_ref[h] = inv
            v = v * gains[kind]
            v = v * r.cosv[...] + swap(v) * r.sinv[...]
            if kind == "q":
                v = v * scale_q
            low_ref[h] = v.astype(bf16)
        lane = 576 + 72 * h
        r.vl[h] = jnp.where(head_lane, r.qkv[:, lane : lane + 128], 0.0).astype(bf16)

    turn_heads(0)
    turn_heads(1)
    turn_heads(2)
    turn_heads(3)
    def attend(h):
        scores = jnp.where(key_ok, nt(r.ql[h], r.kl[h]), -1e30)
        scores = jnp.exp(scores - jnp.max(scores, axis=-1, keepdims=True))
        prob = scores / jnp.sum(scores, axis=-1, keepdims=True)
        r.pf[h] = prob
        r.al[:, 72 * h : 72 * h + 72] = nn(prob.astype(bf16), r.vl[h])[:, 0:72].astype(bf16)

    attend(0)
    attend(1)
    attend(2)
    attend(3)

    gather_done("wo")

    def project_out(j):
        r.rsa[:, at128(j * 384, 384)] = nt(r.al[...], r.wo[at128(j * 384, 384), :]).astype(bf16)

    loop(3, project_out)
    sum_a = Scatter("a")
    sum_a.relay()

    gather_z("c2", (1,))
    gather_x("c0", 1)
    gather_core("c0", 0)
    gather_x("c1", 0)
    gather_x("c1", 1)
    arrived(r.rg, t_in)
    r.gb[tp] = tn(r.spread[...], r.rg[...]).astype(bf16)
    gb_all = Gather(lambda t: r.gb.at[t], head_of(r.gb))
    attention = sum_a.total()
    r.share[ATT] = attention
    middle = r.share[RESID] + r.modf[2:3, :] * attention
    r.share[MID] = middle
    normed, inv = norm_of(middle)
    r.share[NORM2] = normed
    r.invs[1] = inv
    r.h2[at16(tp * 64, 64), :] = (normed * (1.0 + r.modf[4:5, :]) + r.modf[3:4, :]).astype(bf16)
    h2_all = Gather(rows_view(r.h2), first64(r.h2))
    gather_z("c2", (0,))
    gather_core("c0", 1)
    gather_x("c2", 0)
    gb_all.relay()
    h2_all.relay()
    gather_x("c2", 1)
    gather_core("c1", 0)
    gather_core("c1", 1)
    transpose(r.h1, r.h1t)
    chunks = (r.wc0, r.wc1, r.wc2)

    def swiglu(k):
        full = chunks[k]
        gate = nn(r.h2[...], full[:, 0:256])
        up = nn(r.h2[...], full[:, 256:512])
        grad = nn(r.fg[...], full[:, 512:768])
        sig = jax.nn.sigmoid(gate)
        act = gate * sig
        r.inner[k] = (act * up).astype(bf16)
        r.gug[k, :, 0:256] = (grad * up * sig * (1.0 + gate * (1.0 - sig))).astype(bf16)
        r.gug[k, :, 256:512] = (grad * act).astype(bf16)

    def hidden_back(k):
        full = chunks[k]

        def step(j):
            rows = at128(j * 384, 384)
            part = nt(r.gug[k], full[rows, 0:512])
            if k > 0:
                part = part + r.h2sum[:, rows]
            if k < 2:
                r.h2sum[:, rows] = part
            else:
                r.rsh2[:, rows] = part.astype(bf16)

        loop(3, step)

    gb_all.done()
    def feed_rows(i):
        rows = lax.broadcasted_iota(jnp.int32, (64, 1), 0).astype(f32) + (i * 64).astype(f32)
        factor = jnp.where(rows < used, weight, 0.0)
        r.fg[at16(i * 64, 64), :] = (joined_grad(i * 64) * factor * r.modf[5:6, :]).astype(bf16)

    loop(4, feed_rows)
    r.share[TOP] = joined_grad(tp * 64) * (weight * valid_share)
    transpose(r.fg, r.fgt)

    h2_all.done()
    gather_done("c0")
    swiglu(0)
    transpose(r.h2, r.h2t)
    reduce_core("c0")
    gather_core("c2", 0)
    gather_done("c1")
    swiglu(1)
    reduce_x("c0", 1)
    reduce_x("c0", 0)
    reduce_core("c1")
    gather_core("c2", 1)
    hidden_back(0)
    hidden_back(1)
    gather_done("c2")
    swiglu(2)
    hidden_back(2)
    sum_h2 = Scatter("h2")
    reduce_x("c1", 1)
    reduce_z("c0", 1)
    reduce_x("c1", 0)
    reduce_core("c2")
    reduce_x("c2", 1)
    reduce_x("c2", 0)
    sum_h2.relay()
    reduce_z("c0", 0)

    def feed_out(j):
        rows = at128(j * 384, 384)
        part = nt(r.inner[0], r.wc0[rows, 512:768])
        part = part + nt(r.inner[1], r.wc1[rows, 512:768])
        part = part + nt(r.inner[2], r.wc2[rows, 512:768])
        r.rsf[:, rows] = part.astype(bf16)

    loop(3, feed_out)
    sum_f = Scatter("f")
    reduce_z("c1", 1)
    grad_h2 = sum_h2.total()
    normed = r.share[NORM2]
    r.gpart[3:4, :] = jnp.sum(grad_h2, axis=0, keepdims=True)
    r.gpart[4:5, :] = jnp.sum(grad_h2 * normed, axis=0, keepdims=True)
    mid_grad = r.share[TOP] + back(grad_h2 * (1.0 + r.modf[4:5, :]), normed, r.invs[1])
    r.share[MIDG] = mid_grad
    r.gpart[2:3, :] = jnp.sum(mid_grad * r.share[ATT], axis=0, keepdims=True)
    r.ag[at16(tp * 64, 64), :] = (r.modf[2:3, :] * mid_grad).astype(bf16)
    ag_all = Gather(rows_view(r.ag), first64(r.ag))
    reduce_z("c1", 0)
    sum_f.relay()

    ag_all.relay()
    reduce_z("c2", 1)
    ag_all.done()
    r.da[:, 0:288] = nn(r.ag[...], r.wo[...])
    transpose(r.ag, r.agt)

    reduce_core("out")
    def total_of(v):
        return jnp.sum(jnp.sum(v, axis=0, keepdims=True), axis=1, keepdims=True)

    squares = []
    kept = []

    def result_part():
        feed = sum_f.total()
        fed = r.modf[5:6, :] * feed
        result = r.share[MID] + fed
        r.gpart[5:6, :] = jnp.sum(r.share[TOP] * feed, axis=0, keepdims=True)
        att = r.modf[2:3, :] * r.share[ATT]

        squares[:] = [total_of(valid_share * v * v) for v in (result, att, fed)]
        low_result = result.astype(bf16)
        for t in range(4):
            r.ras[t] = low_result[:, 288 * t : 288 * t + 256]
            r.ias[t, :, 320:352] = low_result[:, 288 * t + 256 : 288 * t + 288]
        r.rar[tp] = r.ras[tp]
        kept.append(mates_send(lambda t: r.ras.at[t], r.rar.at[tp], r.rar.at[pl.ds(0, 3)]))

    def rows_part():
        arrived(r.rar.at[pl.ds(0, 3)], kept[0])
        rar = jnp.concatenate([r.rar[t] for t in range(4)], axis=0)
        r.bs[...] = nn(r.spread[...], rar).astype(bf16)
        kept.append(to_homes(slots64(r.bs), slots64(r.br), first64(r.br)))


    sums = [jnp.zeros((1, PAD), f32), jnp.zeros((1, PAD), f32)]

    def attend_back(h):
        grad = jnp.where(head_lane, r.da[:, 72 * h : 72 * h + 128], 0.0).astype(bf16)
        prob = r.pf[h]
        prob_grad = nt(grad, r.vl[h])
        mixed = jnp.sum(prob * prob_grad, axis=-1, keepdims=True)
        score = (prob * (prob_grad - mixed)).astype(bf16)
        value_grad = tn(prob.astype(bf16), grad)
        r.dqkv[:, 576 + 72 * h : 648 + 72 * h] = value_grad[:, 0:72].astype(bf16)
        for kind, offset, normed_ref, inv_ref in (
            ("q", 0, r.qn, r.qi),
            ("k", 288, r.kn, r.ki),
        ):
            if kind == "q":
                turned = nn(score, r.kl[h]) * scale_q
            else:
                turned = tn(score, r.ql[h])
            turned = turned * r.cosv[...] - swap(turned) * r.sinv[...]
            normed = normed_ref[h]
            along = jnp.sum(turned * normed, axis=0, keepdims=True)
            if kind == "q":
                sums[0] = sums[0] + along
            else:
                sums[1] = sums[1] + along
            g = turned * gains[kind]
            mean = jnp.sum(g * normed, axis=-1, keepdims=True) * (1.0 / 72)
            g = inv_ref[h] * (g - normed * mean)
            r.dqkv[:, offset + 72 * h : offset + 72 * h + 72] = g[:, 0:72].astype(bf16)

    attend_back(0)
    result_part()
    reduce_x("out", 1)
    reduce_x("out", 0)
    attend_back(1)
    reduce_z("c2", 0)
    attend_back(2)
    rows_part()
    reduce_z("out", 1)
    attend_back(3)
    def first_back(j):
        r.rsh1[:, at128(j * 384, 384)] = nt(r.dqkv[...], r.w1[at128(j * 384, 384), 0:864]).astype(bf16)

    loop(3, first_back)
    sum_h1 = Scatter("h1")
    reduce_z("out", 0)
    reduce_core("qkv")
    reduce_x("qkv", 1)
    reduce_x("qkv", 0)
    sum_h1.relay()
    grad_h1 = sum_h1.total()
    normed = r.share[NORM1]
    r.gpart[0:1, :] = jnp.sum(grad_h1, axis=0, keepdims=True)
    r.gpart[1:2, :] = jnp.sum(grad_h1 * normed, axis=0, keepdims=True)
    in_grad = r.share[MIDG] + back(grad_h1 * (1.0 + r.modf[1:2, :]), normed, r.invs[0])
    low_grad = in_grad.astype(bf16)
    for t in range(4):
        r.ias[t, :, 0:288] = low_grad[:, 288 * t : 288 * t + 288]
    numbers = jnp.concatenate(
        [sums[0][:, 0:72], sums[1][:, 0:72], squares[0], squares[1], squares[2],
         total_of(valid_share), jnp.zeros((1, 288 - 148), f32)],
        axis=-1,
    )
    for t in range(4):
        for k in range(6):
            r.hs[t, k] = r.gpart[k : k + 1, 288 * t : 288 * t + 288]
        r.hs[t, 6] = numbers
    r.hr[tp] = r.hs[tp]
    h_in = mates_send(lambda t: r.hs.at[t], r.hr.at[tp], r.hr.at[pl.ds(0, 3)])
    r.iar[tp] = r.ias[tp]
    ia_in = mates_send(lambda t: r.ias.at[t], r.iar.at[tp], r.iar.at[pl.ds(0, 3)])

    arrived(r.hr.at[pl.ds(0, 3)], h_in)
    total = r.hr[0] + r.hr[1] + r.hr[2] + r.hr[3]
    for k in range(6):
        r.gs[k] = total[k].astype(bf16).astype(f32)
    r.gs[6] = total[6]
    g2_in = to_homes(lambda i: r.gs, lambda i: r.grec.at[i], head_of(r.grec))
    reduce_z("qkv", 1)
    arrived(r.iar.at[pl.ds(0, 3)], ia_in)
    iar = jnp.concatenate([r.iar[t] for t in range(4)], axis=0)
    r.bgs[...] = nn(r.spread[...], iar).astype(bf16)
    bg_in = to_homes(slots64(r.bgs), slots64(r.bgr), first64(r.bgr))
    reduce_z("qkv", 0)
    arrived(r.grec, g2_in)
    cond_part = jnp.zeros((8, 144), f32)
    for k in range(6):
        grads = jnp.concatenate([r.grec[i, k] for i in range(8)], axis=0)
        low = grads.astype(bf16)
        r.gada[k] = tn(silu_own, low)
        r.gbada[k : k + 1, :] = jnp.sum(grads, axis=0, keepdims=True)
        cond_part = cond_part + nt(low, r.wada[k])
    totals = r.grec[0, 6]
    for i in range(1, 8):
        totals = totals + r.grec[i, 6]
    r.gqg[...] = totals[:, 0:72]
    r.gkg[...] = totals[:, 72:144]
    ratio = totals[:, 144:147] / (totals[:, 147:148] * 1152.0)
    r.stats[...] = jnp.sqrt(ratio)
    r.cps[...] = cond_part
    c_in = sems(2)
    r.cpr[mp] = cond_part
    for step in range(1, 4):
        start(r.cps, r.cpr.at[mp], c_in, c_in + 1, (dp, mp ^ step))
    sent(r.cpr.at[pl.ds(0, 3)], c_in)
    arrived(r.cpr.at[pl.ds(0, 3)], c_in + 1)
    cond_sum = r.cpr[0] + r.cpr[1] + r.cpr[2] + r.cpr[3]
    for i in range(8):
        r.cts[i] = cond_sum[i : i + 1, :]
    r.ctr[dp] = r.cts[dp]
    ct_in = to_others(lambda i: r.cts.at[i], r.ctr.at[dp], r.ctr.at[pl.ds(0, 7)])

    for k in range(3):
        grad = reduce_end(f"c{k}")
        lanes = slice(256 * k, 256 * k + 256)
        r.ggu[:, 0, lanes] = grad[:, 0:256]
        r.ggu[:, 1, lanes] = grad[:, 256:512]
        r.gdn[:, lanes] = grad[:, 512:768]
    arrived(r.br, kept[1])
    r.outt[0:256, :] = tn(r.br[...], r.place[...]).astype(bf16)
    grad = reduce_end("qkv")
    for p in range(3):
        r.gqkv[p] = grad[:, 288 * p : 288 * p + 288]
    r.gout[...] = reduce_end("out")
    arrived(r.bgr, bg_in)
    both = tn(r.bgr[...], r.place[...]).astype(bf16)
    r.gint[...] = both[0:288, :]
    r.outt[256:288, :] = both[320:352, :]
    arrived(r.ctr.at[pl.ds(0, 7)], ct_in)
    for s in range(8):
        r.gcond[0:1, 144 * s : 144 * s + 144] = r.ctr[s]
    cond = r.cond[...].astype(f32)
    sig_c = jax.nn.sigmoid(cond)
    r.gcond[...] = r.gcond[...] * sig_c * (1.0 + cond * (1.0 - sig_c))
    for finish in pending:
        finish()
    assert taken[0] == 126


def copy_out(*refs):
    count = len(refs) // 2
    sem = refs[-1]
    copies = [pltpu.make_async_copy(refs[i], refs[count + i], sem.at[i]) for i in range(count)]
    for copy in copies:
        copy.start()
    for copy in copies:
        copy.wait()


def body_kernel(
    x_src, cotangent, route_dest, route_count, item_grid, noise_bin, cond, w_ada, b_ada,
    w_qkv, q_gain, k_gain, w_out, w_gu, w_down,
):
    scratch = scratch_list()
    vmem = pl.BlockSpec(memory_space=pltpu.VMEM)
    smem = pl.BlockSpec(memory_space=pltpu.SMEM)
    shapes = [
        ((288, 512), bf16), ((288, 512), bf16), ((1, 1152), f32), ((6, 144, 288), f32),
        ((6, 288), f32), ((3, 144, 288), f32), ((1, 72), f32), ((1, 72), f32),
        ((144, 288), f32), ((144, 2, 768), f32), ((144, 768), f32), ((1, 3), f32),
    ]
    outs = pl.pallas_call(
        functools.partial(block_kernel, list(scratch)),
        out_shape=[pltpu.VMEM(s, d) for s, d in shapes],
        in_specs=[vmem, vmem, vmem, smem, smem, smem] + [vmem] * 9,
        out_specs=[vmem] * len(shapes),
        scratch_shapes=list(scratch.values()),
        compiler_params=pltpu.CompilerParams(
            has_side_effects=True, vmem_limit_bytes=57500000, collective_id=0
        ),
        name="block",
    )(
        x_src.T, cotangent.T, route_dest.reshape(1, SRC_CAP), route_count, item_grid, noise_bin,
        cond, jnp.transpose(w_ada, (1, 0, 2)), b_ada, jnp.transpose(w_qkv, (1, 0, 2)),
        q_gain.reshape(1, DH), k_gain.reshape(1, DH), w_out.T, w_gu, w_down.T,
    )
    outs = pl.pallas_call(
        copy_out,
        out_shape=[jax.ShapeDtypeStruct(s, d) for s, d in shapes],
        in_specs=[vmem] * len(shapes),
        out_specs=[pl.BlockSpec(memory_space=pl.ANY)] * len(shapes),
        scratch_shapes=[pltpu.SemaphoreType.DMA((len(shapes),))],
        compiler_params=pltpu.CompilerParams(vmem_limit_bytes=2000000),
        name="store",
    )(*outs)
    (outt, gint, gcond, gada, gbada, gqkv, gqg, gkg, gout, ggu, gdn, stats) = outs
    return (
        outt.T, gint.T, gcond, jnp.transpose(gada, (1, 0, 2)), gbada,
        jnp.transpose(gqkv, (1, 0, 2)), gqg.reshape(DH), gkg.reshape(DH), gout.T, ggu, gdn.T,
        stats.reshape(3),
    )


def solution(mesh):
    one_kernel = mesh.shape["dp"] == 8 and mesh.shape["mp"] == 4
    return jax.shard_map(
        body_kernel if one_kernel else body,
        mesh=mesh,
        in_specs=(
            P("dp", "mp"),
            P("dp", "mp"),
            P("dp"),
            P("dp"),
            P("dp", None),
            P("dp"),
            P("dp", None),
            P("dp", None, "mp"),
            P(None, "mp"),
            P("dp", None, "mp"),
            P(),
            P(),
            P("mp", "dp"),
            P("dp", None, "mp"),
            P("mp", "dp"),
        ),
        out_specs=(
            P("dp", "mp"),
            P("dp", "mp"),
            P("dp", None),
            P("dp", None, "mp"),
            P(None, "mp"),
            P("dp", None, "mp"),
            P(),
            P(),
            P("mp", "dp"),
            P("dp", None, "mp"),
            P("mp", "dp"),
            P(),
        ),
        check_vma=False,
    )
```

```python
import functools
import math

import jax
import jax.numpy as jnp
from jax import lax
from jax.experimental import pallas as pl
from jax.experimental.pallas import tpu as pltpu
from jax.sharding import PartitionSpec as P

D = 1152
DH = 72
NBINS = 16
BLOCK = 256
ROWS_DEV = 256
SRC_CAP = 512


epsilon = 1e-06


def grad_share(part, dim):
    sent = part.astype(jnp.bfloat16)
    total = lax.psum_scatter(sent, "dp", scatter_dimension=dim, tiled=True)
    return total.astype(jnp.float32)


def norm_rows(values):
    scale = lax.rsqrt(jnp.mean(values * values, axis=-1, keepdims=True) + epsilon)
    return (values * scale, scale)


def norm_back(grad_normed, normed, scale):
    return scale * (grad_normed - normed * jnp.mean(grad_normed * normed, axis=-1, keepdims=True))


def rotate(values, cos_h, sin_h, cos_w, sin_w, sign):
    quarter = values.shape[-1] // 4
    first = values[..., :quarter]
    second = values[..., quarter : 2 * quarter]
    third = values[..., 2 * quarter : 3 * quarter]
    fourth = values[..., 3 * quarter :]
    return jnp.concatenate(
        [
            first * cos_h - sign * second * sin_h,
            sign * first * sin_h + second * cos_h,
            third * cos_w - sign * fourth * sin_w,
            sign * third * sin_w + fourth * cos_w,
        ],
        axis=-1,
    )


def angle_tables(grid, block, head_dim):
    quarter = head_dim // 4
    place = lax.broadcasted_iota(jnp.int32, (grid.shape[0], block), 1)
    width = grid[:, 1:2]
    height_pos = (place // width).astype(jnp.float32)
    width_pos = (place % width).astype(jnp.float32)
    freqs = jnp.exp(-math.log(10000.0) * jnp.arange(quarter).astype(jnp.float32) / quarter)
    angle_h = (height_pos[:, :, None] * freqs)[:, :, None, :]
    angle_w = (width_pos[:, :, None] * freqs)[:, :, None, :]
    return (jnp.cos(angle_h), jnp.sin(angle_h), jnp.cos(angle_w), jnp.sin(angle_w))


def row_share(values):
    return lax.psum_scatter(values, "mp", scatter_dimension=0, tiled=True)


def row_whole(values):
    return lax.all_gather(values, "mp", axis=0, tiled=True)


def body(
    x_src,
    cotangent,
    route_dest,
    route_count,
    item_grid,
    noise_bin,
    cond,
    w_ada,
    b_ada,
    w_qkv,
    q_gain,
    k_gain,
    w_out,
    w_gu,
    w_down,
):
    peers = lax.axis_size("dp")
    model_rank = lax.axis_index("mp")
    blocks_here = item_grid.shape[0]
    local_width = x_src.shape[1]
    heads_here = local_width // DH
    slot_rows = 2 * ROWS_DEV // peers
    share = ROWS_DEV // lax.axis_size("mp")
    row_first = model_rank * share
    live = jnp.arange(SRC_CAP) < route_count[0]
    target = route_dest // ROWS_DEV
    member = (target[:, None] == jnp.arange(peers)[None, :]) & live[:, None]
    running = jnp.cumsum(member.astype(jnp.int32), axis=0)
    rank_in = jnp.sum(running * member, axis=1) - 1
    place = jnp.where(live, target * slot_rows + rank_in, peers * slot_rows)
    send_rows = (
        jnp.zeros((peers * slot_rows, local_width), jnp.bfloat16).at[place].set(x_src, mode="drop")
    )
    send_grads = (
        jnp.zeros((peers * slot_rows, local_width), jnp.bfloat16)
        .at[place]
        .set(cotangent, mode="drop")
    )
    send_index = (
        jnp.full((peers * slot_rows,), ROWS_DEV, jnp.int32)
        .at[place]
        .set(route_dest % ROWS_DEV, mode="drop")
    )
    recv_rows, recv_grads, recv_index = (
        lax.all_to_all(
            send_rows.reshape(peers, slot_rows, local_width),
            "dp",
            split_axis=0,
            concat_axis=0,
            tiled=True,
        ),
        lax.all_to_all(
            send_grads.reshape(peers, slot_rows, local_width),
            "dp",
            split_axis=0,
            concat_axis=0,
            tiled=True,
        ),
        lax.all_to_all(
            send_index.reshape(peers, slot_rows), "dp", split_axis=0, concat_axis=0, tiled=True
        ),
    )
    flat_index = recv_index.reshape(-1)
    rows_cols = (
        jnp.zeros((ROWS_DEV, local_width), jnp.bfloat16)
        .at[flat_index]
        .set(recv_rows.reshape(-1, local_width), mode="drop")
    )
    grads_cols = (
        jnp.zeros((ROWS_DEV, local_width), jnp.bfloat16)
        .at[flat_index]
        .set(recv_grads.reshape(-1, local_width), mode="drop")
    )
    qkv_full, out_full, gu_full, down_full = (
        lax.all_gather(w_qkv, "dp", axis=0, tiled=True),
        lax.all_gather(w_out, "dp", axis=1, tiled=True),
        lax.all_gather(w_gu, "dp", axis=0, tiled=True),
        lax.all_gather(w_down, "dp", axis=1, tiled=True),
    )
    cond_wide = cond.astype(jnp.float32)
    cond_sig = jax.nn.sigmoid(cond_wide)
    silu_cond = (cond_wide * cond_sig).astype(jnp.bfloat16)
    ada_rows = w_ada.shape[0]
    silu_all = lax.all_gather(silu_cond, "dp", axis=0, tiled=True)
    silu_own = lax.dynamic_slice_in_dim(silu_all, lax.axis_index("dp") * ada_rows, ada_rows, 1)
    mod_sums = jnp.einsum("id,dkc->ikc", silu_own, w_ada, preferred_element_type=jnp.float32)
    mod_part = (
        lax.psum_scatter(mod_sums, "dp", scatter_dimension=0, tiled=True)
        + b_ada.astype(jnp.float32)
    ).astype(jnp.bfloat16)
    rows_full, grads_full, mod_full = (
        lax.all_gather(rows_cols, "mp", axis=1, tiled=True),
        lax.all_gather(grads_cols, "mp", axis=1, tiled=True),
        lax.all_gather(mod_part, "mp", axis=2, tiled=True),
    )
    modulation = mod_full.astype(jnp.float32)
    shift_one = modulation[:, 0][:, None, :]
    scale_one = modulation[:, 1][:, None, :]
    gate_two = modulation[:, 5][:, None, :]
    resid = rows_full.astype(jnp.float32).reshape(blocks_here, BLOCK, D)
    normed_one, inv_one = norm_rows(resid)
    hidden_one = (normed_one * (1.0 + scale_one) + shift_one).astype(jnp.bfloat16)
    qkv = jnp.einsum("ibd,dkc->ibkc", hidden_one, qkv_full, preferred_element_type=jnp.float32)
    query = qkv[:, :, 0].reshape(blocks_here, BLOCK, heads_here, DH)
    keys = qkv[:, :, 1].reshape(blocks_here, BLOCK, heads_here, DH)
    value = qkv[:, :, 2].reshape(blocks_here, BLOCK, heads_here, DH)
    query_normed, query_inv = norm_rows(query)
    key_normed, key_inv = norm_rows(keys)
    cos_h, sin_h, cos_w, sin_w = angle_tables(item_grid, BLOCK, DH)
    query_low = (
        rotate(query_normed * q_gain, cos_h, sin_h, cos_w, sin_w, 1.0) * DH ** (-0.5)
    ).astype(jnp.bfloat16)
    key_low = rotate(key_normed * k_gain, cos_h, sin_h, cos_w, sin_w, 1.0).astype(jnp.bfloat16)
    value_low = value.astype(jnp.bfloat16)
    positions = lax.broadcasted_iota(jnp.int32, (blocks_here, BLOCK), 1)
    valid = positions < (item_grid[:, 0] * item_grid[:, 1])[:, None]
    key_ok = valid[:, None, None, :]
    valid_wide = valid.astype(jnp.float32)[:, :, None]
    valid_share = lax.dynamic_slice_in_dim(
        valid.astype(jnp.float32).reshape(ROWS_DEV), row_first, share, 0
    )[:, None]
    bin_onehot = (noise_bin[:, None] == jnp.arange(NBINS)[None, :]).astype(jnp.float32)
    bin_local = jnp.sum(bin_onehot, axis=0) * (model_rank == 0).astype(jnp.float32)

    def masked_scores():
        raw = jnp.einsum("iqhc,ikhc->ihqk", query_low, key_low, preferred_element_type=jnp.float32)
        return jnp.where(key_ok, raw, -1e30)

    scores = masked_scores()
    top = jnp.max(scores, axis=-1, keepdims=True)
    log_total = top + jnp.log(jnp.sum(jnp.exp(scores - top), axis=-1, keepdims=True))
    prob_low = jnp.exp(scores - log_total).astype(jnp.bfloat16)
    attn_low = jnp.einsum(
        "ihqk,ikhc->iqhc", prob_low, value_low, preferred_element_type=jnp.float32
    ).astype(jnp.bfloat16)
    out_heads = out_full.reshape(heads_here, DH, D)
    attn_part = jnp.einsum("iqhc,hcd->iqd", attn_low, out_heads, preferred_element_type=jnp.float32)

    def own_rows_of(values):
        return lax.dynamic_slice_in_dim(values.reshape(ROWS_DEV, D), row_first, share, 0)

    row_item = (row_first + jnp.arange(share)) // BLOCK
    item_onehot = (row_item[:, None] == jnp.arange(blocks_here)[None, :]).astype(jnp.float32)

    def per_item(values):
        return jnp.einsum("si,sd->id", item_onehot, values, precision=lax.Precision.HIGHEST)

    mod_rows = jnp.einsum("si,ikd->skd", item_onehot, modulation, precision=lax.Precision.HIGHEST)
    scale_one_r = mod_rows[:, 1]
    gate_one_r = mod_rows[:, 2]
    shift_two_r = mod_rows[:, 3]
    scale_two_r = mod_rows[:, 4]
    gate_two_r = mod_rows[:, 5]
    resid_share = own_rows_of(resid)
    normed_one_share = own_rows_of(normed_one)
    inv_one_share = lax.dynamic_slice_in_dim(inv_one.reshape(ROWS_DEV, 1), row_first, share, 0)
    attention_share = row_share(attn_part.reshape(ROWS_DEV, D))
    mid_share = resid_share + gate_one_r * attention_share
    normed_two_share, inv_two_share = norm_rows(mid_share)
    hidden_two_share = (normed_two_share * (1.0 + scale_two_r) + shift_two_r).astype(jnp.bfloat16)
    hidden_two = row_whole(hidden_two_share).reshape(blocks_here, BLOCK, D)
    gate_up = jnp.einsum("ibd,dkf->ibkf", hidden_two, gu_full, preferred_element_type=jnp.float32)
    gate_raw = gate_up[:, :, 0]
    up_raw = gate_up[:, :, 1]
    gate_sig = jax.nn.sigmoid(gate_raw)
    gate_act = gate_raw * gate_sig
    inner = (gate_act * up_raw).astype(jnp.bfloat16)
    feed_part = jnp.einsum("ibf,fd->ibd", inner, down_full, preferred_element_type=jnp.float32)
    feed_part, kept = (feed_part, (inner, up_raw, gate_raw, gate_sig, gate_act))
    feed_share = row_share(feed_part.reshape(ROWS_DEV, D))
    result_share = mid_share + gate_two_r * feed_share
    result_whole = row_whole(result_share.astype(jnp.bfloat16))
    squares = jnp.stack(
        [
            jnp.sum(valid_share * result_share * result_share),
            jnp.sum(valid_share * (gate_one_r * attention_share) ** 2),
            jnp.sum(valid_share * (gate_two_r * feed_share) ** 2),
        ]
    )
    square_total, valid_total, bin_total = lax.psum(
        (squares, jnp.sum(valid_share), bin_local), ("dp", "mp")
    )
    stats_value = jnp.sqrt(square_total / (valid_total * D))
    item_count = jnp.sum(bin_onehot * bin_total[None, :], axis=1)
    weight_value = blocks_here * peers / (NBINS * item_count)
    top_grad = grads_full.astype(jnp.float32).reshape(blocks_here, BLOCK, D) * (
        weight_value[:, None, None] * valid_wide
    )
    top_share = own_rows_of(top_grad)
    feed_grad = (gate_two * top_grad).astype(jnp.bfloat16)
    grad_gate_two = per_item(top_share * feed_share)
    inner, up_raw, gate_raw, gate_sig, gate_act = kept
    inner_grad = jnp.einsum("ibd,fd->ibf", feed_grad, down_full, preferred_element_type=jnp.float32)
    grad_down_part = jnp.einsum("ibf,ibd->fd", inner, feed_grad, preferred_element_type=jnp.float32)
    gate_grad = (inner_grad * up_raw * gate_sig * (1.0 + gate_raw * (1.0 - gate_sig))).astype(
        jnp.bfloat16
    )
    up_grad = (inner_grad * gate_act).astype(jnp.bfloat16)
    gate_up_grad = jnp.stack([gate_grad, up_grad], axis=2)
    grad_gu_part = jnp.einsum(
        "ibd,ibkf->dkf", hidden_two, gate_up_grad, preferred_element_type=jnp.float32
    )
    hidden_two_part = jnp.einsum(
        "ibkf,dkf->ibd", gate_up_grad, gu_full, preferred_element_type=jnp.float32
    )
    grad_down, grad_gu, hidden_two_part = (grad_down_part, grad_gu_part, hidden_two_part)
    h2_grad_share = row_share(hidden_two_part.reshape(ROWS_DEV, D))
    grad_shift_two = per_item(h2_grad_share)
    grad_scale_two = per_item(h2_grad_share * normed_two_share)
    mid_grad_share = top_share + norm_back(
        h2_grad_share * (1.0 + scale_two_r), normed_two_share, inv_two_share
    )
    attention_grad_share = (gate_one_r * mid_grad_share).astype(jnp.bfloat16)
    grad_gate_one = per_item(mid_grad_share * attention_share)
    attention_grad = row_whole(attention_grad_share).reshape(blocks_here, BLOCK, D)
    attn_low_grad = jnp.einsum(
        "iqd,hcd->iqhc", attention_grad, out_heads, preferred_element_type=jnp.float32
    ).astype(jnp.bfloat16)
    grad_out_part = jnp.einsum(
        "iqhc,iqd->hcd", attn_low, attention_grad, preferred_element_type=jnp.float32
    ).reshape(local_width, D)
    prob_full = jnp.exp(masked_scores() - log_total)
    prob_grad = jnp.einsum(
        "iqhc,ikhc->ihqk", attn_low_grad, value_low, preferred_element_type=jnp.float32
    )
    value_grad = jnp.einsum(
        "ihqk,iqhc->ikhc", prob_low, attn_low_grad, preferred_element_type=jnp.float32
    )
    score_grad = (
        prob_full * (prob_grad - jnp.sum(prob_full * prob_grad, axis=-1, keepdims=True))
    ).astype(jnp.bfloat16)
    query_rot_grad = jnp.einsum(
        "ihqk,ikhc->iqhc", score_grad, key_low, preferred_element_type=jnp.float32
    ) * DH ** (-0.5)
    key_rot_grad = jnp.einsum(
        "ihqk,iqhc->ikhc", score_grad, query_low, preferred_element_type=jnp.float32
    )
    query_scaled_grad = rotate(query_rot_grad, cos_h, sin_h, cos_w, sin_w, -1.0)
    key_scaled_grad = rotate(key_rot_grad, cos_h, sin_h, cos_w, sin_w, -1.0)
    qgain_local = jnp.sum(query_scaled_grad * query_normed, axis=(0, 1, 2))
    kgain_local = jnp.sum(key_scaled_grad * key_normed, axis=(0, 1, 2))
    query_grad = norm_back(query_scaled_grad * q_gain, query_normed, query_inv)
    key_grad = norm_back(key_scaled_grad * k_gain, key_normed, key_inv)
    qkv_grad = jnp.stack(
        [
            query_grad.reshape(blocks_here, BLOCK, local_width),
            key_grad.reshape(blocks_here, BLOCK, local_width),
            value_grad.reshape(blocks_here, BLOCK, local_width),
        ],
        axis=2,
    ).astype(jnp.bfloat16)
    grad_qkv_part = jnp.einsum(
        "ibd,ibkc->dkc", hidden_one, qkv_grad, preferred_element_type=jnp.float32
    )
    hidden_one_part = jnp.einsum(
        "ibkc,dkc->ibd", qkv_grad, qkv_full, preferred_element_type=jnp.float32
    )
    grad_out, grad_qkv, qgain_part, kgain_part, hidden_one_part = (
        grad_out_part,
        grad_qkv_part,
        qgain_local,
        kgain_local,
        hidden_one_part,
    )
    h1_grad_share = row_share(hidden_one_part.reshape(ROWS_DEV, D))
    grad_shift_one = per_item(h1_grad_share)
    grad_scale_one = per_item(h1_grad_share * normed_one_share)
    input_share = mid_grad_share + norm_back(
        h1_grad_share * (1.0 + scale_one_r), normed_one_share, inv_one_share
    )
    input_whole = row_whole(input_share.astype(jnp.bfloat16))
    mod_partial = jnp.stack(
        [
            grad_shift_one,
            grad_scale_one,
            grad_gate_one,
            grad_shift_two,
            grad_scale_two,
            grad_gate_two,
        ],
        axis=1,
    )
    mod_grad = lax.psum(mod_partial, "mp").astype(jnp.bfloat16)
    mod_grad_own = lax.dynamic_slice_in_dim(mod_grad, model_rank * local_width, local_width, 2)
    mod_all = lax.all_gather(mod_grad_own, "dp", axis=0, tiled=True)
    cond_part = jnp.einsum("ikc,dkc->id", mod_all, w_ada, preferred_element_type=jnp.float32)
    cond_sum = lax.psum(cond_part, "mp")
    cond_total = lax.all_to_all(
        cond_sum.reshape(peers, blocks_here, ada_rows), "dp", split_axis=0, concat_axis=0, tiled=True
    )
    cond_total = jnp.moveaxis(cond_total, 0, 1).reshape(blocks_here, peers * ada_rows)
    grad_cond = cond_total * cond_sig * (1.0 + cond_wide * (1.0 - cond_sig))
    grad_ada = jnp.einsum("ir,ikc->rkc", silu_own, mod_all, preferred_element_type=jnp.float32)
    grad_bada = jnp.sum(mod_all.astype(jnp.float32), axis=0)
    qgain_total, kgain_total = lax.psum((qgain_part, kgain_part), ("dp", "mp"))
    qkv_own, out_own, gu_own, down_own = (
        grad_share(grad_qkv, 0),
        grad_share(grad_out, 1),
        grad_share(grad_gu, 0),
        grad_share(grad_down, 1),
    )
    result_cols = lax.dynamic_slice_in_dim(result_whole, model_rank * local_width, local_width, 1)
    input_cols = lax.dynamic_slice_in_dim(input_whole, model_rank * local_width, local_width, 1)
    back_index = jnp.minimum(flat_index, ROWS_DEV - 1)
    back_rows = result_cols[back_index].reshape(peers, slot_rows, local_width)
    back_grads = input_cols[back_index].reshape(peers, slot_rows, local_width)
    returned_rows, returned_grads = (
        lax.all_to_all(back_rows, "dp", split_axis=0, concat_axis=0, tiled=True),
        lax.all_to_all(back_grads, "dp", split_axis=0, concat_axis=0, tiled=True),
    )
    pick = jnp.minimum(place, peers * slot_rows - 1)
    empty = jnp.zeros((), jnp.bfloat16)
    out_rows = jnp.where(live[:, None], returned_rows.reshape(-1, local_width)[pick], empty)
    out_grads = jnp.where(live[:, None], returned_grads.reshape(-1, local_width)[pick], empty)
    return (
        out_rows,
        out_grads,
        grad_cond,
        grad_ada,
        grad_bada,
        qkv_own,
        qgain_total,
        kgain_total,
        out_own,
        gu_own,
        down_own,
        stats_value,
    )


MESH = pl.DeviceIdType.MESH
f32 = jnp.float32
bf16 = jnp.bfloat16
LANE_INDEX = 288
META = 1152
PAD = 128


def nn(left, right):
    return jnp.dot(left, right, preferred_element_type=f32)


def nt(left, right):
    return lax.dot_general(left, right, (((1,), (1,)), ((), ())), preferred_element_type=f32)


def tn(left, right):
    return lax.dot_general(left, right, (((0,), (0,)), ((), ())), preferred_element_type=f32)


def loop(count, step):
    def run(index, carry):
        step(index)
        return carry

    lax.fori_loop(0, count, run, 0)


def at128(index, size):
    return pl.ds(pl.multiple_of(index, 128), size)


def at16(index, size):
    return pl.ds(pl.multiple_of(index, 16), size)


GROUPS = (("c0", 768), ("c1", 768), ("c2", 768), ("out", 256), ("qkv", 896))


def scratch_list():
    vm = pltpu.VMEM
    items = dict(
        sem=pltpu.SemaphoreType.DMA((130,)),
        arow=vm((1, 1280), f32),
        arec=vm((8, 1, 1280), f32),
        amat=vm((8, 1280), f32),
        xe=vm((384, 512), bf16),
        place=vm((512, 512), bf16),
        sx=vm((512, 384), bf16),
        rx=vm((512, 384), bf16),
        sg=vm((512, 256), bf16),
        rg=vm((512, 256), bf16),
        spread=vm((512, 256), bf16),
        rb=vm((4, 256, 384), bf16),
        gb=vm((4, 256, 256), bf16),
        pms=vm((8, 6, 1, 288), f32),
        pmr=vm((8, 6, 1, 288), f32),
        mdb=vm((4, 6, 1, 288), f32),
        modf=vm((8, 1152), f32),
        h1=vm((256, 1152), bf16),
        h1t=vm((1152, 256), bf16),
        w1=vm((1152, 896), bf16),
        wc0=vm((1152, 768), bf16),
        wc1=vm((1152, 768), bf16),
        wc2=vm((1152, 768), bf16),
        wp1=vm((144, 896), bf16),
        wqkv_in=vm((3, 144, 288), bf16),
        wgu_in=vm((144, 2, 768), bf16),
        wada_in=vm((6, 144, 288), bf16),
        wdn_in=vm((144, 768), bf16),
        wp=vm((3, 144, 768), bf16),
        wb=vm((1152, 256), bf16),
        wpb=vm((144, 256), bf16),
        qkv=vm((256, 1024), f32),
        qn=vm((4, 256, 128), f32),
        kn=vm((4, 256, 128), f32),
        qi=vm((4, 256, 1), f32),
        ki=vm((4, 256, 1), f32),
        ql=vm((4, 256, 128), bf16),
        kl=vm((4, 256, 128), bf16),
        vl=vm((4, 256, 128), bf16),
        pf=vm((4, 256, 256), f32),
        cosv=vm((256, 128), f32),
        sinv=vm((256, 128), f32),
        al1=vm((256, 32), bf16),
        al2=vm((256, 256), bf16),
        rsa=vm((256, 1152), bf16),
        rra=vm((3, 64, 1152), bf16),
        rta=vm((64, 1152), bf16),
        rsf=vm((256, 1152), bf16),
        rrf=vm((3, 64, 1152), bf16),
        rtf=vm((64, 1152), bf16),
        rsh2=vm((256, 1152), bf16),
        rrh2=vm((3, 64, 1152), bf16),
        rth2=vm((64, 1152), bf16),
        rsh1=vm((256, 1152), bf16),
        rrh1=vm((3, 64, 1152), bf16),
        rth1=vm((64, 1152), bf16),
        h2=vm((256, 1152), bf16),
        h2t=vm((1152, 256), bf16),
        ag=vm((256, 1152), bf16),
        agt=vm((1152, 256), bf16),
        h2sum=vm((256, 1152), f32),
        inner=vm((3, 256, 256), bf16),
        gug=vm((3, 256, 512), bf16),
        fg=vm((256, 1152), bf16),
        fgt=vm((1152, 256), bf16),
        da=vm((256, 384), f32),
        dqkv=vm((256, 864), bf16),
        share=vm((8, 64, 1152), f32),
        invs=vm((2, 64, 1), f32),
        gpart=vm((8, 1152), f32),
        ras=vm((4, 64, 256), bf16),
        rar=vm((4, 64, 256), bf16),
        ias=vm((4, 64, 384), bf16),
        iar=vm((4, 64, 384), bf16),
        bs=vm((512, 256), bf16),
        br=vm((512, 256), bf16),
        bgs=vm((512, 384), bf16),
        bgr=vm((512, 384), bf16),
        hs=vm((4, 7, 1, 288), f32),
        hr=vm((4, 7, 1, 288), f32),
        gs=vm((7, 1, 288), f32),
        grec=vm((8, 7, 1, 288), f32),
        ms=vm((8, 6, 288), f32),
        cps=vm((8, 144), f32),
        cpr=vm((4, 8, 144), f32),
        cts=vm((8, 1, 144), f32),
        ctr=vm((8, 1, 144), f32),
    )
    for name, width in GROUPS:
        items["cs_" + name] = vm((4, 144, width), bf16)
        items["cr_" + name] = vm((4, 144, width), bf16)
        items["xs_" + name] = vm((2, 144, width), bf16)
        items["xr_" + name] = vm((2, 144, width), bf16)
        items["zs_" + name] = vm((2, 144, width), bf16)
        items["zr_" + name] = vm((2, 144, width), bf16)
    return items


class Refs:
    pass


def block_kernel(
    names, xt, ct, dest, count, grid, bin, cond, wada, bada, wqkv, qg, kg, woin, wgu, wdn, outt, gint, gcond, gada, gbada, gqkv, gqg, gkg, gout, ggu, gdn, stats, *scratch
):
    r = Refs()
    r.__dict__.update(locals())
    for name, ref in zip(names, scratch):
        setattr(r, name, ref)
    dp = lax.axis_index("dp")
    mp = lax.axis_index("mp")
    z, x, y, c = dp // 2, dp % 2, mp // 2, mp % 2
    zh, zl = z // 2, z % 2
    item = (2 * zh + c) * 2 + x
    tp = y * 2 + zl
    home = zl == c
    away = zl != c
    sem = r.sem
    taken = [0]

    def sems(count):
        first = taken[0]
        taken[0] += count
        return first

    def device(zz, xx, yy, cc):
        return (zz * 2 + xx, yy * 2 + cc)

    def worker(index, part):
        zi, xi = index // 2, index % 2
        return device(2 * (zi // 2) + part % 2, xi, part // 2, zi % 2)

    def mate(step):
        return device(2 * zh + (zl ^ (step & 1)), x, y ^ (step >> 1), c)

    def remote(src, dst, ss, rs, dev):
        return pltpu.make_async_remote_copy(
            src_ref=src,
            dst_ref=dst,
            send_sem=sem.at[ss],
            recv_sem=sem.at[rs],
            device_id=dev,
            device_id_type=MESH,
        )

    pending = []

    def start(src, dst, ss, rs, dev):
        remote(src, dst, ss, rs, dev).start()

    def start_unless(same, src, dst, ss, rs, dev):
        @pl.when(same)
        def _():
            pltpu.make_async_copy(src, dst, sem.at[rs]).start()

        @pl.when(jnp.logical_not(same))
        def _():
            remote(src, dst, ss, rs, dev).start()

    def arrived(dst, rs):
        pltpu.make_async_copy(dst, dst, sem.at[rs]).wait()

    def sent(ref, ss):
        pending.append(lambda: arrived(ref, ss))

    def sent_or_kept(size, count, ss):
        def finish():
            @pl.when(home)
            def _():
                arrived(size(count - 1), ss)

            @pl.when(away)
            def _():
                arrived(size(count), ss)

        pending.append(finish)

    def to_workers(source, target, size):
        base = sems(2)
        for step in range(8):
            index = (dp + step) % 8
            args = (source(index), target(dp), base, base + 1, worker(index, mp))
            if step == 0:
                start_unless(home, *args)
            else:
                start(*args)
        sent_or_kept(size, 8, base)
        return base + 1

    def to_homes(source, target, size):
        base = sems(2)
        for step in range(8):
            index = (dp + step) % 8
            args = (source(index), target(item), base, base + 1, (index, tp))
            if step == 0:
                start_unless(home, *args)
            else:
                start(*args)
        sent_or_kept(size, 8, base)
        return base + 1

    def to_others(source, target, size):
        base = sems(2)
        for step in range(1, 8):
            index = (dp + step) % 8
            start(source(index), target, base, base + 1, (index, mp))
        sent(size, base)
        return base + 1

    def slots64(ref):
        return lambda i: ref.at[at16(i * 64, 64)]

    def first64(ref):
        return lambda n: ref.at[pl.ds(0, 64 * n)]

    def head_of(ref):
        return lambda n: ref.at[pl.ds(0, n)]

    groups = {
        "attn": (r.wp1, r.w1),
        "wo": (r.wpb, r.wb),
        "c0": (r.wp.at[0], r.wc0),
        "c1": (r.wp.at[1], r.wc1),
        "c2": (r.wp.at[2], r.wc2),
    }
    w_base = {g: sems(6) for g in groups}

    def slot(ref, index):
        return ref.at[at16(index * 144, 144)]

    for g in groups:
        whole = groups[g][1]
        sent_or_kept(lambda n, whole=whole: whole.at[pl.ds(0, 144 * n)], 8, w_base[g] + 5)

    def gather_z(g, rels=(1, 0)):
        src, full = groups[g]
        base = w_base[g]
        for rel in rels:
            zt = c + 2 * (zh ^ rel)
            args = (src, slot(full, dp), base + 5, base + rel, device(zt, x, y, zl))
            if rel == 0:
                start_unless(home, *args)
            else:
                start(*args)

    def gather_x(g, rel):
        full, base = groups[g][1], w_base[g]
        mine = slot(full, (c + 2 * (zh ^ rel)) * 2 + x)
        arrived(mine, base + rel)
        start(mine, mine, base + 5, base + 2 + rel, device(z, 1 - x, y, c))
        start(mine, mine, base + 5, base + 4, device(z, x, y, 1 - c))

    def gather_core(g, rel):
        full, base = groups[g][1], w_base[g]
        mine = slot(full, (c + 2 * (zh ^ rel)) * 2 + 1 - x)
        arrived(mine, base + 2 + rel)
        start(mine, mine, base + 5, base + 4, device(z, x, y, 1 - c))

    def gather_done(g):
        arrived(groups[g][1].at[pl.ds(0, 144 * 4)], w_base[g] + 4)

    z_mate = device(2 * zh + 1 - zl, x, y, c)
    y_mate = device(z, x, 1 - y, c)

    class Gather:
        def __init__(self, view, size):
            self.view, self.size, self.base = view, size, sems(3)
            mine = view(tp)
            start(mine, mine, self.base, self.base + 1, z_mate)
            start(mine, mine, self.base, self.base + 2, y_mate)
            sent(size(3), self.base)

        def relay(self):
            other = self.view(tp ^ 1)
            arrived(other, self.base + 1)
            start(other, other, self.base, self.base + 2, y_mate)

        def done(self):
            arrived(self.size(2), self.base + 2)

    class Scatter:
        def __init__(self, name):
            self.base = sems(3)
            self.sent, self.rec, self.sum = (getattr(r, k + name) for k in ("rs", "rr", "rt"))
            start(self.view(tp ^ 3), self.rec.at[0], self.base, self.base + 1, y_mate)
            start(self.view(tp ^ 2), self.rec.at[1], self.base, self.base + 2, y_mate)
            sent(self.rec, self.base)

        def view(self, t):
            return self.sent.at[at16(t * 64, 64)]

        def relay(self):
            arrived(self.rec.at[0], self.base + 1)
            both = self.view(tp ^ 1)[...].astype(f32) + self.rec[0].astype(f32)
            self.sum[...] = both.astype(bf16)
            start(self.sum, self.rec.at[2], self.base, self.base + 2, z_mate)

        def total(self):
            arrived(self.rec.at[pl.ds(1, 2)], self.base + 2)
            total = self.view(tp)[...].astype(f32) + self.rec[1].astype(f32)
            return total + self.rec[2].astype(f32)

    def rows_view(buf):
        return lambda t: buf.at[at16(t * 64, 64)]

    def mates_send(source, target, size):
        base = sems(2)
        for step in range(1, 4):
            start(source(tp ^ step), target, base, base + 1, mate(step))
        sent(size, base)
        return base + 1

    g_base = {name: sems(9) for name, _ in GROUPS}

    def block(name, s):
        rows = at16(s * 144, 144)
        if name == "out":
            return nn(r.agt[rows, :], r.al2[...])
        if name == "qkv":
            return jnp.concatenate(
                [nn(r.h1t[rows, :], r.dqkv[...]), nn(r.agt[rows, :], r.al1[...])], axis=-1
            )
        k = int(name[1:])
        return jnp.concatenate(
            [nn(r.h2t[rows, :], r.gug[k]), nn(r.fgt[rows, :], r.inner[k])], axis=-1
        )

    for name, _ in GROUPS:
        buf = getattr(r, "cs_" + name)
        sent(buf, g_base[name] + 7)
        sent_or_kept(head_of(buf), 4, g_base[name] + 8)

    def reduce_core(name):
        base = g_base[name]
        cs, cr = getattr(r, "cs_" + name), getattr(r, "cr_" + name)
        for xx in (1 - x, x):
            for rel in (1 - zh, zh):
                q = 2 * rel + xx
                cs[q] = block(name, (1 - c + 2 * rel) * 2 + xx).astype(bf16)
                start(cs.at[q], cr.at[q], base + 7, base + q, device(z, x, y, 1 - c))

    def reduce_x(name, far):
        base = g_base[name]
        cr, xs, xr = (getattr(r, k + name) for k in ("cr_", "xs_", "xr_"))
        rel = zh ^ far
        q = 2 * rel + 1 - x
        part = block(name, (c + 2 * rel) * 2 + 1 - x)
        arrived(cr.at[q], base + q)
        xs[rel] = (part + cr[q].astype(f32)).astype(bf16)
        start(xs.at[rel], xr.at[rel], base + 8, base + 4 + rel, device(z, 1 - x, y, c))

    def reduce_z(name, far):
        base = g_base[name]
        cr, xr, zs, zr = (getattr(r, k + name) for k in ("cr_", "xr_", "zs_", "zr_"))
        rel = zh ^ far
        q = 2 * rel + x
        part = block(name, (c + 2 * rel) * 2 + x)
        arrived(cr.at[q], base + q)
        part = part + cr[q].astype(f32)
        arrived(xr.at[rel], base + 4 + rel)
        zs[far] = (part + xr[rel].astype(f32)).astype(bf16)
        args = (zs.at[far], zr.at[zh], base + 8, base + 6, device(c + 2 * rel, x, y, zl))
        if far == 0:
            start_unless(home, *args)
        else:
            start(*args)

    def reduce_end(name):
        zr = getattr(r, "zr_" + name)
        arrived(zr, g_base[name] + 6)
        return zr[0].astype(f32) + zr[1].astype(f32)

    def transpose(src, dst):
        def step(j):
            dst[at128(j * 128, 128), :] = src[:, at128(j * 128, 128)].T

        loop(9, step)

    lane128 = lax.broadcasted_iota(jnp.int32, (1, PAD), 1)
    head_lane = lane128 < 72
    quarter = lane128 // 18
    even = quarter % 2 == 0

    def swap(v):
        return jnp.where(even, pltpu.roll(v, PAD - 18, 1), pltpu.roll(v, 18, 1))

    def norm_of(v):
        inv = lax.rsqrt(jnp.mean(v * v, axis=-1, keepdims=True) + epsilon)
        return v * inv, inv

    def back(g, normed, inv):
        return inv * (g - normed * jnp.mean(g * normed, axis=-1, keepdims=True))

    barrier = pltpu.get_barrier_semaphore()
    for i in range(8):
        for j in range(4):
            if i or j:
                pl.semaphore_signal(
                    barrier, inc=1, device_id=((dp + i) % 8, mp ^ j), device_id_type=MESH
                )

    late = []
    for src, dst in (
        (r.wqkv, r.wqkv_in), (r.wgu, r.wgu_in), (r.wada, r.wada_in), (r.wdn, r.wdn_in)
    ):
        late.append(pltpu.make_async_copy(src, dst, sem.at[sems(1)]))
        late[-1].start()
    cond = r.cond[...].astype(f32)
    sig_c = jax.nn.sigmoid(cond)
    r.arow[0:1, 0:META] = (cond * sig_c).astype(bf16).astype(f32)
    meta = jnp.where(lane128 == 0, r.bin[0].astype(f32), 0.0)
    meta = jnp.where(lane128 == 1, r.grid[0, 0].astype(f32), meta)
    meta = jnp.where(lane128 == 2, r.grid[0, 1].astype(f32), meta)
    r.arow[0:1, META : META + 128] = meta
    r.arec[dp] = r.arow[...]

    dest = r.dest[...]
    lane512 = lax.broadcasted_iota(jnp.int32, (1, 512), 1)
    live = lane512 < r.count[0]
    target = dest >> 8
    within = dest & 255
    owner = lax.broadcasted_iota(jnp.int32, (8, 512), 0)
    member = jnp.where((owner == target) & live, 1.0, 0.0)
    upper = lax.broadcasted_iota(jnp.int32, (512, 512), 0) <= lax.broadcasted_iota(
        jnp.int32, (512, 512), 1
    )
    running = nn(member.astype(bf16), jnp.where(upper, 1.0, 0.0).astype(bf16))
    rank = jnp.sum(running * member, axis=0, keepdims=True).astype(jnp.int32) - 1
    spot = jnp.where(live, target * 64 + rank, -1)
    slots = lax.broadcasted_iota(jnp.int32, (512, 512), 0)
    r.place[...] = jnp.where(slots == spot, 1.0, 0.0).astype(bf16)
    r.xe[0:288, :] = r.xt[...]
    top_row = lax.broadcasted_iota(jnp.int32, (32, 512), 0) == 0
    r.xe[288:320, :] = jnp.where(top_row, within + 1, 0).astype(f32).astype(bf16)
    r.xe[320:352, :] = r.ct[256:288, :]
    r.xe[352:384, :] = jnp.zeros((32, 512), bf16)
    r.sx[...] = nt(r.place[...], r.xe[...]).astype(bf16)

    pl.semaphore_wait(barrier, 31)
    a_in = to_others(lambda i: r.arow, r.arec.at[dp], r.arec.at[pl.ds(0, 7)])
    x_in = to_workers(slots64(r.sx), slots64(r.rx), first64(r.rx))
    late[0].wait()
    late[1].wait()
    late[3].wait()
    for p in range(3):
        r.wp1[:, 288 * p : 288 * p + 288] = r.wqkv_in[p]
    r.wp1[:, 864:896] = r.woin[:, 0:32]
    r.wpb[...] = r.woin[:, 32:288]
    for k in range(3):
        r.wp[k, :, 0:256] = r.wgu_in[:, 0, 256 * k : 256 * k + 256]
        r.wp[k, :, 256:512] = r.wgu_in[:, 1, 256 * k : 256 * k + 256]
        r.wp[k, :, 512:768] = r.wdn_in[:, 256 * k : 256 * k + 256]
    r.sg[...] = nt(r.place[...], r.ct[0:256, :]).astype(bf16)

    arrived(r.arec.at[pl.ds(0, 7)], a_in)
    late[2].wait()
    for i in range(8):
        r.amat[i : i + 1, :] = r.arec[i]
    pick = lax.broadcasted_iota(jnp.int32, (1152, 144), 0) == (
        lax.broadcasted_iota(jnp.int32, (1152, 144), 1) + 144 * dp
    )
    silu_own = nn(r.amat[:, 0:META].astype(bf16), jnp.where(pick, 1.0, 0.0).astype(bf16)).astype(bf16)
    first = (dp == 0).astype(f32)
    for k in range(6):
        part = nn(silu_own, r.wada_in[k]) + first * r.bada[k : k + 1, :].astype(f32)
        for i in range(8):
            r.pms[i, k] = part[i : i + 1, :]
    m_in = to_workers(lambda i: r.pms.at[i], lambda i: r.pmr.at[i], head_of(r.pmr))
    gather_z("attn")
    gather_z("wo")

    about = r.arec[item]
    height = about[:, META + 1 : META + 2]
    width = about[:, META + 2 : META + 3]
    bins = r.amat[:, META : META + 1]
    alike = jnp.sum(
        jnp.where(bins == about[:, META : META + 1], 1.0, 0.0), axis=0, keepdims=True
    )
    weight = 8.0 / (NBINS * alike)
    spots = lax.broadcasted_iota(jnp.int32, (256, 1), 0).astype(f32)
    high = jnp.floor((spots + 0.5) / width)
    wide = spots - high * width
    freq = jnp.exp(-math.log(10000.0) * (lane128 - 18 * quarter).astype(f32) / 18.0)
    angle = jnp.where(quarter < 2, high, wide) * freq
    r.cosv[...] = jnp.where(head_lane, jnp.cos(angle), 0.0)
    r.sinv[...] = jnp.where(head_lane, jnp.where(even, -jnp.sin(angle), jnp.sin(angle)), 0.0)
    used = height * width
    key_ok = lax.broadcasted_iota(jnp.int32, (1, 256), 1).astype(f32) < used
    row_first = (tp * 64).astype(f32)
    share_spots = lax.broadcasted_iota(jnp.int32, (64, 1), 0).astype(f32) + row_first
    valid_share = jnp.where(share_spots < used, 1.0, 0.0)

    arrived(r.rx, x_in)
    number = r.rx[:, 288:289].astype(jnp.int32)
    r.spread[...] = jnp.where(
        number == lax.broadcasted_iota(jnp.int32, (512, 256), 1) + 1, 1.0, 0.0
    ).astype(bf16)
    r.rb[tp] = tn(r.spread[...], r.rx[...]).astype(bf16)
    rb_all = Gather(lambda t: r.rb.at[t], head_of(r.rb))

    gather_x("attn", 0)
    gather_x("attn", 1)
    arrived(r.pmr, m_in)
    total = r.pmr[0]
    for s in range(1, 8):
        total = total + r.pmr[s]
    r.mdb[tp] = total.astype(bf16).astype(f32)
    mdb_all = Gather(lambda t: r.mdb.at[t], head_of(r.mdb))
    rb_all.relay()
    mdb_all.relay()
    t_in = to_workers(slots64(r.sg), slots64(r.rg), first64(r.rg))
    gather_z("c0")
    gather_z("c1")
    gather_core("attn", 0)
    gather_core("attn", 1)

    gather_x("wo", 0)
    gather_x("wo", 1)
    rb_all.done()
    mdb_all.done()
    for k in range(6):
        for t in range(4):
            r.modf[k : k + 1, 288 * t : 288 * t + 288] = r.mdb[t, k]

    def joined(start):
        return jnp.concatenate(
            [r.rb[t, at16(start, 64), 0:288].astype(f32) for t in range(4)], axis=-1
        )

    def joined_grad(start):
        parts = []
        for t in range(4):
            parts.append(r.gb[t, at16(start, 64), :].astype(f32))
            parts.append(r.rb[t, at16(start, 64), 320:352].astype(f32))
        return jnp.concatenate(parts, axis=-1)

    def first_hidden(i):
        normed, _ = norm_of(joined(i * 64))
        shift, scale = r.modf[0:1, :], r.modf[1:2, :]
        r.h1[at16(i * 64, 64), :] = (normed * (1.0 + scale) + shift).astype(bf16)

    loop(4, first_hidden)
    RESID, NORM1, ATT, MID, NORM2, TOP, MIDG = range(7)
    mine = joined(tp * 64)
    normed, inv = norm_of(mine)
    r.share[RESID] = mine
    r.share[NORM1] = normed
    r.invs[0] = inv
    gather_done("attn")

    def project(j):
        r.qkv[:, at128(j * 256, 256)] = nn(r.h1[...], r.w1[:, at128(j * 256, 256)])

    loop(3, project)
    r.qkv[:, 768:896] = nn(r.h1[...], r.w1[:, 768:896])

    gather_x("c0", 0)
    gather_core("wo", 0)
    gather_core("wo", 1)
    scale_q = 72 ** (-0.5)
    pad = jnp.zeros((1, PAD - 72), f32)
    gains = {k: jnp.concatenate([g[...], pad], axis=-1) for k, g in (("q", r.qg), ("k", r.kg))}
    def turn_heads(h):
        for kind, offset, normed_ref, inv_ref, low_ref in (
            ("q", 0, r.qn, r.qi, r.ql),
            ("k", 288, r.kn, r.ki, r.kl),
        ):
            lane = offset + 72 * h
            v = jnp.where(head_lane, r.qkv[:, lane : lane + 128], 0.0)
            inv = lax.rsqrt(jnp.sum(v * v, axis=-1, keepdims=True) * (1.0 / 72) + epsilon)
            v = v * inv
            normed_ref[h] = v
            inv_ref[h] = inv
            v = v * gains[kind]
            v = v * r.cosv[...] + swap(v) * r.sinv[...]
            if kind == "q":
                v = v * scale_q
            low_ref[h] = v.astype(bf16)
        lane = 576 + 72 * h
        r.vl[h] = jnp.where(head_lane, r.qkv[:, lane : lane + 128], 0.0).astype(bf16)

    turn_heads(0)
    turn_heads(1)
    turn_heads(2)
    turn_heads(3)
    def attend(h):
        scores = jnp.where(key_ok, nt(r.ql[h], r.kl[h]), -1e30)
        scores = jnp.exp(scores - jnp.max(scores, axis=-1, keepdims=True))
        prob = scores / jnp.sum(scores, axis=-1, keepdims=True)
        r.pf[h] = prob
        low = nn(prob.astype(bf16), r.vl[h]).astype(bf16)
        if h == 0:
            r.al1[...] = low[:, 0:32]
            r.al2[:, 0:40] = low[:, 32:72]
        else:
            r.al2[:, 72 * h - 32 : 72 * h + 40] = low[:, 0:72]

    attend(0)
    attend(1)
    attend(2)
    attend(3)

    gather_done("wo")

    def project_out(j):
        rows = at128(j * 384, 384)
        part = nt(r.al2[...], r.wb[rows, :]) + nt(r.al1[...], r.w1[rows, 864:896])
        r.rsa[:, rows] = part.astype(bf16)

    loop(3, project_out)
    sum_a = Scatter("a")
    arrived(r.rg, t_in)
    r.gb[tp] = tn(r.spread[...], r.rg[...]).astype(bf16)
    gb_all = Gather(lambda t: r.gb.at[t], head_of(r.gb))
    sum_a.relay()

    gather_z("c2", (1,))
    gather_x("c0", 1)
    gather_core("c0", 0)
    gather_x("c1", 0)
    gb_all.relay()
    gather_x("c1", 1)
    attention = sum_a.total()
    r.share[ATT] = attention
    middle = r.share[RESID] + r.modf[2:3, :] * attention
    r.share[MID] = middle
    normed, inv = norm_of(middle)
    r.share[NORM2] = normed
    r.invs[1] = inv
    r.h2[at16(tp * 64, 64), :] = (normed * (1.0 + r.modf[4:5, :]) + r.modf[3:4, :]).astype(bf16)
    h2_all = Gather(rows_view(r.h2), first64(r.h2))
    gather_z("c2", (0,))
    gather_core("c0", 1)
    h2_all.relay()
    gather_x("c2", 0)
    gather_x("c2", 1)
    gather_core("c1", 0)
    gather_core("c1", 1)
    transpose(r.h1, r.h1t)
    chunks = (r.wc0, r.wc1, r.wc2)

    def swiglu(k):
        full = chunks[k]
        gate = nn(r.h2[...], full[:, 0:256])
        up = nn(r.h2[...], full[:, 256:512])
        grad = nn(r.fg[...], full[:, 512:768])
        sig = jax.nn.sigmoid(gate)
        act = gate * sig
        r.inner[k] = (act * up).astype(bf16)
        r.gug[k, :, 0:256] = (grad * up * sig * (1.0 + gate * (1.0 - sig))).astype(bf16)
        r.gug[k, :, 256:512] = (grad * act).astype(bf16)

    def hidden_back(k):
        full = chunks[k]

        def step(j):
            rows = at128(j * 384, 384)
            part = nt(r.gug[k], full[rows, 0:512])
            if k > 0:
                part = part + r.h2sum[:, rows]
            if k < 2:
                r.h2sum[:, rows] = part
            else:
                r.rsh2[:, rows] = part.astype(bf16)

        loop(3, step)

    gb_all.done()
    def feed_rows(i):
        rows = lax.broadcasted_iota(jnp.int32, (64, 1), 0).astype(f32) + (i * 64).astype(f32)
        factor = jnp.where(rows < used, weight, 0.0)
        r.fg[at16(i * 64, 64), :] = (joined_grad(i * 64) * factor * r.modf[5:6, :]).astype(bf16)

    loop(4, feed_rows)
    r.share[TOP] = joined_grad(tp * 64) * (weight * valid_share)
    transpose(r.fg, r.fgt)

    h2_all.done()
    gather_done("c0")
    swiglu(0)
    transpose(r.h2, r.h2t)
    reduce_core("c0")
    gather_core("c2", 0)
    gather_done("c1")
    swiglu(1)
    reduce_x("c0", 1)
    reduce_x("c0", 0)
    reduce_core("c1")
    gather_core("c2", 1)
    hidden_back(0)
    hidden_back(1)
    gather_done("c2")
    swiglu(2)
    hidden_back(2)
    sum_h2 = Scatter("h2")
    reduce_x("c1", 1)
    reduce_z("c0", 1)
    reduce_x("c1", 0)
    reduce_core("c2")
    reduce_x("c2", 1)
    reduce_x("c2", 0)
    sum_h2.relay()
    reduce_z("c0", 0)

    def feed_out(j):
        rows = at128(j * 384, 384)
        part = nt(r.inner[0], r.wc0[rows, 512:768])
        part = part + nt(r.inner[1], r.wc1[rows, 512:768])
        part = part + nt(r.inner[2], r.wc2[rows, 512:768])
        r.rsf[:, rows] = part.astype(bf16)

    loop(3, feed_out)
    sum_f = Scatter("f")
    grad_h2 = sum_h2.total()
    normed = r.share[NORM2]
    r.gpart[3:4, :] = jnp.sum(grad_h2, axis=0, keepdims=True)
    r.gpart[4:5, :] = jnp.sum(grad_h2 * normed, axis=0, keepdims=True)
    mid_grad = r.share[TOP] + back(grad_h2 * (1.0 + r.modf[4:5, :]), normed, r.invs[1])
    r.share[MIDG] = mid_grad
    r.gpart[2:3, :] = jnp.sum(mid_grad * r.share[ATT], axis=0, keepdims=True)
    r.ag[at16(tp * 64, 64), :] = (r.modf[2:3, :] * mid_grad).astype(bf16)
    ag_all = Gather(rows_view(r.ag), first64(r.ag))
    sum_f.relay()

    reduce_z("c1", 1)
    reduce_z("c1", 0)
    ag_all.relay()
    reduce_z("c2", 1)
    def total_of(v):
        return jnp.sum(jnp.sum(v, axis=0, keepdims=True), axis=1, keepdims=True)

    squares = []
    kept = []

    def result_part():
        feed = sum_f.total()
        fed = r.modf[5:6, :] * feed
        result = r.share[MID] + fed
        r.gpart[5:6, :] = jnp.sum(r.share[TOP] * feed, axis=0, keepdims=True)
        att = r.modf[2:3, :] * r.share[ATT]

        squares[:] = [total_of(valid_share * v * v) for v in (result, att, fed)]
        low_result = result.astype(bf16)
        for t in range(4):
            r.ras[t] = low_result[:, 288 * t : 288 * t + 256]
            r.ias[t, :, 320:352] = low_result[:, 288 * t + 256 : 288 * t + 288]
        r.rar[tp] = r.ras[tp]
        kept.append(mates_send(lambda t: r.ras.at[t], r.rar.at[tp], r.rar.at[pl.ds(0, 3)]))

    def rows_part():
        arrived(r.rar.at[pl.ds(0, 3)], kept[0])
        rar = jnp.concatenate([r.rar[t] for t in range(4)], axis=0)
        r.bs[...] = nn(r.spread[...], rar).astype(bf16)
        kept.append(to_homes(slots64(r.bs), slots64(r.br), first64(r.br)))


    ag_all.done()
    r.da[:, 0:32] = nn(r.ag[...], r.w1[:, 864:896])
    r.da[:, 32:288] = nn(r.ag[...], r.wb[...])
    result_part()
    transpose(r.ag, r.agt)

    reduce_core("out")
    sums = [jnp.zeros((1, PAD), f32), jnp.zeros((1, PAD), f32)]

    def attend_back(h):
        grad = jnp.where(head_lane, r.da[:, 72 * h : 72 * h + 128], 0.0).astype(bf16)
        prob = r.pf[h]
        prob_grad = nt(grad, r.vl[h])
        mixed = jnp.sum(prob * prob_grad, axis=-1, keepdims=True)
        score = (prob * (prob_grad - mixed)).astype(bf16)
        value_grad = tn(prob.astype(bf16), grad)
        r.dqkv[:, 576 + 72 * h : 648 + 72 * h] = value_grad[:, 0:72].astype(bf16)
        for kind, offset, normed_ref, inv_ref in (
            ("q", 0, r.qn, r.qi),
            ("k", 288, r.kn, r.ki),
        ):
            if kind == "q":
                turned = nn(score, r.kl[h]) * scale_q
            else:
                turned = tn(score, r.ql[h])
            turned = turned * r.cosv[...] - swap(turned) * r.sinv[...]
            normed = normed_ref[h]
            along = jnp.sum(turned * normed, axis=0, keepdims=True)
            if kind == "q":
                sums[0] = sums[0] + along
            else:
                sums[1] = sums[1] + along
            g = turned * gains[kind]
            mean = jnp.sum(g * normed, axis=-1, keepdims=True) * (1.0 / 72)
            g = inv_ref[h] * (g - normed * mean)
            r.dqkv[:, offset + 72 * h : offset + 72 * h + 72] = g[:, 0:72].astype(bf16)

    attend_back(0)
    reduce_x("out", 1)
    reduce_x("out", 0)
    attend_back(1)
    reduce_z("c2", 0)
    attend_back(2)
    rows_part()
    reduce_z("out", 1)
    attend_back(3)
    def first_back(j):
        r.rsh1[:, at128(j * 384, 384)] = nt(r.dqkv[...], r.w1[at128(j * 384, 384), 0:864]).astype(bf16)

    loop(3, first_back)
    sum_h1 = Scatter("h1")
    reduce_z("out", 0)
    reduce_core("qkv")
    reduce_x("qkv", 1)
    reduce_x("qkv", 0)
    sum_h1.relay()
    grad_h1 = sum_h1.total()
    normed = r.share[NORM1]
    r.gpart[0:1, :] = jnp.sum(grad_h1, axis=0, keepdims=True)
    r.gpart[1:2, :] = jnp.sum(grad_h1 * normed, axis=0, keepdims=True)
    in_grad = r.share[MIDG] + back(grad_h1 * (1.0 + r.modf[1:2, :]), normed, r.invs[0])
    low_grad = in_grad.astype(bf16)
    for t in range(4):
        r.ias[t, :, 0:288] = low_grad[:, 288 * t : 288 * t + 288]
    numbers = jnp.concatenate(
        [sums[0][:, 0:72], sums[1][:, 0:72], squares[0], squares[1], squares[2],
         total_of(valid_share), jnp.zeros((1, 288 - 148), f32)],
        axis=-1,
    )
    for t in range(4):
        for k in range(6):
            r.hs[t, k] = r.gpart[k : k + 1, 288 * t : 288 * t + 288]
        r.hs[t, 6] = numbers
    r.hr[tp] = r.hs[tp]
    h_in = mates_send(lambda t: r.hs.at[t], r.hr.at[tp], r.hr.at[pl.ds(0, 3)])
    r.iar[tp] = r.ias[tp]
    ia_in = mates_send(lambda t: r.ias.at[t], r.iar.at[tp], r.iar.at[pl.ds(0, 3)])

    arrived(r.hr.at[pl.ds(0, 3)], h_in)
    total = r.hr[0] + r.hr[1] + r.hr[2] + r.hr[3]
    for k in range(6):
        r.gs[k] = total[k].astype(bf16).astype(f32)
    r.gs[6] = total[6]
    g2_in = to_homes(lambda i: r.gs, lambda i: r.grec.at[i], head_of(r.grec))
    reduce_z("qkv", 1)
    arrived(r.iar.at[pl.ds(0, 3)], ia_in)
    iar = jnp.concatenate([r.iar[t] for t in range(4)], axis=0)
    r.bgs[...] = nn(r.spread[...], iar).astype(bf16)
    bg_in = to_homes(slots64(r.bgs), slots64(r.bgr), first64(r.bgr))
    reduce_z("qkv", 0)
    arrived(r.grec, g2_in)
    cond_part = jnp.zeros((8, 144), f32)
    for k in range(6):
        grads = jnp.concatenate([r.grec[i, k] for i in range(8)], axis=0)
        low = grads.astype(bf16)
        r.gada[k] = tn(silu_own, low)
        r.gbada[k : k + 1, :] = jnp.sum(grads, axis=0, keepdims=True)
        cond_part = cond_part + nt(low, r.wada_in[k])
    totals = r.grec[0, 6]
    for i in range(1, 8):
        totals = totals + r.grec[i, 6]
    r.gqg[...] = totals[:, 0:72]
    r.gkg[...] = totals[:, 72:144]
    ratio = totals[:, 144:147] / (totals[:, 147:148] * 1152.0)
    r.stats[...] = jnp.sqrt(ratio)
    r.cps[...] = cond_part
    c_in = sems(2)
    r.cpr[mp] = cond_part
    for step in range(1, 4):
        start(r.cps, r.cpr.at[mp], c_in, c_in + 1, (dp, mp ^ step))
    sent(r.cpr.at[pl.ds(0, 3)], c_in)
    arrived(r.cpr.at[pl.ds(0, 3)], c_in + 1)
    cond_sum = r.cpr[0] + r.cpr[1] + r.cpr[2] + r.cpr[3]
    for i in range(8):
        r.cts[i] = cond_sum[i : i + 1, :]
    r.ctr[dp] = r.cts[dp]
    ct_in = to_others(lambda i: r.cts.at[i], r.ctr.at[dp], r.ctr.at[pl.ds(0, 7)])

    for k in range(3):
        grad = reduce_end(f"c{k}")
        lanes = slice(256 * k, 256 * k + 256)
        r.ggu[:, 0, lanes] = grad[:, 0:256]
        r.ggu[:, 1, lanes] = grad[:, 256:512]
        r.gdn[:, lanes] = grad[:, 512:768]
    arrived(r.br, kept[1])
    r.outt[0:256, :] = tn(r.br[...], r.place[...]).astype(bf16)
    grad = reduce_end("qkv")
    for p in range(3):
        r.gqkv[p] = grad[:, 288 * p : 288 * p + 288]
    r.gout[:, 0:32] = grad[:, 864:896]
    r.gout[:, 32:288] = reduce_end("out")
    arrived(r.bgr, bg_in)
    both = tn(r.bgr[...], r.place[...]).astype(bf16)
    r.gint[...] = both[0:288, :]
    r.outt[256:288, :] = both[320:352, :]
    arrived(r.ctr.at[pl.ds(0, 7)], ct_in)
    for s in range(8):
        r.gcond[0:1, 144 * s : 144 * s + 144] = r.ctr[s]
    cond = r.cond[...].astype(f32)
    sig_c = jax.nn.sigmoid(cond)
    r.gcond[...] = r.gcond[...] * sig_c * (1.0 + cond * (1.0 - sig_c))
    for finish in pending:
        finish()
    assert taken[0] == 130


def copy_out(*refs):
    count = len(refs) // 2
    sem = refs[-1]
    copies = [pltpu.make_async_copy(refs[i], refs[count + i], sem.at[i]) for i in range(count)]
    for copy in copies:
        copy.start()
    for copy in copies:
        copy.wait()


def body_kernel(
    x_src, cotangent, route_dest, route_count, item_grid, noise_bin, cond, w_ada, b_ada,
    w_qkv, q_gain, k_gain, w_out, w_gu, w_down,
):
    scratch = scratch_list()
    vmem = pl.BlockSpec(memory_space=pltpu.VMEM)
    smem = pl.BlockSpec(memory_space=pltpu.SMEM)
    far = pl.BlockSpec(memory_space=pl.ANY)
    shapes = [
        ((288, 512), bf16), ((288, 512), bf16), ((1, 1152), f32), ((6, 144, 288), f32),
        ((6, 288), f32), ((3, 144, 288), f32), ((1, 72), f32), ((1, 72), f32),
        ((144, 288), f32), ((144, 2, 768), f32), ((144, 768), f32), ((1, 3), f32),
    ]
    outs = pl.pallas_call(
        functools.partial(block_kernel, list(scratch)),
        out_shape=[pltpu.VMEM(s, d) for s, d in shapes],
        in_specs=[vmem, vmem, vmem, smem, smem, smem, vmem, far, vmem, far, vmem, vmem, vmem, far, far],
        out_specs=[vmem] * len(shapes),
        scratch_shapes=list(scratch.values()),
        compiler_params=pltpu.CompilerParams(
            has_side_effects=True, vmem_limit_bytes=57500000, collective_id=0
        ),
        name="block",
    )(
        x_src.T, cotangent.T, route_dest.reshape(1, SRC_CAP), route_count, item_grid, noise_bin,
        cond, jnp.transpose(w_ada, (1, 0, 2)), b_ada, jnp.transpose(w_qkv, (1, 0, 2)),
        q_gain.reshape(1, DH), k_gain.reshape(1, DH), w_out.T, w_gu, w_down.T,
    )
    outs = pl.pallas_call(
        copy_out,
        out_shape=[jax.ShapeDtypeStruct(s, d) for s, d in shapes],
        in_specs=[vmem] * len(shapes),
        out_specs=[pl.BlockSpec(memory_space=pl.ANY)] * len(shapes),
        scratch_shapes=[pltpu.SemaphoreType.DMA((len(shapes),))],
        compiler_params=pltpu.CompilerParams(vmem_limit_bytes=2000000),
        name="store",
    )(*outs)
    (outt, gint, gcond, gada, gbada, gqkv, gqg, gkg, gout, ggu, gdn, stats) = outs
    return (
        outt.T, gint.T, gcond, jnp.transpose(gada, (1, 0, 2)), gbada,
        jnp.transpose(gqkv, (1, 0, 2)), gqg.reshape(DH), gkg.reshape(DH), gout.T, ggu, gdn.T,
        stats.reshape(3),
    )


def solution(mesh):
    one_kernel = mesh.shape["dp"] == 8 and mesh.shape["mp"] == 4
    return jax.shard_map(
        body_kernel if one_kernel else body,
        mesh=mesh,
        in_specs=(
            P("dp", "mp"),
            P("dp", "mp"),
            P("dp"),
            P("dp"),
            P("dp", None),
            P("dp"),
            P("dp", None),
            P("dp", None, "mp"),
            P(None, "mp"),
            P("dp", None, "mp"),
            P(),
            P(),
            P("mp", "dp"),
            P("dp", None, "mp"),
            P("mp", "dp"),
        ),
        out_specs=(
            P("dp", "mp"),
            P("dp", "mp"),
            P("dp", None),
            P("dp", None, "mp"),
            P(None, "mp"),
            P("dp", None, "mp"),
            P(),
            P(),
            P("mp", "dp"),
            P("dp", None, "mp"),
            P("mp", "dp"),
            P(),
        ),
        check_vma=False,
    )
```

```python
import functools
import math

import jax
import jax.numpy as jnp
from jax import lax
from jax.experimental import pallas as pl
from jax.experimental.pallas import tpu as pltpu
from jax.sharding import PartitionSpec as P

D = 1152
DH = 72
NBINS = 16
BLOCK = 256
ROWS_DEV = 256
SRC_CAP = 512


epsilon = 1e-06


def grad_share(part, dim):
    sent = part.astype(jnp.bfloat16)
    total = lax.psum_scatter(sent, "dp", scatter_dimension=dim, tiled=True)
    return total.astype(jnp.float32)


def norm_rows(values):
    scale = lax.rsqrt(jnp.mean(values * values, axis=-1, keepdims=True) + epsilon)
    return (values * scale, scale)


def norm_back(grad_normed, normed, scale):
    return scale * (grad_normed - normed * jnp.mean(grad_normed * normed, axis=-1, keepdims=True))


def rotate(values, cos_h, sin_h, cos_w, sin_w, sign):
    quarter = values.shape[-1] // 4
    first = values[..., :quarter]
    second = values[..., quarter : 2 * quarter]
    third = values[..., 2 * quarter : 3 * quarter]
    fourth = values[..., 3 * quarter :]
    return jnp.concatenate(
        [
            first * cos_h - sign * second * sin_h,
            sign * first * sin_h + second * cos_h,
            third * cos_w - sign * fourth * sin_w,
            sign * third * sin_w + fourth * cos_w,
        ],
        axis=-1,
    )


def angle_tables(grid, block, head_dim):
    quarter = head_dim // 4
    place = lax.broadcasted_iota(jnp.int32, (grid.shape[0], block), 1)
    width = grid[:, 1:2]
    height_pos = (place // width).astype(jnp.float32)
    width_pos = (place % width).astype(jnp.float32)
    freqs = jnp.exp(-math.log(10000.0) * jnp.arange(quarter).astype(jnp.float32) / quarter)
    angle_h = (height_pos[:, :, None] * freqs)[:, :, None, :]
    angle_w = (width_pos[:, :, None] * freqs)[:, :, None, :]
    return (jnp.cos(angle_h), jnp.sin(angle_h), jnp.cos(angle_w), jnp.sin(angle_w))


def row_share(values):
    return lax.psum_scatter(values, "mp", scatter_dimension=0, tiled=True)


def row_whole(values):
    return lax.all_gather(values, "mp", axis=0, tiled=True)


def body(
    x_src,
    cotangent,
    route_dest,
    route_count,
    item_grid,
    noise_bin,
    cond,
    w_ada,
    b_ada,
    w_qkv,
    q_gain,
    k_gain,
    w_out,
    w_gu,
    w_down,
):
    peers = lax.axis_size("dp")
    model_rank = lax.axis_index("mp")
    blocks_here = item_grid.shape[0]
    local_width = x_src.shape[1]
    heads_here = local_width // DH
    slot_rows = 2 * ROWS_DEV // peers
    share = ROWS_DEV // lax.axis_size("mp")
    row_first = model_rank * share
    live = jnp.arange(SRC_CAP) < route_count[0]
    target = route_dest // ROWS_DEV
    member = (target[:, None] == jnp.arange(peers)[None, :]) & live[:, None]
    running = jnp.cumsum(member.astype(jnp.int32), axis=0)
    rank_in = jnp.sum(running * member, axis=1) - 1
    place = jnp.where(live, target * slot_rows + rank_in, peers * slot_rows)
    send_rows = (
        jnp.zeros((peers * slot_rows, local_width), jnp.bfloat16).at[place].set(x_src, mode="drop")
    )
    send_grads = (
        jnp.zeros((peers * slot_rows, local_width), jnp.bfloat16)
        .at[place]
        .set(cotangent, mode="drop")
    )
    send_index = (
        jnp.full((peers * slot_rows,), ROWS_DEV, jnp.int32)
        .at[place]
        .set(route_dest % ROWS_DEV, mode="drop")
    )
    recv_rows, recv_grads, recv_index = (
        lax.all_to_all(
            send_rows.reshape(peers, slot_rows, local_width),
            "dp",
            split_axis=0,
            concat_axis=0,
            tiled=True,
        ),
        lax.all_to_all(
            send_grads.reshape(peers, slot_rows, local_width),
            "dp",
            split_axis=0,
            concat_axis=0,
            tiled=True,
        ),
        lax.all_to_all(
            send_index.reshape(peers, slot_rows), "dp", split_axis=0, concat_axis=0, tiled=True
        ),
    )
    flat_index = recv_index.reshape(-1)
    rows_cols = (
        jnp.zeros((ROWS_DEV, local_width), jnp.bfloat16)
        .at[flat_index]
        .set(recv_rows.reshape(-1, local_width), mode="drop")
    )
    grads_cols = (
        jnp.zeros((ROWS_DEV, local_width), jnp.bfloat16)
        .at[flat_index]
        .set(recv_grads.reshape(-1, local_width), mode="drop")
    )
    qkv_full, out_full, gu_full, down_full = (
        lax.all_gather(w_qkv, "dp", axis=0, tiled=True),
        lax.all_gather(w_out, "dp", axis=1, tiled=True),
        lax.all_gather(w_gu, "dp", axis=0, tiled=True),
        lax.all_gather(w_down, "dp", axis=1, tiled=True),
    )
    cond_wide = cond.astype(jnp.float32)
    cond_sig = jax.nn.sigmoid(cond_wide)
    silu_cond = (cond_wide * cond_sig).astype(jnp.bfloat16)
    ada_rows = w_ada.shape[0]
    silu_all = lax.all_gather(silu_cond, "dp", axis=0, tiled=True)
    silu_own = lax.dynamic_slice_in_dim(silu_all, lax.axis_index("dp") * ada_rows, ada_rows, 1)
    mod_sums = jnp.einsum("id,dkc->ikc", silu_own, w_ada, preferred_element_type=jnp.float32)
    mod_part = (
        lax.psum_scatter(mod_sums, "dp", scatter_dimension=0, tiled=True)
        + b_ada.astype(jnp.float32)
    ).astype(jnp.bfloat16)
    rows_full, grads_full, mod_full = (
        lax.all_gather(rows_cols, "mp", axis=1, tiled=True),
        lax.all_gather(grads_cols, "mp", axis=1, tiled=True),
        lax.all_gather(mod_part, "mp", axis=2, tiled=True),
    )
    modulation = mod_full.astype(jnp.float32)
    shift_one = modulation[:, 0][:, None, :]
    scale_one = modulation[:, 1][:, None, :]
    gate_two = modulation[:, 5][:, None, :]
    resid = rows_full.astype(jnp.float32).reshape(blocks_here, BLOCK, D)
    normed_one, inv_one = norm_rows(resid)
    hidden_one = (normed_one * (1.0 + scale_one) + shift_one).astype(jnp.bfloat16)
    qkv = jnp.einsum("ibd,dkc->ibkc", hidden_one, qkv_full, preferred_element_type=jnp.float32)
    query = qkv[:, :, 0].reshape(blocks_here, BLOCK, heads_here, DH)
    keys = qkv[:, :, 1].reshape(blocks_here, BLOCK, heads_here, DH)
    value = qkv[:, :, 2].reshape(blocks_here, BLOCK, heads_here, DH)
    query_normed, query_inv = norm_rows(query)
    key_normed, key_inv = norm_rows(keys)
    cos_h, sin_h, cos_w, sin_w = angle_tables(item_grid, BLOCK, DH)
    query_low = (
        rotate(query_normed * q_gain, cos_h, sin_h, cos_w, sin_w, 1.0) * DH ** (-0.5)
    ).astype(jnp.bfloat16)
    key_low = rotate(key_normed * k_gain, cos_h, sin_h, cos_w, sin_w, 1.0).astype(jnp.bfloat16)
    value_low = value.astype(jnp.bfloat16)
    positions = lax.broadcasted_iota(jnp.int32, (blocks_here, BLOCK), 1)
    valid = positions < (item_grid[:, 0] * item_grid[:, 1])[:, None]
    key_ok = valid[:, None, None, :]
    valid_wide = valid.astype(jnp.float32)[:, :, None]
    valid_share = lax.dynamic_slice_in_dim(
        valid.astype(jnp.float32).reshape(ROWS_DEV), row_first, share, 0
    )[:, None]
    bin_onehot = (noise_bin[:, None] == jnp.arange(NBINS)[None, :]).astype(jnp.float32)
    bin_local = jnp.sum(bin_onehot, axis=0) * (model_rank == 0).astype(jnp.float32)

    def masked_scores():
        raw = jnp.einsum("iqhc,ikhc->ihqk", query_low, key_low, preferred_element_type=jnp.float32)
        return jnp.where(key_ok, raw, -1e30)

    scores = masked_scores()
    top = jnp.max(scores, axis=-1, keepdims=True)
    log_total = top + jnp.log(jnp.sum(jnp.exp(scores - top), axis=-1, keepdims=True))
    prob_low = jnp.exp(scores - log_total).astype(jnp.bfloat16)
    attn_low = jnp.einsum(
        "ihqk,ikhc->iqhc", prob_low, value_low, preferred_element_type=jnp.float32
    ).astype(jnp.bfloat16)
    out_heads = out_full.reshape(heads_here, DH, D)
    attn_part = jnp.einsum("iqhc,hcd->iqd", attn_low, out_heads, preferred_element_type=jnp.float32)

    def own_rows_of(values):
        return lax.dynamic_slice_in_dim(values.reshape(ROWS_DEV, D), row_first, share, 0)

    row_item = (row_first + jnp.arange(share)) // BLOCK
    item_onehot = (row_item[:, None] == jnp.arange(blocks_here)[None, :]).astype(jnp.float32)

    def per_item(values):
        return jnp.einsum("si,sd->id", item_onehot, values, precision=lax.Precision.HIGHEST)

    mod_rows = jnp.einsum("si,ikd->skd", item_onehot, modulation, precision=lax.Precision.HIGHEST)
    scale_one_r = mod_rows[:, 1]
    gate_one_r = mod_rows[:, 2]
    shift_two_r = mod_rows[:, 3]
    scale_two_r = mod_rows[:, 4]
    gate_two_r = mod_rows[:, 5]
    resid_share = own_rows_of(resid)
    normed_one_share = own_rows_of(normed_one)
    inv_one_share = lax.dynamic_slice_in_dim(inv_one.reshape(ROWS_DEV, 1), row_first, share, 0)
    attention_share = row_share(attn_part.reshape(ROWS_DEV, D))
    mid_share = resid_share + gate_one_r * attention_share
    normed_two_share, inv_two_share = norm_rows(mid_share)
    hidden_two_share = (normed_two_share * (1.0 + scale_two_r) + shift_two_r).astype(jnp.bfloat16)
    hidden_two = row_whole(hidden_two_share).reshape(blocks_here, BLOCK, D)
    gate_up = jnp.einsum("ibd,dkf->ibkf", hidden_two, gu_full, preferred_element_type=jnp.float32)
    gate_raw = gate_up[:, :, 0]
    up_raw = gate_up[:, :, 1]
    gate_sig = jax.nn.sigmoid(gate_raw)
    gate_act = gate_raw * gate_sig
    inner = (gate_act * up_raw).astype(jnp.bfloat16)
    feed_part = jnp.einsum("ibf,fd->ibd", inner, down_full, preferred_element_type=jnp.float32)
    feed_part, kept = (feed_part, (inner, up_raw, gate_raw, gate_sig, gate_act))
    feed_share = row_share(feed_part.reshape(ROWS_DEV, D))
    result_share = mid_share + gate_two_r * feed_share
    result_whole = row_whole(result_share.astype(jnp.bfloat16))
    squares = jnp.stack(
        [
            jnp.sum(valid_share * result_share * result_share),
            jnp.sum(valid_share * (gate_one_r * attention_share) ** 2),
            jnp.sum(valid_share * (gate_two_r * feed_share) ** 2),
        ]
    )
    square_total, valid_total, bin_total = lax.psum(
        (squares, jnp.sum(valid_share), bin_local), ("dp", "mp")
    )
    stats_value = jnp.sqrt(square_total / (valid_total * D))
    item_count = jnp.sum(bin_onehot * bin_total[None, :], axis=1)
    weight_value = blocks_here * peers / (NBINS * item_count)
    top_grad = grads_full.astype(jnp.float32).reshape(blocks_here, BLOCK, D) * (
        weight_value[:, None, None] * valid_wide
    )
    top_share = own_rows_of(top_grad)
    feed_grad = (gate_two * top_grad).astype(jnp.bfloat16)
    grad_gate_two = per_item(top_share * feed_share)
    inner, up_raw, gate_raw, gate_sig, gate_act = kept
    inner_grad = jnp.einsum("ibd,fd->ibf", feed_grad, down_full, preferred_element_type=jnp.float32)
    grad_down_part = jnp.einsum("ibf,ibd->fd", inner, feed_grad, preferred_element_type=jnp.float32)
    gate_grad = (inner_grad * up_raw * gate_sig * (1.0 + gate_raw * (1.0 - gate_sig))).astype(
        jnp.bfloat16
    )
    up_grad = (inner_grad * gate_act).astype(jnp.bfloat16)
    gate_up_grad = jnp.stack([gate_grad, up_grad], axis=2)
    grad_gu_part = jnp.einsum(
        "ibd,ibkf->dkf", hidden_two, gate_up_grad, preferred_element_type=jnp.float32
    )
    hidden_two_part = jnp.einsum(
        "ibkf,dkf->ibd", gate_up_grad, gu_full, preferred_element_type=jnp.float32
    )
    grad_down, grad_gu, hidden_two_part = (grad_down_part, grad_gu_part, hidden_two_part)
    h2_grad_share = row_share(hidden_two_part.reshape(ROWS_DEV, D))
    grad_shift_two = per_item(h2_grad_share)
    grad_scale_two = per_item(h2_grad_share * normed_two_share)
    mid_grad_share = top_share + norm_back(
        h2_grad_share * (1.0 + scale_two_r), normed_two_share, inv_two_share
    )
    attention_grad_share = (gate_one_r * mid_grad_share).astype(jnp.bfloat16)
    grad_gate_one = per_item(mid_grad_share * attention_share)
    attention_grad = row_whole(attention_grad_share).reshape(blocks_here, BLOCK, D)
    attn_low_grad = jnp.einsum(
        "iqd,hcd->iqhc", attention_grad, out_heads, preferred_element_type=jnp.float32
    ).astype(jnp.bfloat16)
    grad_out_part = jnp.einsum(
        "iqhc,iqd->hcd", attn_low, attention_grad, preferred_element_type=jnp.float32
    ).reshape(local_width, D)
    prob_full = jnp.exp(masked_scores() - log_total)
    prob_grad = jnp.einsum(
        "iqhc,ikhc->ihqk", attn_low_grad, value_low, preferred_element_type=jnp.float32
    )
    value_grad = jnp.einsum(
        "ihqk,iqhc->ikhc", prob_low, attn_low_grad, preferred_element_type=jnp.float32
    )
    score_grad = (
        prob_full * (prob_grad - jnp.sum(prob_full * prob_grad, axis=-1, keepdims=True))
    ).astype(jnp.bfloat16)
    query_rot_grad = jnp.einsum(
        "ihqk,ikhc->iqhc", score_grad, key_low, preferred_element_type=jnp.float32
    ) * DH ** (-0.5)
    key_rot_grad = jnp.einsum(
        "ihqk,iqhc->ikhc", score_grad, query_low, preferred_element_type=jnp.float32
    )
    query_scaled_grad = rotate(query_rot_grad, cos_h, sin_h, cos_w, sin_w, -1.0)
    key_scaled_grad = rotate(key_rot_grad, cos_h, sin_h, cos_w, sin_w, -1.0)
    qgain_local = jnp.sum(query_scaled_grad * query_normed, axis=(0, 1, 2))
    kgain_local = jnp.sum(key_scaled_grad * key_normed, axis=(0, 1, 2))
    query_grad = norm_back(query_scaled_grad * q_gain, query_normed, query_inv)
    key_grad = norm_back(key_scaled_grad * k_gain, key_normed, key_inv)
    qkv_grad = jnp.stack(
        [
            query_grad.reshape(blocks_here, BLOCK, local_width),
            key_grad.reshape(blocks_here, BLOCK, local_width),
            value_grad.reshape(blocks_here, BLOCK, local_width),
        ],
        axis=2,
    ).astype(jnp.bfloat16)
    grad_qkv_part = jnp.einsum(
        "ibd,ibkc->dkc", hidden_one, qkv_grad, preferred_element_type=jnp.float32
    )
    hidden_one_part = jnp.einsum(
        "ibkc,dkc->ibd", qkv_grad, qkv_full, preferred_element_type=jnp.float32
    )
    grad_out, grad_qkv, qgain_part, kgain_part, hidden_one_part = (
        grad_out_part,
        grad_qkv_part,
        qgain_local,
        kgain_local,
        hidden_one_part,
    )
    h1_grad_share = row_share(hidden_one_part.reshape(ROWS_DEV, D))
    grad_shift_one = per_item(h1_grad_share)
    grad_scale_one = per_item(h1_grad_share * normed_one_share)
    input_share = mid_grad_share + norm_back(
        h1_grad_share * (1.0 + scale_one_r), normed_one_share, inv_one_share
    )
    input_whole = row_whole(input_share.astype(jnp.bfloat16))
    mod_partial = jnp.stack(
        [
            grad_shift_one,
            grad_scale_one,
            grad_gate_one,
            grad_shift_two,
            grad_scale_two,
            grad_gate_two,
        ],
        axis=1,
    )
    mod_grad = lax.psum(mod_partial, "mp").astype(jnp.bfloat16)
    mod_grad_own = lax.dynamic_slice_in_dim(mod_grad, model_rank * local_width, local_width, 2)
    mod_all = lax.all_gather(mod_grad_own, "dp", axis=0, tiled=True)
    cond_part = jnp.einsum("ikc,dkc->id", mod_all, w_ada, preferred_element_type=jnp.float32)
    cond_sum = lax.psum(cond_part, "mp")
    cond_total = lax.all_to_all(
        cond_sum.reshape(peers, blocks_here, ada_rows), "dp", split_axis=0, concat_axis=0, tiled=True
    )
    cond_total = jnp.moveaxis(cond_total, 0, 1).reshape(blocks_here, peers * ada_rows)
    grad_cond = cond_total * cond_sig * (1.0 + cond_wide * (1.0 - cond_sig))
    grad_ada = jnp.einsum("ir,ikc->rkc", silu_own, mod_all, preferred_element_type=jnp.float32)
    grad_bada = jnp.sum(mod_all.astype(jnp.float32), axis=0)
    qgain_total, kgain_total = lax.psum((qgain_part, kgain_part), ("dp", "mp"))
    qkv_own, out_own, gu_own, down_own = (
        grad_share(grad_qkv, 0),
        grad_share(grad_out, 1),
        grad_share(grad_gu, 0),
        grad_share(grad_down, 1),
    )
    result_cols = lax.dynamic_slice_in_dim(result_whole, model_rank * local_width, local_width, 1)
    input_cols = lax.dynamic_slice_in_dim(input_whole, model_rank * local_width, local_width, 1)
    back_index = jnp.minimum(flat_index, ROWS_DEV - 1)
    back_rows = result_cols[back_index].reshape(peers, slot_rows, local_width)
    back_grads = input_cols[back_index].reshape(peers, slot_rows, local_width)
    returned_rows, returned_grads = (
        lax.all_to_all(back_rows, "dp", split_axis=0, concat_axis=0, tiled=True),
        lax.all_to_all(back_grads, "dp", split_axis=0, concat_axis=0, tiled=True),
    )
    pick = jnp.minimum(place, peers * slot_rows - 1)
    empty = jnp.zeros((), jnp.bfloat16)
    out_rows = jnp.where(live[:, None], returned_rows.reshape(-1, local_width)[pick], empty)
    out_grads = jnp.where(live[:, None], returned_grads.reshape(-1, local_width)[pick], empty)
    return (
        out_rows,
        out_grads,
        grad_cond,
        grad_ada,
        grad_bada,
        qkv_own,
        qgain_total,
        kgain_total,
        out_own,
        gu_own,
        down_own,
        stats_value,
    )


MESH = pl.DeviceIdType.MESH
f32 = jnp.float32
bf16 = jnp.bfloat16
LANE_INDEX = 288
META = 1152
PAD = 128


def nn(left, right):
    return jnp.dot(left, right, preferred_element_type=f32)


def nt(left, right):
    return lax.dot_general(left, right, (((1,), (1,)), ((), ())), preferred_element_type=f32)


def tn(left, right):
    return lax.dot_general(left, right, (((0,), (0,)), ((), ())), preferred_element_type=f32)


def loop(count, step):
    def run(index, carry):
        step(index)
        return carry

    lax.fori_loop(0, count, run, 0)


def at128(index, size):
    return pl.ds(pl.multiple_of(index, 128), size)


def at16(index, size):
    return pl.ds(pl.multiple_of(index, 16), size)


GROUPS = (("c0", 768), ("c1", 768), ("c2", 768), ("out", 256), ("qkv", 896))


def scratch_list():
    vm = pltpu.VMEM
    items = dict(
        sem=pltpu.SemaphoreType.DMA((132,)),
        arow=vm((1, 1280), f32),
        arec=vm((8, 1, 1280), f32),
        amat=vm((8, 1280), f32),
        xe=vm((64, 512), bf16),
        ids=vm((8, 1, 64), f32),
        idr=vm((8, 1, 64), f32),
        place=vm((512, 512), bf16),
        sx=vm((640, 256), bf16),
        rx=vm((640, 256), bf16),
        sg=vm((512, 256), bf16),
        rg=vm((512, 256), bf16),
        spread=vm((256, 512), bf16),
        rb=vm((4, 320, 256), bf16),
        gb=vm((4, 256, 256), bf16),
        pms=vm((8, 6, 1, 288), f32),
        pmr=vm((8, 6, 1, 288), f32),
        mdb=vm((4, 6, 1, 288), f32),
        modf=vm((8, 1152), f32),
        h1=vm((256, 1152), bf16),
        h1t=vm((1152, 256), bf16),
        w1=vm((1152, 896), bf16),
        wc0=vm((1152, 768), bf16),
        wc1=vm((1152, 768), bf16),
        wc2=vm((1152, 768), bf16),
        wp1=vm((144, 896), bf16),
        wqkv_in=vm((3, 144, 288), bf16),
        wgu_in=vm((144, 2, 768), bf16),
        wada_in=vm((6, 144, 288), bf16),
        wdn_in=vm((144, 768), bf16),
        wp=vm((3, 144, 768), bf16),
        wb=vm((1152, 256), bf16),
        wpb=vm((144, 256), bf16),
        qkv=vm((256, 1024), f32),
        qn=vm((4, 256, 128), f32),
        kn=vm((4, 256, 128), f32),
        qi=vm((4, 256, 1), f32),
        ki=vm((4, 256, 1), f32),
        ql=vm((4, 256, 128), bf16),
        kl=vm((4, 256, 128), bf16),
        vl=vm((4, 256, 128), bf16),
        pf=vm((4, 256, 256), f32),
        cosv=vm((256, 128), f32),
        sinv=vm((256, 128), f32),
        al1=vm((256, 32), bf16),
        al2=vm((256, 256), bf16),
        rsa=vm((256, 1152), bf16),
        rra=vm((3, 64, 1152), bf16),
        rta=vm((64, 1152), bf16),
        rsf=vm((256, 1152), bf16),
        rrf=vm((3, 64, 1152), bf16),
        rtf=vm((64, 1152), bf16),
        rsh2=vm((256, 1152), bf16),
        rrh2=vm((3, 64, 1152), bf16),
        rth2=vm((64, 1152), bf16),
        rsh1=vm((256, 1152), bf16),
        rrh1=vm((3, 64, 1152), bf16),
        rth1=vm((64, 1152), bf16),
        h2=vm((256, 1152), bf16),
        h2t=vm((1152, 256), bf16),
        ag=vm((256, 1152), bf16),
        agt=vm((1152, 256), bf16),
        h2sum=vm((256, 1152), f32),
        inner=vm((3, 256, 256), bf16),
        gug=vm((3, 256, 512), bf16),
        fg=vm((256, 1152), bf16),
        fgt=vm((1152, 256), bf16),
        da=vm((256, 384), f32),
        dqkv=vm((256, 864), bf16),
        share=vm((8, 64, 1152), f32),
        invs=vm((2, 64, 1), f32),
        gpart=vm((8, 1152), f32),
        ras=vm((4, 64, 256), bf16),
        rar=vm((4, 64, 256), bf16),
        ias=vm((4, 64, 384), bf16),
        iar=vm((4, 64, 384), bf16),
        bs=vm((512, 256), bf16),
        br=vm((512, 256), bf16),
        bgs=vm((640, 256), bf16),
        bgr=vm((640, 256), bf16),
        hs=vm((4, 7, 1, 288), f32),
        hr=vm((4, 7, 1, 288), f32),
        gs=vm((7, 1, 288), f32),
        grec=vm((8, 7, 1, 288), f32),
        ms=vm((8, 6, 288), f32),
        cps=vm((8, 144), f32),
        cpr=vm((4, 8, 144), f32),
        cts=vm((8, 1, 144), f32),
        ctr=vm((8, 1, 144), f32),
    )
    for name, width in GROUPS:
        items["cs_" + name] = vm((4, 144, width), bf16)
        items["cr_" + name] = vm((4, 144, width), bf16)
        items["xs_" + name] = vm((2, 144, width), bf16)
        items["xr_" + name] = vm((2, 144, width), bf16)
        items["zs_" + name] = vm((2, 144, width), bf16)
        items["zr_" + name] = vm((2, 144, width), bf16)
    return items


class Refs:
    pass


def block_kernel(
    names, xt, ct, dest, count, grid, bin, cond, wada, bada, wqkv, qg, kg, woin, wgu, wdn, outt, gint, gcond, gada, gbada, gqkv, gqg, gkg, gout, ggu, gdn, stats, *scratch
):
    r = Refs()
    r.__dict__.update(locals())
    for name, ref in zip(names, scratch):
        setattr(r, name, ref)
    dp = lax.axis_index("dp")
    mp = lax.axis_index("mp")
    z, x, y, c = dp // 2, dp % 2, mp // 2, mp % 2
    zh, zl = z // 2, z % 2
    item = (2 * zh + c) * 2 + x
    tp = y * 2 + zl
    home = zl == c
    away = zl != c
    sem = r.sem
    taken = [0]

    def sems(count):
        first = taken[0]
        taken[0] += count
        return first

    def device(zz, xx, yy, cc):
        return (zz * 2 + xx, yy * 2 + cc)

    def worker(index, part):
        zi, xi = index // 2, index % 2
        return device(2 * (zi // 2) + part % 2, xi, part // 2, zi % 2)

    def mate(step):
        return device(2 * zh + (zl ^ (step & 1)), x, y ^ (step >> 1), c)

    def remote(src, dst, ss, rs, dev):
        return pltpu.make_async_remote_copy(
            src_ref=src,
            dst_ref=dst,
            send_sem=sem.at[ss],
            recv_sem=sem.at[rs],
            device_id=dev,
            device_id_type=MESH,
        )

    pending = []

    def start(src, dst, ss, rs, dev):
        remote(src, dst, ss, rs, dev).start()

    def start_unless(same, src, dst, ss, rs, dev):
        @pl.when(same)
        def _():
            pltpu.make_async_copy(src, dst, sem.at[rs]).start()

        @pl.when(jnp.logical_not(same))
        def _():
            remote(src, dst, ss, rs, dev).start()

    def arrived(dst, rs):
        pltpu.make_async_copy(dst, dst, sem.at[rs]).wait()

    def sent(ref, ss):
        pending.append(lambda: arrived(ref, ss))

    def sent_or_kept(size, count, ss):
        def finish():
            @pl.when(home)
            def _():
                arrived(size(count - 1), ss)

            @pl.when(away)
            def _():
                arrived(size(count), ss)

        pending.append(finish)

    def to_workers(source, target, size):
        base = sems(2)
        for step in range(8):
            index = (dp + step) % 8
            args = (source(index), target(dp), base, base + 1, worker(index, mp))
            if step == 0:
                start_unless(home, *args)
            else:
                start(*args)
        sent_or_kept(size, 8, base)
        return base + 1

    def to_homes(source, target, size):
        base = sems(2)
        for step in range(8):
            index = (dp + step) % 8
            args = (source(index), target(item), base, base + 1, (index, tp))
            if step == 0:
                start_unless(home, *args)
            else:
                start(*args)
        sent_or_kept(size, 8, base)
        return base + 1

    def to_others(source, target, size):
        base = sems(2)
        for step in range(1, 8):
            index = (dp + step) % 8
            start(source(index), target, base, base + 1, (index, mp))
        sent(size, base)
        return base + 1

    def slots64(ref):
        return lambda i: ref.at[at16(i * 64, 64)]

    def first64(ref):
        return lambda n: ref.at[pl.ds(0, 64 * n)]

    def slots80(ref):
        return lambda i: ref.at[at16(i * 80, 80)]

    def first80(ref):
        return lambda n: ref.at[pl.ds(0, 80 * n)]

    def fold(ref, main, rest):
        for i in range(8):
            ref[80 * i : 80 * i + 64, :] = main[64 * i : 64 * i + 64, :]
            for g in range(4):
                first_row = 64 * i + 16 * g
                ref[80 * i + 64 : 80 * i + 80, 64 * g : 64 * g + 64] = rest[first_row : first_row + 16, :]

    def unfold(ref):
        main = [ref[80 * i : 80 * i + 64, :] for i in range(8)]
        rest = [
            ref[80 * i + 64 : 80 * i + 80, 64 * g : 64 * g + 64] for i in range(8) for g in range(4)
        ]
        return jnp.concatenate(main, axis=0), jnp.concatenate(rest, axis=0)

    def head_of(ref):
        return lambda n: ref.at[pl.ds(0, n)]

    groups = {
        "attn": (r.wp1, r.w1),
        "wo": (r.wpb, r.wb),
        "c0": (r.wp.at[0], r.wc0),
        "c1": (r.wp.at[1], r.wc1),
        "c2": (r.wp.at[2], r.wc2),
    }
    w_base = {g: sems(6) for g in groups}

    def slot(ref, index):
        return ref.at[at16(index * 144, 144)]

    for g in groups:
        whole = groups[g][1]
        sent_or_kept(lambda n, whole=whole: whole.at[pl.ds(0, 144 * n)], 8, w_base[g] + 5)

    def gather_z(g, rels=(1, 0)):
        src, full = groups[g]
        base = w_base[g]
        for rel in rels:
            zt = c + 2 * (zh ^ rel)
            args = (src, slot(full, dp), base + 5, base + rel, device(zt, x, y, zl))
            if rel == 0:
                start_unless(home, *args)
            else:
                start(*args)

    def gather_x(g, rel):
        full, base = groups[g][1], w_base[g]
        mine = slot(full, (c + 2 * (zh ^ rel)) * 2 + x)
        arrived(mine, base + rel)
        start(mine, mine, base + 5, base + 2 + rel, device(z, 1 - x, y, c))
        start(mine, mine, base + 5, base + 4, device(z, x, y, 1 - c))

    def gather_core(g, rel):
        full, base = groups[g][1], w_base[g]
        mine = slot(full, (c + 2 * (zh ^ rel)) * 2 + 1 - x)
        arrived(mine, base + 2 + rel)
        start(mine, mine, base + 5, base + 4, device(z, x, y, 1 - c))

    def gather_done(g):
        arrived(groups[g][1].at[pl.ds(0, 144 * 4)], w_base[g] + 4)

    z_mate = device(2 * zh + 1 - zl, x, y, c)
    y_mate = device(z, x, 1 - y, c)

    class Gather:
        def __init__(self, view, size):
            self.view, self.size, self.base = view, size, sems(3)
            mine = view(tp)
            start(mine, mine, self.base, self.base + 1, z_mate)
            start(mine, mine, self.base, self.base + 2, y_mate)
            sent(size(3), self.base)

        def relay(self):
            other = self.view(tp ^ 1)
            arrived(other, self.base + 1)
            start(other, other, self.base, self.base + 2, y_mate)

        def done(self):
            arrived(self.size(2), self.base + 2)

    class Scatter:
        def __init__(self, name):
            self.base = sems(3)
            self.sent, self.rec, self.sum = (getattr(r, k + name) for k in ("rs", "rr", "rt"))
            start(self.view(tp ^ 3), self.rec.at[0], self.base, self.base + 1, y_mate)
            start(self.view(tp ^ 2), self.rec.at[1], self.base, self.base + 2, y_mate)
            sent(self.rec, self.base)

        def view(self, t):
            return self.sent.at[at16(t * 64, 64)]

        def relay(self):
            arrived(self.rec.at[0], self.base + 1)
            both = self.view(tp ^ 1)[...].astype(f32) + self.rec[0].astype(f32)
            self.sum[...] = both.astype(bf16)
            start(self.sum, self.rec.at[2], self.base, self.base + 2, z_mate)

        def total(self):
            arrived(self.rec.at[pl.ds(1, 2)], self.base + 2)
            total = self.view(tp)[...].astype(f32) + self.rec[1].astype(f32)
            return total + self.rec[2].astype(f32)

    def rows_view(buf):
        return lambda t: buf.at[at16(t * 64, 64)]

    def mates_send(source, target, size):
        base = sems(2)
        for step in range(1, 4):
            start(source(tp ^ step), target, base, base + 1, mate(step))
        sent(size, base)
        return base + 1

    g_base = {name: sems(9) for name, _ in GROUPS}

    def block(name, s):
        rows = at16(s * 144, 144)
        if name == "out":
            return nn(r.agt[rows, :], r.al2[...])
        if name == "qkv":
            return jnp.concatenate(
                [nn(r.h1t[rows, :], r.dqkv[...]), nn(r.agt[rows, :], r.al1[...])], axis=-1
            )
        k = int(name[1:])
        return jnp.concatenate(
            [nn(r.h2t[rows, :], r.gug[k]), nn(r.fgt[rows, :], r.inner[k])], axis=-1
        )

    for name, _ in GROUPS:
        buf = getattr(r, "cs_" + name)
        sent(buf, g_base[name] + 7)
        sent_or_kept(head_of(buf), 4, g_base[name] + 8)

    def reduce_core(name):
        base = g_base[name]
        cs, cr = getattr(r, "cs_" + name), getattr(r, "cr_" + name)
        for xx in (1 - x, x):
            for rel in (1 - zh, zh):
                q = 2 * rel + xx
                cs[q] = block(name, (1 - c + 2 * rel) * 2 + xx).astype(bf16)
                start(cs.at[q], cr.at[q], base + 7, base + q, device(z, x, y, 1 - c))

    def reduce_x(name, far):
        base = g_base[name]
        cr, xs, xr = (getattr(r, k + name) for k in ("cr_", "xs_", "xr_"))
        rel = zh ^ far
        q = 2 * rel + 1 - x
        part = block(name, (c + 2 * rel) * 2 + 1 - x)
        arrived(cr.at[q], base + q)
        xs[rel] = (part + cr[q].astype(f32)).astype(bf16)
        start(xs.at[rel], xr.at[rel], base + 8, base + 4 + rel, device(z, 1 - x, y, c))

    def reduce_z(name, far):
        base = g_base[name]
        cr, xr, zs, zr = (getattr(r, k + name) for k in ("cr_", "xr_", "zs_", "zr_"))
        rel = zh ^ far
        q = 2 * rel + x
        part = block(name, (c + 2 * rel) * 2 + x)
        arrived(cr.at[q], base + q)
        part = part + cr[q].astype(f32)
        arrived(xr.at[rel], base + 4 + rel)
        zs[far] = (part + xr[rel].astype(f32)).astype(bf16)
        args = (zs.at[far], zr.at[zh], base + 8, base + 6, device(c + 2 * rel, x, y, zl))
        if far == 0:
            start_unless(home, *args)
        else:
            start(*args)

    def reduce_end(name):
        zr = getattr(r, "zr_" + name)
        arrived(zr, g_base[name] + 6)
        return zr[0].astype(f32) + zr[1].astype(f32)

    def transpose(src, dst):
        def step(j):
            dst[at128(j * 128, 128), :] = src[:, at128(j * 128, 128)].T

        loop(9, step)

    lane128 = lax.broadcasted_iota(jnp.int32, (1, PAD), 1)
    head_lane = lane128 < 72
    quarter = lane128 // 18
    even = quarter % 2 == 0

    def swap(v):
        return jnp.where(even, pltpu.roll(v, PAD - 18, 1), pltpu.roll(v, 18, 1))

    def norm_of(v):
        inv = lax.rsqrt(jnp.mean(v * v, axis=-1, keepdims=True) + epsilon)
        return v * inv, inv

    def back(g, normed, inv):
        return inv * (g - normed * jnp.mean(g * normed, axis=-1, keepdims=True))

    barrier = pltpu.get_barrier_semaphore()
    for i in range(8):
        for j in range(4):
            if i or j:
                pl.semaphore_signal(
                    barrier, inc=1, device_id=((dp + i) % 8, mp ^ j), device_id_type=MESH
                )

    late = []
    for src, dst in (
        (r.wqkv, r.wqkv_in), (r.wgu, r.wgu_in), (r.wada, r.wada_in), (r.wdn, r.wdn_in)
    ):
        late.append(pltpu.make_async_copy(src, dst, sem.at[sems(1)]))
        late[-1].start()
    cond = r.cond[...].astype(f32)
    sig_c = jax.nn.sigmoid(cond)
    r.arow[0:1, 0:META] = (cond * sig_c).astype(bf16).astype(f32)
    meta = jnp.where(lane128 == 0, r.bin[0].astype(f32), 0.0)
    meta = jnp.where(lane128 == 1, r.grid[0, 0].astype(f32), meta)
    meta = jnp.where(lane128 == 2, r.grid[0, 1].astype(f32), meta)
    r.arow[0:1, META : META + 128] = meta
    r.arec[dp] = r.arow[...]

    dest = r.dest[...]
    lane512 = lax.broadcasted_iota(jnp.int32, (1, 512), 1)
    live = lane512 < r.count[0]
    target = dest >> 8
    within = dest & 255
    owner = lax.broadcasted_iota(jnp.int32, (8, 512), 0)
    member = jnp.where((owner == target) & live, 1.0, 0.0)
    upper = lax.broadcasted_iota(jnp.int32, (512, 512), 0) <= lax.broadcasted_iota(
        jnp.int32, (512, 512), 1
    )
    running = nn(member.astype(bf16), jnp.where(upper, 1.0, 0.0).astype(bf16))
    rank = jnp.sum(running * member, axis=0, keepdims=True).astype(jnp.int32) - 1
    spot = jnp.where(live, target * 64 + rank, -1)
    slots = lax.broadcasted_iota(jnp.int32, (512, 512), 0)
    r.place[...] = jnp.where(slots == spot, 1.0, 0.0).astype(bf16)
    r.xe[0:32, :] = r.xt[256:288, :]
    r.xe[32:64, :] = r.ct[256:288, :]
    fold(
        r.sx,
        nt(r.place[...], r.xt[0:256, :]).astype(bf16),
        nt(r.place[...], r.xe[...]).astype(bf16),
    )
    named = jnp.broadcast_to((within + 1).astype(f32), (8, 512)).astype(bf16)
    named = nt(named, r.place[...])
    for i in range(8):
        r.ids[i] = named[0:1, 64 * i : 64 * i + 64]

    pl.semaphore_wait(barrier, 31)
    a_in = to_others(lambda i: r.arow, r.arec.at[dp], r.arec.at[pl.ds(0, 7)])
    id_in = to_workers(lambda i: r.ids.at[i], lambda i: r.idr.at[i], head_of(r.idr))
    x_in = to_workers(slots80(r.sx), slots80(r.rx), first80(r.rx))
    late[0].wait()
    late[1].wait()
    late[3].wait()
    for p in range(3):
        r.wp1[:, 288 * p : 288 * p + 288] = r.wqkv_in[p]
    r.wp1[:, 864:896] = r.woin[:, 0:32]
    r.wpb[...] = r.woin[:, 32:288]
    for k in range(3):
        r.wp[k, :, 0:256] = r.wgu_in[:, 0, 256 * k : 256 * k + 256]
        r.wp[k, :, 256:512] = r.wgu_in[:, 1, 256 * k : 256 * k + 256]
        r.wp[k, :, 512:768] = r.wdn_in[:, 256 * k : 256 * k + 256]
    r.sg[...] = nt(r.place[...], r.ct[0:256, :]).astype(bf16)

    arrived(r.arec.at[pl.ds(0, 7)], a_in)
    late[2].wait()
    for i in range(8):
        r.amat[i : i + 1, :] = r.arec[i]
    pick = lax.broadcasted_iota(jnp.int32, (1152, 144), 0) == (
        lax.broadcasted_iota(jnp.int32, (1152, 144), 1) + 144 * dp
    )
    silu_own = nn(r.amat[:, 0:META].astype(bf16), jnp.where(pick, 1.0, 0.0).astype(bf16)).astype(bf16)
    first = (dp == 0).astype(f32)
    for k in range(6):
        part = nn(silu_own, r.wada_in[k]) + first * r.bada[k : k + 1, :].astype(f32)
        for i in range(8):
            r.pms[i, k] = part[i : i + 1, :]
    m_in = to_workers(lambda i: r.pms.at[i], lambda i: r.pmr.at[i], head_of(r.pmr))
    gather_z("attn")
    gather_z("wo")

    about = r.arec[item]
    height = about[:, META + 1 : META + 2]
    width = about[:, META + 2 : META + 3]
    bins = r.amat[:, META : META + 1]
    alike = jnp.sum(
        jnp.where(bins == about[:, META : META + 1], 1.0, 0.0), axis=0, keepdims=True
    )
    weight = 8.0 / (NBINS * alike)
    spots = lax.broadcasted_iota(jnp.int32, (256, 1), 0).astype(f32)
    high = jnp.floor((spots + 0.5) / width)
    wide = spots - high * width
    freq = jnp.exp(-math.log(10000.0) * (lane128 - 18 * quarter).astype(f32) / 18.0)
    angle = jnp.where(quarter < 2, high, wide) * freq
    r.cosv[...] = jnp.where(head_lane, jnp.cos(angle), 0.0)
    r.sinv[...] = jnp.where(head_lane, jnp.where(even, -jnp.sin(angle), jnp.sin(angle)), 0.0)
    used = height * width
    key_ok = lax.broadcasted_iota(jnp.int32, (1, 256), 1).astype(f32) < used
    row_first = (tp * 64).astype(f32)
    share_spots = lax.broadcasted_iota(jnp.int32, (64, 1), 0).astype(f32) + row_first
    valid_share = jnp.where(share_spots < used, 1.0, 0.0)

    arrived(r.idr, id_in)
    number = jnp.concatenate([r.idr[i] for i in range(8)], axis=-1).astype(jnp.int32)
    r.spread[...] = jnp.where(
        number == lax.broadcasted_iota(jnp.int32, (256, 512), 0) + 1, 1.0, 0.0
    ).astype(bf16)
    arrived(r.rx, x_in)
    main, rest = unfold(r.rx)
    r.rb[tp, 0:256, :] = nn(r.spread[...], main).astype(bf16)
    rest = nn(r.spread[...], rest).astype(bf16)
    for i in range(4):
        for g in range(4):
            first_row = 64 * i + 16 * g
            r.rb[tp, 256 + 16 * i : 272 + 16 * i, 64 * g : 64 * g + 64] = rest[first_row : first_row + 16, :]
    rb_all = Gather(lambda t: r.rb.at[t], head_of(r.rb))

    gather_x("attn", 0)
    gather_x("attn", 1)
    arrived(r.pmr, m_in)
    total = r.pmr[0]
    for s in range(1, 8):
        total = total + r.pmr[s]
    r.mdb[tp] = total.astype(bf16).astype(f32)
    mdb_all = Gather(lambda t: r.mdb.at[t], head_of(r.mdb))
    rb_all.relay()
    mdb_all.relay()
    t_in = to_workers(slots64(r.sg), slots64(r.rg), first64(r.rg))
    gather_z("c0")
    gather_z("c1")
    gather_core("attn", 0)
    gather_core("attn", 1)

    gather_x("wo", 0)
    gather_x("wo", 1)
    rb_all.done()
    mdb_all.done()
    for k in range(6):
        for t in range(4):
            r.modf[k : k + 1, 288 * t : 288 * t + 288] = r.mdb[t, k]

    def left_over(t, start):
        piece = r.rb[t, at16(256 + start // 4, 16), :].astype(f32)
        return jnp.concatenate([piece[:, 64 * g : 64 * g + 64] for g in range(4)], axis=0)

    def joined(start):
        parts = []
        for t in range(4):
            parts.append(r.rb[t, at16(start, 64), :].astype(f32))
            parts.append(left_over(t, start)[:, 0:32])
        return jnp.concatenate(parts, axis=-1)

    def joined_grad(start):
        parts = []
        for t in range(4):
            parts.append(r.gb[t, at16(start, 64), :].astype(f32))
            parts.append(left_over(t, start)[:, 32:64])
        return jnp.concatenate(parts, axis=-1)

    def first_hidden(i):
        normed, _ = norm_of(joined(i * 64))
        shift, scale = r.modf[0:1, :], r.modf[1:2, :]
        r.h1[at16(i * 64, 64), :] = (normed * (1.0 + scale) + shift).astype(bf16)

    loop(4, first_hidden)
    RESID, NORM1, ATT, MID, NORM2, TOP, MIDG = range(7)
    mine = joined(tp * 64)
    normed, inv = norm_of(mine)
    r.share[RESID] = mine
    r.share[NORM1] = normed
    r.invs[0] = inv
    gather_done("attn")

    def project(j):
        r.qkv[:, at128(j * 256, 256)] = nn(r.h1[...], r.w1[:, at128(j * 256, 256)])

    loop(3, project)
    r.qkv[:, 768:896] = nn(r.h1[...], r.w1[:, 768:896])

    gather_x("c0", 0)
    gather_core("wo", 0)
    gather_core("wo", 1)
    scale_q = 72 ** (-0.5)
    pad = jnp.zeros((1, PAD - 72), f32)
    gains = {k: jnp.concatenate([g[...], pad], axis=-1) for k, g in (("q", r.qg), ("k", r.kg))}
    def turn_heads(h):
        for kind, offset, normed_ref, inv_ref, low_ref in (
            ("q", 0, r.qn, r.qi, r.ql),
            ("k", 288, r.kn, r.ki, r.kl),
        ):
            lane = offset + 72 * h
            v = jnp.where(head_lane, r.qkv[:, lane : lane + 128], 0.0)
            inv = lax.rsqrt(jnp.sum(v * v, axis=-1, keepdims=True) * (1.0 / 72) + epsilon)
            v = v * inv
            normed_ref[h] = v
            inv_ref[h] = inv
            v = v * gains[kind]
            v = v * r.cosv[...] + swap(v) * r.sinv[...]
            if kind == "q":
                v = v * scale_q
            low_ref[h] = v.astype(bf16)
        lane = 576 + 72 * h
        r.vl[h] = jnp.where(head_lane, r.qkv[:, lane : lane + 128], 0.0).astype(bf16)

    turn_heads(0)
    turn_heads(1)
    turn_heads(2)
    turn_heads(3)
    def attend(h):
        scores = jnp.where(key_ok, nt(r.ql[h], r.kl[h]), -1e30)
        scores = jnp.exp(scores - jnp.max(scores, axis=-1, keepdims=True))
        prob = scores / jnp.sum(scores, axis=-1, keepdims=True)
        r.pf[h] = prob
        low = nn(prob.astype(bf16), r.vl[h]).astype(bf16)
        if h == 0:
            r.al1[...] = low[:, 0:32]
            r.al2[:, 0:40] = low[:, 32:72]
        else:
            r.al2[:, 72 * h - 32 : 72 * h + 40] = low[:, 0:72]

    attend(0)
    attend(1)
    attend(2)
    attend(3)

    gather_done("wo")

    def project_out(j):
        rows = at128(j * 384, 384)
        part = nt(r.al2[...], r.wb[rows, :]) + nt(r.al1[...], r.w1[rows, 864:896])
        r.rsa[:, rows] = part.astype(bf16)

    loop(3, project_out)
    sum_a = Scatter("a")
    arrived(r.rg, t_in)
    r.gb[tp] = nn(r.spread[...], r.rg[...]).astype(bf16)
    gb_all = Gather(lambda t: r.gb.at[t], head_of(r.gb))
    sum_a.relay()

    gather_z("c2", (1,))
    gather_x("c0", 1)
    gather_core("c0", 0)
    gather_x("c1", 0)
    gb_all.relay()
    gather_x("c1", 1)
    attention = sum_a.total()
    r.share[ATT] = attention
    middle = r.share[RESID] + r.modf[2:3, :] * attention
    r.share[MID] = middle
    normed, inv = norm_of(middle)
    r.share[NORM2] = normed
    r.invs[1] = inv
    r.h2[at16(tp * 64, 64), :] = (normed * (1.0 + r.modf[4:5, :]) + r.modf[3:4, :]).astype(bf16)
    h2_all = Gather(rows_view(r.h2), first64(r.h2))
    gather_z("c2", (0,))
    gather_core("c0", 1)
    h2_all.relay()
    gather_x("c2", 0)
    gather_x("c2", 1)
    gather_core("c1", 0)
    gather_core("c1", 1)
    transpose(r.h1, r.h1t)
    chunks = (r.wc0, r.wc1, r.wc2)

    def swiglu(k):
        full = chunks[k]
        gate = nn(r.h2[...], full[:, 0:256])
        up = nn(r.h2[...], full[:, 256:512])
        grad = nn(r.fg[...], full[:, 512:768])
        sig = jax.nn.sigmoid(gate)
        act = gate * sig
        r.inner[k] = (act * up).astype(bf16)
        r.gug[k, :, 0:256] = (grad * up * sig * (1.0 + gate * (1.0 - sig))).astype(bf16)
        r.gug[k, :, 256:512] = (grad * act).astype(bf16)

    def hidden_back(k):
        full = chunks[k]

        def step(j):
            rows = at128(j * 384, 384)
            part = nt(r.gug[k], full[rows, 0:512])
            if k > 0:
                part = part + r.h2sum[:, rows]
            if k < 2:
                r.h2sum[:, rows] = part
            else:
                r.rsh2[:, rows] = part.astype(bf16)

        loop(3, step)

    gb_all.done()
    def feed_rows(i):
        rows = lax.broadcasted_iota(jnp.int32, (64, 1), 0).astype(f32) + (i * 64).astype(f32)
        factor = jnp.where(rows < used, weight, 0.0)
        r.fg[at16(i * 64, 64), :] = (joined_grad(i * 64) * factor * r.modf[5:6, :]).astype(bf16)

    loop(4, feed_rows)
    r.share[TOP] = joined_grad(tp * 64) * (weight * valid_share)
    transpose(r.fg, r.fgt)

    h2_all.done()
    gather_done("c0")
    swiglu(0)
    transpose(r.h2, r.h2t)
    reduce_core("c0")
    gather_core("c2", 0)
    gather_done("c1")
    swiglu(1)
    reduce_x("c0", 1)
    reduce_x("c0", 0)
    reduce_core("c1")
    gather_core("c2", 1)
    hidden_back(0)
    hidden_back(1)
    gather_done("c2")
    swiglu(2)
    hidden_back(2)
    sum_h2 = Scatter("h2")
    reduce_x("c1", 1)
    reduce_z("c0", 1)
    reduce_x("c1", 0)
    reduce_core("c2")
    reduce_x("c2", 1)
    reduce_x("c2", 0)
    sum_h2.relay()
    reduce_z("c0", 0)

    def feed_out(j):
        rows = at128(j * 384, 384)
        part = nt(r.inner[0], r.wc0[rows, 512:768])
        part = part + nt(r.inner[1], r.wc1[rows, 512:768])
        part = part + nt(r.inner[2], r.wc2[rows, 512:768])
        r.rsf[:, rows] = part.astype(bf16)

    loop(3, feed_out)
    sum_f = Scatter("f")
    grad_h2 = sum_h2.total()
    normed = r.share[NORM2]
    r.gpart[3:4, :] = jnp.sum(grad_h2, axis=0, keepdims=True)
    r.gpart[4:5, :] = jnp.sum(grad_h2 * normed, axis=0, keepdims=True)
    mid_grad = r.share[TOP] + back(grad_h2 * (1.0 + r.modf[4:5, :]), normed, r.invs[1])
    r.share[MIDG] = mid_grad
    r.gpart[2:3, :] = jnp.sum(mid_grad * r.share[ATT], axis=0, keepdims=True)
    r.ag[at16(tp * 64, 64), :] = (r.modf[2:3, :] * mid_grad).astype(bf16)
    ag_all = Gather(rows_view(r.ag), first64(r.ag))
    sum_f.relay()

    reduce_z("c1", 1)
    reduce_z("c1", 0)
    ag_all.relay()
    reduce_z("c2", 1)
    def total_of(v):
        return jnp.sum(jnp.sum(v, axis=0, keepdims=True), axis=1, keepdims=True)

    squares = []
    kept = []

    def result_part():
        feed = sum_f.total()
        fed = r.modf[5:6, :] * feed
        result = r.share[MID] + fed
        r.gpart[5:6, :] = jnp.sum(r.share[TOP] * feed, axis=0, keepdims=True)
        att = r.modf[2:3, :] * r.share[ATT]

        squares[:] = [total_of(valid_share * v * v) for v in (result, att, fed)]
        low_result = result.astype(bf16)
        for t in range(4):
            r.ras[t] = low_result[:, 288 * t : 288 * t + 256]
            r.ias[t, :, 320:352] = low_result[:, 288 * t + 256 : 288 * t + 288]
        r.rar[tp] = r.ras[tp]
        kept.append(mates_send(lambda t: r.ras.at[t], r.rar.at[tp], r.rar.at[pl.ds(0, 3)]))

    def rows_part():
        arrived(r.rar.at[pl.ds(0, 3)], kept[0])
        rar = jnp.concatenate([r.rar[t] for t in range(4)], axis=0)
        r.bs[...] = tn(r.spread[...], rar).astype(bf16)
        kept.append(to_homes(slots64(r.bs), slots64(r.br), first64(r.br)))


    ag_all.done()
    r.da[:, 0:32] = nn(r.ag[...], r.w1[:, 864:896])
    r.da[:, 32:288] = nn(r.ag[...], r.wb[...])
    result_part()
    transpose(r.ag, r.agt)

    reduce_core("out")
    sums = [jnp.zeros((1, PAD), f32), jnp.zeros((1, PAD), f32)]

    def attend_back(h):
        grad = jnp.where(head_lane, r.da[:, 72 * h : 72 * h + 128], 0.0).astype(bf16)
        prob = r.pf[h]
        prob_grad = nt(grad, r.vl[h])
        mixed = jnp.sum(prob * prob_grad, axis=-1, keepdims=True)
        score = (prob * (prob_grad - mixed)).astype(bf16)
        value_grad = tn(prob.astype(bf16), grad)
        r.dqkv[:, 576 + 72 * h : 648 + 72 * h] = value_grad[:, 0:72].astype(bf16)
        for kind, offset, normed_ref, inv_ref in (
            ("q", 0, r.qn, r.qi),
            ("k", 288, r.kn, r.ki),
        ):
            if kind == "q":
                turned = nn(score, r.kl[h]) * scale_q
            else:
                turned = tn(score, r.ql[h])
            turned = turned * r.cosv[...] - swap(turned) * r.sinv[...]
            normed = normed_ref[h]
            along = jnp.sum(turned * normed, axis=0, keepdims=True)
            if kind == "q":
                sums[0] = sums[0] + along
            else:
                sums[1] = sums[1] + along
            g = turned * gains[kind]
            mean = jnp.sum(g * normed, axis=-1, keepdims=True) * (1.0 / 72)
            g = inv_ref[h] * (g - normed * mean)
            r.dqkv[:, offset + 72 * h : offset + 72 * h + 72] = g[:, 0:72].astype(bf16)

    attend_back(0)
    reduce_x("out", 1)
    reduce_x("out", 0)
    attend_back(1)
    reduce_z("c2", 0)
    attend_back(2)
    rows_part()
    reduce_z("out", 1)
    attend_back(3)
    def first_back(j):
        r.rsh1[:, at128(j * 384, 384)] = nt(r.dqkv[...], r.w1[at128(j * 384, 384), 0:864]).astype(bf16)

    loop(3, first_back)
    sum_h1 = Scatter("h1")
    reduce_z("out", 0)
    reduce_core("qkv")
    reduce_x("qkv", 1)
    reduce_x("qkv", 0)
    sum_h1.relay()
    grad_h1 = sum_h1.total()
    normed = r.share[NORM1]
    r.gpart[0:1, :] = jnp.sum(grad_h1, axis=0, keepdims=True)
    r.gpart[1:2, :] = jnp.sum(grad_h1 * normed, axis=0, keepdims=True)
    in_grad = r.share[MIDG] + back(grad_h1 * (1.0 + r.modf[1:2, :]), normed, r.invs[0])
    low_grad = in_grad.astype(bf16)
    for t in range(4):
        r.ias[t, :, 0:288] = low_grad[:, 288 * t : 288 * t + 288]
    numbers = jnp.concatenate(
        [sums[0][:, 0:72], sums[1][:, 0:72], squares[0], squares[1], squares[2],
         total_of(valid_share), jnp.zeros((1, 288 - 148), f32)],
        axis=-1,
    )
    for t in range(4):
        for k in range(6):
            r.hs[t, k] = r.gpart[k : k + 1, 288 * t : 288 * t + 288]
        r.hs[t, 6] = numbers
    r.hr[tp] = r.hs[tp]
    h_in = mates_send(lambda t: r.hs.at[t], r.hr.at[tp], r.hr.at[pl.ds(0, 3)])
    r.iar[tp] = r.ias[tp]
    ia_in = mates_send(lambda t: r.ias.at[t], r.iar.at[tp], r.iar.at[pl.ds(0, 3)])

    arrived(r.hr.at[pl.ds(0, 3)], h_in)
    total = r.hr[0] + r.hr[1] + r.hr[2] + r.hr[3]
    for k in range(6):
        r.gs[k] = total[k].astype(bf16).astype(f32)
    r.gs[6] = total[6]
    g2_in = to_homes(lambda i: r.gs, lambda i: r.grec.at[i], head_of(r.grec))
    reduce_z("qkv", 1)
    arrived(r.iar.at[pl.ds(0, 3)], ia_in)
    iar = jnp.concatenate([r.iar[t] for t in range(4)], axis=0)
    rest = jnp.concatenate([iar[:, 256:288], iar[:, 320:352]], axis=-1)
    fold(
        r.bgs,
        tn(r.spread[...], iar[:, 0:256]).astype(bf16),
        tn(r.spread[...], rest).astype(bf16),
    )
    bg_in = to_homes(slots80(r.bgs), slots80(r.bgr), first80(r.bgr))
    reduce_z("qkv", 0)
    arrived(r.grec, g2_in)
    cond_part = jnp.zeros((8, 144), f32)
    for k in range(6):
        grads = jnp.concatenate([r.grec[i, k] for i in range(8)], axis=0)
        low = grads.astype(bf16)
        r.gada[k] = tn(silu_own, low)
        r.gbada[k : k + 1, :] = jnp.sum(grads, axis=0, keepdims=True)
        cond_part = cond_part + nt(low, r.wada_in[k])
    totals = r.grec[0, 6]
    for i in range(1, 8):
        totals = totals + r.grec[i, 6]
    r.gqg[...] = totals[:, 0:72]
    r.gkg[...] = totals[:, 72:144]
    ratio = totals[:, 144:147] / (totals[:, 147:148] * 1152.0)
    r.stats[...] = jnp.sqrt(ratio)
    r.cps[...] = cond_part
    c_in = sems(2)
    r.cpr[mp] = cond_part
    for step in range(1, 4):
        start(r.cps, r.cpr.at[mp], c_in, c_in + 1, (dp, mp ^ step))
    sent(r.cpr.at[pl.ds(0, 3)], c_in)
    arrived(r.cpr.at[pl.ds(0, 3)], c_in + 1)
    cond_sum = r.cpr[0] + r.cpr[1] + r.cpr[2] + r.cpr[3]
    for i in range(8):
        r.cts[i] = cond_sum[i : i + 1, :]
    r.ctr[dp] = r.cts[dp]
    ct_in = to_others(lambda i: r.cts.at[i], r.ctr.at[dp], r.ctr.at[pl.ds(0, 7)])

    for k in range(3):
        grad = reduce_end(f"c{k}")
        lanes = slice(256 * k, 256 * k + 256)
        r.ggu[:, 0, lanes] = grad[:, 0:256]
        r.ggu[:, 1, lanes] = grad[:, 256:512]
        r.gdn[:, lanes] = grad[:, 512:768]
    arrived(r.br, kept[1])
    r.outt[0:256, :] = tn(r.br[...], r.place[...]).astype(bf16)
    grad = reduce_end("qkv")
    for p in range(3):
        r.gqkv[p] = grad[:, 288 * p : 288 * p + 288]
    r.gout[:, 0:32] = grad[:, 864:896]
    r.gout[:, 32:288] = reduce_end("out")
    arrived(r.bgr, bg_in)
    main, rest = unfold(r.bgr)
    rest = tn(rest, r.place[...]).astype(bf16)
    r.gint[0:256, :] = tn(main, r.place[...]).astype(bf16)
    r.gint[256:288, :] = rest[0:32, :]
    r.outt[256:288, :] = rest[32:64, :]
    arrived(r.ctr.at[pl.ds(0, 7)], ct_in)
    for s in range(8):
        r.gcond[0:1, 144 * s : 144 * s + 144] = r.ctr[s]
    cond = r.cond[...].astype(f32)
    sig_c = jax.nn.sigmoid(cond)
    r.gcond[...] = r.gcond[...] * sig_c * (1.0 + cond * (1.0 - sig_c))
    for finish in pending:
        finish()
    assert taken[0] == 132


def copy_out(*refs):
    count = len(refs) // 2
    sem = refs[-1]
    copies = [pltpu.make_async_copy(refs[i], refs[count + i], sem.at[i]) for i in range(count)]
    for copy in copies:
        copy.start()
    for copy in copies:
        copy.wait()


def body_kernel(
    x_src, cotangent, route_dest, route_count, item_grid, noise_bin, cond, w_ada, b_ada,
    w_qkv, q_gain, k_gain, w_out, w_gu, w_down,
):
    scratch = scratch_list()
    vmem = pl.BlockSpec(memory_space=pltpu.VMEM)
    smem = pl.BlockSpec(memory_space=pltpu.SMEM)
    far = pl.BlockSpec(memory_space=pl.ANY)
    shapes = [
        ((288, 512), bf16), ((288, 512), bf16), ((1, 1152), f32), ((6, 144, 288), f32),
        ((6, 288), f32), ((3, 144, 288), f32), ((1, 72), f32), ((1, 72), f32),
        ((144, 288), f32), ((144, 2, 768), f32), ((144, 768), f32), ((1, 3), f32),
    ]
    outs = pl.pallas_call(
        functools.partial(block_kernel, list(scratch)),
        out_shape=[pltpu.VMEM(s, d) for s, d in shapes],
        in_specs=[vmem, vmem, vmem, smem, smem, smem, vmem, far, vmem, far, vmem, vmem, vmem, far, far],
        out_specs=[vmem] * len(shapes),
        scratch_shapes=list(scratch.values()),
        compiler_params=pltpu.CompilerParams(
            has_side_effects=True, vmem_limit_bytes=57500000, collective_id=0
        ),
        name="block",
    )(
        x_src.T, cotangent.T, route_dest.reshape(1, SRC_CAP), route_count, item_grid, noise_bin,
        cond, jnp.transpose(w_ada, (1, 0, 2)), b_ada, jnp.transpose(w_qkv, (1, 0, 2)),
        q_gain.reshape(1, DH), k_gain.reshape(1, DH), w_out.T, w_gu, w_down.T,
    )
    outs = pl.pallas_call(
        copy_out,
        out_shape=[jax.ShapeDtypeStruct(s, d) for s, d in shapes],
        in_specs=[vmem] * len(shapes),
        out_specs=[pl.BlockSpec(memory_space=pl.ANY)] * len(shapes),
        scratch_shapes=[pltpu.SemaphoreType.DMA((len(shapes),))],
        compiler_params=pltpu.CompilerParams(vmem_limit_bytes=2000000),
        name="store",
    )(*outs)
    (outt, gint, gcond, gada, gbada, gqkv, gqg, gkg, gout, ggu, gdn, stats) = outs
    return (
        outt.T, gint.T, gcond, jnp.transpose(gada, (1, 0, 2)), gbada,
        jnp.transpose(gqkv, (1, 0, 2)), gqg.reshape(DH), gkg.reshape(DH), gout.T, ggu, gdn.T,
        stats.reshape(3),
    )


def solution(mesh):
    one_kernel = mesh.shape["dp"] == 8 and mesh.shape["mp"] == 4
    return jax.shard_map(
        body_kernel if one_kernel else body,
        mesh=mesh,
        in_specs=(
            P("dp", "mp"),
            P("dp", "mp"),
            P("dp"),
            P("dp"),
            P("dp", None),
            P("dp"),
            P("dp", None),
            P("dp", None, "mp"),
            P(None, "mp"),
            P("dp", None, "mp"),
            P(),
            P(),
            P("mp", "dp"),
            P("dp", None, "mp"),
            P("mp", "dp"),
        ),
        out_specs=(
            P("dp", "mp"),
            P("dp", "mp"),
            P("dp", None),
            P("dp", None, "mp"),
            P(None, "mp"),
            P("dp", None, "mp"),
            P(),
            P(),
            P("mp", "dp"),
            P("dp", None, "mp"),
            P("mp", "dp"),
            P(),
        ),
        check_vma=False,
    )
```

```python
import functools
import math

import jax
import jax.numpy as jnp
from jax import lax
from jax.experimental import pallas as pl
from jax.experimental.pallas import tpu as pltpu
from jax.sharding import PartitionSpec as P

D = 1152
DH = 72
NBINS = 16
BLOCK = 256
ROWS_DEV = 256
SRC_CAP = 512


epsilon = 1e-06


def grad_share(part, dim):
    sent = part.astype(jnp.bfloat16)
    total = lax.psum_scatter(sent, "dp", scatter_dimension=dim, tiled=True)
    return total.astype(jnp.float32)


def norm_rows(values):
    scale = lax.rsqrt(jnp.mean(values * values, axis=-1, keepdims=True) + epsilon)
    return (values * scale, scale)


def norm_back(grad_normed, normed, scale):
    return scale * (grad_normed - normed * jnp.mean(grad_normed * normed, axis=-1, keepdims=True))


def rotate(values, cos_h, sin_h, cos_w, sin_w, sign):
    quarter = values.shape[-1] // 4
    first = values[..., :quarter]
    second = values[..., quarter : 2 * quarter]
    third = values[..., 2 * quarter : 3 * quarter]
    fourth = values[..., 3 * quarter :]
    return jnp.concatenate(
        [
            first * cos_h - sign * second * sin_h,
            sign * first * sin_h + second * cos_h,
            third * cos_w - sign * fourth * sin_w,
            sign * third * sin_w + fourth * cos_w,
        ],
        axis=-1,
    )


def angle_tables(grid, block, head_dim):
    quarter = head_dim // 4
    place = lax.broadcasted_iota(jnp.int32, (grid.shape[0], block), 1)
    width = grid[:, 1:2]
    height_pos = (place // width).astype(jnp.float32)
    width_pos = (place % width).astype(jnp.float32)
    freqs = jnp.exp(-math.log(10000.0) * jnp.arange(quarter).astype(jnp.float32) / quarter)
    angle_h = (height_pos[:, :, None] * freqs)[:, :, None, :]
    angle_w = (width_pos[:, :, None] * freqs)[:, :, None, :]
    return (jnp.cos(angle_h), jnp.sin(angle_h), jnp.cos(angle_w), jnp.sin(angle_w))


def row_share(values):
    return lax.psum_scatter(values, "mp", scatter_dimension=0, tiled=True)


def row_whole(values):
    return lax.all_gather(values, "mp", axis=0, tiled=True)


def body(
    x_src,
    cotangent,
    route_dest,
    route_count,
    item_grid,
    noise_bin,
    cond,
    w_ada,
    b_ada,
    w_qkv,
    q_gain,
    k_gain,
    w_out,
    w_gu,
    w_down,
):
    peers = lax.axis_size("dp")
    model_rank = lax.axis_index("mp")
    blocks_here = item_grid.shape[0]
    local_width = x_src.shape[1]
    heads_here = local_width // DH
    slot_rows = 2 * ROWS_DEV // peers
    share = ROWS_DEV // lax.axis_size("mp")
    row_first = model_rank * share
    live = jnp.arange(SRC_CAP) < route_count[0]
    target = route_dest // ROWS_DEV
    member = (target[:, None] == jnp.arange(peers)[None, :]) & live[:, None]
    running = jnp.cumsum(member.astype(jnp.int32), axis=0)
    rank_in = jnp.sum(running * member, axis=1) - 1
    place = jnp.where(live, target * slot_rows + rank_in, peers * slot_rows)
    send_rows = (
        jnp.zeros((peers * slot_rows, local_width), jnp.bfloat16).at[place].set(x_src, mode="drop")
    )
    send_grads = (
        jnp.zeros((peers * slot_rows, local_width), jnp.bfloat16)
        .at[place]
        .set(cotangent, mode="drop")
    )
    send_index = (
        jnp.full((peers * slot_rows,), ROWS_DEV, jnp.int32)
        .at[place]
        .set(route_dest % ROWS_DEV, mode="drop")
    )
    recv_rows, recv_grads, recv_index = (
        lax.all_to_all(
            send_rows.reshape(peers, slot_rows, local_width),
            "dp",
            split_axis=0,
            concat_axis=0,
            tiled=True,
        ),
        lax.all_to_all(
            send_grads.reshape(peers, slot_rows, local_width),
            "dp",
            split_axis=0,
            concat_axis=0,
            tiled=True,
        ),
        lax.all_to_all(
            send_index.reshape(peers, slot_rows), "dp", split_axis=0, concat_axis=0, tiled=True
        ),
    )
    flat_index = recv_index.reshape(-1)
    rows_cols = (
        jnp.zeros((ROWS_DEV, local_width), jnp.bfloat16)
        .at[flat_index]
        .set(recv_rows.reshape(-1, local_width), mode="drop")
    )
    grads_cols = (
        jnp.zeros((ROWS_DEV, local_width), jnp.bfloat16)
        .at[flat_index]
        .set(recv_grads.reshape(-1, local_width), mode="drop")
    )
    qkv_full, out_full, gu_full, down_full = (
        lax.all_gather(w_qkv, "dp", axis=0, tiled=True),
        lax.all_gather(w_out, "dp", axis=1, tiled=True),
        lax.all_gather(w_gu, "dp", axis=0, tiled=True),
        lax.all_gather(w_down, "dp", axis=1, tiled=True),
    )
    cond_wide = cond.astype(jnp.float32)
    cond_sig = jax.nn.sigmoid(cond_wide)
    silu_cond = (cond_wide * cond_sig).astype(jnp.bfloat16)
    ada_rows = w_ada.shape[0]
    silu_all = lax.all_gather(silu_cond, "dp", axis=0, tiled=True)
    silu_own = lax.dynamic_slice_in_dim(silu_all, lax.axis_index("dp") * ada_rows, ada_rows, 1)
    mod_sums = jnp.einsum("id,dkc->ikc", silu_own, w_ada, preferred_element_type=jnp.float32)
    mod_part = (
        lax.psum_scatter(mod_sums, "dp", scatter_dimension=0, tiled=True)
        + b_ada.astype(jnp.float32)
    ).astype(jnp.bfloat16)
    rows_full, grads_full, mod_full = (
        lax.all_gather(rows_cols, "mp", axis=1, tiled=True),
        lax.all_gather(grads_cols, "mp", axis=1, tiled=True),
        lax.all_gather(mod_part, "mp", axis=2, tiled=True),
    )
    modulation = mod_full.astype(jnp.float32)
    shift_one = modulation[:, 0][:, None, :]
    scale_one = modulation[:, 1][:, None, :]
    gate_two = modulation[:, 5][:, None, :]
    resid = rows_full.astype(jnp.float32).reshape(blocks_here, BLOCK, D)
    normed_one, inv_one = norm_rows(resid)
    hidden_one = (normed_one * (1.0 + scale_one) + shift_one).astype(jnp.bfloat16)
    qkv = jnp.einsum("ibd,dkc->ibkc", hidden_one, qkv_full, preferred_element_type=jnp.float32)
    query = qkv[:, :, 0].reshape(blocks_here, BLOCK, heads_here, DH)
    keys = qkv[:, :, 1].reshape(blocks_here, BLOCK, heads_here, DH)
    value = qkv[:, :, 2].reshape(blocks_here, BLOCK, heads_here, DH)
    query_normed, query_inv = norm_rows(query)
    key_normed, key_inv = norm_rows(keys)
    cos_h, sin_h, cos_w, sin_w = angle_tables(item_grid, BLOCK, DH)
    query_low = (
        rotate(query_normed * q_gain, cos_h, sin_h, cos_w, sin_w, 1.0) * DH ** (-0.5)
    ).astype(jnp.bfloat16)
    key_low = rotate(key_normed * k_gain, cos_h, sin_h, cos_w, sin_w, 1.0).astype(jnp.bfloat16)
    value_low = value.astype(jnp.bfloat16)
    positions = lax.broadcasted_iota(jnp.int32, (blocks_here, BLOCK), 1)
    valid = positions < (item_grid[:, 0] * item_grid[:, 1])[:, None]
    key_ok = valid[:, None, None, :]
    valid_wide = valid.astype(jnp.float32)[:, :, None]
    valid_share = lax.dynamic_slice_in_dim(
        valid.astype(jnp.float32).reshape(ROWS_DEV), row_first, share, 0
    )[:, None]
    bin_onehot = (noise_bin[:, None] == jnp.arange(NBINS)[None, :]).astype(jnp.float32)
    bin_local = jnp.sum(bin_onehot, axis=0) * (model_rank == 0).astype(jnp.float32)

    def masked_scores():
        raw = jnp.einsum("iqhc,ikhc->ihqk", query_low, key_low, preferred_element_type=jnp.float32)
        return jnp.where(key_ok, raw, -1e30)

    scores = masked_scores()
    top = jnp.max(scores, axis=-1, keepdims=True)
    log_total = top + jnp.log(jnp.sum(jnp.exp(scores - top), axis=-1, keepdims=True))
    prob_low = jnp.exp(scores - log_total).astype(jnp.bfloat16)
    attn_low = jnp.einsum(
        "ihqk,ikhc->iqhc", prob_low, value_low, preferred_element_type=jnp.float32
    ).astype(jnp.bfloat16)
    out_heads = out_full.reshape(heads_here, DH, D)
    attn_part = jnp.einsum("iqhc,hcd->iqd", attn_low, out_heads, preferred_element_type=jnp.float32)

    def own_rows_of(values):
        return lax.dynamic_slice_in_dim(values.reshape(ROWS_DEV, D), row_first, share, 0)

    row_item = (row_first + jnp.arange(share)) // BLOCK
    item_onehot = (row_item[:, None] == jnp.arange(blocks_here)[None, :]).astype(jnp.float32)

    def per_item(values):
        return jnp.einsum("si,sd->id", item_onehot, values, precision=lax.Precision.HIGHEST)

    mod_rows = jnp.einsum("si,ikd->skd", item_onehot, modulation, precision=lax.Precision.HIGHEST)
    scale_one_r = mod_rows[:, 1]
    gate_one_r = mod_rows[:, 2]
    shift_two_r = mod_rows[:, 3]
    scale_two_r = mod_rows[:, 4]
    gate_two_r = mod_rows[:, 5]
    resid_share = own_rows_of(resid)
    normed_one_share = own_rows_of(normed_one)
    inv_one_share = lax.dynamic_slice_in_dim(inv_one.reshape(ROWS_DEV, 1), row_first, share, 0)
    attention_share = row_share(attn_part.reshape(ROWS_DEV, D))
    mid_share = resid_share + gate_one_r * attention_share
    normed_two_share, inv_two_share = norm_rows(mid_share)
    hidden_two_share = (normed_two_share * (1.0 + scale_two_r) + shift_two_r).astype(jnp.bfloat16)
    hidden_two = row_whole(hidden_two_share).reshape(blocks_here, BLOCK, D)
    gate_up = jnp.einsum("ibd,dkf->ibkf", hidden_two, gu_full, preferred_element_type=jnp.float32)
    gate_raw = gate_up[:, :, 0]
    up_raw = gate_up[:, :, 1]
    gate_sig = jax.nn.sigmoid(gate_raw)
    gate_act = gate_raw * gate_sig
    inner = (gate_act * up_raw).astype(jnp.bfloat16)
    feed_part = jnp.einsum("ibf,fd->ibd", inner, down_full, preferred_element_type=jnp.float32)
    feed_part, kept = (feed_part, (inner, up_raw, gate_raw, gate_sig, gate_act))
    feed_share = row_share(feed_part.reshape(ROWS_DEV, D))
    result_share = mid_share + gate_two_r * feed_share
    result_whole = row_whole(result_share.astype(jnp.bfloat16))
    squares = jnp.stack(
        [
            jnp.sum(valid_share * result_share * result_share),
            jnp.sum(valid_share * (gate_one_r * attention_share) ** 2),
            jnp.sum(valid_share * (gate_two_r * feed_share) ** 2),
        ]
    )
    square_total, valid_total, bin_total = lax.psum(
        (squares, jnp.sum(valid_share), bin_local), ("dp", "mp")
    )
    stats_value = jnp.sqrt(square_total / (valid_total * D))
    item_count = jnp.sum(bin_onehot * bin_total[None, :], axis=1)
    weight_value = blocks_here * peers / (NBINS * item_count)
    top_grad = grads_full.astype(jnp.float32).reshape(blocks_here, BLOCK, D) * (
        weight_value[:, None, None] * valid_wide
    )
    top_share = own_rows_of(top_grad)
    feed_grad = (gate_two * top_grad).astype(jnp.bfloat16)
    grad_gate_two = per_item(top_share * feed_share)
    inner, up_raw, gate_raw, gate_sig, gate_act = kept
    inner_grad = jnp.einsum("ibd,fd->ibf", feed_grad, down_full, preferred_element_type=jnp.float32)
    grad_down_part = jnp.einsum("ibf,ibd->fd", inner, feed_grad, preferred_element_type=jnp.float32)
    gate_grad = (inner_grad * up_raw * gate_sig * (1.0 + gate_raw * (1.0 - gate_sig))).astype(
        jnp.bfloat16
    )
    up_grad = (inner_grad * gate_act).astype(jnp.bfloat16)
    gate_up_grad = jnp.stack([gate_grad, up_grad], axis=2)
    grad_gu_part = jnp.einsum(
        "ibd,ibkf->dkf", hidden_two, gate_up_grad, preferred_element_type=jnp.float32
    )
    hidden_two_part = jnp.einsum(
        "ibkf,dkf->ibd", gate_up_grad, gu_full, preferred_element_type=jnp.float32
    )
    grad_down, grad_gu, hidden_two_part = (grad_down_part, grad_gu_part, hidden_two_part)
    h2_grad_share = row_share(hidden_two_part.reshape(ROWS_DEV, D))
    grad_shift_two = per_item(h2_grad_share)
    grad_scale_two = per_item(h2_grad_share * normed_two_share)
    mid_grad_share = top_share + norm_back(
        h2_grad_share * (1.0 + scale_two_r), normed_two_share, inv_two_share
    )
    attention_grad_share = (gate_one_r * mid_grad_share).astype(jnp.bfloat16)
    grad_gate_one = per_item(mid_grad_share * attention_share)
    attention_grad = row_whole(attention_grad_share).reshape(blocks_here, BLOCK, D)
    attn_low_grad = jnp.einsum(
        "iqd,hcd->iqhc", attention_grad, out_heads, preferred_element_type=jnp.float32
    ).astype(jnp.bfloat16)
    grad_out_part = jnp.einsum(
        "iqhc,iqd->hcd", attn_low, attention_grad, preferred_element_type=jnp.float32
    ).reshape(local_width, D)
    prob_full = jnp.exp(masked_scores() - log_total)
    prob_grad = jnp.einsum(
        "iqhc,ikhc->ihqk", attn_low_grad, value_low, preferred_element_type=jnp.float32
    )
    value_grad = jnp.einsum(
        "ihqk,iqhc->ikhc", prob_low, attn_low_grad, preferred_element_type=jnp.float32
    )
    score_grad = (
        prob_full * (prob_grad - jnp.sum(prob_full * prob_grad, axis=-1, keepdims=True))
    ).astype(jnp.bfloat16)
    query_rot_grad = jnp.einsum(
        "ihqk,ikhc->iqhc", score_grad, key_low, preferred_element_type=jnp.float32
    ) * DH ** (-0.5)
    key_rot_grad = jnp.einsum(
        "ihqk,iqhc->ikhc", score_grad, query_low, preferred_element_type=jnp.float32
    )
    query_scaled_grad = rotate(query_rot_grad, cos_h, sin_h, cos_w, sin_w, -1.0)
    key_scaled_grad = rotate(key_rot_grad, cos_h, sin_h, cos_w, sin_w, -1.0)
    qgain_local = jnp.sum(query_scaled_grad * query_normed, axis=(0, 1, 2))
    kgain_local = jnp.sum(key_scaled_grad * key_normed, axis=(0, 1, 2))
    query_grad = norm_back(query_scaled_grad * q_gain, query_normed, query_inv)
    key_grad = norm_back(key_scaled_grad * k_gain, key_normed, key_inv)
    qkv_grad = jnp.stack(
        [
            query_grad.reshape(blocks_here, BLOCK, local_width),
            key_grad.reshape(blocks_here, BLOCK, local_width),
            value_grad.reshape(blocks_here, BLOCK, local_width),
        ],
        axis=2,
    ).astype(jnp.bfloat16)
    grad_qkv_part = jnp.einsum(
        "ibd,ibkc->dkc", hidden_one, qkv_grad, preferred_element_type=jnp.float32
    )
    hidden_one_part = jnp.einsum(
        "ibkc,dkc->ibd", qkv_grad, qkv_full, preferred_element_type=jnp.float32
    )
    grad_out, grad_qkv, qgain_part, kgain_part, hidden_one_part = (
        grad_out_part,
        grad_qkv_part,
        qgain_local,
        kgain_local,
        hidden_one_part,
    )
    h1_grad_share = row_share(hidden_one_part.reshape(ROWS_DEV, D))
    grad_shift_one = per_item(h1_grad_share)
    grad_scale_one = per_item(h1_grad_share * normed_one_share)
    input_share = mid_grad_share + norm_back(
        h1_grad_share * (1.0 + scale_one_r), normed_one_share, inv_one_share
    )
    input_whole = row_whole(input_share.astype(jnp.bfloat16))
    mod_partial = jnp.stack(
        [
            grad_shift_one,
            grad_scale_one,
            grad_gate_one,
            grad_shift_two,
            grad_scale_two,
            grad_gate_two,
        ],
        axis=1,
    )
    mod_grad = lax.psum(mod_partial, "mp").astype(jnp.bfloat16)
    mod_grad_own = lax.dynamic_slice_in_dim(mod_grad, model_rank * local_width, local_width, 2)
    mod_all = lax.all_gather(mod_grad_own, "dp", axis=0, tiled=True)
    cond_part = jnp.einsum("ikc,dkc->id", mod_all, w_ada, preferred_element_type=jnp.float32)
    cond_sum = lax.psum(cond_part, "mp")
    cond_total = lax.all_to_all(
        cond_sum.reshape(peers, blocks_here, ada_rows), "dp", split_axis=0, concat_axis=0, tiled=True
    )
    cond_total = jnp.moveaxis(cond_total, 0, 1).reshape(blocks_here, peers * ada_rows)
    grad_cond = cond_total * cond_sig * (1.0 + cond_wide * (1.0 - cond_sig))
    grad_ada = jnp.einsum("ir,ikc->rkc", silu_own, mod_all, preferred_element_type=jnp.float32)
    grad_bada = jnp.sum(mod_all.astype(jnp.float32), axis=0)
    qgain_total, kgain_total = lax.psum((qgain_part, kgain_part), ("dp", "mp"))
    qkv_own, out_own, gu_own, down_own = (
        grad_share(grad_qkv, 0),
        grad_share(grad_out, 1),
        grad_share(grad_gu, 0),
        grad_share(grad_down, 1),
    )
    result_cols = lax.dynamic_slice_in_dim(result_whole, model_rank * local_width, local_width, 1)
    input_cols = lax.dynamic_slice_in_dim(input_whole, model_rank * local_width, local_width, 1)
    back_index = jnp.minimum(flat_index, ROWS_DEV - 1)
    back_rows = result_cols[back_index].reshape(peers, slot_rows, local_width)
    back_grads = input_cols[back_index].reshape(peers, slot_rows, local_width)
    returned_rows, returned_grads = (
        lax.all_to_all(back_rows, "dp", split_axis=0, concat_axis=0, tiled=True),
        lax.all_to_all(back_grads, "dp", split_axis=0, concat_axis=0, tiled=True),
    )
    pick = jnp.minimum(place, peers * slot_rows - 1)
    empty = jnp.zeros((), jnp.bfloat16)
    out_rows = jnp.where(live[:, None], returned_rows.reshape(-1, local_width)[pick], empty)
    out_grads = jnp.where(live[:, None], returned_grads.reshape(-1, local_width)[pick], empty)
    return (
        out_rows,
        out_grads,
        grad_cond,
        grad_ada,
        grad_bada,
        qkv_own,
        qgain_total,
        kgain_total,
        out_own,
        gu_own,
        down_own,
        stats_value,
    )


MESH = pl.DeviceIdType.MESH
f32 = jnp.float32
bf16 = jnp.bfloat16
LANE_INDEX = 288
META = 1152
PAD = 128


def nn(left, right):
    return jnp.dot(left, right, preferred_element_type=f32)


def nt(left, right):
    return lax.dot_general(left, right, (((1,), (1,)), ((), ())), preferred_element_type=f32)


def tn(left, right):
    return lax.dot_general(left, right, (((0,), (0,)), ((), ())), preferred_element_type=f32)


def loop(count, step):
    def run(index, carry):
        step(index)
        return carry

    lax.fori_loop(0, count, run, 0)


def at128(index, size):
    return pl.ds(pl.multiple_of(index, 128), size)


def at16(index, size):
    return pl.ds(pl.multiple_of(index, 16), size)


GROUPS = (("c0", 768), ("c1", 768), ("c2", 768), ("out", 256), ("qkv", 896))


def scratch_list():
    vm = pltpu.VMEM
    items = dict(
        sem=pltpu.SemaphoreType.DMA((132,)),
        arow=vm((1, 1280), f32),
        arec=vm((8, 1, 1280), f32),
        amat=vm((8, 1280), f32),
        xe=vm((64, 512), bf16),
        ids=vm((8, 1, 64), f32),
        idr=vm((8, 1, 64), f32),
        place=vm((512, 512), bf16),
        sx=vm((640, 256), bf16),
        rx=vm((640, 256), bf16),
        sg=vm((512, 256), bf16),
        rg=vm((512, 256), bf16),
        spread=vm((256, 512), bf16),
        rb=vm((4, 320, 256), bf16),
        gb=vm((4, 256, 256), bf16),
        pms=vm((8, 6, 1, 288), f32),
        pmr=vm((8, 6, 1, 288), f32),
        mdb=vm((4, 6, 1, 288), f32),
        modf=vm((8, 1152), f32),
        h1=vm((256, 1152), bf16),
        h1t=vm((1152, 256), bf16),
        w1=vm((1152, 896), bf16),
        wc0=vm((1152, 768), bf16),
        wc1=vm((1152, 768), bf16),
        wc2=vm((1152, 768), bf16),
        wp1=vm((144, 896), bf16),
        wqkv_in=vm((3, 144, 288), bf16),
        wgu_in=vm((144, 2, 768), bf16),
        wada_in=vm((6, 144, 288), bf16),
        wdn_in=vm((144, 768), bf16),
        wp=vm((3, 144, 768), bf16),
        wb=vm((1152, 256), bf16),
        wpb=vm((144, 256), bf16),
        qkv=vm((256, 1024), f32),
        qn=vm((4, 256, 128), f32),
        kn=vm((4, 256, 128), f32),
        qi=vm((4, 256, 1), f32),
        ki=vm((4, 256, 1), f32),
        ql=vm((4, 256, 128), bf16),
        kl=vm((4, 256, 128), bf16),
        vl=vm((4, 256, 128), bf16),
        pf=vm((4, 256, 256), f32),
        cosv=vm((256, 128), f32),
        sinv=vm((256, 128), f32),
        al1=vm((256, 32), bf16),
        al2=vm((256, 256), bf16),
        rsa=vm((256, 1152), bf16),
        rra=vm((3, 64, 1152), bf16),
        rta=vm((64, 1152), bf16),
        rsf=vm((256, 1152), bf16),
        rrf=vm((3, 64, 1152), bf16),
        rtf=vm((64, 1152), bf16),
        rsh2=vm((256, 1152), bf16),
        rrh2=vm((3, 64, 1152), bf16),
        rth2=vm((64, 1152), bf16),
        rsh1=vm((256, 1152), bf16),
        rrh1=vm((3, 64, 1152), bf16),
        rth1=vm((64, 1152), bf16),
        h2=vm((256, 1152), bf16),
        h2t=vm((1152, 256), bf16),
        ag=vm((256, 1152), bf16),
        agt=vm((1152, 256), bf16),
        h2sum=vm((256, 1152), f32),
        inner=vm((3, 256, 256), bf16),
        gug=vm((3, 256, 512), bf16),
        fg=vm((256, 1152), bf16),
        fgt=vm((1152, 256), bf16),
        da=vm((256, 384), f32),
        dqkv=vm((256, 864), bf16),
        share=vm((8, 64, 1152), f32),
        invs=vm((2, 64, 1), f32),
        gpart=vm((8, 1152), f32),
        ras=vm((4, 64, 256), bf16),
        rar=vm((4, 64, 256), bf16),
        ias=vm((4, 64, 384), bf16),
        iar=vm((4, 64, 384), bf16),
        bs=vm((512, 256), bf16),
        br=vm((512, 256), bf16),
        bgs=vm((640, 256), bf16),
        bgr=vm((640, 256), bf16),
        hs=vm((4, 7, 1, 288), f32),
        hr=vm((4, 7, 1, 288), f32),
        gs=vm((7, 1, 288), f32),
        grec=vm((8, 7, 1, 288), f32),
        mod_all=vm((6, 8, 288), f32),
        cps=vm((8, 144), f32),
        cpr=vm((4, 8, 144), f32),
        cts=vm((8, 1, 144), f32),
        ctr=vm((8, 1, 144), f32),
    )
    for name, width in GROUPS:
        items["cs_" + name] = vm((4, 144, width), bf16)
        items["cr_" + name] = vm((4, 144, width), bf16)
        items["xs_" + name] = vm((2, 144, width), bf16)
        items["xr_" + name] = vm((2, 144, width), bf16)
        items["zs_" + name] = vm((2, 144, width), bf16)
        items["zr_" + name] = vm((2, 144, width), bf16)
    return items


class Refs:
    pass


def block_kernel(
    names, xt, ct, dest, count, grid, bin, cond, wada, bada, wqkv, qg, kg, woin, wgu, wdn, outt, gint, gcond, gada, gbada, gqkv, gqg, gkg, gout, ggu, gdn, stats, *scratch
):
    r = Refs()
    r.__dict__.update(locals())
    for name, ref in zip(names, scratch):
        setattr(r, name, ref)
    dp = lax.axis_index("dp")
    mp = lax.axis_index("mp")
    z, x, y, c = dp // 2, dp % 2, mp // 2, mp % 2
    zh, zl = z // 2, z % 2
    item = (2 * zh + c) * 2 + x
    tp = y * 2 + zl
    home = zl == c
    away = zl != c
    sem = r.sem
    taken = [0]

    def sems(count):
        first = taken[0]
        taken[0] += count
        return first

    def device(zz, xx, yy, cc):
        return (zz * 2 + xx, yy * 2 + cc)

    def worker(index, part):
        zi, xi = index // 2, index % 2
        return device(2 * (zi // 2) + part % 2, xi, part // 2, zi % 2)

    def mate(step):
        return device(2 * zh + (zl ^ (step & 1)), x, y ^ (step >> 1), c)

    def remote(src, dst, ss, rs, dev):
        return pltpu.make_async_remote_copy(
            src_ref=src,
            dst_ref=dst,
            send_sem=sem.at[ss],
            recv_sem=sem.at[rs],
            device_id=dev,
            device_id_type=MESH,
        )

    pending = []

    def start(src, dst, ss, rs, dev):
        remote(src, dst, ss, rs, dev).start()

    def start_unless(same, src, dst, ss, rs, dev):
        @pl.when(same)
        def _():
            pltpu.make_async_copy(src, dst, sem.at[rs]).start()

        @pl.when(jnp.logical_not(same))
        def _():
            remote(src, dst, ss, rs, dev).start()

    def arrived(dst, rs):
        pltpu.make_async_copy(dst, dst, sem.at[rs]).wait()

    def sent(ref, ss):
        pending.append(lambda: arrived(ref, ss))

    def sent_or_kept(size, count, ss):
        def finish():
            @pl.when(home)
            def _():
                arrived(size(count - 1), ss)

            @pl.when(away)
            def _():
                arrived(size(count), ss)

        pending.append(finish)

    def to_workers(source, target, size):
        base = sems(2)
        for step in range(8):
            index = (dp + step) % 8
            args = (source(index), target(dp), base, base + 1, worker(index, mp))
            if step == 0:
                start_unless(home, *args)
            else:
                start(*args)
        sent_or_kept(size, 8, base)
        return base + 1

    def to_homes(source, target, size):
        base = sems(2)
        for step in range(8):
            index = (dp + step) % 8
            args = (source(index), target(item), base, base + 1, (index, tp))
            if step == 0:
                start_unless(home, *args)
            else:
                start(*args)
        sent_or_kept(size, 8, base)
        return base + 1

    def to_others(source, target, size):
        base = sems(2)
        for step in range(1, 8):
            index = (dp + step) % 8
            start(source(index), target, base, base + 1, (index, mp))
        sent(size, base)
        return base + 1

    def slots64(ref):
        return lambda i: ref.at[at16(i * 64, 64)]

    def first64(ref):
        return lambda n: ref.at[pl.ds(0, 64 * n)]

    def slots80(ref):
        return lambda i: ref.at[at16(i * 80, 80)]

    def first80(ref):
        return lambda n: ref.at[pl.ds(0, 80 * n)]

    def fold(ref, main, rest):
        for i in range(8):
            ref[80 * i : 80 * i + 64, :] = main[64 * i : 64 * i + 64, :]
            for g in range(4):
                first_row = 64 * i + 16 * g
                ref[80 * i + 64 : 80 * i + 80, 64 * g : 64 * g + 64] = rest[first_row : first_row + 16, :]

    def unfold(ref):
        main = [ref[80 * i : 80 * i + 64, :] for i in range(8)]
        rest = [
            ref[80 * i + 64 : 80 * i + 80, 64 * g : 64 * g + 64] for i in range(8) for g in range(4)
        ]
        return jnp.concatenate(main, axis=0), jnp.concatenate(rest, axis=0)

    def head_of(ref):
        return lambda n: ref.at[pl.ds(0, n)]

    groups = {
        "attn": (r.wp1, r.w1),
        "wo": (r.wpb, r.wb),
        "c0": (r.wp.at[0], r.wc0),
        "c1": (r.wp.at[1], r.wc1),
        "c2": (r.wp.at[2], r.wc2),
    }
    w_base = {g: sems(6) for g in groups}

    def slot(ref, index):
        return ref.at[at16(index * 144, 144)]

    for g in groups:
        whole = groups[g][1]
        sent_or_kept(lambda n, whole=whole: whole.at[pl.ds(0, 144 * n)], 8, w_base[g] + 5)

    def gather_z(g, rels=(1, 0)):
        src, full = groups[g]
        base = w_base[g]
        for rel in rels:
            zt = c + 2 * (zh ^ rel)
            args = (src, slot(full, dp), base + 5, base + rel, device(zt, x, y, zl))
            if rel == 0:
                start_unless(home, *args)
            else:
                start(*args)

    def gather_x(g, rel):
        full, base = groups[g][1], w_base[g]
        mine = slot(full, (c + 2 * (zh ^ rel)) * 2 + x)
        arrived(mine, base + rel)
        start(mine, mine, base + 5, base + 2 + rel, device(z, 1 - x, y, c))
        start(mine, mine, base + 5, base + 4, device(z, x, y, 1 - c))

    def gather_core(g, rel):
        full, base = groups[g][1], w_base[g]
        mine = slot(full, (c + 2 * (zh ^ rel)) * 2 + 1 - x)
        arrived(mine, base + 2 + rel)
        start(mine, mine, base + 5, base + 4, device(z, x, y, 1 - c))

    def gather_done(g):
        arrived(groups[g][1].at[pl.ds(0, 144 * 4)], w_base[g] + 4)

    z_mate = device(2 * zh + 1 - zl, x, y, c)
    y_mate = device(z, x, 1 - y, c)

    class Gather:
        def __init__(self, view, size):
            self.view, self.size, self.base = view, size, sems(3)
            mine = view(tp)
            start(mine, mine, self.base, self.base + 1, z_mate)
            start(mine, mine, self.base, self.base + 2, y_mate)
            sent(size(3), self.base)

        def relay(self):
            other = self.view(tp ^ 1)
            arrived(other, self.base + 1)
            start(other, other, self.base, self.base + 2, y_mate)

        def done(self):
            arrived(self.size(2), self.base + 2)

    class Scatter:
        def __init__(self, name):
            self.base = sems(3)
            self.sent, self.rec, self.sum = (getattr(r, k + name) for k in ("rs", "rr", "rt"))
            start(self.view(tp ^ 3), self.rec.at[0], self.base, self.base + 1, y_mate)
            start(self.view(tp ^ 2), self.rec.at[1], self.base, self.base + 2, y_mate)
            sent(self.rec, self.base)

        def view(self, t):
            return self.sent.at[at16(t * 64, 64)]

        def relay(self):
            arrived(self.rec.at[0], self.base + 1)
            both = self.view(tp ^ 1)[...].astype(f32) + self.rec[0].astype(f32)
            self.sum[...] = both.astype(bf16)
            start(self.sum, self.rec.at[2], self.base, self.base + 2, z_mate)

        def total(self):
            arrived(self.rec.at[pl.ds(1, 2)], self.base + 2)
            total = self.view(tp)[...].astype(f32) + self.rec[1].astype(f32)
            return total + self.rec[2].astype(f32)

    def rows_view(buf):
        return lambda t: buf.at[at16(t * 64, 64)]

    def mates_send(source, target, size):
        base = sems(2)
        for step in range(1, 4):
            start(source(tp ^ step), target, base, base + 1, mate(step))
        sent(size, base)
        return base + 1

    g_base = {name: sems(9) for name, _ in GROUPS}

    def block(name, s):
        rows = at16(s * 144, 144)
        if name == "out":
            return nn(r.agt[rows, :], r.al2[...])
        if name == "qkv":
            return jnp.concatenate(
                [nn(r.h1t[rows, :], r.dqkv[...]), nn(r.agt[rows, :], r.al1[...])], axis=-1
            )
        k = int(name[1:])
        return jnp.concatenate(
            [nn(r.h2t[rows, :], r.gug[k]), nn(r.fgt[rows, :], r.inner[k])], axis=-1
        )

    for name, _ in GROUPS:
        buf = getattr(r, "cs_" + name)
        sent(buf, g_base[name] + 7)
        sent_or_kept(head_of(buf), 4, g_base[name] + 8)

    def reduce_core(name):
        base = g_base[name]
        cs, cr = getattr(r, "cs_" + name), getattr(r, "cr_" + name)
        for xx in (1 - x, x):
            for rel in (1 - zh, zh):
                q = 2 * rel + xx
                cs[q] = block(name, (1 - c + 2 * rel) * 2 + xx).astype(bf16)
                start(cs.at[q], cr.at[q], base + 7, base + q, device(z, x, y, 1 - c))

    def reduce_x(name, far):
        base = g_base[name]
        cr, xs, xr = (getattr(r, k + name) for k in ("cr_", "xs_", "xr_"))
        rel = zh ^ far
        q = 2 * rel + 1 - x
        part = block(name, (c + 2 * rel) * 2 + 1 - x)
        arrived(cr.at[q], base + q)
        xs[rel] = (part + cr[q].astype(f32)).astype(bf16)
        start(xs.at[rel], xr.at[rel], base + 8, base + 4 + rel, device(z, 1 - x, y, c))

    def reduce_z(name, far):
        base = g_base[name]
        cr, xr, zs, zr = (getattr(r, k + name) for k in ("cr_", "xr_", "zs_", "zr_"))
        rel = zh ^ far
        q = 2 * rel + x
        part = block(name, (c + 2 * rel) * 2 + x)
        arrived(cr.at[q], base + q)
        part = part + cr[q].astype(f32)
        arrived(xr.at[rel], base + 4 + rel)
        zs[far] = (part + xr[rel].astype(f32)).astype(bf16)
        args = (zs.at[far], zr.at[zh], base + 8, base + 6, device(c + 2 * rel, x, y, zl))
        if far == 0:
            start_unless(home, *args)
        else:
            start(*args)

    def reduce_end(name):
        zr = getattr(r, "zr_" + name)
        arrived(zr, g_base[name] + 6)
        return zr[0].astype(f32) + zr[1].astype(f32)

    def transpose(src, dst):
        def step(j):
            dst[at128(j * 128, 128), :] = src[:, at128(j * 128, 128)].T

        loop(9, step)

    lane128 = lax.broadcasted_iota(jnp.int32, (1, PAD), 1)
    head_lane = lane128 < 72
    quarter = lane128 // 18
    even = quarter % 2 == 0

    def swap(v):
        return jnp.where(even, pltpu.roll(v, PAD - 18, 1), pltpu.roll(v, 18, 1))

    def norm_of(v):
        inv = lax.rsqrt(jnp.mean(v * v, axis=-1, keepdims=True) + epsilon)
        return v * inv, inv

    def back(g, normed, inv):
        return inv * (g - normed * jnp.mean(g * normed, axis=-1, keepdims=True))

    barrier = pltpu.get_barrier_semaphore()
    for i in range(8):
        for j in range(4):
            if i or j:
                pl.semaphore_signal(
                    barrier, inc=1, device_id=((dp + i) % 8, mp ^ j), device_id_type=MESH
                )

    late = []
    for src, dst in (
        (r.wqkv, r.wqkv_in), (r.wgu, r.wgu_in), (r.wada, r.wada_in), (r.wdn, r.wdn_in)
    ):
        late.append(pltpu.make_async_copy(src, dst, sem.at[sems(1)]))
        late[-1].start()
    cond = r.cond[...].astype(f32)
    sig_c = jax.nn.sigmoid(cond)
    r.arow[0:1, 0:META] = (cond * sig_c).astype(bf16).astype(f32)
    meta = jnp.where(lane128 == 0, r.bin[0].astype(f32), 0.0)
    meta = jnp.where(lane128 == 1, r.grid[0, 0].astype(f32), meta)
    meta = jnp.where(lane128 == 2, r.grid[0, 1].astype(f32), meta)
    r.arow[0:1, META : META + 128] = meta
    r.arec[dp] = r.arow[...]

    dest = r.dest[...]
    lane512 = lax.broadcasted_iota(jnp.int32, (1, 512), 1)
    live = lane512 < r.count[0]
    target = dest >> 8
    within = dest & 255
    owner = lax.broadcasted_iota(jnp.int32, (8, 512), 0)
    member = jnp.where((owner == target) & live, 1.0, 0.0)
    upper = lax.broadcasted_iota(jnp.int32, (512, 512), 0) <= lax.broadcasted_iota(
        jnp.int32, (512, 512), 1
    )
    running = nn(member.astype(bf16), jnp.where(upper, 1.0, 0.0).astype(bf16))
    rank = jnp.sum(running * member, axis=0, keepdims=True).astype(jnp.int32) - 1
    spot = jnp.where(live, target * 64 + rank, -1)
    slots = lax.broadcasted_iota(jnp.int32, (512, 512), 0)
    r.place[...] = jnp.where(slots == spot, 1.0, 0.0).astype(bf16)
    r.xe[0:32, :] = r.xt[256:288, :]
    r.xe[32:64, :] = r.ct[256:288, :]
    fold(
        r.sx,
        nt(r.place[...], r.xt[0:256, :]).astype(bf16),
        nt(r.place[...], r.xe[...]).astype(bf16),
    )
    named = jnp.broadcast_to((within + 1).astype(f32), (8, 512)).astype(bf16)
    named = nt(named, r.place[...])
    for i in range(8):
        r.ids[i] = named[0:1, 64 * i : 64 * i + 64]

    pl.semaphore_wait(barrier, 31)
    a_in = to_others(lambda i: r.arow, r.arec.at[dp], r.arec.at[pl.ds(0, 7)])
    id_in = to_workers(lambda i: r.ids.at[i], lambda i: r.idr.at[i], head_of(r.idr))
    x_in = to_workers(slots80(r.sx), slots80(r.rx), first80(r.rx))
    late[0].wait()
    late[1].wait()
    late[3].wait()
    for p in range(3):
        r.wp1[:, 288 * p : 288 * p + 288] = r.wqkv_in[p]
    r.wp1[:, 864:896] = r.woin[:, 0:32]
    r.wpb[...] = r.woin[:, 32:288]
    for k in range(3):
        r.wp[k, :, 0:256] = r.wgu_in[:, 0, 256 * k : 256 * k + 256]
        r.wp[k, :, 256:512] = r.wgu_in[:, 1, 256 * k : 256 * k + 256]
        r.wp[k, :, 512:768] = r.wdn_in[:, 256 * k : 256 * k + 256]
    r.sg[...] = nt(r.place[...], r.ct[0:256, :]).astype(bf16)

    arrived(r.arec.at[pl.ds(0, 7)], a_in)
    late[2].wait()
    for i in range(8):
        r.amat[i : i + 1, :] = r.arec[i]
    pick = lax.broadcasted_iota(jnp.int32, (1152, 144), 0) == (
        lax.broadcasted_iota(jnp.int32, (1152, 144), 1) + 144 * dp
    )
    silu_own = nn(r.amat[:, 0:META].astype(bf16), jnp.where(pick, 1.0, 0.0).astype(bf16)).astype(bf16)
    first = (dp == 0).astype(f32)
    for k in range(6):
        part = nn(silu_own, r.wada_in[k]) + first * r.bada[k : k + 1, :].astype(f32)
        for i in range(8):
            r.pms[i, k] = part[i : i + 1, :]
    m_in = to_workers(lambda i: r.pms.at[i], lambda i: r.pmr.at[i], head_of(r.pmr))
    gather_z("attn")
    gather_z("wo")

    about = r.arec[item]
    height = about[:, META + 1 : META + 2]
    width = about[:, META + 2 : META + 3]
    bins = r.amat[:, META : META + 1]
    alike = jnp.sum(
        jnp.where(bins == about[:, META : META + 1], 1.0, 0.0), axis=0, keepdims=True
    )
    weight = 8.0 / (NBINS * alike)
    spots = lax.broadcasted_iota(jnp.int32, (256, 1), 0).astype(f32)
    high = jnp.floor((spots + 0.5) / width)
    wide = spots - high * width
    freq = jnp.exp(-math.log(10000.0) * (lane128 - 18 * quarter).astype(f32) / 18.0)
    angle = jnp.where(quarter < 2, high, wide) * freq
    r.cosv[...] = jnp.where(head_lane, jnp.cos(angle), 0.0)
    r.sinv[...] = jnp.where(head_lane, jnp.where(even, -jnp.sin(angle), jnp.sin(angle)), 0.0)
    used = height * width
    key_ok = lax.broadcasted_iota(jnp.int32, (1, 256), 1).astype(f32) < used
    row_first = (tp * 64).astype(f32)
    share_spots = lax.broadcasted_iota(jnp.int32, (64, 1), 0).astype(f32) + row_first
    valid_share = jnp.where(share_spots < used, 1.0, 0.0)

    arrived(r.idr, id_in)
    number = jnp.concatenate([r.idr[i] for i in range(8)], axis=-1).astype(jnp.int32)
    r.spread[...] = jnp.where(
        number == lax.broadcasted_iota(jnp.int32, (256, 512), 0) + 1, 1.0, 0.0
    ).astype(bf16)
    arrived(r.rx, x_in)
    main, rest = unfold(r.rx)
    r.rb[tp, 0:256, :] = nn(r.spread[...], main).astype(bf16)
    rest = nn(r.spread[...], rest).astype(bf16)
    for i in range(4):
        for g in range(4):
            first_row = 64 * i + 16 * g
            r.rb[tp, 256 + 16 * i : 272 + 16 * i, 64 * g : 64 * g + 64] = rest[first_row : first_row + 16, :]
    rb_all = Gather(lambda t: r.rb.at[t], head_of(r.rb))

    gather_x("attn", 0)
    gather_x("attn", 1)
    arrived(r.pmr, m_in)
    total = r.pmr[0]
    for s in range(1, 8):
        total = total + r.pmr[s]
    r.mdb[tp] = total.astype(bf16).astype(f32)
    mdb_all = Gather(lambda t: r.mdb.at[t], head_of(r.mdb))
    rb_all.relay()
    mdb_all.relay()
    t_in = to_workers(slots64(r.sg), slots64(r.rg), first64(r.rg))
    gather_z("c0")
    gather_z("c1")
    gather_core("attn", 0)
    gather_core("attn", 1)

    gather_x("wo", 0)
    gather_x("wo", 1)
    rb_all.done()
    mdb_all.done()
    for k in range(6):
        for t in range(4):
            r.modf[k : k + 1, 288 * t : 288 * t + 288] = r.mdb[t, k]

    def left_over(t, start):
        piece = r.rb[t, at16(256 + start // 4, 16), :].astype(f32)
        return jnp.concatenate([piece[:, 64 * g : 64 * g + 64] for g in range(4)], axis=0)

    def joined(start):
        parts = []
        for t in range(4):
            parts.append(r.rb[t, at16(start, 64), :].astype(f32))
            parts.append(left_over(t, start)[:, 0:32])
        return jnp.concatenate(parts, axis=-1)

    def joined_grad(start):
        parts = []
        for t in range(4):
            parts.append(r.gb[t, at16(start, 64), :].astype(f32))
            parts.append(left_over(t, start)[:, 32:64])
        return jnp.concatenate(parts, axis=-1)

    def first_hidden(i):
        normed, _ = norm_of(joined(i * 64))
        shift, scale = r.modf[0:1, :], r.modf[1:2, :]
        r.h1[at16(i * 64, 64), :] = (normed * (1.0 + scale) + shift).astype(bf16)

    loop(4, first_hidden)
    RESID, NORM1, ATT, MID, NORM2, TOP, MIDG = range(7)
    mine = joined(tp * 64)
    normed, inv = norm_of(mine)
    r.share[RESID] = mine
    r.share[NORM1] = normed
    r.invs[0] = inv
    gather_done("attn")

    def project(j):
        r.qkv[:, at128(j * 256, 256)] = nn(r.h1[...], r.w1[:, at128(j * 256, 256)])

    loop(3, project)
    r.qkv[:, 768:896] = nn(r.h1[...], r.w1[:, 768:896])

    gather_x("c0", 0)
    gather_core("wo", 0)
    gather_core("wo", 1)
    scale_q = 72 ** (-0.5)
    pad = jnp.zeros((1, PAD - 72), f32)
    gains = {k: jnp.concatenate([g[...], pad], axis=-1) for k, g in (("q", r.qg), ("k", r.kg))}
    def turn_heads(h):
        for kind, offset, normed_ref, inv_ref, low_ref in (
            ("q", 0, r.qn, r.qi, r.ql),
            ("k", 288, r.kn, r.ki, r.kl),
        ):
            lane = offset + 72 * h
            v = jnp.where(head_lane, r.qkv[:, lane : lane + 128], 0.0)
            inv = lax.rsqrt(jnp.sum(v * v, axis=-1, keepdims=True) * (1.0 / 72) + epsilon)
            v = v * inv
            normed_ref[h] = v
            inv_ref[h] = inv
            v = v * gains[kind]
            v = v * r.cosv[...] + swap(v) * r.sinv[...]
            if kind == "q":
                v = v * scale_q
            low_ref[h] = v.astype(bf16)
        lane = 576 + 72 * h
        r.vl[h] = jnp.where(head_lane, r.qkv[:, lane : lane + 128], 0.0).astype(bf16)

    turn_heads(0)
    turn_heads(1)
    turn_heads(2)
    turn_heads(3)
    def attend(h):
        scores = jnp.where(key_ok, nt(r.ql[h], r.kl[h]), -1e30)
        scores = jnp.exp(scores - jnp.max(scores, axis=-1, keepdims=True))
        prob = scores / jnp.sum(scores, axis=-1, keepdims=True)
        r.pf[h] = prob
        low = nn(prob.astype(bf16), r.vl[h]).astype(bf16)
        if h == 0:
            r.al1[...] = low[:, 0:32]
            r.al2[:, 0:40] = low[:, 32:72]
        else:
            r.al2[:, 72 * h - 32 : 72 * h + 40] = low[:, 0:72]

    attend(0)
    attend(1)
    attend(2)
    attend(3)

    gather_done("wo")

    def project_out(j):
        rows = at128(j * 384, 384)
        part = nt(r.al2[...], r.wb[rows, :]) + nt(r.al1[...], r.w1[rows, 864:896])
        r.rsa[:, rows] = part.astype(bf16)

    loop(3, project_out)
    sum_a = Scatter("a")
    arrived(r.rg, t_in)
    r.gb[tp] = nn(r.spread[...], r.rg[...]).astype(bf16)
    gb_all = Gather(lambda t: r.gb.at[t], head_of(r.gb))
    sum_a.relay()

    gather_z("c2", (1,))
    gather_x("c0", 1)
    gather_core("c0", 0)
    gather_x("c1", 0)
    gb_all.relay()
    gather_x("c1", 1)
    attention = sum_a.total()
    r.share[ATT] = attention
    middle = r.share[RESID] + r.modf[2:3, :] * attention
    r.share[MID] = middle
    normed, inv = norm_of(middle)
    r.share[NORM2] = normed
    r.invs[1] = inv
    r.h2[at16(tp * 64, 64), :] = (normed * (1.0 + r.modf[4:5, :]) + r.modf[3:4, :]).astype(bf16)
    h2_all = Gather(rows_view(r.h2), first64(r.h2))
    gather_z("c2", (0,))
    gather_core("c0", 1)
    h2_all.relay()
    gather_x("c2", 0)
    gather_x("c2", 1)
    gather_core("c1", 0)
    gather_core("c1", 1)
    transpose(r.h1, r.h1t)
    chunks = (r.wc0, r.wc1, r.wc2)

    def swiglu(k):
        full = chunks[k]
        gate = nn(r.h2[...], full[:, 0:256])
        up = nn(r.h2[...], full[:, 256:512])
        grad = nn(r.fg[...], full[:, 512:768])
        sig = jax.nn.sigmoid(gate)
        act = gate * sig
        r.inner[k] = (act * up).astype(bf16)
        r.gug[k, :, 0:256] = (grad * up * sig * (1.0 + gate * (1.0 - sig))).astype(bf16)
        r.gug[k, :, 256:512] = (grad * act).astype(bf16)

    def hidden_back(k):
        full = chunks[k]

        def step(j):
            rows = at128(j * 384, 384)
            part = nt(r.gug[k], full[rows, 0:512])
            if k > 0:
                part = part + r.h2sum[:, rows]
            if k < 2:
                r.h2sum[:, rows] = part
            else:
                r.rsh2[:, rows] = part.astype(bf16)

        loop(3, step)

    gb_all.done()
    def feed_rows(i):
        rows = lax.broadcasted_iota(jnp.int32, (64, 1), 0).astype(f32) + (i * 64).astype(f32)
        factor = jnp.where(rows < used, weight, 0.0)
        r.fg[at16(i * 64, 64), :] = (joined_grad(i * 64) * factor * r.modf[5:6, :]).astype(bf16)

    loop(4, feed_rows)
    r.share[TOP] = joined_grad(tp * 64) * (weight * valid_share)
    transpose(r.fg, r.fgt)

    h2_all.done()
    gather_done("c0")
    swiglu(0)
    transpose(r.h2, r.h2t)
    reduce_core("c0")
    gather_core("c2", 0)
    gather_done("c1")
    swiglu(1)
    reduce_x("c0", 1)
    reduce_x("c0", 0)
    reduce_core("c1")
    gather_core("c2", 1)
    hidden_back(0)
    hidden_back(1)
    reduce_x("c1", 1)
    gather_done("c2")
    swiglu(2)
    hidden_back(2)
    sum_h2 = Scatter("h2")
    reduce_z("c0", 1)
    reduce_x("c1", 0)
    reduce_core("c2")
    reduce_x("c2", 1)
    reduce_x("c2", 0)
    sum_h2.relay()
    reduce_z("c0", 0)

    def feed_out(j):
        rows = at128(j * 384, 384)
        part = nt(r.inner[0], r.wc0[rows, 512:768])
        part = part + nt(r.inner[1], r.wc1[rows, 512:768])
        part = part + nt(r.inner[2], r.wc2[rows, 512:768])
        r.rsf[:, rows] = part.astype(bf16)

    loop(3, feed_out)
    sum_f = Scatter("f")
    grad_h2 = sum_h2.total()
    normed = r.share[NORM2]
    r.gpart[3:4, :] = jnp.sum(grad_h2, axis=0, keepdims=True)
    r.gpart[4:5, :] = jnp.sum(grad_h2 * normed, axis=0, keepdims=True)
    mid_grad = r.share[TOP] + back(grad_h2 * (1.0 + r.modf[4:5, :]), normed, r.invs[1])
    r.share[MIDG] = mid_grad
    r.gpart[2:3, :] = jnp.sum(mid_grad * r.share[ATT], axis=0, keepdims=True)
    r.ag[at16(tp * 64, 64), :] = (r.modf[2:3, :] * mid_grad).astype(bf16)
    ag_all = Gather(rows_view(r.ag), first64(r.ag))
    sum_f.relay()

    reduce_z("c1", 1)
    reduce_z("c1", 0)
    ag_all.relay()
    reduce_z("c2", 1)
    def total_of(v):
        return jnp.sum(jnp.sum(v, axis=0, keepdims=True), axis=1, keepdims=True)

    squares = []
    kept = []

    def result_part():
        feed = sum_f.total()
        fed = r.modf[5:6, :] * feed
        result = r.share[MID] + fed
        r.gpart[5:6, :] = jnp.sum(r.share[TOP] * feed, axis=0, keepdims=True)
        att = r.modf[2:3, :] * r.share[ATT]

        squares[:] = [total_of(valid_share * v * v) for v in (result, att, fed)]
        low_result = result.astype(bf16)
        for t in range(4):
            r.ras[t] = low_result[:, 288 * t : 288 * t + 256]
            r.ias[t, :, 320:352] = low_result[:, 288 * t + 256 : 288 * t + 288]
        r.rar[tp] = r.ras[tp]
        kept.append(mates_send(lambda t: r.ras.at[t], r.rar.at[tp], r.rar.at[pl.ds(0, 3)]))

    def rows_part():
        arrived(r.rar.at[pl.ds(0, 3)], kept[0])
        rar = jnp.concatenate([r.rar[t] for t in range(4)], axis=0)
        r.bs[...] = tn(r.spread[...], rar).astype(bf16)
        kept.append(to_homes(slots64(r.bs), slots64(r.br), first64(r.br)))


    ag_all.done()
    r.da[:, 0:32] = nn(r.ag[...], r.w1[:, 864:896])
    r.da[:, 32:288] = nn(r.ag[...], r.wb[...])
    result_part()
    transpose(r.ag, r.agt)

    reduce_core("out")
    sums = [jnp.zeros((1, PAD), f32), jnp.zeros((1, PAD), f32)]

    def attend_back(h):
        grad = jnp.where(head_lane, r.da[:, 72 * h : 72 * h + 128], 0.0).astype(bf16)
        prob = r.pf[h]
        prob_grad = nt(grad, r.vl[h])
        mixed = jnp.sum(prob * prob_grad, axis=-1, keepdims=True)
        score = (prob * (prob_grad - mixed)).astype(bf16)
        value_grad = tn(prob.astype(bf16), grad)
        r.dqkv[:, 576 + 72 * h : 648 + 72 * h] = value_grad[:, 0:72].astype(bf16)
        for kind, offset, normed_ref, inv_ref in (
            ("q", 0, r.qn, r.qi),
            ("k", 288, r.kn, r.ki),
        ):
            if kind == "q":
                turned = nn(score, r.kl[h]) * scale_q
            else:
                turned = tn(score, r.ql[h])
            turned = turned * r.cosv[...] - swap(turned) * r.sinv[...]
            normed = normed_ref[h]
            along = jnp.sum(turned * normed, axis=0, keepdims=True)
            if kind == "q":
                sums[0] = sums[0] + along
            else:
                sums[1] = sums[1] + along
            g = turned * gains[kind]
            mean = jnp.sum(g * normed, axis=-1, keepdims=True) * (1.0 / 72)
            g = inv_ref[h] * (g - normed * mean)
            r.dqkv[:, offset + 72 * h : offset + 72 * h + 72] = g[:, 0:72].astype(bf16)

    attend_back(0)
    reduce_x("out", 1)
    reduce_x("out", 0)
    attend_back(1)
    reduce_z("c2", 0)
    attend_back(2)
    rows_part()
    reduce_z("out", 1)
    attend_back(3)
    def first_back(j):
        r.rsh1[:, at128(j * 384, 384)] = nt(r.dqkv[...], r.w1[at128(j * 384, 384), 0:864]).astype(bf16)

    loop(3, first_back)
    sum_h1 = Scatter("h1")
    reduce_z("out", 0)
    reduce_core("qkv")
    reduce_x("qkv", 1)
    reduce_x("qkv", 0)
    sum_h1.relay()
    grad_h1 = sum_h1.total()
    normed = r.share[NORM1]
    r.gpart[0:1, :] = jnp.sum(grad_h1, axis=0, keepdims=True)
    r.gpart[1:2, :] = jnp.sum(grad_h1 * normed, axis=0, keepdims=True)
    in_grad = r.share[MIDG] + back(grad_h1 * (1.0 + r.modf[1:2, :]), normed, r.invs[0])
    low_grad = in_grad.astype(bf16)
    for t in range(4):
        r.ias[t, :, 0:288] = low_grad[:, 288 * t : 288 * t + 288]
    numbers = jnp.concatenate(
        [sums[0][:, 0:72], sums[1][:, 0:72], squares[0], squares[1], squares[2],
         total_of(valid_share), jnp.zeros((1, 288 - 148), f32)],
        axis=-1,
    )
    for t in range(4):
        for k in range(6):
            r.hs[t, k] = r.gpart[k : k + 1, 288 * t : 288 * t + 288]
        r.hs[t, 6] = numbers
    r.hr[tp] = r.hs[tp]
    h_in = mates_send(lambda t: r.hs.at[t], r.hr.at[tp], r.hr.at[pl.ds(0, 3)])
    r.iar[tp] = r.ias[tp]
    ia_in = mates_send(lambda t: r.ias.at[t], r.iar.at[tp], r.iar.at[pl.ds(0, 3)])

    arrived(r.hr.at[pl.ds(0, 3)], h_in)
    total = r.hr[0] + r.hr[1] + r.hr[2] + r.hr[3]
    for k in range(6):
        r.gs[k] = total[k].astype(bf16).astype(f32)
    r.gs[6] = total[6]
    g2_in = to_homes(lambda i: r.gs, lambda i: r.grec.at[i], head_of(r.grec))
    reduce_z("qkv", 1)
    arrived(r.iar.at[pl.ds(0, 3)], ia_in)
    iar = jnp.concatenate([r.iar[t] for t in range(4)], axis=0)
    rest = jnp.concatenate([iar[:, 256:288], iar[:, 320:352]], axis=-1)
    fold(
        r.bgs,
        tn(r.spread[...], iar[:, 0:256]).astype(bf16),
        tn(r.spread[...], rest).astype(bf16),
    )
    bg_in = to_homes(slots80(r.bgs), slots80(r.bgr), first80(r.bgr))
    reduce_z("qkv", 0)
    arrived(r.grec, g2_in)
    cond_part = jnp.zeros((8, 144), f32)
    for k in range(6):
        grads = jnp.concatenate([r.grec[i, k] for i in range(8)], axis=0)
        r.mod_all[k] = grads
        cond_part = cond_part + nt(grads.astype(bf16), r.wada_in[k])
    r.cps[...] = cond_part
    c_in = sems(2)
    r.cpr[mp] = cond_part
    for step in range(1, 4):
        start(r.cps, r.cpr.at[mp], c_in, c_in + 1, (dp, mp ^ step))
    sent(r.cpr.at[pl.ds(0, 3)], c_in)
    for k in range(6):
        grads = r.mod_all[k]
        r.gada[k] = tn(silu_own, grads.astype(bf16))
        r.gbada[k : k + 1, :] = jnp.sum(grads, axis=0, keepdims=True)
    totals = r.grec[0, 6]
    for i in range(1, 8):
        totals = totals + r.grec[i, 6]
    r.gqg[...] = totals[:, 0:72]
    r.gkg[...] = totals[:, 72:144]
    ratio = totals[:, 144:147] / (totals[:, 147:148] * 1152.0)
    r.stats[...] = jnp.sqrt(ratio)
    arrived(r.cpr.at[pl.ds(0, 3)], c_in + 1)
    cond_sum = r.cpr[0] + r.cpr[1] + r.cpr[2] + r.cpr[3]
    for i in range(8):
        r.cts[i] = cond_sum[i : i + 1, :]
    r.ctr[dp] = r.cts[dp]
    ct_in = to_others(lambda i: r.cts.at[i], r.ctr.at[dp], r.ctr.at[pl.ds(0, 7)])

    for k in range(3):
        grad = reduce_end(f"c{k}")
        lanes = slice(256 * k, 256 * k + 256)
        r.ggu[:, 0, lanes] = grad[:, 0:256]
        r.ggu[:, 1, lanes] = grad[:, 256:512]
        r.gdn[:, lanes] = grad[:, 512:768]
    arrived(r.br, kept[1])
    r.outt[0:256, :] = tn(r.br[...], r.place[...]).astype(bf16)
    grad = reduce_end("qkv")
    for p in range(3):
        r.gqkv[p] = grad[:, 288 * p : 288 * p + 288]
    r.gout[:, 0:32] = grad[:, 864:896]
    r.gout[:, 32:288] = reduce_end("out")
    arrived(r.bgr, bg_in)
    main, rest = unfold(r.bgr)
    rest = tn(rest, r.place[...]).astype(bf16)
    r.gint[0:256, :] = tn(main, r.place[...]).astype(bf16)
    r.gint[256:288, :] = rest[0:32, :]
    r.outt[256:288, :] = rest[32:64, :]
    arrived(r.ctr.at[pl.ds(0, 7)], ct_in)
    for s in range(8):
        r.gcond[0:1, 144 * s : 144 * s + 144] = r.ctr[s]
    cond = r.cond[...].astype(f32)
    sig_c = jax.nn.sigmoid(cond)
    r.gcond[...] = r.gcond[...] * sig_c * (1.0 + cond * (1.0 - sig_c))
    for finish in pending:
        finish()
    assert taken[0] == 132


def copy_out(*refs):
    count = len(refs) // 2
    sem = refs[-1]
    copies = [pltpu.make_async_copy(refs[i], refs[count + i], sem.at[i]) for i in range(count)]
    for copy in copies:
        copy.start()
    for copy in copies:
        copy.wait()


def body_kernel(
    x_src, cotangent, route_dest, route_count, item_grid, noise_bin, cond, w_ada, b_ada,
    w_qkv, q_gain, k_gain, w_out, w_gu, w_down,
):
    scratch = scratch_list()
    vmem = pl.BlockSpec(memory_space=pltpu.VMEM)
    smem = pl.BlockSpec(memory_space=pltpu.SMEM)
    far = pl.BlockSpec(memory_space=pl.ANY)
    shapes = [
        ((288, 512), bf16), ((288, 512), bf16), ((1, 1152), f32), ((6, 144, 288), f32),
        ((6, 288), f32), ((3, 144, 288), f32), ((1, 72), f32), ((1, 72), f32),
        ((144, 288), f32), ((144, 2, 768), f32), ((144, 768), f32), ((1, 3), f32),
    ]
    outs = pl.pallas_call(
        functools.partial(block_kernel, list(scratch)),
        out_shape=[pltpu.VMEM(s, d) for s, d in shapes],
        in_specs=[vmem, vmem, vmem, smem, smem, smem, vmem, far, vmem, far, vmem, vmem, vmem, far, far],
        out_specs=[vmem] * len(shapes),
        scratch_shapes=list(scratch.values()),
        compiler_params=pltpu.CompilerParams(
            has_side_effects=True, vmem_limit_bytes=57500000, collective_id=0
        ),
        name="block",
    )(
        x_src.T, cotangent.T, route_dest.reshape(1, SRC_CAP), route_count, item_grid, noise_bin,
        cond, jnp.transpose(w_ada, (1, 0, 2)), b_ada, jnp.transpose(w_qkv, (1, 0, 2)),
        q_gain.reshape(1, DH), k_gain.reshape(1, DH), w_out.T, w_gu, w_down.T,
    )
    outs = pl.pallas_call(
        copy_out,
        out_shape=[jax.ShapeDtypeStruct(s, d) for s, d in shapes],
        in_specs=[vmem] * len(shapes),
        out_specs=[pl.BlockSpec(memory_space=pl.ANY)] * len(shapes),
        scratch_shapes=[pltpu.SemaphoreType.DMA((len(shapes),))],
        compiler_params=pltpu.CompilerParams(vmem_limit_bytes=2000000),
        name="store",
    )(*outs)
    (outt, gint, gcond, gada, gbada, gqkv, gqg, gkg, gout, ggu, gdn, stats) = outs
    return (
        outt.T, gint.T, gcond, jnp.transpose(gada, (1, 0, 2)), gbada,
        jnp.transpose(gqkv, (1, 0, 2)), gqg.reshape(DH), gkg.reshape(DH), gout.T, ggu, gdn.T,
        stats.reshape(3),
    )


def solution(mesh):
    one_kernel = mesh.shape["dp"] == 8 and mesh.shape["mp"] == 4
    return jax.shard_map(
        body_kernel if one_kernel else body,
        mesh=mesh,
        in_specs=(
            P("dp", "mp"),
            P("dp", "mp"),
            P("dp"),
            P("dp"),
            P("dp", None),
            P("dp"),
            P("dp", None),
            P("dp", None, "mp"),
            P(None, "mp"),
            P("dp", None, "mp"),
            P(),
            P(),
            P("mp", "dp"),
            P("dp", None, "mp"),
            P("mp", "dp"),
        ),
        out_specs=(
            P("dp", "mp"),
            P("dp", "mp"),
            P("dp", None),
            P("dp", None, "mp"),
            P(None, "mp"),
            P("dp", None, "mp"),
            P(),
            P(),
            P("mp", "dp"),
            P("dp", None, "mp"),
            P("mp", "dp"),
            P(),
        ),
        check_vma=False,
    )
```
